32 devices in a mesh: wide: 8 (over z, x), narrow: 4 (over y, core).
Axes of the slice: x: 2, y: 2, z: 4, core: 2. Of those that a mesh axis runs over, the one named last changes fastest.
Arguments:
- query_states: bfloat16 [2, 128, 32, 768], P(None, ('wide', 'narrow')), may hold values from -6 to 6
- passage_states: bfloat16 [2, 32, 512, 768], P(None, ('narrow', 'wide')), may hold values from -6 to 6
- lengths: int32 [2, 32], replicated, may hold values from 1 to 512, 8192 in all within a row
- positives: int32 [2, 128], replicated, may hold values from 0 to 31
- query_weight: bfloat16 [768, 768], replicated, may hold values from -0.21875 to 0.21875
- query_bias: bfloat16 [768], replicated, may hold values from -3 to 3
- key_weight: bfloat16 [768, 768], replicated, may hold values from -0.21875 to 0.21875
- value_weight: bfloat16 [768, 768], replicated, may hold values from -0.21875 to 0.21875
- value_bias: bfloat16 [768], replicated, may hold values from -3 to 3
- out_weight: bfloat16 [768, 768], replicated, may hold values from -0.875 to 0.875
- out_bias: bfloat16 [768], replicated, may hold values from -3 to 3
- first_gain: bfloat16 [768], replicated, may hold values from 0.099609375 to 1.8984375
- first_shift: bfloat16 [768], replicated, may hold values from -2 to 2
- inner_weight: bfloat16 [768, 3072], replicated, may hold values from -0.21875 to 0.21875
- inner_bias: bfloat16 [3072], replicated, may hold values from -3 to 3
- outer_weight: bfloat16 [3072, 768], replicated, may hold values from -0.109375 to 0.109375
- outer_bias: bfloat16 [768], replicated, may hold values from -3 to 3
- second_gain: bfloat16 [768], replicated, may hold values from 0.099609375 to 1.8984375
- second_shift: bfloat16 [768], replicated, may hold values from -2 to 2
- linear_weight: bfloat16 [768, 128], replicated, may hold values from -0.21875 to 0.21875
Outputs:
- scores: float32 [2, 128, 32], P(None, 'wide', 'narrow')
- losses: float32 [2, 128], P(None, 'wide')
- query_states_gradient: float32 [2, 128, 32, 768], P(None, ('wide', 'narrow'))
- passage_states_gradient: float32 [2, 32, 512, 768], P(None, ('narrow', 'wide'))
- query_weight_gradient: float32 [768, 768], P('wide')
- query_bias_gradient: float32 [768], P('wide')
- key_weight_gradient: float32 [768, 768], P('wide')
- value_weight_gradient: float32 [768, 768], P('wide')
- value_bias_gradient: float32 [768], P('wide')
- out_weight_gradient: float32 [768, 768], P('wide')
- out_bias_gradient: float32 [768], P('wide')
- first_gain_gradient: float32 [768], P('wide')
- first_shift_gradient: float32 [768], P('wide')
- inner_weight_gradient: float32 [768, 3072], P('wide')
- inner_bias_gradient: float32 [3072], P('wide')
- outer_weight_gradient: float32 [3072, 768], P('wide')
- outer_bias_gradient: float32 [768], P('wide')
- second_gain_gradient: float32 [768], P('wide')
- second_shift_gradient: float32 [768], P('wide')
- linear_weight_gradient: float32 [768, 128], P('wide')
The draws below stay inside these ranges and needn't reach their ends.
Inputs may be any that keep to these rules, and one draw needn't show every extreme that they name: In each micro-batch the lengths sum to 8192, and the largest is 512.
All inputs are finite; a program needn't handle non-finite values.
Results may differ from the reference program's by a relative error of at most 0.02.
Values may be sent and summed in bfloat16 or wider, within the bound.
A program may use at most 320 MiB of HBM per device.

```python
import math
import jax
import jax.numpy as jnp
import numpy as np
from jax import lax

D = 768
HEADS = 12
FF = 3072
EMBED = 128
QUERY_LEN = 32
PASSAGE_LEN = 512
MICRO = 2
QUERIES = 128
PASSAGES = 32


def plant(array, own_key, smallest, high):
    index_at = [jax.random.randint(jax.random.fold_in(own_key, axis), (), 0, length) for axis, length in enumerate(array.shape)]
    widest = array.shape.index(max(array.shape))
    next_to = index_at[:widest] + [(index_at[widest] + 1) % array.shape[widest]] + index_at[widest + 1:]
    return array.at[tuple(index_at)].set(smallest).at[tuple(next_to)].set(high)


def steps_of(own_key, dims, shards, least, high):
    loudness, own = 1.0, jax.random.fold_in(own_key, 6)
    for position, parts in shards:
        draws = jnp.exp(jax.random.uniform(jax.random.fold_in(own, position), (parts,), jnp.float32, least / len(shards), high / len(shards)))
        loudness = loudness * jnp.repeat(draws, dims[position] // parts).reshape([-1 if axis == position else 1 for axis in range(len(dims))])
    return loudness


def split_up(number_of, total, reach, slope):
    portions = [(1 << 20) // math.isqrt(rank ** slope) + 1 for rank in range(2, number_of + 1)]
    spare, counts = total - reach - (number_of - 1), [1] * (number_of - 1)
    while spare > 0:
        candidates = [i for i in range(number_of - 1) if counts[i] < reach]
        whole, remaining = sum([portions[i] for i in candidates]), spare
        for i in candidates:
            addition = min(reach - counts[i], max(1, remaining * portions[i] // whole), spare)
            counts[i] = counts[i] + addition
            spare = spare - addition
    return np.array([reach] + counts)


def ragged(rng, amount, total, limit, lean):
    if amount == 2:
        one = jax.random.randint(rng, (), max(1, total - limit), min(limit, total - 1) + 1)
        return jnp.stack([one, total - one])
    sizes = jnp.asarray(split_up(amount, total, limit, lean), jnp.int32)
    twos = (amount - 1) // 2
    donor, receiver = sizes[1:1 + 2 * twos:2], sizes[2:2 + 2 * twos:2]
    margin = jnp.minimum(donor - 1, limit - receiver)
    passed = jax.random.randint(jax.random.fold_in(rng, 1), (twos,), 0, 1 << 20) % (margin + 1)
    sizes = sizes.at[1:1 + 2 * twos:2].set(donor - passed).at[2:2 + 2 * twos:2].set(receiver + passed)
    return sizes[jax.random.permutation(jax.random.fold_in(rng, 2), amount)]


def centred(stream_key, extent, scale, most, split=(), kind=jnp.bfloat16):
    drawn = jax.random.normal(stream_key, extent, jnp.float32) * scale
    if len(split) > 0:
        drawn = steps_of(stream_key, extent, split, -0.22, 0.18) * drawn
    return jnp.clip(drawn, min=-most, max=most).astype(kind)


def setup_inputs(seed: int = 0) -> dict:
    key_list = jax.random.split(jax.random.key(seed), 21)
    return {
        "query_states": centred(key_list[0], (MICRO, QUERIES, QUERY_LEN, D), 1.0, 6.0, ((1, 32),)),
        "passage_states": centred(key_list[1], (MICRO, PASSAGES, PASSAGE_LEN, D), 1.0, 6.0, ((1, 32),)),
        "lengths": jax.vmap(lambda own: ragged(own, PASSAGES, PASSAGES * PASSAGE_LEN // 2, PASSAGE_LEN, 2))(jax.random.split(key_list[2], MICRO)).reshape((MICRO, PASSAGES)).astype(jnp.int32),
        "positives": plant(jax.random.randint(key_list[3], (MICRO, QUERIES), 0, PASSAGES), jax.random.fold_in(key_list[3], 1), 0, PASSAGES - 1).astype(jnp.int32),
        "query_weight": centred(key_list[4], (D, D), D ** -0.5, 0.21875),
        "query_bias": centred(key_list[5], (D,), 0.5, 3.0),
        "key_weight": centred(key_list[6], (D, D), D ** -0.5, 0.21875),
        "value_weight": centred(key_list[7], (D, D), D ** -0.5, 0.21875),
        "value_bias": centred(key_list[8], (D,), 0.5, 3.0),
        "out_weight": centred(key_list[9], (D, D), (D // 16) ** -0.5, 0.875),
        "out_bias": centred(key_list[10], (D,), 0.5, 3.0),
        "first_gain": jnp.clip(1.0 + 0.18 * jax.random.normal(key_list[11], (D,), jnp.float32), 0.099609375, 1.8984375).astype(jnp.bfloat16),
        "first_shift": centred(key_list[12], (D,), 0.3, 2.0),
        "inner_weight": centred(key_list[13], (D, FF), D ** -0.5, 0.21875),
        "inner_bias": centred(key_list[14], (FF,), 0.5, 3.0),
        "outer_weight": centred(key_list[15], (FF, D), FF ** -0.5, 0.109375),
        "outer_bias": centred(key_list[16], (D,), 0.5, 3.0),
        "second_gain": jnp.clip(1.0 + 0.18 * jax.random.normal(key_list[17], (D,), jnp.float32), 0.099609375, 1.8984375).astype(jnp.bfloat16),
        "second_shift": centred(key_list[18], (D,), 0.3, 2.0),
        "linear_weight": centred(key_list[19], (D, EMBED), D ** -0.5, 0.21875),
    }


@jax.custom_vjp
def low(v):
    return lax.optimization_barrier(v.astype(jnp.bfloat16)).astype(jnp.float32)

@jax.custom_vjp
def low_back(v):
    return v

def low_keep(v):
    return (low(v), None)

def low_pass(kept, grad):
    return (grad,)

def back_keep(v):
    return (v, None)

def back_low(kept, grad):
    return (low(grad),)
low.defvjp(low_keep, low_pass)
low_back.defvjp(back_keep, back_low)
SHARP = 16.0
LAYER_EPS = 1e-12
NORM_EPS = 1e-06
MASKED = -1e+30
HIGHEST = lax.Precision.HIGHEST

def layer_norm(field, norm_gain, norm_shift):
    center = field - lax.optimization_barrier(jnp.mean(field, axis=-1, keepdims=True))
    spread = lax.optimization_barrier(jnp.mean(center * center, axis=-1, keepdims=True))
    return center * lax.rsqrt(spread + LAYER_EPS) * norm_gain + norm_shift

def encode(params, states, valid_keys):
    query_weight, query_bias, key_weight, value_weight, value_bias, out_weight, out_bias, first_gain, first_shift, inner_weight, inner_bias, outer_weight, outer_bias, second_gain, second_shift, linear_weight = params
    sequences, length, model_width = states.shape
    head_dim = model_width // HEADS
    score_scale = head_dim ** (-0.5)
    head_shape = (sequences, length, HEADS, head_dim)
    queries = low(low_back(jnp.matmul(states, query_weight, precision=HIGHEST) + query_bias))
    key_rows = low(low_back(jnp.matmul(states, key_weight, precision=HIGHEST)))
    value_rows = low(low_back(jnp.matmul(states, value_weight, precision=HIGHEST) + value_bias))
    logits = low_back(jnp.einsum('blhd,bmhd->bhlm', queries.reshape(head_shape), key_rows.reshape(head_shape), precision=HIGHEST) * score_scale)
    logits = jnp.where(valid_keys[:, None, None, :], logits, MASKED)
    attention = jax.nn.softmax(logits, axis=-1)
    context = jnp.einsum('bhlm,bmhd->blhd', low(attention), value_rows.reshape(head_shape), precision=HIGHEST)
    context = low(low_back(context.reshape(sequences, length, model_width)))
    attended = low_back(jnp.matmul(context, out_weight, precision=HIGHEST) + out_bias)
    first_norm = layer_norm(states + attended, first_gain, first_shift)
    inner_pre = low_back(jnp.matmul(low(first_norm), inner_weight, precision=HIGHEST) + inner_bias)
    activated = low(jax.nn.gelu(inner_pre, approximate=False))
    outer_out = low_back(jnp.matmul(activated, outer_weight, precision=HIGHEST) + outer_bias)
    final_norm = layer_norm(first_norm + outer_out, second_gain, second_shift)
    projected = low_back(jnp.matmul(low(final_norm), linear_weight, precision=HIGHEST))
    unit_rows = projected * lax.rsqrt(lax.optimization_barrier(jnp.sum(projected * projected, axis=-1, keepdims=True)) + NORM_EPS)
    return low(unit_rows)

def reference(query_states, passage_states, lengths, positives, query_weight, query_bias, key_weight, value_weight, value_bias, out_weight, out_bias, first_gain, first_shift, inner_weight, inner_bias, outer_weight, outer_bias, second_gain, second_shift, linear_weight):
    params = tuple((weight_in.astype(jnp.float32) for weight_in in (query_weight, query_bias, key_weight, value_weight, value_bias, out_weight, out_bias, first_gain, first_shift, inner_weight, inner_bias, outer_weight, outer_bias, second_gain, second_shift, linear_weight)))
    query_float = query_states.astype(jnp.float32)
    passage_float = passage_states.astype(jnp.float32)
    group_size = 16
    slot_positions = jnp.arange(PASSAGE_LEN, dtype=jnp.int32)
    query_valid = jnp.broadcast_to(jnp.arange(QUERY_LEN, dtype=jnp.int32)[None, :] >= 0, (group_size, QUERY_LEN))

    def forward(params, query_float, passage_float):
        score_list = []
        loss_list = []
        for micro_step in range(MICRO):

            def encode_queries(query_group):
                return encode(params, query_group, query_valid)
            query_groups = query_float[micro_step].reshape(QUERIES // group_size, group_size, QUERY_LEN, D)
            query_embed = lax.map(jax.checkpoint(encode_queries), query_groups)
            lengths_now = lengths[micro_step]

            def encode_passage(item):
                states_one, length_one = item
                valid_keys = slot_positions[None, :] < length_one
                return encode(params, states_one[None], valid_keys)[0]
            passage_embed = lax.map(jax.checkpoint(encode_passage), (passage_float[micro_step], lengths_now))
            query_flat = query_embed.reshape(QUERIES * QUERY_LEN, EMBED)

            def score_passage(item):
                embed_one, length_one = item
                sims = low_back(jnp.matmul(query_flat, embed_one.T, precision=HIGHEST))
                sharpened = jnp.where(slot_positions[None, :] < length_one, SHARP * sims, MASKED)
                token_best = jax.nn.logsumexp(sharpened, axis=1) / SHARP
                return lax.optimization_barrier(jnp.sum(token_best.reshape(QUERIES, QUERY_LEN), axis=1))
            scores_now = lax.map(jax.checkpoint(score_passage), (passage_embed, lengths_now)).T
            total_log = jax.nn.logsumexp(scores_now, axis=1)
            picked = jnp.take_along_axis(scores_now, positives[micro_step][:, None], axis=1)[:, 0]
            score_list.append(scores_now)
            loss_list.append(total_log - picked)
        scores_all = jnp.stack(score_list)
        losses_all = jnp.stack(loss_list)
        return (jnp.sum(losses_all), (scores_all, losses_all))
    objective, pullback, aux_out = jax.vjp(forward, params, query_float, passage_float, has_aux=True)
    param_grads, query_gradient, passage_gradient = pullback(jnp.ones_like(objective))
    return (aux_out[0], aux_out[1], query_gradient, passage_gradient, param_grads[0], param_grads[1], param_grads[2], param_grads[3], param_grads[4], param_grads[5], param_grads[6], param_grads[7], param_grads[8], param_grads[9], param_grads[10], param_grads[11], param_grads[12], param_grads[13], param_grads[14], param_grads[15])
```

```python
import functools

import jax
import jax.numpy as jnp
from jax import lax
from jax.experimental import pallas as pl
from jax.experimental.pallas import tpu as pltpu
from jax.sharding import PartitionSpec as P

HEADS = 12
HEAD_DIM = 64
SHARP = 16.0
LAYER_EPS = 1e-12
NORM_EPS = 1e-06
MASKED = -1e30
SLOPE_CONST = 0.3989422804014327
ROOT_HALF = 0.7071067811865476
BF16 = jnp.bfloat16
F32 = jnp.float32
VMEM_LIMIT = 62 * 1024 * 1024

NN = (((1,), (0,)), ((), ()))
NT = (((1,), (1,)), ((), ()))
TN = (((0,), (0,)), ((), ()))


def mm(left, right, dims=NN):
    return lax.dot_general(left, right, dims, preferred_element_type=F32)


ANY = pl.BlockSpec(memory_space=pl.ANY)

ROW_BQ, ROW_BV, ROW_BO, ROW_G1, ROW_S1, ROW_B2, ROW_G2, ROW_S2, ROW_BI = range(9)


def vec_row(vec_ref, row):
    return vec_ref[row : row + 1, :]


def mean_row(value):
    return jnp.sum(value, axis=-1, keepdims=True) * (1.0 / value.shape[-1])


class Loader:
    def __init__(self, sources, targets, sem):
        self.copies = [
            pltpu.make_async_copy(source, target, sem.at[index])
            for index, (source, target) in enumerate(zip(sources, targets))
        ]
        self.first = pl.program_id(0) == 0

    def start(self):
        @pl.when(self.first)
        def _():
            for copy in self.copies:
                copy.start()

    def need(self, *indices):
        @pl.when(self.first)
        def _():
            for index in indices:
                self.copies[index].wait()


def fwd_kernel(grouped, alias_count, *refs):
    lens_ref, x_ref, vec_ref = refs[:3]
    sources = refs[3:10]
    refs = refs[10 + alias_count :]
    (
        q_ref,
        k_ref,
        v_ref,
        att_ref,
        ctx_ref,
        n1_ref,
        r1_ref,
        first_ref,
        act_ref,
        slope_ref,
        n2_ref,
        r2_ref,
        final_ref,
        unit_ref,
        uinv_ref,
        embed_ref,
    ) = refs[:16]
    wq, wk, wv, wo, wi, w2, wl, sem, acc_ref = refs[16:]
    loader = Loader(sources, (wq, wk, wv, wo, wi, w2, wl), sem)
    loader.start()
    rows = x_ref.shape[0]
    x = x_ref[...]
    scale = HEAD_DIM ** (-0.5)
    loader.need(0)
    q_ref[...] = ((mm(x, wq[...]) + vec_row(vec_ref, ROW_BQ)).astype(BF16) * scale).astype(BF16)
    loader.need(1)
    k_ref[...] = mm(x, wk[...]).astype(BF16)
    loader.need(2)
    v_ref[...] = (mm(x, wv[...]) + vec_row(vec_ref, ROW_BV)).astype(BF16)
    if grouped:
        valid = (
            lax.broadcasted_iota(jnp.int32, (rows, rows), 0) // grouped
            == lax.broadcasted_iota(jnp.int32, (rows, rows), 1) // grouped
        )
    else:
        length = lens_ref[pl.program_id(0)]
        valid = lax.broadcasted_iota(jnp.int32, (1, rows), 1) < length
    bias = jnp.where(valid, 0.0, MASKED)
    low_half = lax.broadcasted_iota(jnp.int32, (rows, 128), 1) < HEAD_DIM

    def pair_body(pair, carry):
        cols = pl.ds(pl.multiple_of(pair * 128, 128), 128)
        q_pair, k_pair, v_pair = q_ref[:, cols], k_ref[:, cols], v_ref[:, cols]
        parts = []
        for half in range(2):
            mask = low_half if half == 0 else jnp.logical_not(low_half)
            logits = mm(jnp.where(mask, q_pair, jnp.zeros_like(q_pair)), k_pair, NT) + bias
            peak = jnp.max(logits, axis=-1, keepdims=True)
            e = jnp.exp(logits - peak)
            inv = 1.0 / jnp.sum(e, axis=-1, keepdims=True)
            low = (e * inv).astype(BF16)
            att_ref[0, 2 * pair + half] = low
            parts.append(mm(low, v_pair))
        ctx_ref[:, cols] = jnp.where(low_half, parts[0], parts[1]).astype(BF16)
        return carry

    lax.fori_loop(0, HEADS // 2, pair_body, 0)
    loader.need(3)
    field = x.astype(F32) + (mm(ctx_ref[...], wo[...]) + vec_row(vec_ref, ROW_BO))
    center = field - mean_row(field)
    inverse = lax.rsqrt(mean_row(center * center) + LAYER_EPS)
    normed = center * inverse
    n1_ref[...] = normed.astype(BF16)
    r1_ref[...] = jnp.broadcast_to(inverse, r1_ref.shape)
    first = normed * vec_row(vec_ref, ROW_G1) + vec_row(vec_ref, ROW_S1)
    first_ref[...] = first.astype(BF16)
    acc_ref[...] = first + vec_row(vec_ref, ROW_B2)
    loader.need(4, 5)
    width = x.shape[1]

    def chunk_body(chunk, carry):
        cols = pl.ds(pl.multiple_of(chunk * width, width), width)
        inner = mm(first_ref[...], wi[:, cols]) + vec_ref[pl.ds(ROW_BI + chunk, 1), :]
        phi = 0.5 * (1.0 + lax.erf(inner * ROOT_HALF))
        activated = (inner * phi).astype(BF16)
        act_ref[:, cols] = activated
        slope_ref[:, cols] = (phi + inner * jnp.exp(-0.5 * inner * inner) * SLOPE_CONST).astype(
            BF16
        )
        acc_ref[...] += mm(activated, w2[cols, :])
        return carry

    lax.fori_loop(0, wi.shape[1] // width, chunk_body, 0)
    field = acc_ref[...]
    center = field - mean_row(field)
    inverse = lax.rsqrt(mean_row(center * center) + LAYER_EPS)
    normed = center * inverse
    n2_ref[...] = normed.astype(BF16)
    r2_ref[...] = jnp.broadcast_to(inverse, r2_ref.shape)
    final = (normed * vec_row(vec_ref, ROW_G2) + vec_row(vec_ref, ROW_S2)).astype(BF16)
    final_ref[...] = final
    loader.need(6)
    projected = mm(final, wl[...])
    uinv = lax.rsqrt(jnp.sum(projected * projected, axis=-1, keepdims=True) + NORM_EPS)
    unit = projected * uinv
    unit_ref[...] = unit
    uinv_ref[...] = jnp.broadcast_to(uinv, uinv_ref.shape)
    embed_ref[...] = unit.astype(BF16)


def encode(x, lens, vec, weights, blocks, grouped, total, offset, earlier):
    rows = x.shape[0] // blocks
    width = x.shape[1]
    wide = weights[4].shape[1]
    embed_width = weights[6].shape[1]
    base = offset // rows

    def row_spec(columns):
        return pl.BlockSpec((rows, columns), lambda i, lens: (base + i, 0))

    def own_spec(columns):
        return pl.BlockSpec((rows, columns), lambda i, lens: (i, 0))

    def shape(count, columns, dtype):
        return jax.ShapeDtypeStruct((count, columns), dtype)

    own = x.shape[0]
    out_shapes = [
        shape(own, width, BF16),
        shape(own, width, BF16),
        shape(own, width, BF16),
        jax.ShapeDtypeStruct((blocks, HEADS, rows, rows), BF16),
        shape(total, width, BF16),
        shape(own, width, BF16),
        shape(own, embed_width, F32),
        shape(total, width, BF16),
        shape(total, wide, BF16),
        shape(own, wide, BF16),
        shape(own, width, BF16),
        shape(own, embed_width, F32),
        shape(total, width, BF16),
        shape(own, embed_width, F32),
        shape(own, embed_width, F32),
        shape(own, embed_width, BF16),
    ]
    shared = (4, 7, 8, 12)
    out_specs = [
        pl.BlockSpec((1, HEADS, rows, rows), lambda i, lens: (i, 0, 0, 0))
        if index == 3
        else (row_spec if index in shared else own_spec)(out.shape[1])
        for index, out in enumerate(out_shapes)
    ]
    aliased = [] if earlier is None else [earlier[index] for index in shared]
    return pl.pallas_call(
        functools.partial(fwd_kernel, grouped, len(aliased)),
        out_shape=out_shapes,
        grid_spec=pltpu.PrefetchScalarGridSpec(
            num_scalar_prefetch=1,
            grid=(blocks,),
            in_specs=[
                own_spec(width),
                pl.BlockSpec(vec.shape, lambda i, lens: (0, 0)),
            ]
            + [ANY] * (7 + len(aliased)),
            out_specs=out_specs,
            scratch_shapes=[pltpu.VMEM(weight.shape, BF16) for weight in weights]
            + [pltpu.SemaphoreType.DMA((7,)), pltpu.VMEM((rows, width), F32)],
        ),
        input_output_aliases={10 + index: shared[index] for index in range(len(aliased))},
        compiler_params=pltpu.CompilerParams(vmem_limit_bytes=VMEM_LIMIT),
        name="encode_queries" if grouped else "encode_passages",
    )(lens, x, vec, *weights, *aliased)


def sims_kernel(lens_ref, q_ref, p_ref, e_ref, z_ref):
    count = q_ref.shape[0]
    tokens = count * q_ref.shape[2]
    query = q_ref[...].reshape(tokens, q_ref.shape[3])
    sims = mm(p_ref[0], query, NT)
    slot = lax.broadcasted_iota(jnp.int32, sims.shape, 0)
    e = jnp.where(slot < lens_ref[pl.program_id(0)], jnp.exp(SHARP * sims - SHARP), 0.0)
    e_ref[0] = e.astype(BF16)
    z = jnp.sum(e, axis=0, keepdims=True)
    step = q_ref.shape[2]
    for index in range(count):
        z_ref[0, index : index + 1, :] = z[:, index * step : (index + 1) * step]


def sims_back_kernel(e_ref, w_ref, q_ref, p_ref, gp_ref, gq_ref):
    count = q_ref.shape[0]
    step = q_ref.shape[2]
    query = q_ref[...].reshape(count * step, q_ref.shape[3])
    weight = jnp.concatenate([w_ref[0, index : index + 1, :] for index in range(count)], axis=1)
    grads = (e_ref[0].astype(F32) * weight).astype(BF16)
    part = mm(grads, query)

    @pl.when(pl.program_id(1) == 0)
    def _():
        gp_ref[0] = part

    @pl.when(pl.program_id(1) > 0)
    def _():
        gp_ref[0] += part

    gq_ref[...] = mm(grads, p_ref[0], TN).astype(BF16).reshape(gq_ref.shape)


def similarity(queries, passages, lens):
    devices, micro, tokens, width = queries.shape
    slots = passages.shape[1]
    group = 8
    e, z = pl.pallas_call(
        sims_kernel,
        out_shape=(
            jax.ShapeDtypeStruct((micro, slots, devices * tokens), BF16),
            jax.ShapeDtypeStruct((micro, devices, tokens), F32),
        ),
        grid_spec=pltpu.PrefetchScalarGridSpec(
            num_scalar_prefetch=1,
            grid=(micro, devices // group),
            in_specs=[
                pl.BlockSpec((group, 1, tokens, width), lambda m, b, lens: (b, m, 0, 0)),
                pl.BlockSpec((1, slots, width), lambda m, b, lens: (m, 0, 0)),
            ],
            out_specs=(
                pl.BlockSpec((1, slots, group * tokens), lambda m, b, lens: (m, 0, b)),
                pl.BlockSpec((1, group, tokens), lambda m, b, lens: (m, b, 0)),
            ),
        ),
        compiler_params=pltpu.CompilerParams(vmem_limit_bytes=VMEM_LIMIT),
        name="similarity",
    )(lens, queries, passages)
    return e, z


def similarity_back(e, weights, queries, passages):
    devices, micro, tokens, width = queries.shape
    slots = passages.shape[1]
    group = 8
    return pl.pallas_call(
        sims_back_kernel,
        out_shape=(
            jax.ShapeDtypeStruct((micro, slots, width), F32),
            jax.ShapeDtypeStruct((devices, micro, tokens, width), BF16),
        ),
        grid=(micro, devices // group),
        in_specs=[
            pl.BlockSpec((1, slots, group * tokens), lambda m, b: (m, 0, b)),
            pl.BlockSpec((1, group, tokens), lambda m, b: (m, b, 0)),
            pl.BlockSpec((group, 1, tokens, width), lambda m, b: (b, m, 0, 0)),
            pl.BlockSpec((1, slots, width), lambda m, b: (m, 0, 0)),
        ],
        out_specs=(
            pl.BlockSpec((1, slots, width), lambda m, b: (m, 0, 0)),
            pl.BlockSpec((group, 1, tokens, width), lambda m, b: (b, m, 0, 0)),
        ),
        compiler_params=pltpu.CompilerParams(vmem_limit_bytes=VMEM_LIMIT),
        name="similarity_back",
    )(e, weights, queries, passages)


def accumulate(ref, row, value):
    ref[row : row + 1, :] += jnp.sum(value, axis=0, keepdims=True)


def mlp_back_kernel(alias_count, *refs):
    (
        ge_ref,
        unit_ref,
        uinv_ref,
        n2_ref,
        r2_ref,
        slope_ref,
        n1_ref,
        r1_ref,
        vec_ref,
    ) = refs[:9]
    sources = refs[9:12]
    refs = refs[12 + alias_count :]
    gp_ref, go_ref, gi_ref, gh_ref, ga_ref, sums_ref = refs[:6]
    wl, w2, wi, sem, acc_ref = refs[6:]
    loader = Loader(sources, (wl, w2, wi), sem)
    loader.start()

    @pl.when(loader.first)
    def _():
        sums_ref[...] = jnp.zeros_like(sums_ref)

    grad = ge_ref[...]
    unit = unit_ref[...]
    projected_low = (
        uinv_ref[...] * (grad - unit * jnp.sum(grad * unit, axis=-1, keepdims=True))
    ).astype(BF16)
    gp_ref[...] = projected_low
    loader.need(0)
    grad_final = mm(projected_low, wl[...], NT)
    normed = n2_ref[...].astype(F32)
    accumulate(sums_ref, ROW_G2, grad_final * normed)
    accumulate(sums_ref, ROW_S2, grad_final)
    scaled = grad_final * vec_row(vec_ref, ROW_G2)
    grad_second = r2_ref[:, :1] * (scaled - mean_row(scaled) - normed * mean_row(scaled * normed))
    outer_low = grad_second.astype(BF16)
    go_ref[...] = outer_low
    accumulate(sums_ref, ROW_B2, outer_low.astype(F32))
    acc_ref[...] = grad_second
    loader.need(1, 2)
    width = go_ref.shape[1]

    def chunk_body(chunk, carry):
        cols = pl.ds(pl.multiple_of(chunk * width, width), width)
        grad_act = mm(go_ref[...], w2[cols, :], NT)
        inner = (grad_act * slope_ref[:, cols].astype(F32)).astype(BF16)
        gi_ref[:, cols] = inner
        sums_ref[pl.ds(ROW_BI + chunk, 1), :] += jnp.sum(
            inner.astype(F32), axis=0, keepdims=True
        )
        acc_ref[...] += mm(inner, wi[:, cols], NT)
        return carry

    lax.fori_loop(0, wi.shape[1] // width, chunk_body, 0)
    grad_first = acc_ref[...]
    normed = n1_ref[...].astype(F32)
    accumulate(sums_ref, ROW_G1, grad_first * normed)
    accumulate(sums_ref, ROW_S1, grad_first)
    scaled = grad_first * vec_row(vec_ref, ROW_G1)
    hidden = r1_ref[:, :1] * (scaled - mean_row(scaled) - normed * mean_row(scaled * normed))
    gh_ref[...] = hidden
    low = hidden.astype(BF16)
    ga_ref[...] = low
    accumulate(sums_ref, ROW_BO, low.astype(F32))


def mlp_back(grad_embed, kept, vec, weights, blocks, total, offset, earlier):
    own = grad_embed.shape[0]
    rows = own // blocks
    base = offset // rows
    _, _, _, _, wi, w2, wl = weights
    width, wide = wi.shape
    embed_width = wl.shape[1]

    def row_spec(columns):
        return pl.BlockSpec((rows, columns), lambda i: (base + i, 0))

    def own_spec(columns):
        return pl.BlockSpec((rows, columns), lambda i: (i, 0))

    args = [grad_embed] + [kept[index] for index in (13, 14, 10, 11, 9, 5, 6)]
    out_shapes = [
        jax.ShapeDtypeStruct((total, embed_width), BF16),
        jax.ShapeDtypeStruct((total, width), BF16),
        jax.ShapeDtypeStruct((total, wide), BF16),
        jax.ShapeDtypeStruct((own, width), F32),
        jax.ShapeDtypeStruct((total, width), BF16),
        jax.ShapeDtypeStruct((16, width), F32),
    ]
    shared = (0, 1, 2, 4)
    out_specs = [
        (row_spec if index in shared else own_spec)(out.shape[1])
        for index, out in enumerate(out_shapes[:5])
    ] + [pl.BlockSpec((16, width), lambda i: (0, 0))]
    aliased = [] if earlier is None else [earlier[index] for index in shared]
    return pl.pallas_call(
        functools.partial(mlp_back_kernel, len(aliased)),
        out_shape=out_shapes,
        grid=(blocks,),
        in_specs=[own_spec(arg.shape[1]) for arg in args]
        + [pl.BlockSpec(vec.shape, lambda i: (0, 0))]
        + [ANY] * (3 + len(aliased)),
        out_specs=out_specs,
        scratch_shapes=[pltpu.VMEM(weight.shape, BF16) for weight in (wl, w2, wi)]
        + [pltpu.SemaphoreType.DMA((3,)), pltpu.VMEM((rows, width), F32)],
        input_output_aliases={12 + index: shared[index] for index in range(len(aliased))},
        compiler_params=pltpu.CompilerParams(vmem_limit_bytes=VMEM_LIMIT),
        name="mlp_back_queries" if earlier is not None else "mlp_back_passages",
    )(*args, vec, wl, w2, wi, *aliased)


def attention_back_kernel(alias_count, *refs):
    ga_ref, gh_ref, att_ref, q_ref, k_ref, v_ref = refs[:6]
    sources = refs[6:10]
    refs = refs[10 + alias_count :]
    gqkv_ref, gx_ref, sums_ref = refs[:3]
    wo, wq, wk, wv, sem, gc_ref = refs[3:]
    loader = Loader(sources, (wo, wq, wk, wv), sem)
    loader.start()

    @pl.when(loader.first)
    def _():
        sums_ref[...] = jnp.zeros_like(sums_ref)

    rows, width = gh_ref.shape
    scale = HEAD_DIM ** (-0.5)
    loader.need(0)
    gc_ref[...] = mm(ga_ref[...], wo[...], NT).astype(BF16)
    low_half = lax.broadcasted_iota(jnp.int32, (rows, 128), 1) < HEAD_DIM

    def pair_body(pair, carry):
        cols = pl.ds(pl.multiple_of(pair * 128, 128), 128)
        q_pair, k_pair, v_pair, gc_pair = q_ref[:, cols], k_ref[:, cols], v_ref[:, cols], gc_ref[:, cols]
        parts = []
        for half in range(2):
            mask = low_half if half == 0 else jnp.logical_not(low_half)
            low = att_ref[0, 2 * pair + half]
            att = low.astype(F32)
            grad_att = mm(jnp.where(mask, gc_pair, jnp.zeros_like(gc_pair)), v_pair, NT)
            weighted = grad_att * att
            grad_logits = (weighted - att * jnp.sum(weighted, axis=-1, keepdims=True)).astype(BF16)
            parts.append(
                (
                    mm(grad_logits, k_pair) * scale,
                    mm(grad_logits, q_pair, TN),
                    mm(low, gc_pair, TN),
                )
            )
        for index in range(3):
            gqkv_ref[:, pl.ds(pl.multiple_of(index * width + pair * 128, 128), 128)] = jnp.where(
                low_half, parts[0][index], parts[1][index]
            ).astype(BF16)
        return carry

    lax.fori_loop(0, HEADS // 2, pair_body, 0)
    loader.need(1, 2, 3)
    grad_q, grad_k, grad_v = (
        gqkv_ref[:, :width],
        gqkv_ref[:, width : 2 * width],
        gqkv_ref[:, 2 * width :],
    )
    accumulate(sums_ref, 0, grad_q.astype(F32))
    accumulate(sums_ref, 1, grad_v.astype(F32))
    gx_ref[...] = (
        gh_ref[...]
        + mm(grad_q, wq[...], NT)
        + mm(grad_k, wk[...], NT)
        + mm(grad_v, wv[...], NT)
    )


def attention_back(attended, hidden, kept, weights, blocks, total, offset, earlier):
    own, width = hidden.shape
    rows = own // blocks
    base = offset // rows
    wq, wk, wv, wo = weights[:4]

    def row_spec(columns):
        return pl.BlockSpec((rows, columns), lambda i: (base + i, 0))

    def own_spec(columns):
        return pl.BlockSpec((rows, columns), lambda i: (i, 0))

    aliased = [] if earlier is None else [earlier]
    return pl.pallas_call(
        functools.partial(attention_back_kernel, len(aliased)),
        out_shape=(
            jax.ShapeDtypeStruct((total, 3 * width), BF16),
            jax.ShapeDtypeStruct((own, width), F32),
            jax.ShapeDtypeStruct((8, width), F32),
        ),
        grid=(blocks,),
        in_specs=[
            row_spec(width),
            own_spec(width),
            pl.BlockSpec((1, HEADS, rows, rows), lambda i: (i, 0, 0, 0)),
            own_spec(width),
            own_spec(width),
            own_spec(width),
        ]
        + [ANY] * (4 + len(aliased)),
        out_specs=(
            row_spec(3 * width),
            own_spec(width),
            pl.BlockSpec((8, width), lambda i: (0, 0)),
        ),
        scratch_shapes=[pltpu.VMEM(weight.shape, BF16) for weight in weights[:4]]
        + [pltpu.SemaphoreType.DMA((4,)), pltpu.VMEM((rows, width), BF16)],
        input_output_aliases={10: 0} if aliased else {},
        compiler_params=pltpu.CompilerParams(vmem_limit_bytes=VMEM_LIMIT),
        name="attention_back_queries" if aliased else "attention_back_passages",
    )(attended, hidden, kept[3], kept[0], kept[1], kept[2], wo, wq, wk, wv, *aliased)


MESH = pl.DeviceIdType.MESH


def remote(source, target, sems, index, device):
    return pltpu.make_async_remote_copy(
        src_ref=source,
        dst_ref=target,
        send_sem=sems[0].at[index],
        recv_sem=sems[1].at[index],
        device_id=device,
        device_id_type=MESH,
    )


def share_kernel(n_wide, n_narrow, own_ref, all_ref, send_sem, recv_sem):
    me = lax.axis_index("narrow") * n_wide + lax.axis_index("wide")
    total = n_wide * n_narrow
    sems = (send_sem, recv_sem)

    def device(index):
        return (lax.rem(index, n_wide), index // n_wide)

    barrier = pltpu.get_barrier_semaphore()

    def signal(step, carry):
        pl.semaphore_signal(
            barrier, inc=1, device_id=device(lax.rem(me + step, total)), device_id_type=MESH
        )
        return carry

    def send(step, carry):
        target = device(lax.rem(me + step, total))
        remote(own_ref, all_ref.at[me], sems, step, target).start()
        return carry

    def wait(step, carry):
        source = lax.rem(me - step + total, total)
        copy = remote(own_ref, all_ref.at[source], sems, step, device(source))
        copy.wait_recv()
        copy.wait_send()
        return carry

    lax.fori_loop(1, total, signal, 0)
    all_ref[me] = own_ref[...]
    pl.semaphore_wait(barrier, total - 1)
    lax.fori_loop(1, total, send, 0)
    lax.fori_loop(1, total, wait, 0)


def share_scores(own, n_wide, n_narrow):
    total = n_wide * n_narrow
    return pl.pallas_call(
        functools.partial(share_kernel, n_wide, n_narrow),
        out_shape=jax.ShapeDtypeStruct((total,) + own.shape, own.dtype),
        in_specs=[pl.BlockSpec(memory_space=pltpu.VMEM)],
        out_specs=pl.BlockSpec(memory_space=pltpu.VMEM),
        scratch_shapes=[pltpu.SemaphoreType.DMA((total,))] * 2,
        compiler_params=pltpu.CompilerParams(collective_id=1, has_side_effects=True),
        name="share_scores",
    )(own)


def exchange_kernel(n_wide, n_narrow, g_ref, out_ref, half, arrived, inbox, *sems):
    pair_sems, far_sems = sems[:2], sems[2:]
    wide, narrow = lax.axis_index("wide"), lax.axis_index("narrow")
    core = lax.rem(narrow, 2)
    partner = (wide, narrow + 1 - 2 * core)
    rows = n_narrow // 2
    chips = n_wide * rows
    me = wide * rows + narrow // 2

    def device(chip):
        return (chip // rows, lax.rem(chip, rows) * 2 + core)

    barrier = pltpu.get_barrier_semaphore()

    def signal(step, carry):
        pl.semaphore_signal(
            barrier, inc=1, device_id=device(lax.rem(me + step, chips)), device_id_type=MESH
        )
        return carry

    pl.semaphore_signal(barrier, inc=1, device_id=partner, device_id_type=MESH)
    lax.fori_loop(1, chips, signal, 0)
    pl.semaphore_wait(barrier, chips)
    pair = remote(g_ref.at[:, 1 - core], arrived, pair_sems, 0, partner)
    pair.start()
    pair.wait_recv()

    def add(step, carry):
        chip = lax.rem(me + step, chips)
        total = g_ref[chip, core].astype(F32) + arrived[chip].astype(F32)
        half[chip] = total.astype(BF16)
        remote(half.at[chip], inbox.at[step], far_sems, step, device(chip)).start()
        return carry

    lax.fori_loop(1, chips, add, 0)
    out_ref[...] = g_ref[me, core].astype(F32) + arrived[me].astype(F32)

    def collect(step, carry):
        chip = lax.rem(me - step + chips, chips)
        copy = remote(half.at[chip], inbox.at[step], far_sems, step, device(chip))
        copy.wait_recv()
        copy.wait_send()
        out_ref[...] += inbox[step].astype(F32)
        return carry

    lax.fori_loop(1, chips, collect, 0)
    pair.wait_send()


def exchange(grads, n_wide, n_narrow):
    rows, width = grads.shape[1:]
    chips = n_wide * n_narrow // 2
    block = pltpu.VMEM((chips, rows, width), BF16)
    return pl.pallas_call(
        functools.partial(exchange_kernel, n_wide, n_narrow),
        out_shape=jax.ShapeDtypeStruct((rows, width), F32),
        in_specs=[pl.BlockSpec(memory_space=pltpu.VMEM)],
        out_specs=pl.BlockSpec(memory_space=pltpu.VMEM),
        scratch_shapes=[block, block, block]
        + [pltpu.SemaphoreType.DMA((1,))] * 2
        + [pltpu.SemaphoreType.DMA((chips,))] * 2,
        compiler_params=pltpu.CompilerParams(
            collective_id=2, has_side_effects=True, vmem_limit_bytes=VMEM_LIMIT
        ),
        name="exchange_query_gradients",
    )(grads.reshape(chips, 2, rows, width))


UNITS = ((0, 80), (160, 80), (80, 80), (240, 64))
SHARE_ROWS = 304


def tree_kernel(
    n_z, g_ref, out_ref, held, near, over_a, over_b, then_a, then_b, line, *sems
):
    (local_sem,) = sems[:1]
    core_sems, one_sems, two_sems, line_sems, copy_sems = (
        sems[1 + 2 * index : 3 + 2 * index] for index in range(5)
    )
    wide, narrow = lax.axis_index("wide"), lax.axis_index("narrow")
    z, x = wide // 2, lax.rem(wide, 2)
    y, core = narrow // 2, lax.rem(narrow, 2)
    mate = (wide, y * 2 + 1 - core)
    over_y = (wide, (1 - y) * 2 + core)
    over_x = (z * 2 + 1 - x, narrow)
    right, left = (wide + 2, narrow), (wide - 2, narrow)
    barrier = pltpu.get_barrier_semaphore()
    for device in (mate, over_y, over_x):
        pl.semaphore_signal(barrier, inc=1, device_id=device, device_id_type=MESH)

    @pl.when(z < n_z - 1)
    def _():
        pl.semaphore_signal(barrier, inc=1, device_id=right, device_id_type=MESH)

    @pl.when(z > 0)
    def _():
        pl.semaphore_signal(barrier, inc=1, device_id=left, device_id_type=MESH)

    inside = jnp.logical_and(z > 0, z < n_z - 1)
    pl.semaphore_wait(barrier, jnp.where(inside, 5, 4))

    def rows_of(unit):
        start, count = UNITS[unit]
        return pl.ds(start, count)

    def core_copy(unit):
        rows = rows_of(unit)
        return remote(
            g_ref.at[:, 1 - core, :, :, rows], near.at[:, :, :, rows], core_sems, unit, mate
        )

    def local_copy(unit):
        rows = rows_of(unit)
        return pltpu.make_async_copy(
            g_ref.at[:, core, :, :, rows], held.at[:, :, :, rows], local_sem.at[unit]
        )

    def one_copy(unit):
        rows = rows_of(unit)
        count = UNITS[unit][1]
        if unit % 2 == 0:
            return remote(
                held.at[1 - y, :, :, rows], over_a.at[unit // 2], one_sems, unit, over_y
            )
        return remote(
            held.at[:, :, 1 - x, rows],
            over_b.at[unit // 2, :, :, pl.ds(0, count)],
            one_sems,
            unit,
            over_x,
        )

    def two_copy(unit):
        rows = rows_of(unit)
        count = UNITS[unit][1]
        if unit % 2 == 0:
            return remote(held.at[y, :, 1 - x, rows], then_a.at[unit // 2], two_sems, unit, over_x)
        return remote(
            held.at[1 - y, :, x, rows],
            then_b.at[unit // 2, :, pl.ds(0, count)],
            two_sems,
            unit,
            over_y,
        )

    def line_copy(unit, target, way):
        rows = rows_of(unit)
        index = (unit * n_z + target) * 2 + way
        return remote(
            held.at[y, target, x, rows],
            line.at[way, target, rows],
            line_sems,
            index,
            right if way == 0 else left,
        )

    def add(target, extra):
        target[...] = (target[...].astype(F32) + extra[...].astype(F32)).astype(BF16)

    count_units = len(UNITS)
    for unit in range(count_units):
        core_copy(unit).start()
        local_copy(unit).start()
    for unit in range(count_units):
        rows = rows_of(unit)
        local_copy(unit).wait()
        core_copy(unit).wait_recv()

        def add_near(index, carry, rows=rows):
            row_y, rest = index // (n_z * 2), lax.rem(index, n_z * 2)
            at = (row_y, rest // 2, lax.rem(rest, 2), rows)
            add(held.at[at], near.at[at])
            return carry

        lax.fori_loop(0, 4 * n_z, add_near, 0)
        one_copy(unit).start()
    for unit in range(count_units):
        rows = rows_of(unit)
        count = UNITS[unit][1]
        copy = one_copy(unit)
        copy.wait_recv()

        def add_one(index, carry, rows=rows, unit=unit, count=count):
            first, second = index // 2, lax.rem(index, 2)
            if unit % 2 == 0:
                add(held.at[y, first, second, rows], over_a.at[unit // 2, first, second])
            else:
                add(
                    held.at[second, first, x, rows],
                    over_b.at[unit // 2, second, first, pl.ds(0, count)],
                )
            return carry

        lax.fori_loop(0, 2 * n_z, add_one, 0)
        two_copy(unit).start()
    for unit in range(count_units):
        rows = rows_of(unit)
        count = UNITS[unit][1]
        two_copy(unit).wait_recv()

        def add_two(index, carry, rows=rows, unit=unit, count=count):
            extra = then_a if unit % 2 == 0 else then_b
            add(held.at[y, index, x, rows], extra.at[unit // 2, index, pl.ds(0, count)])
            return carry

        lax.fori_loop(0, n_z, add_two, 0)
        for step in range(n_z - 1):
            for way in range(2):
                target = n_z - 1 - step if way == 0 else step
                sends = z < target if way == 0 else z > target
                edge = z > 0 if way == 0 else z < n_z - 1

                @pl.when(jnp.logical_and(sends, edge))
                def _(unit=unit, target=target, way=way, rows=rows):
                    line_copy(unit, target, way).wait_recv()
                    add(held.at[y, target, x, rows], line.at[way, target, rows])

                @pl.when(sends)
                def _(unit=unit, target=target, way=way):
                    line_copy(unit, target, way).start()

    def own_copy(unit, step):
        rows = rows_of(unit)
        index = unit * 3 + step
        slot = narrow if step < 2 else (1 - y) * 2 + core
        return remote(
            out_ref.at[slot, rows],
            out_ref.at[slot, rows],
            copy_sems,
            index,
            over_y if step == 1 else mate,
        )

    def arrived_copy(unit, step):
        rows = rows_of(unit)
        index = unit * 3 + step
        slot = (
            y * 2 + 1 - core,
            (1 - y) * 2 + core,
            (1 - y) * 2 + 1 - core,
        )[step]
        return remote(
            out_ref.at[slot, rows],
            out_ref.at[slot, rows],
            copy_sems,
            index,
            over_y if step == 1 else mate,
        )

    for unit in range(count_units):
        rows = rows_of(unit)
        for target in range(n_z):

            @pl.when(z == target)
            def _(unit=unit, target=target, rows=rows):
                if target > 0:
                    line_copy(unit, target, 0).wait_recv()
                    add(held.at[y, target, x, rows], line.at[0, target, rows])
                if target < n_z - 1:
                    line_copy(unit, target, 1).wait_recv()
                    add(held.at[y, target, x, rows], line.at[1, target, rows])

        out_ref[narrow, rows] = held[y, z, x, rows]
        own_copy(unit, 1).start()
        own_copy(unit, 0).start()
    for unit in range(count_units):
        arrived_copy(unit, 1).wait_recv()
        own_copy(unit, 2).start()
    for unit in range(count_units):
        arrived_copy(unit, 0).wait_recv()
        arrived_copy(unit, 2).wait_recv()
        for step in range(3):
            own_copy(unit, step).wait_send()
        core_copy(unit).wait_send()
        one_copy(unit).wait_send()
        two_copy(unit).wait_send()
        for target in range(n_z):
            for way in range(2):

                @pl.when(z < target if way == 0 else z > target)
                def _(unit=unit, target=target, way=way):
                    line_copy(unit, target, way).wait_send()


def tree(grads, n_wide):
    n_z = n_wide // 2
    width = grads.shape[-1]
    rows = SHARE_ROWS
    units = len(UNITS)
    sem = pltpu.SemaphoreType.DMA
    return pl.pallas_call(
        functools.partial(tree_kernel, n_z),
        out_shape=jax.ShapeDtypeStruct((4, rows, width), BF16),
        in_specs=[ANY],
        out_specs=pl.BlockSpec(memory_space=pltpu.VMEM),
        scratch_shapes=[
            pltpu.VMEM((2, n_z, 2, rows, width), BF16),
            pltpu.VMEM((2, n_z, 2, rows, width), BF16),
            pltpu.VMEM((2, n_z, 2, 80, width), BF16),
            pltpu.VMEM((2, 2, n_z, 80, width), BF16),
            pltpu.VMEM((2, n_z, 80, width), BF16),
            pltpu.VMEM((2, n_z, 80, width), BF16),
            pltpu.VMEM((2, n_z, rows, width), BF16),
            sem((units,)),
        ]
        + [sem((units,))] * 6
        + [sem((units * n_z * 2,))] * 2
        + [sem((units * 3,))] * 2,
        compiler_params=pltpu.CompilerParams(
            collective_id=3, has_side_effects=True, vmem_limit_bytes=VMEM_LIMIT
        ),
        name="sum_weight_gradients",
    )(grads.reshape(2, 2, n_z, 2, rows, width))


def outer(left, right):
    return lax.dot_general(left, right, TN, preferred_element_type=F32)


def local(
    query_states,
    passage_states,
    lengths,
    positives,
    query_weight,
    query_bias,
    key_weight,
    value_weight,
    value_bias,
    out_weight,
    out_bias,
    first_gain,
    first_shift,
    inner_weight,
    inner_bias,
    outer_weight,
    outer_bias,
    second_gain,
    second_shift,
    linear_weight,
):
    everyone = ("wide", "narrow")
    n_wide = lax.axis_size("wide")
    n_narrow = lax.axis_size("narrow")
    wide_index = lax.axis_index("wide")
    narrow_index = lax.axis_index("narrow")
    micro, own_queries, query_len, width = query_states.shape
    own_passages, slots = passage_states.shape[1:3]
    weights = (
        query_weight,
        key_weight,
        value_weight,
        out_weight,
        inner_weight,
        outer_weight,
        linear_weight,
    )
    embed_width = linear_weight.shape[1]
    vec = (
        jnp.concatenate(
            [
                query_bias,
                value_bias,
                out_bias,
                first_gain,
                first_shift,
                outer_bias,
                second_gain,
                second_shift,
                inner_bias,
            ]
        )
        .astype(F32)
        .reshape(-1, width)
    )
    vec = jnp.pad(vec, ((0, -vec.shape[0] % 8), (0, 0)))
    own_index = narrow_index * n_wide + wide_index
    own_lengths = lax.dynamic_slice_in_dim(lengths, own_index * own_passages, own_passages, axis=1)
    lens = own_lengths.reshape(-1)
    x_query = query_states.reshape(-1, width)
    x_passage = passage_states.reshape(-1, width)
    query_rows, passage_rows = x_query.shape[0], x_passage.shape[0]
    total = query_rows + passage_rows
    kept_q = encode(
        x_query, lens, vec, weights, 1, query_len, total, passage_rows, None
    )
    queries = lax.all_gather(kept_q[15].reshape(micro, -1, embed_width), everyone, axis=0)
    kept_p = encode(
        x_passage, lens, vec, weights, micro * own_passages, 0, total, 0, kept_q
    )
    ctx, first_low, act, final_low = (kept_p[index] for index in (4, 7, 8, 12))
    passages = kept_p[15].reshape(micro * own_passages, slots, embed_width)
    e, z = similarity(queries, passages, lens)
    best = SHARP + jnp.log(z)
    own_scores = jnp.sum(best.reshape(micro, -1, query_len), axis=-1) / SHARP
    full = share_scores(own_scores, n_wide, n_narrow)
    row_total = jax.nn.logsumexp(full, axis=0)
    passage_ids = jnp.arange(full.shape[0], dtype=jnp.int32)
    picked = jnp.sum(
        jnp.where(passage_ids[:, None, None] == positives[None], full, 0.0), axis=0
    )
    row_count = own_queries * n_narrow
    losses = lax.dynamic_slice_in_dim(row_total - picked, wide_index * row_count, row_count, axis=1)
    block = lax.dynamic_slice(
        full,
        (narrow_index * n_wide, 0, wide_index * row_count),
        (n_wide, micro, row_count),
    )
    scores = jnp.transpose(block, (1, 2, 0))
    grads = jnp.exp(own_scores - row_total) - (positives == own_index).astype(F32)
    token_weights = jnp.repeat(grads, query_len, axis=1).reshape(z.shape) / z
    grad_passage, grad_query = similarity_back(e, token_weights, queries, passages)
    grad_query = exchange(
        grad_query.reshape(-1, query_rows, embed_width), n_wide, n_narrow
    )
    grad_passage = grad_passage.reshape(passage_rows, embed_width)
    back_p = mlp_back(grad_passage, kept_p, vec, weights, micro * own_passages, total, 0, None)
    back_q = mlp_back(grad_query, kept_q, vec, weights, 1, total, passage_rows, back_p)
    gp, go, gi, _, ga, sums_q = back_q
    d_outer = outer(act, go)
    d_inner = outer(first_low, gi)
    d_linear = outer(final_low, gp)
    att_p = attention_back(ga, back_p[3], kept_p, weights, micro * own_passages, total, 0, None)
    att_q = attention_back(ga, back_q[3], kept_q, weights, 1, total, passage_rows, att_p[0])
    gqkv = att_q[0]
    x_all = jnp.concatenate([x_passage, x_query], axis=0)
    d_out = outer(ctx, ga)
    d_qkv = outer(x_all, gqkv)

    sums = back_p[5] + sums_q
    sums = jnp.concatenate([sums, att_p[2] + att_q[2]], axis=0)
    part = width // n_wide

    if part % 16 == 0 and n_narrow == 4:
        picks = (16, 17, ROW_BO, ROW_G1, ROW_S1, ROW_B2, ROW_G2, ROW_S2)
        vectors = jnp.concatenate(
            [sums[pick].reshape(n_wide, part) for pick in picks]
            + [sums[ROW_BI : ROW_BI + 4].reshape(n_wide, 4 * part)],
            axis=1,
        )
        vectors = jnp.pad(vectors, ((0, 0), (0, 16 * width - vectors.shape[1])))
        linear_rows = d_linear.astype(BF16).reshape(n_wide, -1, width)
        tails = jnp.stack(
            [linear_rows, vectors.astype(BF16).reshape(n_wide, 16, width)]
            + [jnp.zeros((n_wide, 16, width), BF16)] * 2
        )
        packed = jnp.concatenate(
            [
                d_outer.astype(BF16).reshape(n_wide, 4, part, width).transpose(1, 0, 2, 3),
                d_inner.astype(BF16).reshape(n_wide, part, 4, width).transpose(2, 0, 1, 3),
                jnp.stack(
                    [
                        d_qkv[:, index * width : (index + 1) * width]
                        .astype(BF16)
                        .reshape(n_wide, part, width)
                        for index in range(3)
                    ]
                    + [d_out.astype(BF16).reshape(n_wide, part, width)]
                ),
                tails,
            ],
            axis=2,
        )
        summed = tree(packed, n_wide).astype(F32)
        r_outer = summed[:, :part].reshape(4 * part, width)
        r_inner = summed[:, part : 2 * part].transpose(1, 0, 2).reshape(part, 4 * width)
        r_q, r_k, r_v, r_out = (summed[index, 2 * part : 3 * part] for index in range(4))
        r_linear = summed[0, 3 * part :].reshape(part, embed_width)
        flat = summed[1, 3 * part : 3 * part + 2].reshape(-1)
        v_q, v_v, v_o, v_g1, v_s1, v_2, v_g2, v_s2 = (
            flat[index * part : (index + 1) * part] for index in range(8)
        )
        v_i = flat[8 * part : 12 * part]
    else:

        def reduce(value):
            piece = lax.psum_scatter(value.astype(BF16), everyone, scatter_dimension=0, tiled=True)
            return lax.all_gather(piece, "narrow", axis=0, tiled=True).astype(F32)

        def vector(rows):
            flat = rows.reshape(-1)
            share = flat.shape[0] // n_wide
            return lax.dynamic_slice_in_dim(flat, wide_index * share, share)

        sums = lax.psum(sums, everyone)
        r_outer, r_inner, r_linear, r_out, r_qkv = (
            reduce(value) for value in (d_outer, d_inner, d_linear, d_out, d_qkv)
        )
        r_q, r_k, r_v = (r_qkv[:, index * width : (index + 1) * width] for index in range(3))
        v_q, v_v, v_o, v_g1, v_s1, v_2, v_g2, v_s2 = (
            vector(sums[pick])
            for pick in (16, 17, ROW_BO, ROW_G1, ROW_S1, ROW_B2, ROW_G2, ROW_S2)
        )
        v_i = vector(sums[ROW_BI : ROW_BI + 4])
    return (
        scores,
        losses,
        att_q[1].reshape(query_states.shape),
        att_p[1].reshape(passage_states.shape),
        r_q,
        v_q,
        r_k,
        r_v,
        v_v,
        r_out,
        v_o,
        v_g1,
        v_s1,
        r_inner,
        v_i,
        r_outer,
        v_2,
        v_g2,
        v_s2,
        r_linear,
    )


def solution(mesh):
    return jax.shard_map(
        local,
        mesh=mesh,
        in_specs=(
            P(None, ("wide", "narrow"), None, None),
            P(None, ("narrow", "wide"), None, None),
        )
        + (P(),) * 18,
        out_specs=(
            P(None, "wide", "narrow"),
            P(None, "wide"),
            P(None, ("wide", "narrow"), None, None),
            P(None, ("narrow", "wide"), None, None),
            P("wide", None),
            P("wide"),
            P("wide", None),
            P("wide", None),
            P("wide"),
            P("wide", None),
            P("wide"),
            P("wide"),
            P("wide"),
            P("wide", None),
            P("wide"),
            P("wide", None),
            P("wide"),
            P("wide"),
            P("wide"),
            P("wide", None),
        ),
        check_vma=False,
    )
```

```python
import functools

import jax
import jax.numpy as jnp
from jax import lax
from jax.experimental import pallas as pl
from jax.experimental.pallas import tpu as pltpu
from jax.sharding import PartitionSpec as P

HEADS = 12
HEAD_DIM = 64
SHARP = 16.0
LAYER_EPS = 1e-12
NORM_EPS = 1e-06
MASKED = -1e30
SLOPE_CONST = 0.3989422804014327
ROOT_HALF = 0.7071067811865476
BF16 = jnp.bfloat16
F32 = jnp.float32
VMEM_LIMIT = 62 * 1024 * 1024

NN = (((1,), (0,)), ((), ()))
NT = (((1,), (1,)), ((), ()))
TN = (((0,), (0,)), ((), ()))


def mm(left, right, dims=NN):
    return lax.dot_general(left, right, dims, preferred_element_type=F32)


ANY = pl.BlockSpec(memory_space=pl.ANY)

ROW_BQ, ROW_BV, ROW_BO, ROW_G1, ROW_S1, ROW_B2, ROW_G2, ROW_S2, ROW_BI = range(9)


def vec_row(vec_ref, row):
    return vec_ref[row : row + 1, :]


def mean_row(value):
    return jnp.sum(value, axis=-1, keepdims=True) * (1.0 / value.shape[-1])


class Loader:
    def __init__(self, sources, targets, sem):
        self.copies = [
            pltpu.make_async_copy(source, target, sem.at[index])
            for index, (source, target) in enumerate(zip(sources, targets))
        ]
        self.first = pl.program_id(0) == 0

    def start(self):
        @pl.when(self.first)
        def _():
            for copy in self.copies:
                copy.start()

    def need(self, *indices):
        @pl.when(self.first)
        def _():
            for index in indices:
                self.copies[index].wait()


MESH = pl.DeviceIdType.MESH


def remote(source, target, sems, index, device):
    return pltpu.make_async_remote_copy(
        src_ref=source,
        dst_ref=target,
        send_sem=sems[0].at[index],
        recv_sem=sems[1].at[index],
        device_id=device,
        device_id_type=MESH,
    )


class Chips:
    def __init__(self, n_wide, n_narrow):
        self.wide, self.narrow = lax.axis_index("wide"), lax.axis_index("narrow")
        self.core = lax.rem(self.narrow, 2)
        self.rows = n_narrow // 2
        self.count = n_wide * self.rows
        self.me = self.wide * self.rows + self.narrow // 2
        self.mate = (self.wide, self.narrow + 1 - 2 * self.core)

    def at(self, step):
        return lax.rem(self.me + step + self.count, self.count)

    def device(self, chip):
        return (chip // self.rows, lax.rem(chip, self.rows) * 2 + self.core)

    def loop(self, body):
        def step_body(step, carry):
            body(step)
            return carry

        lax.fori_loop(1, self.count, step_body, 0)

    def barrier(self):
        barrier = pltpu.get_barrier_semaphore()

        def signal(step):
            pl.semaphore_signal(
                barrier, inc=1, device_id=self.device(self.at(step)), device_id_type=MESH
            )

        pl.semaphore_signal(barrier, inc=1, device_id=self.mate, device_id_type=MESH)
        self.loop(signal)
        pl.semaphore_wait(barrier, self.count)


class Gather:
    def __init__(self, chips, own, out, sems):
        self.chips, self.own, self.out = chips, own, out
        self.far, self.pair, self.local = sems[:2], sems[2:4], sems[4]

    def far_copy(self, step, chip):
        slot = self.out.at[chip, self.chips.core]
        return remote(self.own, slot, self.far, step, self.chips.device(self.chips.at(step)))

    def mate_copy(self, core):
        block = self.out.at[:, core]
        return remote(block, block, self.pair, 0, self.chips.mate)

    def local_copy(self):
        slot = self.out.at[self.chips.me, self.chips.core]
        return pltpu.make_async_copy(self.own, slot, self.local.at[0])

    def start(self):
        self.local_copy().start()
        self.chips.barrier()
        self.chips.loop(lambda step: self.far_copy(step, self.chips.me).start())

    def forward(self):
        self.local_copy().wait()
        self.chips.loop(lambda step: self.far_copy(step, self.chips.at(-step)).wait_recv())
        self.mate_copy(self.chips.core).start()

    def finish(self):
        self.chips.loop(lambda step: self.far_copy(step, self.chips.me).wait_send())
        self.mate_copy(1 - self.chips.core).wait_recv()
        self.mate_copy(self.chips.core).wait_send()


class Exchange:
    def __init__(self, chips, grads, out, scratch):
        self.chips, self.grads, self.out = chips, grads, out
        self.half, self.arrived, self.inbox = scratch[:3]
        self.pair, self.far, self.local = scratch[3:5], scratch[5:7], scratch[7]

    def pair_copy(self):
        away = self.grads.at[:, 1 - self.chips.core]
        return remote(away, self.arrived, self.pair, 0, self.chips.mate)

    def local_copy(self):
        mine = self.grads.at[:, self.chips.core]
        return pltpu.make_async_copy(mine, self.half, self.local.at[0])

    def far_copy(self, step):
        chip = self.chips.at(step)
        return remote(
            self.half.at[chip], self.inbox.at[step], self.far, step, self.chips.device(chip)
        )

    def start(self):
        self.local_copy().start()
        self.chips.barrier()
        self.pair_copy().start()

    def push(self):
        self.local_copy().wait()
        self.pair_copy().wait_recv()

        def add(step):
            chip = self.chips.at(step)
            total = self.half[chip].astype(F32) + self.arrived[chip].astype(F32)
            self.half[chip] = total.astype(BF16)
            self.far_copy(step).start()

        self.chips.loop(add)
        me = self.chips.me
        self.out[...] = self.half[me].astype(F32) + self.arrived[me].astype(F32)

    def finish(self):
        def collect(step):
            copy = self.far_copy(step)
            copy.wait_recv()
            copy.wait_send()
            self.out[...] += self.inbox[step].astype(F32)

        self.chips.loop(collect)
        self.pair_copy().wait_send()


def exchange_scratch(chips, rows, width):
    sem = pltpu.SemaphoreType.DMA
    return [pltpu.VMEM((chips, rows, width), BF16)] * 3 + [
        sem((1,)),
        sem((1,)),
        sem((chips,)),
        sem((chips,)),
        sem((1,)),
    ]


def fwd_kernel(grouped, alias_count, sizes, *refs):
    lens_ref, x_ref, vec_ref = refs[:3]
    sources = refs[3:10]
    refs = refs[10 + alias_count :]
    gather = None
    if sizes:
        gather = Gather(Chips(*sizes), refs[0], refs[17], refs[-5:])
        refs = refs[1:17] + refs[18:-5]
    (
        q_ref,
        k_ref,
        v_ref,
        att_ref,
        ctx_ref,
        n1_ref,
        r1_ref,
        first_ref,
        act_ref,
        slope_ref,
        n2_ref,
        r2_ref,
        final_ref,
        unit_ref,
        uinv_ref,
        embed_ref,
    ) = refs[:16]
    wq, wk, wv, wo, wi, w2, wl, sem, acc_ref = refs[16:]
    loader = Loader(sources, (wq, wk, wv, wo, wi, w2, wl), sem)
    loader.start()
    if gather:
        last = pl.program_id(0) == pl.num_programs(0) - 1
        pl.when(loader.first)(gather.start)
        pl.when(last)(gather.forward)
    rows = x_ref.shape[0]
    x = x_ref[...]
    scale = HEAD_DIM ** (-0.5)
    loader.need(0)
    q_ref[...] = ((mm(x, wq[...]) + vec_row(vec_ref, ROW_BQ)).astype(BF16) * scale).astype(BF16)
    loader.need(1)
    k_ref[...] = mm(x, wk[...]).astype(BF16)
    loader.need(2)
    v_ref[...] = (mm(x, wv[...]) + vec_row(vec_ref, ROW_BV)).astype(BF16)
    if grouped:
        valid = (
            lax.broadcasted_iota(jnp.int32, (rows, rows), 0) // grouped
            == lax.broadcasted_iota(jnp.int32, (rows, rows), 1) // grouped
        )
    else:
        length = lens_ref[pl.program_id(0)]
        valid = lax.broadcasted_iota(jnp.int32, (1, rows), 1) < length
    bias = jnp.where(valid, 0.0, MASKED)
    low_half = lax.broadcasted_iota(jnp.int32, (rows, 128), 1) < HEAD_DIM

    def pair_body(pair, carry):
        cols = pl.ds(pl.multiple_of(pair * 128, 128), 128)
        q_pair, k_pair, v_pair = q_ref[:, cols], k_ref[:, cols], v_ref[:, cols]
        parts = []
        for half in range(2):
            mask = low_half if half == 0 else jnp.logical_not(low_half)
            logits = mm(jnp.where(mask, q_pair, jnp.zeros_like(q_pair)), k_pair, NT) + bias
            peak = jnp.max(logits, axis=-1, keepdims=True)
            e = jnp.exp(logits - peak)
            inv = 1.0 / jnp.sum(e, axis=-1, keepdims=True)
            low = (e * inv).astype(BF16)
            att_ref[0, 2 * pair + half] = low
            parts.append(mm(low, v_pair))
        ctx_ref[:, cols] = jnp.where(low_half, parts[0], parts[1]).astype(BF16)
        return carry

    lax.fori_loop(0, HEADS // 2, pair_body, 0)
    loader.need(3)
    field = x.astype(F32) + (mm(ctx_ref[...], wo[...]) + vec_row(vec_ref, ROW_BO))
    center = field - mean_row(field)
    inverse = lax.rsqrt(mean_row(center * center) + LAYER_EPS)
    normed = center * inverse
    n1_ref[...] = normed.astype(BF16)
    r1_ref[...] = jnp.broadcast_to(inverse, r1_ref.shape)
    first = normed * vec_row(vec_ref, ROW_G1) + vec_row(vec_ref, ROW_S1)
    first_ref[...] = first.astype(BF16)
    acc_ref[...] = first + vec_row(vec_ref, ROW_B2)
    loader.need(4, 5)
    width = x.shape[1]

    def chunk_body(chunk, carry):
        cols = pl.ds(pl.multiple_of(chunk * width, width), width)
        inner = mm(first_ref[...], wi[:, cols]) + vec_ref[pl.ds(ROW_BI + chunk, 1), :]
        phi = 0.5 * (1.0 + lax.erf(inner * ROOT_HALF))
        activated = (inner * phi).astype(BF16)
        act_ref[:, cols] = activated
        slope_ref[:, cols] = (phi + inner * jnp.exp(-0.5 * inner * inner) * SLOPE_CONST).astype(
            BF16
        )
        acc_ref[...] += mm(activated, w2[cols, :])
        return carry

    lax.fori_loop(0, wi.shape[1] // width, chunk_body, 0)
    field = acc_ref[...]
    center = field - mean_row(field)
    inverse = lax.rsqrt(mean_row(center * center) + LAYER_EPS)
    normed = center * inverse
    n2_ref[...] = normed.astype(BF16)
    r2_ref[...] = jnp.broadcast_to(inverse, r2_ref.shape)
    final = (normed * vec_row(vec_ref, ROW_G2) + vec_row(vec_ref, ROW_S2)).astype(BF16)
    final_ref[...] = final
    loader.need(6)
    projected = mm(final, wl[...])
    uinv = lax.rsqrt(jnp.sum(projected * projected, axis=-1, keepdims=True) + NORM_EPS)
    unit = projected * uinv
    unit_ref[...] = unit
    uinv_ref[...] = jnp.broadcast_to(uinv, uinv_ref.shape)
    embed_ref[...] = unit.astype(BF16)
    if gather:
        pl.when(last)(gather.finish)


def encode(x, lens, vec, weights, blocks, grouped, total, offset, earlier, sizes):
    rows = x.shape[0] // blocks
    width = x.shape[1]
    wide = weights[4].shape[1]
    embed_width = weights[6].shape[1]
    base = offset // rows

    def row_spec(columns):
        return pl.BlockSpec((rows, columns), lambda i, lens: (base + i, 0))

    def own_spec(columns):
        return pl.BlockSpec((rows, columns), lambda i, lens: (i, 0))

    def shape(count, columns, dtype):
        return jax.ShapeDtypeStruct((count, columns), dtype)

    own = x.shape[0]
    out_shapes = [
        shape(own, width, BF16),
        shape(own, width, BF16),
        shape(own, width, BF16),
        jax.ShapeDtypeStruct((blocks, HEADS, rows, rows), BF16),
        shape(total, width, BF16),
        shape(own, width, BF16),
        shape(own, embed_width, F32),
        shape(total, width, BF16),
        shape(total, wide, BF16),
        shape(own, wide, BF16),
        shape(own, width, BF16),
        shape(own, embed_width, F32),
        shape(total, width, BF16),
        shape(own, embed_width, F32),
        shape(own, embed_width, F32),
        shape(own, embed_width, BF16),
    ]
    shared = (4, 7, 8, 12)
    out_specs = [
        pl.BlockSpec((1, HEADS, rows, rows), lambda i, lens: (i, 0, 0, 0))
        if index == 3
        else (row_spec if index in shared else own_spec)(out.shape[1])
        for index, out in enumerate(out_shapes)
    ]
    aliased = [] if earlier is None else [earlier[index] for index in shared]
    sends, sem_shapes, params = [], [], {}
    if sizes:
        sends = [earlier[15]]
        chips = sizes[0] * sizes[1] // 2
        out_shapes.append(jax.ShapeDtypeStruct((chips, 2) + earlier[15].shape, BF16))
        out_specs.append(ANY)
        sem = pltpu.SemaphoreType.DMA
        sem_shapes = [sem((chips,)), sem((chips,)), sem((1,)), sem((1,)), sem((1,))]
        params = {"collective_id": 4, "has_side_effects": True}
    return pl.pallas_call(
        functools.partial(fwd_kernel, grouped, len(aliased), sizes),
        out_shape=out_shapes,
        grid_spec=pltpu.PrefetchScalarGridSpec(
            num_scalar_prefetch=1,
            grid=(blocks,),
            in_specs=[
                own_spec(width),
                pl.BlockSpec(vec.shape, lambda i, lens: (0, 0)),
            ]
            + [ANY] * (7 + len(aliased) + len(sends)),
            out_specs=out_specs,
            scratch_shapes=[pltpu.VMEM(weight.shape, BF16) for weight in weights]
            + [pltpu.SemaphoreType.DMA((7,)), pltpu.VMEM((rows, width), F32)]
            + sem_shapes,
        ),
        input_output_aliases={10 + index: shared[index] for index in range(len(aliased))},
        compiler_params=pltpu.CompilerParams(vmem_limit_bytes=VMEM_LIMIT, **params),
        name="encode_queries" if grouped else "encode_passages",
    )(lens, x, vec, *weights, *aliased, *sends)


def sims_kernel(lens_ref, q_ref, p_ref, e_ref, z_ref):
    count = q_ref.shape[0]
    tokens = count * q_ref.shape[2]
    query = q_ref[...].reshape(tokens, q_ref.shape[3])
    sims = mm(p_ref[0], query, NT)
    slot = lax.broadcasted_iota(jnp.int32, sims.shape, 0)
    e = jnp.where(slot < lens_ref[pl.program_id(0)], jnp.exp(SHARP * sims - SHARP), 0.0)
    e_ref[0] = e.astype(BF16)
    z = jnp.sum(e, axis=0, keepdims=True)
    step = q_ref.shape[2]
    for index in range(count):
        z_ref[0, index : index + 1, :] = z[:, index * step : (index + 1) * step]


def sims_back_kernel(e_ref, w_ref, q_ref, p_ref, gp_ref, gq_ref):
    count = q_ref.shape[0]
    step = q_ref.shape[2]
    query = q_ref[...].reshape(count * step, q_ref.shape[3])
    weight = jnp.concatenate([w_ref[0, index : index + 1, :] for index in range(count)], axis=1)
    grads = (e_ref[0].astype(F32) * weight).astype(BF16)
    part = mm(grads, query)

    @pl.when(pl.program_id(1) == 0)
    def _():
        gp_ref[0] = part

    @pl.when(pl.program_id(1) > 0)
    def _():
        gp_ref[0] += part

    gq_ref[...] = mm(grads, p_ref[0], TN).astype(BF16).reshape(gq_ref.shape)


def similarity(queries, passages, lens):
    devices, micro, tokens, width = queries.shape
    slots = passages.shape[1]
    group = 8
    e, z = pl.pallas_call(
        sims_kernel,
        out_shape=(
            jax.ShapeDtypeStruct((micro, slots, devices * tokens), BF16),
            jax.ShapeDtypeStruct((micro, devices, tokens), F32),
        ),
        grid_spec=pltpu.PrefetchScalarGridSpec(
            num_scalar_prefetch=1,
            grid=(micro, devices // group),
            in_specs=[
                pl.BlockSpec((group, 1, tokens, width), lambda m, b, lens: (b, m, 0, 0)),
                pl.BlockSpec((1, slots, width), lambda m, b, lens: (m, 0, 0)),
            ],
            out_specs=(
                pl.BlockSpec((1, slots, group * tokens), lambda m, b, lens: (m, 0, b)),
                pl.BlockSpec((1, group, tokens), lambda m, b, lens: (m, b, 0)),
            ),
        ),
        compiler_params=pltpu.CompilerParams(vmem_limit_bytes=VMEM_LIMIT),
        name="similarity",
    )(lens, queries, passages)
    return e, z


def similarity_back(e, weights, queries, passages):
    devices, micro, tokens, width = queries.shape
    slots = passages.shape[1]
    group = 8
    return pl.pallas_call(
        sims_back_kernel,
        out_shape=(
            jax.ShapeDtypeStruct((micro, slots, width), F32),
            jax.ShapeDtypeStruct((devices, micro, tokens, width), BF16),
        ),
        grid=(micro, devices // group),
        in_specs=[
            pl.BlockSpec((1, slots, group * tokens), lambda m, b: (m, 0, b)),
            pl.BlockSpec((1, group, tokens), lambda m, b: (m, b, 0)),
            pl.BlockSpec((group, 1, tokens, width), lambda m, b: (b, m, 0, 0)),
            pl.BlockSpec((1, slots, width), lambda m, b: (m, 0, 0)),
        ],
        out_specs=(
            pl.BlockSpec((1, slots, width), lambda m, b: (m, 0, 0)),
            pl.BlockSpec((group, 1, tokens, width), lambda m, b: (b, m, 0, 0)),
        ),
        compiler_params=pltpu.CompilerParams(vmem_limit_bytes=VMEM_LIMIT),
        name="similarity_back",
    )(e, weights, queries, passages)


def accumulate(ref, row, value):
    ref[row : row + 1, :] += jnp.sum(value, axis=0, keepdims=True)


def mlp_back_kernel(alias_count, sizes, *refs):
    (
        ge_ref,
        unit_ref,
        uinv_ref,
        n2_ref,
        r2_ref,
        slope_ref,
        n1_ref,
        r1_ref,
        vec_ref,
    ) = refs[:9]
    sources = refs[9:12]
    refs = refs[12 + alias_count :]
    swap = None
    if sizes:
        swap = Exchange(Chips(*sizes), refs[0], refs[7], refs[-8:])
        refs = refs[1:7] + refs[8:-8]
    gp_ref, go_ref, gi_ref, gh_ref, ga_ref, sums_ref = refs[:6]
    wl, w2, wi, sem, acc_ref = refs[6:]
    loader = Loader(sources, (wl, w2, wi), sem)
    loader.start()
    if swap:
        pl.when(loader.first)(swap.start)

    @pl.when(loader.first)
    def _():
        sums_ref[...] = jnp.zeros_like(sums_ref)

    grad = ge_ref[...]
    unit = unit_ref[...]
    projected_low = (
        uinv_ref[...] * (grad - unit * jnp.sum(grad * unit, axis=-1, keepdims=True))
    ).astype(BF16)
    gp_ref[...] = projected_low
    loader.need(0)
    grad_final = mm(projected_low, wl[...], NT)
    normed = n2_ref[...].astype(F32)
    accumulate(sums_ref, ROW_G2, grad_final * normed)
    accumulate(sums_ref, ROW_S2, grad_final)
    scaled = grad_final * vec_row(vec_ref, ROW_G2)
    grad_second = r2_ref[:, :1] * (scaled - mean_row(scaled) - normed * mean_row(scaled * normed))
    outer_low = grad_second.astype(BF16)
    go_ref[...] = outer_low
    accumulate(sums_ref, ROW_B2, outer_low.astype(F32))
    acc_ref[...] = grad_second
    if swap:
        pl.when(loader.first)(swap.push)
    loader.need(1, 2)
    width = go_ref.shape[1]

    def chunk_body(chunk, carry):
        cols = pl.ds(pl.multiple_of(chunk * width, width), width)
        grad_act = mm(go_ref[...], w2[cols, :], NT)
        inner = (grad_act * slope_ref[:, cols].astype(F32)).astype(BF16)
        gi_ref[:, cols] = inner
        sums_ref[pl.ds(ROW_BI + chunk, 1), :] += jnp.sum(
            inner.astype(F32), axis=0, keepdims=True
        )
        acc_ref[...] += mm(inner, wi[:, cols], NT)
        return carry

    lax.fori_loop(0, wi.shape[1] // width, chunk_body, 0)
    grad_first = acc_ref[...]
    normed = n1_ref[...].astype(F32)
    accumulate(sums_ref, ROW_G1, grad_first * normed)
    accumulate(sums_ref, ROW_S1, grad_first)
    scaled = grad_first * vec_row(vec_ref, ROW_G1)
    hidden = r1_ref[:, :1] * (scaled - mean_row(scaled) - normed * mean_row(scaled * normed))
    gh_ref[...] = hidden
    low = hidden.astype(BF16)
    ga_ref[...] = low
    accumulate(sums_ref, ROW_BO, low.astype(F32))
    if swap:
        pl.when(pl.program_id(0) == pl.num_programs(0) - 1)(swap.finish)


def mlp_back(grad_embed, kept, vec, weights, blocks, total, offset, earlier, sent, sizes):
    own = grad_embed.shape[0]
    rows = own // blocks
    base = offset // rows
    _, _, _, _, wi, w2, wl = weights
    width, wide = wi.shape
    embed_width = wl.shape[1]

    def row_spec(columns):
        return pl.BlockSpec((rows, columns), lambda i: (base + i, 0))

    def own_spec(columns):
        return pl.BlockSpec((rows, columns), lambda i: (i, 0))

    args = [grad_embed] + [kept[index] for index in (13, 14, 10, 11, 9, 5, 6)]
    out_shapes = [
        jax.ShapeDtypeStruct((total, embed_width), BF16),
        jax.ShapeDtypeStruct((total, width), BF16),
        jax.ShapeDtypeStruct((total, wide), BF16),
        jax.ShapeDtypeStruct((own, width), F32),
        jax.ShapeDtypeStruct((total, width), BF16),
        jax.ShapeDtypeStruct((16, width), F32),
    ]
    shared = (0, 1, 2, 4)
    out_specs = [
        (row_spec if index in shared else own_spec)(out.shape[1])
        for index, out in enumerate(out_shapes[:5])
    ] + [pl.BlockSpec((16, width), lambda i: (0, 0))]
    aliased = [] if earlier is None else [earlier[index] for index in shared]
    sends, scratch, params = [], [], {}
    if sizes:
        sends = [sent]
        out_shapes.append(jax.ShapeDtypeStruct(sent.shape[2:], F32))
        out_specs.append(pl.BlockSpec(sent.shape[2:], lambda i: (0, 0)))
        scratch = exchange_scratch(sent.shape[0], *sent.shape[2:])
        params = {"collective_id": 2, "has_side_effects": True}
    return pl.pallas_call(
        functools.partial(mlp_back_kernel, len(aliased), sizes),
        out_shape=out_shapes,
        grid=(blocks,),
        in_specs=[own_spec(arg.shape[1]) for arg in args]
        + [pl.BlockSpec(vec.shape, lambda i: (0, 0))]
        + [ANY] * (3 + len(aliased) + len(sends)),
        out_specs=out_specs,
        scratch_shapes=[pltpu.VMEM(weight.shape, BF16) for weight in (wl, w2, wi)]
        + [pltpu.SemaphoreType.DMA((3,)), pltpu.VMEM((rows, width), F32)]
        + scratch,
        input_output_aliases={12 + index: shared[index] for index in range(len(aliased))},
        compiler_params=pltpu.CompilerParams(vmem_limit_bytes=VMEM_LIMIT, **params),
        name="mlp_back_queries" if earlier is not None else "mlp_back_passages",
    )(*args, vec, wl, w2, wi, *aliased, *sends)


def attention_back_kernel(alias_count, *refs):
    ga_ref, gh_ref, att_ref, q_ref, k_ref, v_ref = refs[:6]
    sources = refs[6:10]
    refs = refs[10 + alias_count :]
    gqkv_ref, gx_ref, sums_ref = refs[:3]
    wo, wq, wk, wv, sem, gc_ref = refs[3:]
    loader = Loader(sources, (wo, wq, wk, wv), sem)
    loader.start()

    @pl.when(loader.first)
    def _():
        sums_ref[...] = jnp.zeros_like(sums_ref)

    rows, width = gh_ref.shape
    scale = HEAD_DIM ** (-0.5)
    loader.need(0)
    gc_ref[...] = mm(ga_ref[...], wo[...], NT).astype(BF16)
    low_half = lax.broadcasted_iota(jnp.int32, (rows, 128), 1) < HEAD_DIM

    def pair_body(pair, carry):
        cols = pl.ds(pl.multiple_of(pair * 128, 128), 128)
        q_pair, k_pair, v_pair, gc_pair = q_ref[:, cols], k_ref[:, cols], v_ref[:, cols], gc_ref[:, cols]
        parts = []
        for half in range(2):
            mask = low_half if half == 0 else jnp.logical_not(low_half)
            low = att_ref[0, 2 * pair + half]
            att = low.astype(F32)
            grad_att = mm(jnp.where(mask, gc_pair, jnp.zeros_like(gc_pair)), v_pair, NT)
            weighted = grad_att * att
            grad_logits = (weighted - att * jnp.sum(weighted, axis=-1, keepdims=True)).astype(BF16)
            parts.append(
                (
                    mm(grad_logits, k_pair) * scale,
                    mm(grad_logits, q_pair, TN),
                    mm(low, gc_pair, TN),
                )
            )
        for index in range(3):
            gqkv_ref[:, pl.ds(pl.multiple_of(index * width + pair * 128, 128), 128)] = jnp.where(
                low_half, parts[0][index], parts[1][index]
            ).astype(BF16)
        return carry

    lax.fori_loop(0, HEADS // 2, pair_body, 0)
    loader.need(1, 2, 3)
    grad_q, grad_k, grad_v = (
        gqkv_ref[:, :width],
        gqkv_ref[:, width : 2 * width],
        gqkv_ref[:, 2 * width :],
    )
    accumulate(sums_ref, 0, grad_q.astype(F32))
    accumulate(sums_ref, 1, grad_v.astype(F32))
    gx_ref[...] = (
        gh_ref[...]
        + mm(grad_q, wq[...], NT)
        + mm(grad_k, wk[...], NT)
        + mm(grad_v, wv[...], NT)
    )


def attention_back(attended, hidden, kept, weights, blocks, total, offset, earlier):
    own, width = hidden.shape
    rows = own // blocks
    base = offset // rows
    wq, wk, wv, wo = weights[:4]

    def row_spec(columns):
        return pl.BlockSpec((rows, columns), lambda i: (base + i, 0))

    def own_spec(columns):
        return pl.BlockSpec((rows, columns), lambda i: (i, 0))

    aliased = [] if earlier is None else [earlier]
    return pl.pallas_call(
        functools.partial(attention_back_kernel, len(aliased)),
        out_shape=(
            jax.ShapeDtypeStruct((total, 3 * width), BF16),
            jax.ShapeDtypeStruct((own, width), F32),
            jax.ShapeDtypeStruct((8, width), F32),
        ),
        grid=(blocks,),
        in_specs=[
            row_spec(width),
            own_spec(width),
            pl.BlockSpec((1, HEADS, rows, rows), lambda i: (i, 0, 0, 0)),
            own_spec(width),
            own_spec(width),
            own_spec(width),
        ]
        + [ANY] * (4 + len(aliased)),
        out_specs=(
            row_spec(3 * width),
            own_spec(width),
            pl.BlockSpec((8, width), lambda i: (0, 0)),
        ),
        scratch_shapes=[pltpu.VMEM(weight.shape, BF16) for weight in weights[:4]]
        + [pltpu.SemaphoreType.DMA((4,)), pltpu.VMEM((rows, width), BF16)],
        input_output_aliases={10: 0} if aliased else {},
        compiler_params=pltpu.CompilerParams(vmem_limit_bytes=VMEM_LIMIT),
        name="attention_back_queries" if aliased else "attention_back_passages",
    )(attended, hidden, kept[3], kept[0], kept[1], kept[2], wo, wq, wk, wv, *aliased)


def share_kernel(n_wide, n_narrow, own_ref, all_ref, send_sem, recv_sem):
    me = lax.axis_index("narrow") * n_wide + lax.axis_index("wide")
    total = n_wide * n_narrow
    sems = (send_sem, recv_sem)

    def device(index):
        return (lax.rem(index, n_wide), index // n_wide)

    barrier = pltpu.get_barrier_semaphore()

    def signal(step, carry):
        pl.semaphore_signal(
            barrier, inc=1, device_id=device(lax.rem(me + step, total)), device_id_type=MESH
        )
        return carry

    def send(step, carry):
        target = device(lax.rem(me + step, total))
        remote(own_ref, all_ref.at[me], sems, step, target).start()
        return carry

    def wait(step, carry):
        source = lax.rem(me - step + total, total)
        copy = remote(own_ref, all_ref.at[source], sems, step, device(source))
        copy.wait_recv()
        copy.wait_send()
        return carry

    lax.fori_loop(1, total, signal, 0)
    all_ref[me] = own_ref[...]
    pl.semaphore_wait(barrier, total - 1)
    lax.fori_loop(1, total, send, 0)
    lax.fori_loop(1, total, wait, 0)


def share_scores(own, n_wide, n_narrow):
    total = n_wide * n_narrow
    return pl.pallas_call(
        functools.partial(share_kernel, n_wide, n_narrow),
        out_shape=jax.ShapeDtypeStruct((total,) + own.shape, own.dtype),
        in_specs=[pl.BlockSpec(memory_space=pltpu.VMEM)],
        out_specs=pl.BlockSpec(memory_space=pltpu.VMEM),
        scratch_shapes=[pltpu.SemaphoreType.DMA((total,))] * 2,
        compiler_params=pltpu.CompilerParams(collective_id=1, has_side_effects=True),
        name="share_scores",
    )(own)


def exchange_kernel(n_wide, n_narrow, g_ref, out_ref, *scratch):
    swap = Exchange(Chips(n_wide, n_narrow), g_ref, out_ref, scratch)
    swap.start()
    swap.push()
    swap.finish()


def exchange(grads, n_wide, n_narrow):
    chips, _, rows, width = grads.shape
    return pl.pallas_call(
        functools.partial(exchange_kernel, n_wide, n_narrow),
        out_shape=jax.ShapeDtypeStruct((rows, width), F32),
        in_specs=[ANY],
        out_specs=pl.BlockSpec(memory_space=pltpu.VMEM),
        scratch_shapes=exchange_scratch(chips, rows, width),
        compiler_params=pltpu.CompilerParams(
            collective_id=2, has_side_effects=True, vmem_limit_bytes=VMEM_LIMIT
        ),
        name="exchange_query_gradients",
    )(grads)


UNITS = ((0, 48), (48, 48), (96, 48), (144, 48), (192, 48), (240, 64))
SHARE_ROWS = 304
HALF = 64
TILES = 12


def weights_kernel(n_z, part, *refs):
    act, go, first, gi, x_p, x_q, gqkv, ctx, ga, final, gp = refs[:11]
    sums = refs[11:15]
    out_ref = refs[15]
    both, near, over_a, over_b, then_a, then_b, line, left_buf, right_buf, thin_buf = refs[16:26]
    load_sem = refs[26]
    core_sems, one_sems, two_sems, line_sems, copy_sems = (
        refs[27 + 2 * index : 29 + 2 * index] for index in range(5)
    )
    wide, narrow = lax.axis_index("wide"), lax.axis_index("narrow")
    z, x = wide // 2, lax.rem(wide, 2)
    y, core = narrow // 2, lax.rem(narrow, 2)
    mate = (wide, y * 2 + 1 - core)
    over_y = (wide, (1 - y) * 2 + core)
    over_x = (z * 2 + 1 - x, narrow)
    right, left = (wide + 2, narrow), (wide - 2, narrow)
    width = go.shape[1]
    p_rows = x_p.shape[0]
    count_units = len(UNITS)
    held = both.at[core]

    def load(tile, wait):
        slot = lax.rem(tile, 2)
        block = pl.ds(pl.multiple_of(lax.rem(tile, 4) * width, width), width)

        def copy(source, target, sem):
            made = pltpu.make_async_copy(source, target, sem)
            if wait:
                made.wait()
            else:
                made.start()

        def pair(source, other):
            copy(source, left_buf.at[slot], load_sem.at[slot, 0])
            copy(other, right_buf.at[slot], load_sem.at[slot, 1])

        pl.when(tile < 4)(lambda: pair(act.at[:, block], go))
        pl.when(jnp.logical_and(tile >= 4, tile < 8))(lambda: pair(first, gi.at[:, block]))

        @pl.when(jnp.logical_and(tile >= 8, tile < 11))
        def _():
            copy(x_p, left_buf.at[slot, pl.ds(0, p_rows)], load_sem.at[slot, 0])
            copy(x_q, left_buf.at[slot, pl.ds(p_rows, x_q.shape[0])], load_sem.at[slot, 2])
            copy(gqkv.at[:, block], right_buf.at[slot], load_sem.at[slot, 1])

        pl.when(tile == 11)(lambda: pair(ctx, ga))

        @pl.when(tile == TILES)
        def _():
            copy(final, left_buf.at[slot], load_sem.at[slot, 0])
            copy(gp, thin_buf, load_sem.at[slot, 1])

    def rows_of(unit):
        start, count = UNITS[unit]
        return pl.ds(start, count)

    def core_copy(unit):
        rows = rows_of(unit)
        return remote(
            both.at[1 - core, :, :, :, rows], near.at[:, :, :, rows], core_sems, unit, mate
        )

    def one_copy(unit):
        rows = rows_of(unit)
        count = UNITS[unit][1]
        if unit % 2 == 0:
            return remote(
                held.at[1 - y, :, :, rows], over_a.at[unit // 2], one_sems, unit, over_y
            )
        return remote(
            held.at[:, :, 1 - x, rows],
            over_b.at[unit // 2, :, :, pl.ds(0, count)],
            one_sems,
            unit,
            over_x,
        )

    def two_copy(unit):
        rows = rows_of(unit)
        count = UNITS[unit][1]
        if unit % 2 == 0:
            return remote(held.at[y, :, 1 - x, rows], then_a.at[unit // 2], two_sems, unit, over_x)
        return remote(
            held.at[1 - y, :, x, rows],
            then_b.at[unit // 2, :, pl.ds(0, count)],
            two_sems,
            unit,
            over_y,
        )

    def line_copy(unit, target, way):
        rows = rows_of(unit)
        index = (unit * n_z + target) * 2 + way
        return remote(
            held.at[y, target, x, rows],
            line.at[way, target, rows],
            line_sems,
            index,
            right if way == 0 else left,
        )

    def share_copy(unit, step, arriving):
        rows = rows_of(unit)
        slots = (
            (y * 2 + 1 - core, (1 - y) * 2 + core, (1 - y) * 2 + 1 - core)
            if arriving
            else (narrow, narrow, (1 - y) * 2 + core)
        )
        block = out_ref.at[slots[step], rows]
        return remote(block, block, copy_sems, unit * 3 + step, over_y if step == 1 else mate)

    def add(target, extra):
        target[...] = (target[...].astype(F32) + extra[...].astype(F32)).astype(BF16)

    def start_core(unit):
        core_copy(unit).start()

    def start_one(unit):
        rows = rows_of(unit)
        core_copy(unit).wait_recv()

        def body(index, carry):
            row_y, rest = index // (n_z * 2), lax.rem(index, n_z * 2)
            at = (row_y, rest // 2, lax.rem(rest, 2), rows)
            add(held.at[at], near.at[at])
            return carry

        lax.fori_loop(0, 4 * n_z, body, 0)
        one_copy(unit).start()

    def start_two(unit):
        rows = rows_of(unit)
        count = UNITS[unit][1]
        one_copy(unit).wait_recv()

        def body(index, carry):
            outer_at, inner_at = index // 2, lax.rem(index, 2)
            if unit % 2 == 0:
                add(held.at[y, outer_at, inner_at, rows], over_a.at[unit // 2, outer_at, inner_at])
            else:
                add(
                    held.at[inner_at, outer_at, x, rows],
                    over_b.at[unit // 2, inner_at, outer_at, pl.ds(0, count)],
                )
            return carry

        lax.fori_loop(0, 2 * n_z, body, 0)
        two_copy(unit).start()

    def start_line(unit):
        rows = rows_of(unit)
        count = UNITS[unit][1]
        two_copy(unit).wait_recv()

        def body(index, carry):
            extra = then_a if unit % 2 == 0 else then_b
            add(held.at[y, index, x, rows], extra.at[unit // 2, index, pl.ds(0, count)])
            return carry

        lax.fori_loop(0, n_z, body, 0)
        for step in range(n_z - 1):
            for way in range(2):
                target = n_z - 1 - step if way == 0 else step
                sends = z < target if way == 0 else z > target
                edge = z > 0 if way == 0 else z < n_z - 1

                @pl.when(jnp.logical_and(sends, edge))
                def _(target=target, way=way):
                    line_copy(unit, target, way).wait_recv()
                    add(held.at[y, target, x, rows], line.at[way, target, rows])

                pl.when(sends)(line_copy(unit, target, way).start)

    def start_share(unit):
        rows = rows_of(unit)
        for target in range(n_z):

            @pl.when(z == target)
            def _(target=target):
                for way in range(2):
                    if target > 0 if way == 0 else target < n_z - 1:
                        line_copy(unit, target, way).wait_recv()
                        add(held.at[y, target, x, rows], line.at[way, target, rows])

        out_ref[narrow, rows] = both[core, y, z, x, rows]
        share_copy(unit, 1, False).start()
        share_copy(unit, 0, False).start()

    def forward(unit):
        share_copy(unit, 1, True).wait_recv()
        share_copy(unit, 2, False).start()

    def finish(unit):
        share_copy(unit, 0, True).wait_recv()
        share_copy(unit, 2, True).wait_recv()
        for step in range(3):
            share_copy(unit, step, False).wait_send()
        core_copy(unit).wait_send()
        one_copy(unit).wait_send()
        two_copy(unit).wait_send()
        for target in range(n_z):
            for way in range(2):
                pl.when(z < target if way == 0 else z > target)(
                    line_copy(unit, target, way).wait_send
                )

    barrier = pltpu.get_barrier_semaphore()
    load(0, False)
    for device in (mate, over_y, over_x):
        pl.semaphore_signal(barrier, inc=1, device_id=device, device_id_type=MESH)

    @pl.when(z < n_z - 1)
    def _():
        pl.semaphore_signal(barrier, inc=1, device_id=right, device_id_type=MESH)

    @pl.when(z > 0)
    def _():
        pl.semaphore_signal(barrier, inc=1, device_id=left, device_id_type=MESH)

    pl.semaphore_wait(barrier, jnp.where(jnp.logical_and(z > 0, z < n_z - 1), 5, 4))

    def tile_body(tile, carry):
        slot = lax.rem(tile, 2)
        load(tile, True)
        load(tile + 1, False)
        kind, owner = tile // 4, lax.rem(tile, 4)

        def half_body(half, carry):
            cols = pl.ds(pl.multiple_of(half * 4 * part, 4 * part), 4 * part)
            made = mm(left_buf[slot, :, cols], right_buf[slot], TN).astype(BF16)

            @pl.when(kind == 0)
            def _():
                for index in range(4):
                    both[index % 2, index // 2, owner, half, :part] = made[
                        index * part : (index + 1) * part
                    ]

            @pl.when(kind > 0)
            def _():
                rows = pl.ds(pl.multiple_of(kind * part, part), part)
                for index in range(4):
                    both[lax.rem(owner, 2), owner // 2, 2 * half + index // 2, index % 2, rows] = (
                        made[index * part : (index + 1) * part]
                    )

            return carry

        lax.fori_loop(0, 2, half_body, 0)
        for when_tile, step, units in (
            (3, start_core, (0, 1)),
            (6, start_one, (0, 1)),
            (7, start_core, (2, 3)),
            (10, start_one, (2, 3)),
        ):

            @pl.when(tile == when_tile)
            def _(step=step, units=units):
                for unit in units:
                    step(unit)

        return carry

    lax.fori_loop(0, TILES, tile_body, 0)
    load(TILES, True)
    made = mm(left_buf[TILES % 2], thin_buf[...], TN).astype(BF16)
    lanes = thin_buf.shape[1]
    top = sums[0][:8] + sums[1][:8] + sums[2][...] + sums[3][...]
    tail = jnp.concatenate([top, sums[0][8:] + sums[1][8:]], axis=0).astype(BF16)
    zeros = jnp.zeros_like(tail)
    last = pl.ds(3 * part, 16)
    for shard in range(2 * n_z):
        at_z, at_x = shard // 2, shard % 2
        for block in range(width // lanes):
            row = shard * part + block * 16
            both[0, 0, at_z, at_x, last, block * lanes : (block + 1) * lanes] = made[row : row + 16]
        both[1, 0, at_z, at_x, last] = tail
        both[0, 1, at_z, at_x, last] = zeros
        both[1, 1, at_z, at_x, last] = zeros
    for step, units in (
        (start_core, (4, 5)),
        (start_two, (0, 1)),
        (start_one, (4, 5)),
        (start_two, (2, 3)),
        (start_line, (0, 1)),
        (start_two, (4, 5)),
        (start_line, (2, 3)),
        (start_share, (0, 1, 2, 3)),
        (start_line, (4, 5)),
        (start_share, (4, 5)),
        (forward, range(count_units)),
        (finish, range(count_units)),
    ):
        for unit in units:
            step(unit)


def weight_gradients(arrays, sums, n_wide):
    n_z = n_wide // 2
    act, go, final, gp = arrays[0], arrays[1], arrays[9], arrays[10]
    total, width = go.shape
    part = width // n_wide
    units = len(UNITS)
    sem = pltpu.SemaphoreType.DMA
    vmem = pl.BlockSpec(memory_space=pltpu.VMEM)
    return pl.pallas_call(
        functools.partial(weights_kernel, n_z, part),
        out_shape=jax.ShapeDtypeStruct((4, SHARE_ROWS, width), BF16),
        in_specs=[ANY] * 11 + [vmem] * 4,
        out_specs=vmem,
        scratch_shapes=[
            pltpu.VMEM((2, 2, n_z, 2, SHARE_ROWS, width), BF16),
            pltpu.VMEM((2, n_z, 2, SHARE_ROWS, width), BF16),
            pltpu.VMEM((units // 2, n_z, 2, 48, width), BF16),
            pltpu.VMEM((units // 2, 2, n_z, HALF, width), BF16),
            pltpu.VMEM((units // 2, n_z, 48, width), BF16),
            pltpu.VMEM((units // 2, n_z, HALF, width), BF16),
            pltpu.VMEM((2, n_z, SHARE_ROWS, width), BF16),
            pltpu.VMEM((2, total, width), BF16),
            pltpu.VMEM((2, total, width), BF16),
            pltpu.VMEM(gp.shape, BF16),
            sem((2, 3)),
        ]
        + [sem((units,))] * 6
        + [sem((units * n_z * 2,))] * 2
        + [sem((units * 3,))] * 2,
        compiler_params=pltpu.CompilerParams(
            collective_id=3, has_side_effects=True, vmem_limit_bytes=VMEM_LIMIT
        ),
        name="weight_gradients",
    )(*arrays, *sums)


def outer(left, right):
    return lax.dot_general(left, right, TN, preferred_element_type=F32)


def local(
    query_states,
    passage_states,
    lengths,
    positives,
    query_weight,
    query_bias,
    key_weight,
    value_weight,
    value_bias,
    out_weight,
    out_bias,
    first_gain,
    first_shift,
    inner_weight,
    inner_bias,
    outer_weight,
    outer_bias,
    second_gain,
    second_shift,
    linear_weight,
):
    everyone = ("wide", "narrow")
    n_wide = lax.axis_size("wide")
    n_narrow = lax.axis_size("narrow")
    wide_index = lax.axis_index("wide")
    narrow_index = lax.axis_index("narrow")
    micro, own_queries, query_len, width = query_states.shape
    own_passages, slots = passage_states.shape[1:3]
    weights = (
        query_weight,
        key_weight,
        value_weight,
        out_weight,
        inner_weight,
        outer_weight,
        linear_weight,
    )
    embed_width = linear_weight.shape[1]
    vec = (
        jnp.concatenate(
            [
                query_bias,
                value_bias,
                out_bias,
                first_gain,
                first_shift,
                outer_bias,
                second_gain,
                second_shift,
                inner_bias,
            ]
        )
        .astype(F32)
        .reshape(-1, width)
    )
    vec = jnp.pad(vec, ((0, -vec.shape[0] % 8), (0, 0)))
    own_index = narrow_index * n_wide + wide_index
    own_lengths = lax.dynamic_slice_in_dim(lengths, own_index * own_passages, own_passages, axis=1)
    lens = own_lengths.reshape(-1)
    x_query = query_states.reshape(-1, width)
    x_passage = passage_states.reshape(-1, width)
    query_rows, passage_rows = x_query.shape[0], x_passage.shape[0]
    total = query_rows + passage_rows
    kept_q = encode(
        x_query, lens, vec, weights, 1, query_len, total, passage_rows, None, None
    )
    sizes = (n_wide, n_narrow)
    kept_p = encode(
        x_passage, lens, vec, weights, micro * own_passages, 0, total, 0, kept_q, sizes
    )
    queries = kept_p[16].reshape(n_wide * n_narrow, micro, -1, embed_width)
    ctx, first_low, act, final_low = (kept_p[index] for index in (4, 7, 8, 12))
    passages = kept_p[15].reshape(micro * own_passages, slots, embed_width)
    e, z = similarity(queries, passages, lens)
    best = SHARP + jnp.log(z)
    own_scores = jnp.sum(best.reshape(micro, -1, query_len), axis=-1) / SHARP
    full = share_scores(own_scores, n_wide, n_narrow)
    row_total = jax.nn.logsumexp(full, axis=0)
    passage_ids = jnp.arange(full.shape[0], dtype=jnp.int32)
    picked = jnp.sum(
        jnp.where(passage_ids[:, None, None] == positives[None], full, 0.0), axis=0
    )
    row_count = own_queries * n_narrow
    losses = lax.dynamic_slice_in_dim(row_total - picked, wide_index * row_count, row_count, axis=1)
    block = lax.dynamic_slice(
        full,
        (narrow_index * n_wide, 0, wide_index * row_count),
        (n_wide, micro, row_count),
    )
    scores = jnp.transpose(block, (1, 2, 0))
    grads = jnp.exp(own_scores - row_total) - (positives == own_index).astype(F32)
    token_weights = jnp.repeat(grads, query_len, axis=1).reshape(z.shape) / z
    grad_passage, grad_query = similarity_back(e, token_weights, queries, passages)
    grad_query = grad_query.reshape(-1, 2, query_rows, embed_width)
    grad_passage = grad_passage.reshape(passage_rows, embed_width)
    together = grad_query.size <= 4 * total * width
    back_p = mlp_back(
        grad_passage,
        kept_p,
        vec,
        weights,
        micro * own_passages,
        total,
        0,
        None,
        grad_query if together else None,
        sizes if together else None,
    )
    grad_query = back_p[6] if together else exchange(grad_query, n_wide, n_narrow)
    back_q = mlp_back(
        grad_query, kept_q, vec, weights, 1, total, passage_rows, back_p, None, None
    )
    gp, go, gi, _, ga, sums_q = back_q[:6]
    att_p = attention_back(ga, back_p[3], kept_p, weights, micro * own_passages, total, 0, None)
    att_q = attention_back(ga, back_q[3], kept_q, weights, 1, total, passage_rows, att_p[0])
    gqkv = att_q[0]
    part = width // n_wide
    if part == 96 and n_narrow == 4 and act.shape[1] == 4 * width:
        summed = weight_gradients(
            (act, go, first_low, gi, x_passage, x_query, gqkv, ctx, ga, final_low, gp),
            (back_p[5], sums_q, att_p[2], att_q[2]),
            n_wide,
        ).astype(F32)
        r_outer = summed[:, :part].reshape(4 * part, width)
        r_inner = summed[:, part : 2 * part].transpose(1, 0, 2).reshape(part, 4 * width)
        r_q, r_k, r_v, r_out = (summed[index, 2 * part : 3 * part] for index in range(4))
        thin = summed[0, 3 * part :].reshape(16, -1, embed_width)
        r_linear = thin.transpose(1, 0, 2).reshape(part, embed_width)
        vectors = summed[1, 3 * part :]
        own = lax.dynamic_slice_in_dim(vectors[:8], wide_index * part, part, axis=1)
        v_q, v_v, v_o, v_g1, v_s1, v_2, v_g2, v_s2 = (
            own[row] for row in (0, 1, ROW_BO, ROW_G1, ROW_S1, ROW_B2, ROW_G2, ROW_S2)
        )
        v_i = lax.dynamic_slice_in_dim(
            vectors[ROW_BI : ROW_BI + 4].reshape(-1), wide_index * 4 * part, 4 * part
        )
    else:

        def reduce(value):
            piece = lax.psum_scatter(value.astype(BF16), everyone, scatter_dimension=0, tiled=True)
            return lax.all_gather(piece, "narrow", axis=0, tiled=True).astype(F32)

        def vector(rows):
            flat = rows.reshape(-1)
            share = flat.shape[0] // n_wide
            return lax.dynamic_slice_in_dim(flat, wide_index * share, share)

        sums = jnp.concatenate([back_p[5] + sums_q, att_p[2] + att_q[2]], axis=0)
        sums = lax.psum(sums, everyone)
        x_all = jnp.concatenate([x_passage, x_query], axis=0)
        pairs = ((act, go), (first_low, gi), (final_low, gp), (ctx, ga), (x_all, gqkv))
        r_outer, r_inner, r_linear, r_out, r_qkv = (
            reduce(outer(*pair)) for pair in pairs
        )
        r_q, r_k, r_v = (r_qkv[:, index * width : (index + 1) * width] for index in range(3))
        v_q, v_v, v_o, v_g1, v_s1, v_2, v_g2, v_s2 = (
            vector(sums[pick])
            for pick in (16, 17, ROW_BO, ROW_G1, ROW_S1, ROW_B2, ROW_G2, ROW_S2)
        )
        v_i = vector(sums[ROW_BI : ROW_BI + 4])
    return (
        scores,
        losses,
        att_q[1].reshape(query_states.shape),
        att_p[1].reshape(passage_states.shape),
        r_q,
        v_q,
        r_k,
        r_v,
        v_v,
        r_out,
        v_o,
        v_g1,
        v_s1,
        r_inner,
        v_i,
        r_outer,
        v_2,
        v_g2,
        v_s2,
        r_linear,
    )


def solution(mesh):
    return jax.shard_map(
        local,
        mesh=mesh,
        in_specs=(
            P(None, ("wide", "narrow"), None, None),
            P(None, ("narrow", "wide"), None, None),
        )
        + (P(),) * 18,
        out_specs=(
            P(None, "wide", "narrow"),
            P(None, "wide"),
            P(None, ("wide", "narrow"), None, None),
            P(None, ("narrow", "wide"), None, None),
            P("wide", None),
            P("wide"),
            P("wide", None),
            P("wide", None),
            P("wide"),
            P("wide", None),
            P("wide"),
            P("wide"),
            P("wide"),
            P("wide", None),
            P("wide"),
            P("wide", None),
            P("wide"),
            P("wide"),
            P("wide"),
            P("wide", None),
        ),
        check_vma=False,
    )
```

```python
import functools

import jax
import jax.numpy as jnp
from jax import lax
from jax.experimental import pallas as pl
from jax.experimental.pallas import tpu as pltpu
from jax.sharding import PartitionSpec as P

HEADS = 12
HEAD_DIM = 64
SHARP = 16.0
LAYER_EPS = 1e-12
NORM_EPS = 1e-06
MASKED = -1e30
SLOPE_CONST = 0.3989422804014327
ROOT_HALF = 0.7071067811865476
BF16 = jnp.bfloat16
F32 = jnp.float32
VMEM_LIMIT = 62 * 1024 * 1024

NN = (((1,), (0,)), ((), ()))
NT = (((1,), (1,)), ((), ()))
TN = (((0,), (0,)), ((), ()))


def mm(left, right, dims=NN):
    return lax.dot_general(left, right, dims, preferred_element_type=F32)


ANY = pl.BlockSpec(memory_space=pl.ANY)

ROW_BQ, ROW_BV, ROW_BO, ROW_G1, ROW_S1, ROW_B2, ROW_G2, ROW_S2, ROW_BI = range(9)


def vec_row(vec_ref, row):
    return vec_ref[row : row + 1, :]


def mean_row(value):
    return jnp.sum(value, axis=-1, keepdims=True) * (1.0 / value.shape[-1])


class Loader:
    def __init__(self, sources, targets, sem):
        self.copies = [
            pltpu.make_async_copy(source, target, sem.at[index])
            for index, (source, target) in enumerate(zip(sources, targets))
        ]
        self.first = pl.program_id(0) == 0

    def start(self):
        @pl.when(self.first)
        def _():
            for copy in self.copies:
                copy.start()

    def need(self, *indices):
        @pl.when(self.first)
        def _():
            for index in indices:
                self.copies[index].wait()


MESH = pl.DeviceIdType.MESH


def remote(source, target, sems, index, device):
    return pltpu.make_async_remote_copy(
        src_ref=source,
        dst_ref=target,
        send_sem=sems[0].at[index],
        recv_sem=sems[1].at[index],
        device_id=device,
        device_id_type=MESH,
    )


class Chips:
    def __init__(self, n_wide, n_narrow):
        self.wide, self.narrow = lax.axis_index("wide"), lax.axis_index("narrow")
        self.core = lax.rem(self.narrow, 2)
        self.rows = n_narrow // 2
        self.count = n_wide * self.rows
        self.me = self.wide * self.rows + self.narrow // 2
        self.mate = (self.wide, self.narrow + 1 - 2 * self.core)

    def at(self, step):
        return lax.rem(self.me + step + self.count, self.count)

    def device(self, chip):
        return (chip // self.rows, lax.rem(chip, self.rows) * 2 + self.core)

    def loop(self, body):
        def step_body(step, carry):
            body(step)
            return carry

        lax.fori_loop(1, self.count, step_body, 0)

    def barrier(self):
        barrier = pltpu.get_barrier_semaphore()

        def signal(step):
            pl.semaphore_signal(
                barrier, inc=1, device_id=self.device(self.at(step)), device_id_type=MESH
            )

        pl.semaphore_signal(barrier, inc=1, device_id=self.mate, device_id_type=MESH)
        self.loop(signal)
        pl.semaphore_wait(barrier, self.count)


class Gather:
    def __init__(self, chips, own, out, sems):
        self.chips, self.own, self.out = chips, own, out
        self.far, self.pair, self.local = sems[:2], sems[2:4], sems[4]

    def far_copy(self, step, chip):
        slot = self.out.at[chip, self.chips.core]
        return remote(self.own, slot, self.far, step, self.chips.device(self.chips.at(step)))

    def mate_copy(self, core):
        block = self.out.at[:, core]
        return remote(block, block, self.pair, 0, self.chips.mate)

    def local_copy(self):
        slot = self.out.at[self.chips.me, self.chips.core]
        return pltpu.make_async_copy(self.own, slot, self.local.at[0])

    def start(self):
        self.local_copy().start()
        self.chips.barrier()
        self.chips.loop(lambda step: self.far_copy(step, self.chips.me).start())

    def forward(self):
        self.local_copy().wait()
        self.chips.loop(lambda step: self.far_copy(step, self.chips.at(-step)).wait_recv())
        self.mate_copy(self.chips.core).start()

    def finish(self):
        self.chips.loop(lambda step: self.far_copy(step, self.chips.me).wait_send())
        self.mate_copy(1 - self.chips.core).wait_recv()
        self.mate_copy(self.chips.core).wait_send()


class Exchange:
    def __init__(self, chips, grads, out, scratch):
        self.chips, self.grads, self.out = chips, grads, out
        self.half, self.arrived, self.inbox = scratch[:3]
        self.pair, self.far, self.local = scratch[3:5], scratch[5:7], scratch[7]

    def pair_copy(self):
        away = self.grads.at[:, 1 - self.chips.core]
        return remote(away, self.arrived, self.pair, 0, self.chips.mate)

    def local_copy(self):
        mine = self.grads.at[:, self.chips.core]
        return pltpu.make_async_copy(mine, self.half, self.local.at[0])

    def far_copy(self, step):
        chip = self.chips.at(step)
        return remote(
            self.half.at[chip], self.inbox.at[step], self.far, step, self.chips.device(chip)
        )

    def start(self):
        self.local_copy().start()
        self.chips.barrier()
        self.pair_copy().start()

    def push(self):
        self.local_copy().wait()
        self.pair_copy().wait_recv()

        def add(step):
            chip = self.chips.at(step)
            total = self.half[chip].astype(F32) + self.arrived[chip].astype(F32)
            self.half[chip] = total.astype(BF16)
            self.far_copy(step).start()

        self.chips.loop(add)
        me = self.chips.me
        self.out[...] = self.half[me].astype(F32) + self.arrived[me].astype(F32)

    def finish(self):
        def collect(step):
            copy = self.far_copy(step)
            copy.wait_recv()
            copy.wait_send()
            self.out[...] += self.inbox[step].astype(F32)

        self.chips.loop(collect)
        self.pair_copy().wait_send()


def exchange_scratch(chips, rows, width):
    sem = pltpu.SemaphoreType.DMA
    return [pltpu.VMEM((chips, rows, width), BF16)] * 3 + [
        sem((1,)),
        sem((1,)),
        sem((chips,)),
        sem((chips,)),
        sem((1,)),
    ]


def fwd_kernel(grouped, alias_count, sizes, *refs):
    lens_ref, x_ref, vec_ref = refs[:3]
    sources = refs[3:10]
    refs = refs[10 + alias_count :]
    gather = None
    if sizes:
        gather = Gather(Chips(*sizes), refs[0], refs[17], refs[-5:])
        refs = refs[1:17] + refs[18:-5]
    (
        q_ref,
        k_ref,
        v_ref,
        att_ref,
        ctx_ref,
        n1_ref,
        r1_ref,
        first_ref,
        act_ref,
        slope_ref,
        n2_ref,
        r2_ref,
        final_ref,
        unit_ref,
        uinv_ref,
        embed_ref,
    ) = refs[:16]
    wq, wk, wv, wo, wi, w2, wl, sem, acc_ref = refs[16:]
    loader = Loader(sources, (wq, wk, wv, wo, wi, w2, wl), sem)
    loader.start()
    if gather:
        last = pl.program_id(0) == pl.num_programs(0) - 1
        pl.when(loader.first)(gather.start)
    rows = x_ref.shape[0]
    x = x_ref[...]
    scale = HEAD_DIM ** (-0.5)
    loader.need(0)
    q_ref[...] = ((mm(x, wq[...]) + vec_row(vec_ref, ROW_BQ)).astype(BF16) * scale).astype(BF16)
    loader.need(1)
    k_ref[...] = mm(x, wk[...]).astype(BF16)
    loader.need(2)
    v_ref[...] = (mm(x, wv[...]) + vec_row(vec_ref, ROW_BV)).astype(BF16)
    if grouped:
        valid = (
            lax.broadcasted_iota(jnp.int32, (rows, rows), 0) // grouped
            == lax.broadcasted_iota(jnp.int32, (rows, rows), 1) // grouped
        )
    else:
        length = lens_ref[pl.program_id(0)]
        valid = lax.broadcasted_iota(jnp.int32, (1, rows), 1) < length
    bias = jnp.where(valid, 0.0, MASKED)
    low_half = lax.broadcasted_iota(jnp.int32, (rows, 128), 1) < HEAD_DIM

    def pair_body(pair, carry):
        cols = pl.ds(pl.multiple_of(pair * 128, 128), 128)
        q_pair, k_pair, v_pair = q_ref[:, cols], k_ref[:, cols], v_ref[:, cols]
        parts = []
        for half in range(2):
            mask = low_half if half == 0 else jnp.logical_not(low_half)
            logits = mm(jnp.where(mask, q_pair, jnp.zeros_like(q_pair)), k_pair, NT) + bias
            peak = jnp.max(logits, axis=-1, keepdims=True)
            e = jnp.exp(logits - peak)
            inv = 1.0 / jnp.sum(e, axis=-1, keepdims=True)
            low = (e * inv).astype(BF16)
            att_ref[0, 2 * pair + half] = low
            parts.append(mm(low, v_pair))
        ctx_ref[:, cols] = jnp.where(low_half, parts[0], parts[1]).astype(BF16)
        return carry

    lax.fori_loop(0, HEADS // 2, pair_body, 0)
    if gather:
        pl.when(last)(gather.forward)
    loader.need(3)
    field = x.astype(F32) + (mm(ctx_ref[...], wo[...]) + vec_row(vec_ref, ROW_BO))
    center = field - mean_row(field)
    inverse = lax.rsqrt(mean_row(center * center) + LAYER_EPS)
    normed = center * inverse
    n1_ref[...] = normed.astype(BF16)
    r1_ref[...] = jnp.broadcast_to(inverse, r1_ref.shape)
    first = normed * vec_row(vec_ref, ROW_G1) + vec_row(vec_ref, ROW_S1)
    first_ref[...] = first.astype(BF16)
    acc_ref[...] = first + vec_row(vec_ref, ROW_B2)
    loader.need(4, 5)
    width = x.shape[1]

    def chunk_body(chunk, carry):
        cols = pl.ds(pl.multiple_of(chunk * width, width), width)
        inner = mm(first_ref[...], wi[:, cols]) + vec_ref[pl.ds(ROW_BI + chunk, 1), :]
        phi = 0.5 * (1.0 + lax.erf(inner * ROOT_HALF))
        activated = (inner * phi).astype(BF16)
        act_ref[:, cols] = activated
        slope_ref[:, cols] = (phi + inner * jnp.exp(-0.5 * inner * inner) * SLOPE_CONST).astype(
            BF16
        )
        acc_ref[...] += mm(activated, w2[cols, :])
        return carry

    lax.fori_loop(0, wi.shape[1] // width, chunk_body, 0)
    field = acc_ref[...]
    center = field - mean_row(field)
    inverse = lax.rsqrt(mean_row(center * center) + LAYER_EPS)
    normed = center * inverse
    n2_ref[...] = normed.astype(BF16)
    r2_ref[...] = jnp.broadcast_to(inverse, r2_ref.shape)
    final = (normed * vec_row(vec_ref, ROW_G2) + vec_row(vec_ref, ROW_S2)).astype(BF16)
    final_ref[...] = final
    loader.need(6)
    projected = mm(final, wl[...])
    uinv = lax.rsqrt(jnp.sum(projected * projected, axis=-1, keepdims=True) + NORM_EPS)
    unit = projected * uinv
    unit_ref[...] = unit
    uinv_ref[...] = jnp.broadcast_to(uinv, uinv_ref.shape)
    embed_ref[...] = unit.astype(BF16)
    if gather:
        pl.when(last)(gather.finish)


def encode(x, lens, vec, weights, blocks, grouped, total, offset, earlier, sizes):
    rows = x.shape[0] // blocks
    width = x.shape[1]
    wide = weights[4].shape[1]
    embed_width = weights[6].shape[1]
    base = offset // rows

    def row_spec(columns):
        return pl.BlockSpec((rows, columns), lambda i, lens: (base + i, 0))

    def own_spec(columns):
        return pl.BlockSpec((rows, columns), lambda i, lens: (i, 0))

    def shape(count, columns, dtype):
        return jax.ShapeDtypeStruct((count, columns), dtype)

    own = x.shape[0]
    out_shapes = [
        shape(own, width, BF16),
        shape(own, width, BF16),
        shape(own, width, BF16),
        jax.ShapeDtypeStruct((blocks, HEADS, rows, rows), BF16),
        shape(total, width, BF16),
        shape(own, width, BF16),
        shape(own, embed_width, F32),
        shape(total, width, BF16),
        shape(total, wide, BF16),
        shape(own, wide, BF16),
        shape(own, width, BF16),
        shape(own, embed_width, F32),
        shape(total, width, BF16),
        shape(own, embed_width, F32),
        shape(own, embed_width, F32),
        shape(own, embed_width, BF16),
    ]
    shared = (4, 7, 8, 12)
    out_specs = [
        pl.BlockSpec((1, HEADS, rows, rows), lambda i, lens: (i, 0, 0, 0))
        if index == 3
        else (row_spec if index in shared else own_spec)(out.shape[1])
        for index, out in enumerate(out_shapes)
    ]
    aliased = [] if earlier is None else [earlier[index] for index in shared]
    sends, sem_shapes, params = [], [], {}
    if sizes:
        sends = [earlier[15]]
        chips = sizes[0] * sizes[1] // 2
        out_shapes.append(jax.ShapeDtypeStruct((chips, 2) + earlier[15].shape, BF16))
        out_specs.append(ANY)
        sem = pltpu.SemaphoreType.DMA
        sem_shapes = [sem((chips,)), sem((chips,)), sem((1,)), sem((1,)), sem((1,))]
        params = {"collective_id": 4, "has_side_effects": True}
    return pl.pallas_call(
        functools.partial(fwd_kernel, grouped, len(aliased), sizes),
        out_shape=out_shapes,
        grid_spec=pltpu.PrefetchScalarGridSpec(
            num_scalar_prefetch=1,
            grid=(blocks,),
            in_specs=[
                own_spec(width),
                pl.BlockSpec(vec.shape, lambda i, lens: (0, 0)),
            ]
            + [ANY] * (7 + len(aliased) + len(sends)),
            out_specs=out_specs,
            scratch_shapes=[pltpu.VMEM(weight.shape, BF16) for weight in weights]
            + [pltpu.SemaphoreType.DMA((7,)), pltpu.VMEM((rows, width), F32)]
            + sem_shapes,
        ),
        input_output_aliases={10 + index: shared[index] for index in range(len(aliased))},
        compiler_params=pltpu.CompilerParams(vmem_limit_bytes=VMEM_LIMIT, **params),
        name="encode_queries" if grouped else "encode_passages",
    )(lens, x, vec, *weights, *aliased, *sends)


def sims_kernel(lens_ref, q_ref, p_ref, e_ref, z_ref):
    count = q_ref.shape[0]
    tokens = count * q_ref.shape[2]
    query = q_ref[...].reshape(tokens, q_ref.shape[3])
    sims = mm(p_ref[0], query, NT)
    slot = lax.broadcasted_iota(jnp.int32, sims.shape, 0)
    e = jnp.where(slot < lens_ref[pl.program_id(0)], jnp.exp(SHARP * sims - SHARP), 0.0)
    e_ref[0] = e.astype(BF16)
    z = jnp.sum(e, axis=0, keepdims=True)
    step = q_ref.shape[2]
    for index in range(count):
        z_ref[0, index : index + 1, :] = z[:, index * step : (index + 1) * step]


def sims_back_kernel(e_ref, w_ref, q_ref, p_ref, gp_ref, gq_ref):
    count = q_ref.shape[0]
    step = q_ref.shape[2]
    query = q_ref[...].reshape(count * step, q_ref.shape[3])
    weight = jnp.concatenate([w_ref[0, index : index + 1, :] for index in range(count)], axis=1)
    grads = (e_ref[0].astype(F32) * weight).astype(BF16)
    part = mm(grads, query)

    @pl.when(pl.program_id(1) == 0)
    def _():
        gp_ref[0] = part

    @pl.when(pl.program_id(1) > 0)
    def _():
        gp_ref[0] += part

    gq_ref[...] = mm(grads, p_ref[0], TN).astype(BF16).reshape(gq_ref.shape)


def similarity(queries, passages, lens):
    devices, micro, tokens, width = queries.shape
    slots = passages.shape[1]
    group = 8
    e, z = pl.pallas_call(
        sims_kernel,
        out_shape=(
            jax.ShapeDtypeStruct((micro, slots, devices * tokens), BF16),
            jax.ShapeDtypeStruct((micro, devices, tokens), F32),
        ),
        grid_spec=pltpu.PrefetchScalarGridSpec(
            num_scalar_prefetch=1,
            grid=(micro, devices // group),
            in_specs=[
                pl.BlockSpec((group, 1, tokens, width), lambda m, b, lens: (b, m, 0, 0)),
                pl.BlockSpec((1, slots, width), lambda m, b, lens: (m, 0, 0)),
            ],
            out_specs=(
                pl.BlockSpec((1, slots, group * tokens), lambda m, b, lens: (m, 0, b)),
                pl.BlockSpec((1, group, tokens), lambda m, b, lens: (m, b, 0)),
            ),
        ),
        compiler_params=pltpu.CompilerParams(vmem_limit_bytes=VMEM_LIMIT),
        name="similarity",
    )(lens, queries, passages)
    return e, z


def similarity_back(e, weights, queries, passages):
    devices, micro, tokens, width = queries.shape
    slots = passages.shape[1]
    group = 8
    return pl.pallas_call(
        sims_back_kernel,
        out_shape=(
            jax.ShapeDtypeStruct((micro, slots, width), F32),
            jax.ShapeDtypeStruct((devices, micro, tokens, width), BF16),
        ),
        grid=(micro, devices // group),
        in_specs=[
            pl.BlockSpec((1, slots, group * tokens), lambda m, b: (m, 0, b)),
            pl.BlockSpec((1, group, tokens), lambda m, b: (m, b, 0)),
            pl.BlockSpec((group, 1, tokens, width), lambda m, b: (b, m, 0, 0)),
            pl.BlockSpec((1, slots, width), lambda m, b: (m, 0, 0)),
        ],
        out_specs=(
            pl.BlockSpec((1, slots, width), lambda m, b: (m, 0, 0)),
            pl.BlockSpec((group, 1, tokens, width), lambda m, b: (b, m, 0, 0)),
        ),
        compiler_params=pltpu.CompilerParams(vmem_limit_bytes=VMEM_LIMIT),
        name="similarity_back",
    )(e, weights, queries, passages)


def accumulate(ref, row, value):
    ref[row : row + 1, :] += jnp.sum(value, axis=0, keepdims=True)


def mlp_back_kernel(alias_count, sizes, *refs):
    (
        ge_ref,
        unit_ref,
        uinv_ref,
        n2_ref,
        r2_ref,
        slope_ref,
        n1_ref,
        r1_ref,
        vec_ref,
    ) = refs[:9]
    sources = refs[9:12]
    refs = refs[12 + alias_count :]
    swap = None
    if sizes:
        swap = Exchange(Chips(*sizes), refs[0], refs[7], refs[-8:])
        refs = refs[1:7] + refs[8:-8]
    gp_ref, go_ref, gi_ref, gh_ref, ga_ref, sums_ref = refs[:6]
    wl, w2, wi, sem, acc_ref = refs[6:]
    loader = Loader(sources, (wl, w2, wi), sem)
    loader.start()
    if swap:
        pl.when(loader.first)(swap.start)

    @pl.when(loader.first)
    def _():
        sums_ref[...] = jnp.zeros_like(sums_ref)

    grad = ge_ref[...]
    unit = unit_ref[...]
    projected_low = (
        uinv_ref[...] * (grad - unit * jnp.sum(grad * unit, axis=-1, keepdims=True))
    ).astype(BF16)
    gp_ref[...] = projected_low
    loader.need(0)
    grad_final = mm(projected_low, wl[...], NT)
    normed = n2_ref[...].astype(F32)
    accumulate(sums_ref, ROW_G2, grad_final * normed)
    accumulate(sums_ref, ROW_S2, grad_final)
    scaled = grad_final * vec_row(vec_ref, ROW_G2)
    grad_second = r2_ref[:, :1] * (scaled - mean_row(scaled) - normed * mean_row(scaled * normed))
    outer_low = grad_second.astype(BF16)
    go_ref[...] = outer_low
    accumulate(sums_ref, ROW_B2, outer_low.astype(F32))
    acc_ref[...] = grad_second
    if swap:
        pl.when(loader.first)(swap.push)
    loader.need(1, 2)
    width = go_ref.shape[1]

    def chunk_body(chunk, carry):
        cols = pl.ds(pl.multiple_of(chunk * width, width), width)
        grad_act = mm(go_ref[...], w2[cols, :], NT)
        inner = (grad_act * slope_ref[:, cols].astype(F32)).astype(BF16)
        gi_ref[:, cols] = inner
        sums_ref[pl.ds(ROW_BI + chunk, 1), :] += jnp.sum(
            inner.astype(F32), axis=0, keepdims=True
        )
        acc_ref[...] += mm(inner, wi[:, cols], NT)
        return carry

    lax.fori_loop(0, wi.shape[1] // width, chunk_body, 0)
    grad_first = acc_ref[...]
    normed = n1_ref[...].astype(F32)
    accumulate(sums_ref, ROW_G1, grad_first * normed)
    accumulate(sums_ref, ROW_S1, grad_first)
    scaled = grad_first * vec_row(vec_ref, ROW_G1)
    hidden = r1_ref[:, :1] * (scaled - mean_row(scaled) - normed * mean_row(scaled * normed))
    gh_ref[...] = hidden
    low = hidden.astype(BF16)
    ga_ref[...] = low
    accumulate(sums_ref, ROW_BO, low.astype(F32))
    if swap:
        pl.when(pl.program_id(0) == pl.num_programs(0) - 1)(swap.finish)


def mlp_back(grad_embed, kept, vec, weights, blocks, total, offset, earlier, sent, sizes):
    own = grad_embed.shape[0]
    rows = own // blocks
    base = offset // rows
    _, _, _, _, wi, w2, wl = weights
    width, wide = wi.shape
    embed_width = wl.shape[1]

    def row_spec(columns):
        return pl.BlockSpec((rows, columns), lambda i: (base + i, 0))

    def own_spec(columns):
        return pl.BlockSpec((rows, columns), lambda i: (i, 0))

    args = [grad_embed] + [kept[index] for index in (13, 14, 10, 11, 9, 5, 6)]
    out_shapes = [
        jax.ShapeDtypeStruct((total, embed_width), BF16),
        jax.ShapeDtypeStruct((total, width), BF16),
        jax.ShapeDtypeStruct((total, wide), BF16),
        jax.ShapeDtypeStruct((own, width), F32),
        jax.ShapeDtypeStruct((total, width), BF16),
        jax.ShapeDtypeStruct((16, width), F32),
    ]
    shared = (0, 1, 2, 4)
    out_specs = [
        (row_spec if index in shared else own_spec)(out.shape[1])
        for index, out in enumerate(out_shapes[:5])
    ] + [pl.BlockSpec((16, width), lambda i: (0, 0))]
    aliased = [] if earlier is None else [earlier[index] for index in shared]
    sends, scratch, params = [], [], {}
    if sizes:
        sends = [sent]
        out_shapes.append(jax.ShapeDtypeStruct(sent.shape[2:], F32))
        out_specs.append(pl.BlockSpec(sent.shape[2:], lambda i: (0, 0)))
        scratch = exchange_scratch(sent.shape[0], *sent.shape[2:])
        params = {"collective_id": 2, "has_side_effects": True}
    return pl.pallas_call(
        functools.partial(mlp_back_kernel, len(aliased), sizes),
        out_shape=out_shapes,
        grid=(blocks,),
        in_specs=[own_spec(arg.shape[1]) for arg in args]
        + [pl.BlockSpec(vec.shape, lambda i: (0, 0))]
        + [ANY] * (3 + len(aliased) + len(sends)),
        out_specs=out_specs,
        scratch_shapes=[pltpu.VMEM(weight.shape, BF16) for weight in (wl, w2, wi)]
        + [pltpu.SemaphoreType.DMA((3,)), pltpu.VMEM((rows, width), F32)]
        + scratch,
        input_output_aliases={12 + index: shared[index] for index in range(len(aliased))},
        compiler_params=pltpu.CompilerParams(vmem_limit_bytes=VMEM_LIMIT, **params),
        name="mlp_back_queries" if earlier is not None else "mlp_back_passages",
    )(*args, vec, wl, w2, wi, *aliased, *sends)


def attention_back_kernel(alias_count, *refs):
    ga_ref, gh_ref, att_ref, q_ref, k_ref, v_ref = refs[:6]
    sources = refs[6:10]
    refs = refs[10 + alias_count :]
    gqkv_ref, gx_ref, sums_ref = refs[:3]
    wo, wq, wk, wv, sem, gc_ref = refs[3:]
    loader = Loader(sources, (wo, wq, wk, wv), sem)
    loader.start()

    @pl.when(loader.first)
    def _():
        sums_ref[...] = jnp.zeros_like(sums_ref)

    rows, width = gh_ref.shape
    scale = HEAD_DIM ** (-0.5)
    loader.need(0)
    gc_ref[...] = mm(ga_ref[...], wo[...], NT).astype(BF16)
    low_half = lax.broadcasted_iota(jnp.int32, (rows, 128), 1) < HEAD_DIM

    def pair_body(pair, carry):
        cols = pl.ds(pl.multiple_of(pair * 128, 128), 128)
        q_pair, k_pair, v_pair, gc_pair = q_ref[:, cols], k_ref[:, cols], v_ref[:, cols], gc_ref[:, cols]
        parts = []
        for half in range(2):
            mask = low_half if half == 0 else jnp.logical_not(low_half)
            low = att_ref[0, 2 * pair + half]
            att = low.astype(F32)
            grad_att = mm(jnp.where(mask, gc_pair, jnp.zeros_like(gc_pair)), v_pair, NT)
            weighted = grad_att * att
            grad_logits = (weighted - att * jnp.sum(weighted, axis=-1, keepdims=True)).astype(BF16)
            parts.append(
                (
                    mm(grad_logits, k_pair) * scale,
                    mm(grad_logits, q_pair, TN),
                    mm(low, gc_pair, TN),
                )
            )
        for index in range(3):
            gqkv_ref[:, pl.ds(pl.multiple_of(index * width + pair * 128, 128), 128)] = jnp.where(
                low_half, parts[0][index], parts[1][index]
            ).astype(BF16)
        return carry

    lax.fori_loop(0, HEADS // 2, pair_body, 0)
    loader.need(1, 2, 3)
    grad_q, grad_k, grad_v = (
        gqkv_ref[:, :width],
        gqkv_ref[:, width : 2 * width],
        gqkv_ref[:, 2 * width :],
    )
    accumulate(sums_ref, 0, grad_q.astype(F32))
    accumulate(sums_ref, 1, grad_v.astype(F32))
    gx_ref[...] = (
        gh_ref[...]
        + mm(grad_q, wq[...], NT)
        + mm(grad_k, wk[...], NT)
        + mm(grad_v, wv[...], NT)
    )


def attention_back(attended, hidden, kept, weights, blocks, total, offset, earlier):
    own, width = hidden.shape
    rows = own // blocks
    base = offset // rows
    wq, wk, wv, wo = weights[:4]

    def row_spec(columns):
        return pl.BlockSpec((rows, columns), lambda i: (base + i, 0))

    def own_spec(columns):
        return pl.BlockSpec((rows, columns), lambda i: (i, 0))

    aliased = [] if earlier is None else [earlier]
    return pl.pallas_call(
        functools.partial(attention_back_kernel, len(aliased)),
        out_shape=(
            jax.ShapeDtypeStruct((total, 3 * width), BF16),
            jax.ShapeDtypeStruct((own, width), F32),
            jax.ShapeDtypeStruct((8, width), F32),
        ),
        grid=(blocks,),
        in_specs=[
            row_spec(width),
            own_spec(width),
            pl.BlockSpec((1, HEADS, rows, rows), lambda i: (i, 0, 0, 0)),
            own_spec(width),
            own_spec(width),
            own_spec(width),
        ]
        + [ANY] * (4 + len(aliased)),
        out_specs=(
            row_spec(3 * width),
            own_spec(width),
            pl.BlockSpec((8, width), lambda i: (0, 0)),
        ),
        scratch_shapes=[pltpu.VMEM(weight.shape, BF16) for weight in weights[:4]]
        + [pltpu.SemaphoreType.DMA((4,)), pltpu.VMEM((rows, width), BF16)],
        input_output_aliases={10: 0} if aliased else {},
        compiler_params=pltpu.CompilerParams(vmem_limit_bytes=VMEM_LIMIT),
        name="attention_back_queries" if aliased else "attention_back_passages",
    )(attended, hidden, kept[3], kept[0], kept[1], kept[2], wo, wq, wk, wv, *aliased)


def pack(vectors, width):
    count = sum(vector.shape[0] for vector in vectors)
    total = -(-count // (8 * width)) * 8 * width
    start, packed = 0, 0.0
    for vector in vectors:
        size = vector.shape[0]
        packed = packed + jnp.pad(vector.astype(F32), (start, total - start - size))
        start += size
    return packed.reshape(-1, width)


def share_kernel(n_wide, n_narrow, own_ref, all_ref, send_sem, recv_sem):
    me = lax.axis_index("narrow") * n_wide + lax.axis_index("wide")
    total = n_wide * n_narrow
    sems = (send_sem, recv_sem)

    def device(index):
        return (lax.rem(index, n_wide), index // n_wide)

    barrier = pltpu.get_barrier_semaphore()

    def signal(step, carry):
        pl.semaphore_signal(
            barrier, inc=1, device_id=device(lax.rem(me + step, total)), device_id_type=MESH
        )
        return carry

    def send(step, carry):
        target = device(lax.rem(me + step, total))
        remote(own_ref, all_ref.at[me], sems, step, target).start()
        return carry

    def wait(step, carry):
        source = lax.rem(me - step + total, total)
        copy = remote(own_ref, all_ref.at[source], sems, step, device(source))
        copy.wait_recv()
        copy.wait_send()
        return carry

    lax.fori_loop(1, total, signal, 0)
    all_ref[me] = own_ref[...]
    pl.semaphore_wait(barrier, total - 1)
    lax.fori_loop(1, total, send, 0)
    lax.fori_loop(1, total, wait, 0)


def share_scores(own, n_wide, n_narrow):
    total = n_wide * n_narrow
    return pl.pallas_call(
        functools.partial(share_kernel, n_wide, n_narrow),
        out_shape=jax.ShapeDtypeStruct((total,) + own.shape, own.dtype),
        in_specs=[pl.BlockSpec(memory_space=pltpu.VMEM)],
        out_specs=pl.BlockSpec(memory_space=pltpu.VMEM),
        scratch_shapes=[pltpu.SemaphoreType.DMA((total,))] * 2,
        compiler_params=pltpu.CompilerParams(collective_id=1, has_side_effects=True),
        name="share_scores",
    )(own)


def exchange_kernel(n_wide, n_narrow, g_ref, out_ref, *scratch):
    swap = Exchange(Chips(n_wide, n_narrow), g_ref, out_ref, scratch)
    swap.start()
    swap.push()
    swap.finish()


def exchange(grads, n_wide, n_narrow):
    chips, _, rows, width = grads.shape
    return pl.pallas_call(
        functools.partial(exchange_kernel, n_wide, n_narrow),
        out_shape=jax.ShapeDtypeStruct((rows, width), F32),
        in_specs=[ANY],
        out_specs=pl.BlockSpec(memory_space=pltpu.VMEM),
        scratch_shapes=exchange_scratch(chips, rows, width),
        compiler_params=pltpu.CompilerParams(
            collective_id=2, has_side_effects=True, vmem_limit_bytes=VMEM_LIMIT
        ),
        name="exchange_query_gradients",
    )(grads)


UNITS = (
    (0, 48, 0),
    (48, 48, 0),
    (96, 48, 48),
    (144, 48, 48),
    (192, 16, 96),
    (240, 16, 96),
    (208, 16, 112),
    (256, 16, 112),
    (224, 16, 128),
    (272, 32, 128),
)
EARLY = (0, 1, 2, 3)
LATE = (4, 5, 6, 7, 8, 9)
SHARE_ROWS = 304
ROWS_A, ROWS_B = 144, 160
TILES = 9


def tail_kernel(n_z, part, *refs):
    act, go, first, gi, x_p, x_q, ctx, ga, final, gp = refs[:10]
    kept = (refs[10:15], refs[15:20])
    sources = refs[20:24]
    sums = refs[24:26]
    out_ref, gx_p, gx_q = refs[26:29]
    both, near, over_a, over_b, then_a, then_b, line, left_buf, right_buf, thin_buf = refs[29:39]
    wo, wq, wk, wv, att_buf, hidden, thin_hidden, grads, att_sums = refs[39:48]
    load_sem, weight_sem, block_sem, att_sem, gx_sem = refs[48:53]
    core_sems, one_sems, two_sems, line_sems, copy_sems = (
        refs[53 + 2 * index : 55 + 2 * index] for index in range(5)
    )
    wide, narrow = lax.axis_index("wide"), lax.axis_index("narrow")
    z, x = wide // 2, lax.rem(wide, 2)
    y, core = narrow // 2, lax.rem(narrow, 2)
    mate = (wide, y * 2 + 1 - core)
    over_y = (wide, (1 - y) * 2 + core)
    over_x = (z * 2 + 1 - x, narrow)
    right, left = (wide + 2, narrow), (wide - 2, narrow)
    total, width = go.shape
    p_rows = x_p.shape[0]
    held = both.at[core]

    def load(tile, wait):
        slot = lax.rem(tile, 2)
        block = pl.ds(pl.multiple_of(lax.rem(tile, 4) * width, width), width)

        def pair(source, other, target):
            for made in (
                pltpu.make_async_copy(source, left_buf.at[slot], load_sem.at[slot, 0]),
                pltpu.make_async_copy(other, target, load_sem.at[slot, 1]),
            ):
                if wait:
                    made.wait()
                else:
                    made.start()

        place = right_buf.at[slot]
        pl.when(tile < 4)(lambda: pair(act.at[:, block], go, place))
        pl.when(jnp.logical_and(tile >= 4, tile < 8))(lambda: pair(first, gi.at[:, block], place))
        pl.when(tile == 8)(lambda: pair(ctx, ga, place))
        pl.when(tile == TILES)(lambda: pair(final, gp, thin_buf))

    def rows_of(unit):
        start, count, _ = UNITS[unit]
        return pl.ds(start, count)

    def place_of(unit):
        _, count, place = UNITS[unit]
        return pl.ds(place, count)

    def core_copy(unit):
        rows = rows_of(unit)
        return remote(
            both.at[1 - core, :, :, :, rows], near.at[:, :, :, rows], core_sems, unit, mate
        )

    def one_copy(unit):
        rows = rows_of(unit)
        place = place_of(unit)
        if unit % 2 == 0:
            return remote(
                held.at[1 - y, :, :, rows],
                over_a.at[:, :, place],
                one_sems,
                unit,
                over_y,
            )
        return remote(
            held.at[:, :, 1 - x, rows],
            over_b.at[:, :, place],
            one_sems,
            unit,
            over_x,
        )

    def two_copy(unit):
        rows = rows_of(unit)
        place = place_of(unit)
        if unit % 2 == 0:
            return remote(
                held.at[y, :, 1 - x, rows],
                then_a.at[:, place],
                two_sems,
                unit,
                over_x,
            )
        return remote(
            held.at[1 - y, :, x, rows],
            then_b.at[:, place],
            two_sems,
            unit,
            over_y,
        )

    def line_copy(unit, target, way):
        rows = rows_of(unit)
        index = (unit * n_z + target) * 2 + way
        return remote(
            held.at[y, target, x, rows],
            line.at[way, target, rows],
            line_sems,
            index,
            right if way == 0 else left,
        )

    def share_copy(unit, step, arriving):
        rows = rows_of(unit)
        slots = (
            (y * 2 + 1 - core, (1 - y) * 2 + core, (1 - y) * 2 + 1 - core)
            if arriving
            else (narrow, narrow, (1 - y) * 2 + core)
        )
        block = out_ref.at[slots[step], rows]
        return remote(block, block, copy_sems, unit * 3 + step, over_y if step == 1 else mate)

    def add(target, extra):
        target[...] = target[...] + extra[...]

    def start_core(unit):
        core_copy(unit).start()

    def start_one(unit):
        rows = rows_of(unit)
        core_copy(unit).wait_recv()

        def body(index, carry):
            row_y, rest = index // (n_z * 2), lax.rem(index, n_z * 2)
            at = (row_y, rest // 2, lax.rem(rest, 2), rows)
            add(held.at[at], near.at[at])
            return carry

        lax.fori_loop(0, 4 * n_z, body, 0)
        one_copy(unit).start()

    def start_two(unit):
        rows = rows_of(unit)
        place = place_of(unit)
        one_copy(unit).wait_recv()

        def body(index, carry):
            outer_at, inner_at = index // 2, lax.rem(index, 2)
            if unit % 2 == 0:
                add(
                    held.at[y, outer_at, inner_at, rows],
                    over_a.at[outer_at, inner_at, place],
                )
            else:
                add(
                    held.at[inner_at, outer_at, x, rows],
                    over_b.at[inner_at, outer_at, place],
                )
            return carry

        lax.fori_loop(0, 2 * n_z, body, 0)
        two_copy(unit).start()

    def line_phase(phase):
        def run(unit):
            rows = rows_of(unit)
            place = place_of(unit)
            extra = then_a if unit % 2 == 0 else then_b

            def body(index, carry):
                add(held.at[y, index, x, rows], extra.at[index, place])
                return carry

            if phase == 0:
                two_copy(unit).wait_recv()
                lax.fori_loop(0, n_z, body, 0)
            for way, at in ((0, phase), (1, n_z - 1 - phase)):

                @pl.when(z == at)
                def _(way=way, at=at):
                    for target in range(n_z - 1, at, -1) if way == 0 else range(at):
                        copy = line_copy(unit, target, way)
                        if phase > 0:
                            copy.wait_recv()
                            add(held.at[y, target, x, rows], line.at[way, target, rows])
                        copy.start()

        return run

    def start_share(unit):
        rows = rows_of(unit)
        for target in range(n_z):

            @pl.when(z == target)
            def _(target=target):
                for way in range(2):
                    if target > 0 if way == 0 else target < n_z - 1:
                        line_copy(unit, target, way).wait_recv()
                        add(held.at[y, target, x, rows], line.at[way, target, rows])

        out_ref[narrow, rows] = both[core, y, z, x, rows]
        share_copy(unit, 1, False).start()
        share_copy(unit, 0, False).start()

    def forward(unit):
        share_copy(unit, 1, True).wait_recv()
        share_copy(unit, 2, False).start()

    def finish(unit):
        share_copy(unit, 0, True).wait_recv()
        share_copy(unit, 2, True).wait_recv()
        for step in range(3):
            share_copy(unit, step, False).wait_send()
        core_copy(unit).wait_send()
        one_copy(unit).wait_send()
        two_copy(unit).wait_send()
        for target in range(n_z):
            for way in range(2):
                pl.when(z < target if way == 0 else z > target)(
                    line_copy(unit, target, way).wait_send
                )

    barrier = pltpu.get_barrier_semaphore()
    load(0, False)
    for device in (mate, over_y, over_x):
        pl.semaphore_signal(barrier, inc=1, device_id=device, device_id_type=MESH)

    @pl.when(z < n_z - 1)
    def _():
        pl.semaphore_signal(barrier, inc=1, device_id=right, device_id_type=MESH)

    @pl.when(z > 0)
    def _():
        pl.semaphore_signal(barrier, inc=1, device_id=left, device_id_type=MESH)

    pl.semaphore_wait(barrier, jnp.where(jnp.logical_and(z > 0, z < n_z - 1), 5, 4))

    def put(kind, owner, half, made):
        rows = pl.ds(pl.multiple_of(kind * part, part), part)
        for index in range(4):
            both[lax.rem(owner, 2), owner // 2, 2 * half + index // 2, index % 2, rows] = made[
                index * part : (index + 1) * part
            ]

    def halves(left_ref, right_ref, store):
        def half_body(half, carry):
            cols = pl.ds(pl.multiple_of(half * 4 * part, 4 * part), 4 * part)
            store(half, mm(left_ref[:, cols], right_ref[...], TN).astype(BF16))
            return carry

        lax.fori_loop(0, 2, half_body, 0)

    def hooks(now, plan):
        for at, step, units in plan:

            @pl.when(now == at)
            def _(step=step, units=units):
                for unit in units:
                    step(unit)

    def tile_body(tile, carry):
        slot = lax.rem(tile, 2)
        load(tile, True)
        load(tile + 1, False)
        kind = tile // 4
        owner = jnp.where(tile == 8, 3, lax.rem(tile, 4))

        def store(half, made):
            @pl.when(kind == 0)
            def _():
                for index in range(4):
                    both[index % 2, index // 2, owner, half, :part] = made[
                        index * part : (index + 1) * part
                    ]

            pl.when(kind > 0)(lambda: put(kind, owner, half, made))

        halves(left_buf.at[slot], right_buf.at[slot], store)
        hooks(
            tile, ((3, start_core, (0, 1)), (6, start_one, (0, 1)), (7, start_core, (2, 3)))
        )
        return carry

    def hidden_of(block):
        return thin_hidden if blocks[block][2] else hidden.at[block]

    def block_copies(block):
        rows, base, source = blocks[block]
        q, k, v, gh, _ = kept[source]
        buf = left_buf if block % 2 == 0 else right_buf
        own = pl.ds(base - (p_rows if source else 0), rows)
        low, high = pl.ds(0, rows), pl.ds(span, rows)
        pairs = (
            (q.at[own], buf.at[0, low]),
            (k.at[own], buf.at[0, high]),
            (v.at[own], buf.at[1, low]),
            (ga.at[pl.ds(base, rows)], buf.at[1, high]),
            (gh.at[own], hidden_of(block)),
        )
        return [
            pltpu.make_async_copy(*pair, block_sem.at[block % 2, index])
            for index, pair in enumerate(pairs)
        ]

    def gx_copy(block):
        rows, base, source = blocks[block]
        target = gx_q if source else gx_p
        own = pl.ds(base - (p_rows if source else 0), rows)
        return pltpu.make_async_copy(hidden_of(block), target.at[own], gx_sem.at[block])

    def states(block):
        rows, base, _ = blocks[block]
        own = pl.ds(base, rows)
        hidden_of(block)[...] += (
            mm(grads[0, own], wq[...], NT)
            + mm(grads[1, own], wk[...], NT)
            + mm(grads[2, own], wv[...], NT)
        )
        gx_copy(block).start()

    def attention(block, plan):
        rows, base, source = blocks[block]
        buf = left_buf if block % 2 == 0 else right_buf
        low, high, own = pl.ds(0, rows), pl.ds(span, rows), pl.ds(base, rows)
        att = kept[source][4]
        q_ref, k_ref, v_ref, ga_ref = (
            buf.at[0, low],
            buf.at[0, high],
            buf.at[1, low],
            buf.at[1, high],
        )
        entry = 0 if source else block
        size = pl.ds(0, rows)

        def att_copy(pair):
            slot = lax.rem(pair, 2)
            return pltpu.make_async_copy(
                att.at[entry, pl.ds(2 * pair, 2)],
                att_buf.at[slot, :, size, size],
                att_sem.at[slot],
            )

        att_copy(0).start()
        for copy in block_copies(block):
            copy.wait()
        grads[2, own] = mm(ga_ref[...], wo[...], NT).astype(BF16)
        low_half = lax.broadcasted_iota(jnp.int32, (rows, 128), 1) < HEAD_DIM
        scale = HEAD_DIM ** (-0.5)

        def pair_body(pair, carry):
            cols = pl.ds(pl.multiple_of(pair * 128, 128), 128)
            slot = lax.rem(pair, 2)
            att_copy(pair).wait()
            pl.when(pair < HEADS // 2 - 1)(lambda: att_copy(pair + 1).start())
            q_pair, k_pair, v_pair = q_ref[:, cols], k_ref[:, cols], v_ref[:, cols]
            gc_pair = grads[2, own, cols]
            parts = []
            for half in range(2):
                mask = low_half if half == 0 else jnp.logical_not(low_half)
                low_att = att_buf[slot, half, size, size]
                wide_att = low_att.astype(F32)
                grad_att = mm(jnp.where(mask, gc_pair, jnp.zeros_like(gc_pair)), v_pair, NT)
                weighted = grad_att * wide_att
                grad_logits = (
                    weighted - wide_att * jnp.sum(weighted, axis=-1, keepdims=True)
                ).astype(BF16)
                parts.append(
                    (
                        mm(grad_logits, k_pair) * scale,
                        mm(grad_logits, q_pair, TN),
                        mm(low_att, gc_pair, TN),
                    )
                )
            for index in range(3):
                grads[index, own, cols] = jnp.where(
                    low_half, parts[0][index], parts[1][index]
                ).astype(BF16)
            hooks(pair, plan)
            return carry

        lax.fori_loop(0, HEADS // 2, pair_body, 0)
        accumulate(att_sums, 0, grads[0, own].astype(F32))
        accumulate(att_sums, 1, grads[2, own].astype(F32))

    def weight_copies():
        return [
            pltpu.make_async_copy(source, target, weight_sem.at[index])
            for index, (source, target) in enumerate(zip(sources, (wo, wq, wk, wv)))
        ]

    span = kept[0][4].shape[-1]
    blocks = [(span, base, 0) for base in range(0, p_rows, span)] + [(x_q.shape[0], p_rows, 1)]
    for copy in weight_copies():
        copy.start()
    att_sums[...] = jnp.zeros_like(att_sums)
    lax.fori_loop(0, TILES, tile_body, 0)
    load(TILES, True)
    slot = TILES % 2
    made = mm(left_buf[slot], thin_buf[...], TN).astype(BF16)
    for copy in block_copies(0):
        copy.start()
    lanes = thin_buf.shape[1]
    last = pl.ds(3 * part, 16)
    for shard in range(2 * n_z):
        for block in range(width // lanes):
            row = shard * part + block * 16
            both[0, 0, shard // 2, shard % 2, last, block * lanes : (block + 1) * lanes] = made[
                row : row + 16
            ]
    for copy in weight_copies():
        copy.wait()
    for unit in (2, 3):
        start_one(unit)
    line_a, line_b, line_c = (line_phase(phase) for phase in range(3))
    for copy in block_copies(1):
        copy.start()
    attention(0, ((1, start_two, (0, 1)),))
    for copy in block_copies(2):
        copy.start()
    attention(
        1,
        (
            (0, start_two, (2, 3)),
            (1, line_a, (0, 1)),
            (2, line_b, (0, 1)),
            (3, line_c, (0, 1)),
            (4, line_a, (2, 3)),
            (5, line_b, (2, 3)),
        ),
    )
    x_copies = [
        pltpu.make_async_copy(x_p, right_buf.at[0, pl.ds(0, p_rows)], load_sem.at[0, 0]),
        pltpu.make_async_copy(
            x_q, right_buf.at[0, pl.ds(p_rows, total - p_rows)], load_sem.at[0, 1]
        ),
    ]
    for copy in x_copies:
        copy.start()
    attention(2, ((1, line_c, (2, 3)), (4, start_share, EARLY)))
    for copy in x_copies:
        copy.wait()

    def late_body(tile, carry):
        halves(right_buf.at[0], grads.at[tile], lambda half, made: put(2, tile, half, made))
        return carry

    lax.fori_loop(0, 3, late_body, 0)
    top = sums[0][:8] + sums[1][:8] + att_sums[...]
    tail = jnp.concatenate([top, sums[0][8:] + sums[1][8:]], axis=0).astype(BF16)
    for shard in range(2 * n_z):
        at_z, at_x = shard // 2, shard % 2
        both[1, 0, at_z, at_x, last] = tail
        both[0, 1, at_z, at_x, last] = jnp.zeros_like(tail)
        both[1, 1, at_z, at_x, last] = jnp.zeros_like(tail)
    for step, units in (
        (start_core, LATE),
        (forward, EARLY),
        (start_one, LATE),
        (states, (0,)),
        (start_two, (4, 5)),
        (states, (1,)),
        (start_two, (6, 7)),
        (line_a, (4, 5)),
        (states, (2,)),
        (line_b, (4, 5)),
        (start_two, (8,)),
        (line_c, (4, 5)),
        (line_a, (6,)),
        (start_two, (9,)),
        (line_a, (7,)),
        (line_b, (6, 7)),
        (start_share, (4, 5)),
        (line_c, (6, 7)),
        (line_a, (8,)),
        (line_b, (8,)),
        (line_a, (9,)),
        (line_c, (8,)),
        (line_b, (9,)),
        (start_share, (6, 7)),
        (line_c, (9,)),
        (start_share, (8, 9)),
        (forward, LATE),
        (finish, EARLY + LATE),
        (lambda block: gx_copy(block).wait(), range(len(blocks))),
    ):
        for unit in units:
            step(unit)


def backward_tail(arrays, passage_kept, query_kept, weights, sums, n_wide):
    n_z = n_wide // 2
    go, x_p, x_q, gp = arrays[1], arrays[4], arrays[5], arrays[9]
    total, width = go.shape
    part = width // n_wide
    units = len(UNITS)
    span = passage_kept[4].shape[-1]
    sem = pltpu.SemaphoreType.DMA
    vmem = pl.BlockSpec(memory_space=pltpu.VMEM)
    return pl.pallas_call(
        functools.partial(tail_kernel, n_z, part),
        out_shape=(
            jax.ShapeDtypeStruct((4, SHARE_ROWS, width), BF16),
            jax.ShapeDtypeStruct(x_p.shape, F32),
            jax.ShapeDtypeStruct(x_q.shape, F32),
        ),
        in_specs=[ANY] * 24 + [vmem] * 2,
        out_specs=(vmem, ANY, ANY),
        scratch_shapes=[
            pltpu.VMEM((2, 2, n_z, 2, SHARE_ROWS, width), BF16),
            pltpu.VMEM((2, n_z, 2, SHARE_ROWS, width), BF16),
            pltpu.VMEM((n_z, 2, ROWS_A, width), BF16),
            pltpu.VMEM((2, n_z, ROWS_B, width), BF16),
            pltpu.VMEM((n_z, ROWS_A, width), BF16),
            pltpu.VMEM((n_z, ROWS_B, width), BF16),
            pltpu.VMEM((2, n_z, SHARE_ROWS, width), BF16),
            pltpu.VMEM((2, total, width), BF16),
            pltpu.VMEM((2, total, width), BF16),
            pltpu.VMEM(gp.shape, BF16),
        ]
        + [pltpu.VMEM((width, width), BF16)] * 4
        + [
            pltpu.VMEM((2, 2, span, span), BF16),
            pltpu.VMEM((2, span, width), F32),
            pltpu.VMEM(x_q.shape, F32),
            pltpu.VMEM((3, total, width), BF16),
            pltpu.VMEM((8, width), F32),
            sem((2, 2)),
            sem((4,)),
            sem((2, 5)),
            sem((2,)),
            sem((3,)),
        ]
        + [sem((units,))] * 6
        + [sem((units * n_z * 2,))] * 2
        + [sem((units * 3,))] * 2,
        compiler_params=pltpu.CompilerParams(
            collective_id=3, has_side_effects=True, vmem_limit_bytes=VMEM_LIMIT
        ),
        name="backward_tail",
    )(*arrays, *passage_kept, *query_kept, *weights, *sums)


def unpack_kernel(part, sums_ref, q_ref, k_ref, v_ref, o_ref, inner_ref, outer_ref, thin_ref, vec_ref):
    width = q_ref.shape[1]
    lanes = thin_ref.shape[1]
    for owner, ref in enumerate((q_ref, k_ref, v_ref, o_ref)):
        ref[...] = sums_ref[owner, 2 * part : 3 * part].astype(F32)
        inner_ref[:, owner * width : (owner + 1) * width] = sums_ref[
            owner, part : 2 * part
        ].astype(F32)
        outer_ref[owner * part : (owner + 1) * part] = sums_ref[owner, :part].astype(F32)
    tail = sums_ref[0, 3 * part :].astype(F32)
    for block in range(width // lanes):
        thin_ref[block * 16 : (block + 1) * 16] = tail[:, block * lanes : (block + 1) * lanes]
    vec_ref[...] = sums_ref[1, 3 * part :].astype(F32)


def unpack(summed, part, embed_width):
    width = summed.shape[-1]
    vmem = pl.BlockSpec(memory_space=pltpu.VMEM)
    shapes = [(part, width)] * 4 + [
        (part, 4 * width),
        (4 * part, width),
        (part, embed_width),
        (16, width),
    ]
    return pl.pallas_call(
        functools.partial(unpack_kernel, part),
        out_shape=[jax.ShapeDtypeStruct(shape, F32) for shape in shapes],
        in_specs=[vmem],
        out_specs=[vmem] * len(shapes),
        compiler_params=pltpu.CompilerParams(vmem_limit_bytes=VMEM_LIMIT),
        name="unpack_gradients",
    )(summed)


def outer(left, right):
    return lax.dot_general(left, right, TN, preferred_element_type=F32)


def local(
    query_states,
    passage_states,
    lengths,
    positives,
    query_weight,
    query_bias,
    key_weight,
    value_weight,
    value_bias,
    out_weight,
    out_bias,
    first_gain,
    first_shift,
    inner_weight,
    inner_bias,
    outer_weight,
    outer_bias,
    second_gain,
    second_shift,
    linear_weight,
):
    everyone = ("wide", "narrow")
    n_wide = lax.axis_size("wide")
    n_narrow = lax.axis_size("narrow")
    wide_index = lax.axis_index("wide")
    narrow_index = lax.axis_index("narrow")
    micro, own_queries, query_len, width = query_states.shape
    own_passages, slots = passage_states.shape[1:3]
    weights = (
        query_weight,
        key_weight,
        value_weight,
        out_weight,
        inner_weight,
        outer_weight,
        linear_weight,
    )
    embed_width = linear_weight.shape[1]
    vec = pack(
        (
            query_bias,
            value_bias,
            out_bias,
            first_gain,
            first_shift,
            outer_bias,
            second_gain,
            second_shift,
            inner_bias,
        ),
        width,
    )
    own_index = narrow_index * n_wide + wide_index
    own_lengths = lax.dynamic_slice_in_dim(lengths, own_index * own_passages, own_passages, axis=1)
    lens = own_lengths.reshape(-1)
    x_query = query_states.reshape(-1, width)
    x_passage = passage_states.reshape(-1, width)
    query_rows, passage_rows = x_query.shape[0], x_passage.shape[0]
    total = query_rows + passage_rows
    kept_q = encode(
        x_query, lens, vec, weights, 1, query_len, total, passage_rows, None, None
    )
    sizes = (n_wide, n_narrow)
    kept_p = encode(
        x_passage, lens, vec, weights, micro * own_passages, 0, total, 0, kept_q, sizes
    )
    queries = kept_p[16].reshape(n_wide * n_narrow, micro, -1, embed_width)
    ctx, first_low, act, final_low = (kept_p[index] for index in (4, 7, 8, 12))
    passages = kept_p[15].reshape(micro * own_passages, slots, embed_width)
    e, z = similarity(queries, passages, lens)
    best = SHARP + jnp.log(z)
    own_scores = jnp.sum(best.reshape(micro, -1, query_len), axis=-1) / SHARP
    full = share_scores(own_scores, n_wide, n_narrow)
    row_total = jax.nn.logsumexp(full, axis=0)
    passage_ids = jnp.arange(full.shape[0], dtype=jnp.int32)
    picked = jnp.sum(
        jnp.where(passage_ids[:, None, None] == positives[None], full, 0.0), axis=0
    )
    row_count = own_queries * n_narrow
    losses = lax.dynamic_slice_in_dim(row_total - picked, wide_index * row_count, row_count, axis=1)
    block = lax.dynamic_slice(
        full,
        (narrow_index * n_wide, 0, wide_index * row_count),
        (n_wide, micro, row_count),
    )
    scores = jnp.transpose(block, (1, 2, 0))
    grads = jnp.exp(own_scores - row_total) - (positives == own_index).astype(F32)
    token_weights = jnp.repeat(grads, query_len, axis=1).reshape(z.shape) / z
    grad_passage, grad_query = similarity_back(e, token_weights, queries, passages)
    grad_query = grad_query.reshape(-1, 2, query_rows, embed_width)
    grad_passage = grad_passage.reshape(passage_rows, embed_width)
    together = grad_query.size <= 4 * total * width
    back_p = mlp_back(
        grad_passage,
        kept_p,
        vec,
        weights,
        micro * own_passages,
        total,
        0,
        None,
        grad_query if together else None,
        sizes if together else None,
    )
    grad_query = back_p[6] if together else exchange(grad_query, n_wide, n_narrow)
    back_q = mlp_back(
        grad_query, kept_q, vec, weights, 1, total, passage_rows, back_p, None, None
    )
    gp, go, gi, _, ga, sums_q = back_q[:6]
    part = width // n_wide
    if part == 96 and n_narrow == 4 and micro * own_passages == 2 and act.shape[1] == 4 * width:
        summed, grad_p, grad_q = backward_tail(
            (act, go, first_low, gi, x_passage, x_query, ctx, ga, final_low, gp),
            (*kept_p[:3], back_p[3], kept_p[3]),
            (*kept_q[:3], back_q[3], kept_q[3]),
            (out_weight, query_weight, key_weight, value_weight),
            (back_p[5], sums_q),
            n_wide,
        )
        r_q, r_k, r_v, r_out, r_inner, r_outer, r_linear, vectors = unpack(
            summed, part, embed_width
        )
        own = lax.dynamic_slice_in_dim(vectors[:8], wide_index * part, part, axis=1)
        v_q, v_v, v_o, v_g1, v_s1, v_2, v_g2, v_s2 = (
            own[row] for row in (0, 1, ROW_BO, ROW_G1, ROW_S1, ROW_B2, ROW_G2, ROW_S2)
        )
        v_i = lax.dynamic_slice_in_dim(
            vectors[ROW_BI : ROW_BI + 4].reshape(-1), wide_index * 4 * part, 4 * part
        )
    else:
        att_p = attention_back(
            ga, back_p[3], kept_p, weights, micro * own_passages, total, 0, None
        )
        att_q = attention_back(ga, back_q[3], kept_q, weights, 1, total, passage_rows, att_p[0])
        gqkv, grad_p, grad_q = att_q[0], att_p[1], att_q[1]

        def reduce(value):
            piece = lax.psum_scatter(value.astype(BF16), everyone, scatter_dimension=0, tiled=True)
            return lax.all_gather(piece, "narrow", axis=0, tiled=True).astype(F32)

        def vector(rows):
            flat = rows.reshape(-1)
            share = flat.shape[0] // n_wide
            return lax.dynamic_slice_in_dim(flat, wide_index * share, share)

        sums = jnp.concatenate([back_p[5] + sums_q, att_p[2] + att_q[2]], axis=0)
        sums = lax.psum(sums, everyone)
        x_all = jnp.concatenate([x_passage, x_query], axis=0)
        pairs = ((act, go), (first_low, gi), (final_low, gp), (ctx, ga), (x_all, gqkv))
        r_outer, r_inner, r_linear, r_out, r_qkv = (
            reduce(outer(*pair)) for pair in pairs
        )
        r_q, r_k, r_v = (r_qkv[:, index * width : (index + 1) * width] for index in range(3))
        v_q, v_v, v_o, v_g1, v_s1, v_2, v_g2, v_s2 = (
            vector(sums[pick])
            for pick in (16, 17, ROW_BO, ROW_G1, ROW_S1, ROW_B2, ROW_G2, ROW_S2)
        )
        v_i = vector(sums[ROW_BI : ROW_BI + 4])
    return (
        scores,
        losses,
        grad_q.reshape(query_states.shape),
        grad_p.reshape(passage_states.shape),
        r_q,
        v_q,
        r_k,
        r_v,
        v_v,
        r_out,
        v_o,
        v_g1,
        v_s1,
        r_inner,
        v_i,
        r_outer,
        v_2,
        v_g2,
        v_s2,
        r_linear,
    )


def solution(mesh):
    return jax.shard_map(
        local,
        mesh=mesh,
        in_specs=(
            P(None, ("wide", "narrow"), None, None),
            P(None, ("narrow", "wide"), None, None),
        )
        + (P(),) * 18,
        out_specs=(
            P(None, "wide", "narrow"),
            P(None, "wide"),
            P(None, ("wide", "narrow"), None, None),
            P(None, ("narrow", "wide"), None, None),
            P("wide", None),
            P("wide"),
            P("wide", None),
            P("wide", None),
            P("wide"),
            P("wide", None),
            P("wide"),
            P("wide"),
            P("wide"),
            P("wide", None),
            P("wide"),
            P("wide", None),
            P("wide"),
            P("wide"),
            P("wide"),
            P("wide", None),
        ),
        check_vma=False,
    )
```

```python
import functools

import jax
import jax.numpy as jnp
from jax import lax
from jax.experimental import pallas as pl
from jax.experimental.pallas import tpu as pltpu
from jax.sharding import PartitionSpec as P

HEADS = 12
HEAD_DIM = 64
SHARP = 16.0
LAYER_EPS = 1e-12
NORM_EPS = 1e-06
MASKED = -1e30
SLOPE_CONST = 0.3989422804014327
ROOT_HALF = 0.7071067811865476
BF16 = jnp.bfloat16
F32 = jnp.float32
VMEM_LIMIT = 62 * 1024 * 1024

NN = (((1,), (0,)), ((), ()))
NT = (((1,), (1,)), ((), ()))
TN = (((0,), (0,)), ((), ()))


def mm(left, right, dims=NN):
    return lax.dot_general(left, right, dims, preferred_element_type=F32)


ANY = pl.BlockSpec(memory_space=pl.ANY)

ROW_BQ, ROW_BV, ROW_BO, ROW_G1, ROW_S1, ROW_B2, ROW_G2, ROW_S2, ROW_BI = range(9)


def vec_row(vec_ref, row):
    return vec_ref[row : row + 1, :]


def mean_row(value):
    return jnp.sum(value, axis=-1, keepdims=True) * (1.0 / value.shape[-1])


class Loader:
    def __init__(self, sources, targets, sem):
        self.copies = [
            pltpu.make_async_copy(source, target, sem.at[index])
            for index, (source, target) in enumerate(zip(sources, targets))
        ]
        self.first = pl.program_id(0) == 0

    def start(self):
        @pl.when(self.first)
        def _():
            for copy in self.copies:
                copy.start()

    def need(self, *indices):
        @pl.when(self.first)
        def _():
            for index in indices:
                self.copies[index].wait()


MESH = pl.DeviceIdType.MESH


def remote(source, target, sems, index, device):
    return pltpu.make_async_remote_copy(
        src_ref=source,
        dst_ref=target,
        send_sem=sems[0].at[index],
        recv_sem=sems[1].at[index],
        device_id=device,
        device_id_type=MESH,
    )


class Chips:
    def __init__(self, n_wide, n_narrow):
        self.wide, self.narrow = lax.axis_index("wide"), lax.axis_index("narrow")
        self.core = lax.rem(self.narrow, 2)
        self.rows = n_narrow // 2
        self.count = n_wide * self.rows
        self.me = self.wide * self.rows + self.narrow // 2
        self.mate = (self.wide, self.narrow + 1 - 2 * self.core)

    def at(self, step):
        return lax.rem(self.me + step + self.count, self.count)

    def device(self, chip):
        return (chip // self.rows, lax.rem(chip, self.rows) * 2 + self.core)

    def loop(self, body):
        def step_body(step, carry):
            body(step)
            return carry

        lax.fori_loop(1, self.count, step_body, 0)

    def barrier(self):
        barrier = pltpu.get_barrier_semaphore()

        def signal(step):
            pl.semaphore_signal(
                barrier, inc=1, device_id=self.device(self.at(step)), device_id_type=MESH
            )

        pl.semaphore_signal(barrier, inc=1, device_id=self.mate, device_id_type=MESH)
        self.loop(signal)
        pl.semaphore_wait(barrier, self.count)


class Gather:
    def __init__(self, chips, own, out, sems):
        self.chips, self.own, self.out = chips, own, out
        self.far, self.pair, self.local = sems[:2], sems[2:4], sems[4]

    def far_copy(self, step, chip):
        slot = self.out.at[chip, self.chips.core]
        return remote(self.own, slot, self.far, step, self.chips.device(self.chips.at(step)))

    def mate_copy(self, core):
        block = self.out.at[:, core]
        return remote(block, block, self.pair, 0, self.chips.mate)

    def local_copy(self):
        slot = self.out.at[self.chips.me, self.chips.core]
        return pltpu.make_async_copy(self.own, slot, self.local.at[0])

    def start(self):
        self.local_copy().start()
        self.chips.barrier()
        self.chips.loop(lambda step: self.far_copy(step, self.chips.me).start())

    def forward(self):
        self.local_copy().wait()
        self.chips.loop(lambda step: self.far_copy(step, self.chips.at(-step)).wait_recv())
        self.mate_copy(self.chips.core).start()

    def finish(self):
        self.chips.loop(lambda step: self.far_copy(step, self.chips.me).wait_send())
        self.mate_copy(1 - self.chips.core).wait_recv()
        self.mate_copy(self.chips.core).wait_send()


class Exchange:
    def __init__(self, chips, grads, out, scratch):
        self.chips, self.grads, self.out = chips, grads, out
        self.half, self.arrived, self.inbox = scratch[:3]
        self.pair, self.far, self.local = scratch[3:5], scratch[5:7], scratch[7]

    def pair_copy(self):
        away = self.grads.at[:, 1 - self.chips.core]
        return remote(away, self.arrived, self.pair, 0, self.chips.mate)

    def local_copy(self):
        mine = self.grads.at[:, self.chips.core]
        return pltpu.make_async_copy(mine, self.half, self.local.at[0])

    def far_copy(self, step):
        chip = self.chips.at(step)
        return remote(
            self.half.at[chip], self.inbox.at[step], self.far, step, self.chips.device(chip)
        )

    def start(self):
        self.local_copy().start()
        self.chips.barrier()
        self.pair_copy().start()

    def push(self):
        self.local_copy().wait()
        self.pair_copy().wait_recv()

        def add(step):
            chip = self.chips.at(step)
            total = self.half[chip].astype(F32) + self.arrived[chip].astype(F32)
            self.half[chip] = total.astype(BF16)
            self.far_copy(step).start()

        self.chips.loop(add)
        me = self.chips.me
        self.out[...] = self.half[me].astype(F32) + self.arrived[me].astype(F32)

    def finish(self):
        def collect(step):
            copy = self.far_copy(step)
            copy.wait_recv()
            copy.wait_send()
            self.out[...] += self.inbox[step].astype(F32)

        self.chips.loop(collect)
        self.pair_copy().wait_send()


class Push:
    def __init__(self, chips, half, out, scratch):
        self.chips, self.half, self.out = chips, half, out
        self.inbox, self.far, self.own = scratch[0], scratch[1:3], scratch[3]

    def far_copy(self, step):
        chip = self.chips.at(step)
        return remote(
            self.half.at[chip], self.inbox.at[step], self.far, step, self.chips.device(chip)
        )

    def own_copy(self):
        return pltpu.make_async_copy(
            self.half.at[self.chips.me], self.inbox.at[0], self.own.at[0]
        )

    def start(self):
        self.own_copy().start()
        self.chips.barrier()
        self.chips.loop(lambda step: self.far_copy(step).start())

    def finish(self):
        self.own_copy().wait()
        self.out[...] = self.inbox[0].astype(F32)

        def collect(step):
            copy = self.far_copy(step)
            copy.wait_recv()
            copy.wait_send()
            self.out[...] += self.inbox[step].astype(F32)

        self.chips.loop(collect)


def push_scratch(chips, rows, width):
    sem = pltpu.SemaphoreType.DMA
    return [pltpu.VMEM((chips, rows, width), BF16), sem((chips,)), sem((chips,)), sem((1,))]


def exchange_scratch(chips, rows, width):
    sem = pltpu.SemaphoreType.DMA
    return [pltpu.VMEM((chips, rows, width), BF16)] * 3 + [
        sem((1,)),
        sem((1,)),
        sem((chips,)),
        sem((chips,)),
        sem((1,)),
    ]


def fwd_kernel(grouped, alias_count, sizes, *refs):
    lens_ref, x_ref, vec_ref = refs[:3]
    sources = refs[3:10]
    refs = refs[10 + alias_count :]
    gather = None
    if sizes:
        gather = Gather(Chips(*sizes), refs[0], refs[17], refs[-5:])
        refs = refs[1:17] + refs[18:-5]
    (
        q_ref,
        k_ref,
        v_ref,
        att_ref,
        ctx_ref,
        n1_ref,
        r1_ref,
        first_ref,
        act_ref,
        slope_ref,
        n2_ref,
        r2_ref,
        final_ref,
        unit_ref,
        uinv_ref,
        embed_ref,
    ) = refs[:16]
    wq, wk, wv, wo, wi, w2, wl, sem, acc_ref = refs[16:]
    loader = Loader(sources, (wq, wk, wv, wo, wi, w2, wl), sem)
    loader.start()
    if gather:
        last = pl.program_id(0) == pl.num_programs(0) - 1
        pl.when(loader.first)(gather.start)
    rows = x_ref.shape[0]
    x = x_ref[...]
    scale = HEAD_DIM ** (-0.5)
    loader.need(0)
    q_ref[...] = ((mm(x, wq[...]) + vec_row(vec_ref, ROW_BQ)).astype(BF16) * scale).astype(BF16)
    loader.need(1)
    k_ref[...] = mm(x, wk[...]).astype(BF16)
    loader.need(2)
    v_ref[...] = (mm(x, wv[...]) + vec_row(vec_ref, ROW_BV)).astype(BF16)
    if grouped:
        valid = (
            lax.broadcasted_iota(jnp.int32, (rows, rows), 0) // grouped
            == lax.broadcasted_iota(jnp.int32, (rows, rows), 1) // grouped
        )
    else:
        length = lens_ref[pl.program_id(0)]
        valid = lax.broadcasted_iota(jnp.int32, (1, rows), 1) < length
    bias = jnp.where(valid, 0.0, MASKED)
    low_half = lax.broadcasted_iota(jnp.int32, (rows, 128), 1) < HEAD_DIM

    def pair_body(pair, carry):
        cols = pl.ds(pl.multiple_of(pair * 128, 128), 128)
        q_pair, k_pair, v_pair = q_ref[:, cols], k_ref[:, cols], v_ref[:, cols]
        parts = []
        for half in range(2):
            mask = low_half if half == 0 else jnp.logical_not(low_half)
            logits = mm(jnp.where(mask, q_pair, jnp.zeros_like(q_pair)), k_pair, NT) + bias
            peak = jnp.max(logits, axis=-1, keepdims=True)
            e = jnp.exp(logits - peak)
            inv = 1.0 / jnp.sum(e, axis=-1, keepdims=True)
            low = (e * inv).astype(BF16)
            att_ref[0, 2 * pair + half] = low
            parts.append(mm(low, v_pair))
        ctx_ref[:, cols] = jnp.where(low_half, parts[0], parts[1]).astype(BF16)
        return carry

    lax.fori_loop(0, HEADS // 2, pair_body, 0)
    if gather:
        pl.when(last)(gather.forward)
    loader.need(3)
    field = x.astype(F32) + (mm(ctx_ref[...], wo[...]) + vec_row(vec_ref, ROW_BO))
    center = field - mean_row(field)
    inverse = lax.rsqrt(mean_row(center * center) + LAYER_EPS)
    normed = center * inverse
    n1_ref[...] = normed.astype(BF16)
    r1_ref[...] = jnp.broadcast_to(inverse, r1_ref.shape)
    first = normed * vec_row(vec_ref, ROW_G1) + vec_row(vec_ref, ROW_S1)
    first_ref[...] = first.astype(BF16)
    acc_ref[...] = first + vec_row(vec_ref, ROW_B2)
    loader.need(4, 5)
    width = x.shape[1]

    def chunk_body(chunk, carry):
        cols = pl.ds(pl.multiple_of(chunk * width, width), width)
        inner = mm(first_ref[...], wi[:, cols]) + vec_ref[pl.ds(ROW_BI + chunk, 1), :]
        phi = 0.5 * (1.0 + lax.erf(inner * ROOT_HALF))
        activated = (inner * phi).astype(BF16)
        act_ref[:, cols] = activated
        slope_ref[:, cols] = (phi + inner * jnp.exp(-0.5 * inner * inner) * SLOPE_CONST).astype(
            BF16
        )
        acc_ref[...] += mm(activated, w2[cols, :])
        return carry

    lax.fori_loop(0, wi.shape[1] // width, chunk_body, 0)
    field = acc_ref[...]
    center = field - mean_row(field)
    inverse = lax.rsqrt(mean_row(center * center) + LAYER_EPS)
    normed = center * inverse
    n2_ref[...] = normed.astype(BF16)
    r2_ref[...] = jnp.broadcast_to(inverse, r2_ref.shape)
    final = (normed * vec_row(vec_ref, ROW_G2) + vec_row(vec_ref, ROW_S2)).astype(BF16)
    final_ref[...] = final
    loader.need(6)
    projected = mm(final, wl[...])
    uinv = lax.rsqrt(jnp.sum(projected * projected, axis=-1, keepdims=True) + NORM_EPS)
    unit = projected * uinv
    unit_ref[...] = unit
    uinv_ref[...] = jnp.broadcast_to(uinv, uinv_ref.shape)
    embed_ref[...] = unit.astype(BF16)
    if gather:
        pl.when(last)(gather.finish)


def encode(x, lens, vec, weights, blocks, grouped, total, offset, earlier, sizes):
    rows = x.shape[0] // blocks
    width = x.shape[1]
    wide = weights[4].shape[1]
    embed_width = weights[6].shape[1]
    base = offset // rows

    def row_spec(columns):
        return pl.BlockSpec((rows, columns), lambda i, lens: (base + i, 0))

    def own_spec(columns):
        return pl.BlockSpec((rows, columns), lambda i, lens: (i, 0))

    def shape(count, columns, dtype):
        return jax.ShapeDtypeStruct((count, columns), dtype)

    own = x.shape[0]
    out_shapes = [
        shape(own, width, BF16),
        shape(own, width, BF16),
        shape(own, width, BF16),
        jax.ShapeDtypeStruct((blocks, HEADS, rows, rows), BF16),
        shape(total, width, BF16),
        shape(own, width, BF16),
        shape(own, embed_width, F32),
        shape(total, width, BF16),
        shape(total, wide, BF16),
        shape(own, wide, BF16),
        shape(own, width, BF16),
        shape(own, embed_width, F32),
        shape(total, width, BF16),
        shape(own, embed_width, F32),
        shape(own, embed_width, F32),
        shape(own, embed_width, BF16),
    ]
    shared = (4, 7, 8, 12)
    out_specs = [
        pl.BlockSpec((1, HEADS, rows, rows), lambda i, lens: (i, 0, 0, 0))
        if index == 3
        else (row_spec if index in shared else own_spec)(out.shape[1])
        for index, out in enumerate(out_shapes)
    ]
    aliased = [] if earlier is None else [earlier[index] for index in shared]
    sends, sem_shapes, params = [], [], {}
    if sizes:
        sends = [earlier[15]]
        chips = sizes[0] * sizes[1] // 2
        out_shapes.append(jax.ShapeDtypeStruct((chips, 2) + earlier[15].shape, BF16))
        out_specs.append(ANY)
        sem = pltpu.SemaphoreType.DMA
        sem_shapes = [sem((chips,)), sem((chips,)), sem((1,)), sem((1,)), sem((1,))]
        params = {"collective_id": 4, "has_side_effects": True}
    return pl.pallas_call(
        functools.partial(fwd_kernel, grouped, len(aliased), sizes),
        out_shape=out_shapes,
        grid_spec=pltpu.PrefetchScalarGridSpec(
            num_scalar_prefetch=1,
            grid=(blocks,),
            in_specs=[
                own_spec(width),
                pl.BlockSpec(vec.shape, lambda i, lens: (0, 0)),
            ]
            + [ANY] * (7 + len(aliased) + len(sends)),
            out_specs=out_specs,
            scratch_shapes=[pltpu.VMEM(weight.shape, BF16) for weight in weights]
            + [pltpu.SemaphoreType.DMA((7,)), pltpu.VMEM((rows, width), F32)]
            + sem_shapes,
        ),
        input_output_aliases={10 + index: shared[index] for index in range(len(aliased))},
        compiler_params=pltpu.CompilerParams(vmem_limit_bytes=VMEM_LIMIT, **params),
        name="encode_queries" if grouped else "encode_passages",
    )(lens, x, vec, *weights, *aliased, *sends)


def sims_kernel(lens_ref, q_ref, p_ref, e_ref, z_ref):
    count = q_ref.shape[0]
    tokens = count * q_ref.shape[2]
    query = q_ref[...].reshape(tokens, q_ref.shape[3])
    sims = mm(p_ref[0], query, NT)
    slot = lax.broadcasted_iota(jnp.int32, sims.shape, 0)
    e = jnp.where(slot < lens_ref[pl.program_id(0)], jnp.exp(SHARP * sims - SHARP), 0.0)
    e_ref[0] = e.astype(BF16)
    z = jnp.sum(e, axis=0, keepdims=True)
    step = q_ref.shape[2]
    for index in range(count):
        z_ref[0, index : index + 1, :] = z[:, index * step : (index + 1) * step]


def sims_back_kernel(e_ref, w_ref, q_ref, p_ref, gp_ref, gq_ref):
    count = q_ref.shape[0]
    step = q_ref.shape[2]
    query = q_ref[...].reshape(count * step, q_ref.shape[3])
    weight = jnp.concatenate([w_ref[0, index : index + 1, :] for index in range(count)], axis=1)
    grads = (e_ref[0].astype(F32) * weight).astype(BF16)
    part = mm(grads, query)

    @pl.when(pl.program_id(1) == 0)
    def _():
        gp_ref[0] = part

    @pl.when(pl.program_id(1) > 0)
    def _():
        gp_ref[0] += part

    gq_ref[...] = mm(grads, p_ref[0], TN).astype(BF16).reshape(gq_ref.shape)


def similarity(queries, passages, lens):
    devices, micro, tokens, width = queries.shape
    slots = passages.shape[1]
    group = 8
    e, z = pl.pallas_call(
        sims_kernel,
        out_shape=(
            jax.ShapeDtypeStruct((micro, slots, devices * tokens), BF16),
            jax.ShapeDtypeStruct((micro, devices, tokens), F32),
        ),
        grid_spec=pltpu.PrefetchScalarGridSpec(
            num_scalar_prefetch=1,
            grid=(micro, devices // group),
            in_specs=[
                pl.BlockSpec((group, 1, tokens, width), lambda m, b, lens: (b, m, 0, 0)),
                pl.BlockSpec((1, slots, width), lambda m, b, lens: (m, 0, 0)),
            ],
            out_specs=(
                pl.BlockSpec((1, slots, group * tokens), lambda m, b, lens: (m, 0, b)),
                pl.BlockSpec((1, group, tokens), lambda m, b, lens: (m, b, 0)),
            ),
        ),
        compiler_params=pltpu.CompilerParams(vmem_limit_bytes=VMEM_LIMIT),
        name="similarity",
    )(lens, queries, passages)
    return e, z


def similarity_back(e, weights, queries, passages):
    devices, micro, tokens, width = queries.shape
    slots = passages.shape[1]
    group = 8
    return pl.pallas_call(
        sims_back_kernel,
        out_shape=(
            jax.ShapeDtypeStruct((micro, slots, width), F32),
            jax.ShapeDtypeStruct((devices, micro, tokens, width), BF16),
        ),
        grid=(micro, devices // group),
        in_specs=[
            pl.BlockSpec((1, slots, group * tokens), lambda m, b: (m, 0, b)),
            pl.BlockSpec((1, group, tokens), lambda m, b: (m, b, 0)),
            pl.BlockSpec((group, 1, tokens, width), lambda m, b: (b, m, 0, 0)),
            pl.BlockSpec((1, slots, width), lambda m, b: (m, 0, 0)),
        ],
        out_specs=(
            pl.BlockSpec((1, slots, width), lambda m, b: (m, 0, 0)),
            pl.BlockSpec((group, 1, tokens, width), lambda m, b: (b, m, 0, 0)),
        ),
        compiler_params=pltpu.CompilerParams(vmem_limit_bytes=VMEM_LIMIT),
        name="similarity_back",
    )(e, weights, queries, passages)


def match_kernel(n_wide, n_narrow, group, query_len, *refs):
    lens_ref, q_ref, p_ref, pos_ref = refs[:4]
    all_ref, loss_ref, gp_ref, half_ref = refs[4:8]
    e_buf, z_buf, own_buf, grad_buf, near, share_send, share_recv, pair_send, pair_recv = refs[8:]
    devices, micro, tokens, width = q_ref.shape
    chips = Chips(n_wide, n_narrow)
    me = chips.narrow * n_wide + chips.wide
    share_sems, pair_sems = (share_send, share_recv), (pair_send, pair_recv)
    pairs = group // 2

    def device(index):
        return (lax.rem(index, n_wide), index // n_wide)

    def each(body):
        def step_body(step, carry):
            body(step)
            return carry

        lax.fori_loop(1, devices, step_body, 0)

    barrier = pltpu.get_barrier_semaphore()
    each(
        lambda step: pl.semaphore_signal(
            barrier, inc=1, device_id=device(lax.rem(me + step, devices)), device_id_type=MESH
        )
    )

    def query_rows(block, m):
        at = pl.ds(block * group, group)
        return q_ref[at, m].reshape(group * tokens, width)

    def forward(block, carry):
        for m in range(micro):
            sims = mm(p_ref[m], query_rows(block, m), NT)
            slot = lax.broadcasted_iota(jnp.int32, sims.shape, 0)
            e = jnp.where(slot < lens_ref[m], jnp.exp(SHARP * sims - SHARP), 0.0)
            e_buf[m, block] = e.astype(BF16)
            z = jnp.sum(e, axis=0, keepdims=True)
            for index in range(group):
                z_buf[m, pl.ds(block * group + index, 1)] = z[
                    :, index * tokens : (index + 1) * tokens
                ]
        return carry

    lax.fori_loop(0, devices // group, forward, 0)
    pl.semaphore_wait(barrier, devices - 1)
    best = SHARP + jnp.log(z_buf[...].reshape(micro * devices, tokens))
    member = (
        lax.broadcasted_iota(jnp.int32, (8, tokens), 0)
        == lax.broadcasted_iota(jnp.int32, (8, tokens), 1) // query_len
    ).astype(F32)
    own = (
        lax.dot_general(
            member, best, NT, precision=lax.Precision.HIGHEST, preferred_element_type=F32
        )
        / SHARP
    )
    own_buf[...] = own
    all_ref[me] = own

    def share(step, source):
        target = device(lax.rem(me + step, devices))
        return remote(own_buf, all_ref.at[source], share_sems, step, target)

    each(lambda step: share(step, me).start())
    each(lambda step: share(step, lax.rem(me - step + devices, devices)).wait_recv())
    each(lambda step: share(step, me).wait_send())
    full = all_ref[...]
    peak = jnp.max(full, axis=0)
    total = peak + jnp.log(jnp.sum(jnp.exp(full - peak[None]), axis=0))
    positive = pos_ref[...]
    passage = lax.broadcasted_iota(jnp.int32, full.shape, 0)
    picked = jnp.sum(jnp.where(passage == positive[None], full, 0.0), axis=0)
    loss_ref[...] = total - picked
    grads = jnp.exp(own - total) - (positive == me).astype(F32)
    spread = lax.dot_general(
        grads, member, TN, precision=lax.Precision.HIGHEST, preferred_element_type=F32
    )
    z_buf[...] = (spread / z_buf[...].reshape(micro * devices, tokens)).reshape(z_buf.shape)
    gp_ref[...] = jnp.zeros_like(gp_ref)

    def pair_copy(block):
        at = pl.ds(block * pairs, pairs)
        return remote(
            grad_buf.at[at, 1 - chips.core], near.at[at], pair_sems, block, chips.mate
        )

    def backward(block, carry):
        for m in range(micro):
            weight = jnp.concatenate(
                [z_buf[m, pl.ds(block * group + index, 1)] for index in range(group)], axis=1
            )
            grads = (e_buf[m, block].astype(F32) * weight).astype(BF16)
            gp_ref[m] += mm(grads, query_rows(block, m))
            part = mm(grads, p_ref[m], TN).astype(BF16)
            for index in range(group):
                grad_buf[block * pairs + index // 2, index % 2, m * tokens : (m + 1) * tokens] = (
                    part[index * tokens : (index + 1) * tokens]
                )
        pair_copy(block).start()
        return carry

    lax.fori_loop(0, devices // group, backward, 0)

    def join(block, carry):
        copy = pair_copy(block)
        copy.wait_recv()
        copy.wait_send()
        at = pl.ds(block * pairs, pairs)
        half_ref[at] = (
            grad_buf[at, chips.core].astype(F32) + near[at].astype(F32)
        ).astype(BF16)
        return carry

    lax.fori_loop(0, devices // group, join, 0)


def match(queries, passages, lens, positives, n_wide, n_narrow, query_len):
    devices, micro, tokens, width = queries.shape
    slots = passages.shape[1]
    group = 8
    own = tokens // query_len
    placed = positives.reshape(micro, devices, own).transpose(2, 0, 1).reshape(own, -1)
    placed = jnp.pad(placed, ((0, 8 - own), (0, 0)))
    sem = pltpu.SemaphoreType.DMA
    vmem = pl.BlockSpec(memory_space=pltpu.VMEM)
    columns = micro * devices
    return pl.pallas_call(
        functools.partial(match_kernel, n_wide, n_narrow, group, query_len),
        out_shape=(
            jax.ShapeDtypeStruct((devices, 8, columns), F32),
            jax.ShapeDtypeStruct((8, columns), F32),
            jax.ShapeDtypeStruct((micro, slots, width), F32),
            jax.ShapeDtypeStruct((devices // 2, micro * tokens, width), BF16),
        ),
        in_specs=[pl.BlockSpec(memory_space=pltpu.SMEM), vmem, vmem, vmem],
        out_specs=(vmem,) * 4,
        scratch_shapes=[
            pltpu.VMEM((micro, devices // group, slots, group * tokens), BF16),
            pltpu.VMEM((micro, devices, tokens), F32),
            pltpu.VMEM((8, columns), F32),
            pltpu.VMEM((devices // 2, 2, micro * tokens, width), BF16),
            pltpu.VMEM((devices // 2, micro * tokens, width), BF16),
            sem((devices,)),
            sem((devices,)),
            sem((devices // group,)),
            sem((devices // group,)),
        ],
        compiler_params=pltpu.CompilerParams(
            collective_id=1, has_side_effects=True, vmem_limit_bytes=VMEM_LIMIT
        ),
        name="match",
    )(lens, queries, passages, placed)


def accumulate(ref, row, value):
    ref[row : row + 1, :] += jnp.sum(value, axis=0, keepdims=True)


def mlp_back_kernel(alias_count, sizes, *refs):
    (
        ge_ref,
        unit_ref,
        uinv_ref,
        n2_ref,
        r2_ref,
        slope_ref,
        n1_ref,
        r1_ref,
        vec_ref,
    ) = refs[:9]
    sources = refs[9:12]
    refs = refs[12 + alias_count :]
    swap = None
    if sizes:
        swap = Push(Chips(*sizes), refs[0], refs[7], refs[-4:])
        refs = refs[1:7] + refs[8:-4]
    gp_ref, go_ref, gi_ref, gh_ref, ga_ref, sums_ref = refs[:6]
    wl, w2, wi, sem, acc_ref = refs[6:]
    loader = Loader(sources, (wl, w2, wi), sem)
    loader.start()
    if swap:
        pl.when(loader.first)(swap.start)

    @pl.when(loader.first)
    def _():
        sums_ref[...] = jnp.zeros_like(sums_ref)

    grad = ge_ref[...]
    unit = unit_ref[...]
    projected_low = (
        uinv_ref[...] * (grad - unit * jnp.sum(grad * unit, axis=-1, keepdims=True))
    ).astype(BF16)
    gp_ref[...] = projected_low
    loader.need(0)
    grad_final = mm(projected_low, wl[...], NT)
    normed = n2_ref[...].astype(F32)
    accumulate(sums_ref, ROW_G2, grad_final * normed)
    accumulate(sums_ref, ROW_S2, grad_final)
    scaled = grad_final * vec_row(vec_ref, ROW_G2)
    grad_second = r2_ref[:, :1] * (scaled - mean_row(scaled) - normed * mean_row(scaled * normed))
    outer_low = grad_second.astype(BF16)
    go_ref[...] = outer_low
    accumulate(sums_ref, ROW_B2, outer_low.astype(F32))
    acc_ref[...] = grad_second
    loader.need(1, 2)
    width = go_ref.shape[1]

    def chunk_body(chunk, carry):
        cols = pl.ds(pl.multiple_of(chunk * width, width), width)
        grad_act = mm(go_ref[...], w2[cols, :], NT)
        inner = (grad_act * slope_ref[:, cols].astype(F32)).astype(BF16)
        gi_ref[:, cols] = inner
        sums_ref[pl.ds(ROW_BI + chunk, 1), :] += jnp.sum(
            inner.astype(F32), axis=0, keepdims=True
        )
        acc_ref[...] += mm(inner, wi[:, cols], NT)
        return carry

    lax.fori_loop(0, wi.shape[1] // width, chunk_body, 0)
    grad_first = acc_ref[...]
    normed = n1_ref[...].astype(F32)
    accumulate(sums_ref, ROW_G1, grad_first * normed)
    accumulate(sums_ref, ROW_S1, grad_first)
    scaled = grad_first * vec_row(vec_ref, ROW_G1)
    hidden = r1_ref[:, :1] * (scaled - mean_row(scaled) - normed * mean_row(scaled * normed))
    gh_ref[...] = hidden
    low = hidden.astype(BF16)
    ga_ref[...] = low
    accumulate(sums_ref, ROW_BO, low.astype(F32))
    if swap:
        pl.when(pl.program_id(0) == pl.num_programs(0) - 1)(swap.finish)


def mlp_back(grad_embed, kept, vec, weights, blocks, total, offset, earlier, sent, sizes):
    own = grad_embed.shape[0]
    rows = own // blocks
    base = offset // rows
    _, _, _, _, wi, w2, wl = weights
    width, wide = wi.shape
    embed_width = wl.shape[1]

    def row_spec(columns):
        return pl.BlockSpec((rows, columns), lambda i: (base + i, 0))

    def own_spec(columns):
        return pl.BlockSpec((rows, columns), lambda i: (i, 0))

    args = [grad_embed] + [kept[index] for index in (13, 14, 10, 11, 9, 5, 6)]
    out_shapes = [
        jax.ShapeDtypeStruct((total, embed_width), BF16),
        jax.ShapeDtypeStruct((total, width), BF16),
        jax.ShapeDtypeStruct((total, wide), BF16),
        jax.ShapeDtypeStruct((own, width), F32),
        jax.ShapeDtypeStruct((total, width), BF16),
        jax.ShapeDtypeStruct((16, width), F32),
    ]
    shared = (0, 1, 2, 4)
    out_specs = [
        (row_spec if index in shared else own_spec)(out.shape[1])
        for index, out in enumerate(out_shapes[:5])
    ] + [pl.BlockSpec((16, width), lambda i: (0, 0))]
    aliased = [] if earlier is None else [earlier[index] for index in shared]
    sends, scratch, params = [], [], {}
    if sizes:
        sends = [sent]
        out_shapes.append(jax.ShapeDtypeStruct(sent.shape[1:], F32))
        out_specs.append(pl.BlockSpec(sent.shape[1:], lambda i: (0, 0)))
        scratch = push_scratch(*sent.shape)
        params = {"collective_id": 5, "has_side_effects": True}
    return pl.pallas_call(
        functools.partial(mlp_back_kernel, len(aliased), sizes),
        out_shape=out_shapes,
        grid=(blocks,),
        in_specs=[own_spec(arg.shape[1]) for arg in args]
        + [pl.BlockSpec(vec.shape, lambda i: (0, 0))]
        + [ANY] * (3 + len(aliased) + len(sends)),
        out_specs=out_specs,
        scratch_shapes=[pltpu.VMEM(weight.shape, BF16) for weight in (wl, w2, wi)]
        + [pltpu.SemaphoreType.DMA((3,)), pltpu.VMEM((rows, width), F32)]
        + scratch,
        input_output_aliases={12 + index: shared[index] for index in range(len(aliased))},
        compiler_params=pltpu.CompilerParams(vmem_limit_bytes=VMEM_LIMIT, **params),
        name="mlp_back_queries" if earlier is not None else "mlp_back_passages",
    )(*args, vec, wl, w2, wi, *aliased, *sends)


def attention_back_kernel(alias_count, *refs):
    ga_ref, gh_ref, att_ref, q_ref, k_ref, v_ref = refs[:6]
    sources = refs[6:10]
    refs = refs[10 + alias_count :]
    gqkv_ref, gx_ref, sums_ref = refs[:3]
    wo, wq, wk, wv, sem, gc_ref = refs[3:]
    loader = Loader(sources, (wo, wq, wk, wv), sem)
    loader.start()

    @pl.when(loader.first)
    def _():
        sums_ref[...] = jnp.zeros_like(sums_ref)

    rows, width = gh_ref.shape
    scale = HEAD_DIM ** (-0.5)
    loader.need(0)
    gc_ref[...] = mm(ga_ref[...], wo[...], NT).astype(BF16)
    low_half = lax.broadcasted_iota(jnp.int32, (rows, 128), 1) < HEAD_DIM

    def pair_body(pair, carry):
        cols = pl.ds(pl.multiple_of(pair * 128, 128), 128)
        q_pair, k_pair, v_pair, gc_pair = q_ref[:, cols], k_ref[:, cols], v_ref[:, cols], gc_ref[:, cols]
        parts = []
        for half in range(2):
            mask = low_half if half == 0 else jnp.logical_not(low_half)
            low = att_ref[0, 2 * pair + half]
            att = low.astype(F32)
            grad_att = mm(jnp.where(mask, gc_pair, jnp.zeros_like(gc_pair)), v_pair, NT)
            weighted = grad_att * att
            grad_logits = (weighted - att * jnp.sum(weighted, axis=-1, keepdims=True)).astype(BF16)
            parts.append(
                (
                    mm(grad_logits, k_pair) * scale,
                    mm(grad_logits, q_pair, TN),
                    mm(low, gc_pair, TN),
                )
            )
        for index in range(3):
            gqkv_ref[:, pl.ds(pl.multiple_of(index * width + pair * 128, 128), 128)] = jnp.where(
                low_half, parts[0][index], parts[1][index]
            ).astype(BF16)
        return carry

    lax.fori_loop(0, HEADS // 2, pair_body, 0)
    loader.need(1, 2, 3)
    grad_q, grad_k, grad_v = (
        gqkv_ref[:, :width],
        gqkv_ref[:, width : 2 * width],
        gqkv_ref[:, 2 * width :],
    )
    accumulate(sums_ref, 0, grad_q.astype(F32))
    accumulate(sums_ref, 1, grad_v.astype(F32))
    gx_ref[...] = (
        gh_ref[...]
        + mm(grad_q, wq[...], NT)
        + mm(grad_k, wk[...], NT)
        + mm(grad_v, wv[...], NT)
    )


def attention_back(attended, hidden, kept, weights, blocks, total, offset, earlier):
    own, width = hidden.shape
    rows = own // blocks
    base = offset // rows
    wq, wk, wv, wo = weights[:4]

    def row_spec(columns):
        return pl.BlockSpec((rows, columns), lambda i: (base + i, 0))

    def own_spec(columns):
        return pl.BlockSpec((rows, columns), lambda i: (i, 0))

    aliased = [] if earlier is None else [earlier]
    return pl.pallas_call(
        functools.partial(attention_back_kernel, len(aliased)),
        out_shape=(
            jax.ShapeDtypeStruct((total, 3 * width), BF16),
            jax.ShapeDtypeStruct((own, width), F32),
            jax.ShapeDtypeStruct((8, width), F32),
        ),
        grid=(blocks,),
        in_specs=[
            row_spec(width),
            own_spec(width),
            pl.BlockSpec((1, HEADS, rows, rows), lambda i: (i, 0, 0, 0)),
            own_spec(width),
            own_spec(width),
            own_spec(width),
        ]
        + [ANY] * (4 + len(aliased)),
        out_specs=(
            row_spec(3 * width),
            own_spec(width),
            pl.BlockSpec((8, width), lambda i: (0, 0)),
        ),
        scratch_shapes=[pltpu.VMEM(weight.shape, BF16) for weight in weights[:4]]
        + [pltpu.SemaphoreType.DMA((4,)), pltpu.VMEM((rows, width), BF16)],
        input_output_aliases={10: 0} if aliased else {},
        compiler_params=pltpu.CompilerParams(vmem_limit_bytes=VMEM_LIMIT),
        name="attention_back_queries" if aliased else "attention_back_passages",
    )(attended, hidden, kept[3], kept[0], kept[1], kept[2], wo, wq, wk, wv, *aliased)


def pack(vectors, width):
    count = sum(vector.shape[0] for vector in vectors)
    total = -(-count // (8 * width)) * 8 * width
    start, packed = 0, 0.0
    for vector in vectors:
        size = vector.shape[0]
        packed = packed + jnp.pad(vector.astype(F32), (start, total - start - size))
        start += size
    return packed.reshape(-1, width)


def share_kernel(n_wide, n_narrow, own_ref, all_ref, send_sem, recv_sem):
    me = lax.axis_index("narrow") * n_wide + lax.axis_index("wide")
    total = n_wide * n_narrow
    sems = (send_sem, recv_sem)

    def device(index):
        return (lax.rem(index, n_wide), index // n_wide)

    barrier = pltpu.get_barrier_semaphore()

    def signal(step, carry):
        pl.semaphore_signal(
            barrier, inc=1, device_id=device(lax.rem(me + step, total)), device_id_type=MESH
        )
        return carry

    def send(step, carry):
        target = device(lax.rem(me + step, total))
        remote(own_ref, all_ref.at[me], sems, step, target).start()
        return carry

    def wait(step, carry):
        source = lax.rem(me - step + total, total)
        copy = remote(own_ref, all_ref.at[source], sems, step, device(source))
        copy.wait_recv()
        copy.wait_send()
        return carry

    lax.fori_loop(1, total, signal, 0)
    all_ref[me] = own_ref[...]
    pl.semaphore_wait(barrier, total - 1)
    lax.fori_loop(1, total, send, 0)
    lax.fori_loop(1, total, wait, 0)


def share_scores(own, n_wide, n_narrow):
    total = n_wide * n_narrow
    return pl.pallas_call(
        functools.partial(share_kernel, n_wide, n_narrow),
        out_shape=jax.ShapeDtypeStruct((total,) + own.shape, own.dtype),
        in_specs=[pl.BlockSpec(memory_space=pltpu.VMEM)],
        out_specs=pl.BlockSpec(memory_space=pltpu.VMEM),
        scratch_shapes=[pltpu.SemaphoreType.DMA((total,))] * 2,
        compiler_params=pltpu.CompilerParams(collective_id=1, has_side_effects=True),
        name="share_scores",
    )(own)


def exchange_kernel(n_wide, n_narrow, g_ref, out_ref, *scratch):
    swap = Exchange(Chips(n_wide, n_narrow), g_ref, out_ref, scratch)
    swap.start()
    swap.push()
    swap.finish()


def exchange(grads, n_wide, n_narrow):
    chips, _, rows, width = grads.shape
    return pl.pallas_call(
        functools.partial(exchange_kernel, n_wide, n_narrow),
        out_shape=jax.ShapeDtypeStruct((rows, width), F32),
        in_specs=[ANY],
        out_specs=pl.BlockSpec(memory_space=pltpu.VMEM),
        scratch_shapes=exchange_scratch(chips, rows, width),
        compiler_params=pltpu.CompilerParams(
            collective_id=2, has_side_effects=True, vmem_limit_bytes=VMEM_LIMIT
        ),
        name="exchange_query_gradients",
    )(grads)


UNITS = (
    (0, 48, 0),
    (48, 48, 0),
    (96, 48, 48),
    (144, 48, 48),
    (192, 16, 96),
    (240, 16, 96),
    (208, 16, 112),
    (256, 16, 112),
    (224, 16, 128),
    (272, 32, 128),
)
EARLY = (0, 1, 2, 3)
LATE = (4, 5, 6, 7, 8, 9)
SHARE_ROWS = 304
LATE_B = 240
ROWS_A, ROWS_B = 144, 160
TILES = 9


def tail_kernel(n_z, part, *refs):
    act, go, first, gi, x_p, x_q, ctx, ga, final, gp = refs[:10]
    kept = (refs[10:15], refs[15:20])
    sources = refs[20:24]
    sums = refs[24:26]
    out_ref, gx_p, gx_q = refs[26:29]
    both, near, over_a, over_b, then_a, then_b, line, left_buf, right_buf, thin_buf = refs[29:39]
    wo, wq, wk, wv, att_buf, hidden, thin_hidden, grads, att_sums = refs[39:48]
    load_sem, weight_sem, block_sem, att_sem, gx_sem = refs[48:53]
    core_sems, one_sems, two_sems, line_sems, copy_sems = (
        refs[53 + 2 * index : 55 + 2 * index] for index in range(5)
    )
    wide, narrow = lax.axis_index("wide"), lax.axis_index("narrow")
    z, x = wide // 2, lax.rem(wide, 2)
    y, core = narrow // 2, lax.rem(narrow, 2)
    mate = (wide, y * 2 + 1 - core)
    over_y = (wide, (1 - y) * 2 + core)
    over_x = (z * 2 + 1 - x, narrow)
    total, width = go.shape
    p_rows = x_p.shape[0]
    held = both.at[core]

    def load(tile, wait):
        slot = lax.rem(tile, 2)
        block = pl.ds(pl.multiple_of(lax.rem(tile, 4) * width, width), width)

        def pair(source, other, target):
            for made in (
                pltpu.make_async_copy(source, left_buf.at[slot], load_sem.at[slot, 0]),
                pltpu.make_async_copy(other, target, load_sem.at[slot, 1]),
            ):
                if wait:
                    made.wait()
                else:
                    made.start()

        place = right_buf.at[slot]
        pl.when(tile < 4)(lambda: pair(act.at[:, block], go, place))
        pl.when(jnp.logical_and(tile >= 4, tile < 8))(lambda: pair(first, gi.at[:, block], place))
        pl.when(tile == 8)(lambda: pair(ctx, ga, place))
        pl.when(tile == TILES)(lambda: pair(final, gp, thin_buf))

    def rows_of(unit):
        start, count, _ = UNITS[unit]
        return pl.ds(start, count)

    def place_of(unit):
        _, count, place = UNITS[unit]
        return pl.ds(place, count)

    def core_copy(unit):
        rows = rows_of(unit)
        return remote(
            both.at[1 - core, :, :, :, rows], near.at[:, :, :, rows], core_sems, unit, mate
        )

    def late_copy(index):
        row_y, start, count = ((0, 2 * part, part + 16), (1, LATE_B, 64), (1, 2 * part, 48))[index]
        rows = pl.ds(start, count)
        return remote(
            both.at[1 - core, row_y, :, :, rows],
            near.at[row_y, :, :, rows],
            core_sems,
            len(EARLY) + index,
            mate,
        )

    def one_copy(unit):
        rows = rows_of(unit)
        place = place_of(unit)
        if unit % 2 == 0:
            return remote(
                held.at[1 - y, :, :, rows],
                over_a.at[:, :, place],
                one_sems,
                unit,
                over_y,
            )
        return remote(
            held.at[:, :, 1 - x, rows],
            over_b.at[:, :, place],
            one_sems,
            unit,
            over_x,
        )

    def two_copy(unit):
        rows = rows_of(unit)
        place = place_of(unit)
        if unit % 2 == 0:
            return remote(
                held.at[y, :, 1 - x, rows],
                then_a.at[:, place],
                two_sems,
                unit,
                over_x,
            )
        return remote(
            held.at[1 - y, :, x, rows],
            then_b.at[:, place],
            two_sems,
            unit,
            over_y,
        )

    def far_copy(unit, step):
        rows = rows_of(unit)
        target = lax.rem(z + step, n_z)
        return remote(
            held.at[y, target, x, rows],
            line.at[step - 1, rows],
            line_sems,
            unit * n_z + step,
            (target * 2 + x, narrow),
        )

    def share_copy(unit, step, arriving):
        rows = rows_of(unit)
        slots = (
            (y * 2 + 1 - core, (1 - y) * 2 + core, (1 - y) * 2 + 1 - core)
            if arriving
            else (narrow, narrow, (1 - y) * 2 + core)
        )
        block = out_ref.at[slots[step], rows]
        return remote(block, block, copy_sems, unit * 3 + step, over_y if step == 1 else mate)

    def add(target, extra):
        target[...] = target[...] + extra[...]

    def start_core(unit):
        core_copy(unit).start()

    def start_one(unit):
        rows = rows_of(unit)
        if unit in EARLY:
            core_copy(unit).wait_recv()

        def body(index, carry):
            row_y, rest = index // (n_z * 2), lax.rem(index, n_z * 2)
            at = (row_y, rest // 2, lax.rem(rest, 2), rows)
            add(held.at[at], near.at[at])
            return carry

        lax.fori_loop(0, 4 * n_z, body, 0)
        one_copy(unit).start()

    def start_two(unit):
        rows = rows_of(unit)
        place = place_of(unit)
        one_copy(unit).wait_recv()

        def body(index, carry):
            outer_at, inner_at = index // 2, lax.rem(index, 2)
            if unit % 2 == 0:
                add(
                    held.at[y, outer_at, inner_at, rows],
                    over_a.at[outer_at, inner_at, place],
                )
            else:
                add(
                    held.at[inner_at, outer_at, x, rows],
                    over_b.at[inner_at, outer_at, place],
                )
            return carry

        lax.fori_loop(0, 2 * n_z, body, 0)
        two_copy(unit).start()

    def start_far(unit):
        rows = rows_of(unit)
        place = place_of(unit)
        extra = then_a if unit % 2 == 0 else then_b
        two_copy(unit).wait_recv()

        def body(index, carry):
            add(held.at[y, index, x, rows], extra.at[index, place])
            return carry

        lax.fori_loop(0, n_z, body, 0)
        for step in range(1, n_z):
            far_copy(unit, step).start()

    def start_share(unit):
        rows = rows_of(unit)
        for step in range(1, n_z):
            far_copy(unit, step).wait_recv()
            add(held.at[y, z, x, rows], line.at[step - 1, rows])
        out_ref[narrow, rows] = both[core, y, z, x, rows]
        share_copy(unit, 1, False).start()
        share_copy(unit, 0, False).start()

    def forward(unit):
        share_copy(unit, 1, True).wait_recv()
        share_copy(unit, 2, False).start()

    def finish(unit):
        share_copy(unit, 0, True).wait_recv()
        share_copy(unit, 2, True).wait_recv()
        for step in range(3):
            share_copy(unit, step, False).wait_send()
        if unit in EARLY:
            core_copy(unit).wait_send()
        one_copy(unit).wait_send()
        two_copy(unit).wait_send()
        for step in range(1, n_z):
            far_copy(unit, step).wait_send()

    barrier = pltpu.get_barrier_semaphore()
    load(0, False)
    partners = [mate, over_y, over_x] + [
        (lax.rem(z + step, n_z) * 2 + x, narrow) for step in range(1, n_z)
    ]
    for device in partners:
        pl.semaphore_signal(barrier, inc=1, device_id=device, device_id_type=MESH)
    pl.semaphore_wait(barrier, len(partners))

    def put(kind, owner, half, made):
        rows = pl.ds(pl.multiple_of(kind * part, part), part)
        for index in range(4):
            both[lax.rem(owner, 2), owner // 2, 2 * half + index // 2, index % 2, rows] = made[
                index * part : (index + 1) * part
            ]

    def halves(left_ref, right_ref, store):
        def half_body(half, carry):
            cols = pl.ds(pl.multiple_of(half * 4 * part, 4 * part), 4 * part)
            store(half, mm(left_ref[:, cols], right_ref[...], TN).astype(BF16))
            return carry

        lax.fori_loop(0, 2, half_body, 0)

    def hooks(now, plan):
        for at, step, units in plan:

            @pl.when(now == at)
            def _(step=step, units=units):
                for unit in units:
                    step(unit)

    def tile_body(tile, carry):
        slot = lax.rem(tile, 2)
        load(tile, True)
        load(tile + 1, False)
        kind = tile // 4
        owner = jnp.where(tile == 8, 3, lax.rem(tile, 4))

        def store(half, made):
            @pl.when(kind == 0)
            def _():
                for index in range(4):
                    both[index % 2, index // 2, owner, half, :part] = made[
                        index * part : (index + 1) * part
                    ]

            pl.when(kind > 0)(lambda: put(kind, owner, half, made))

        halves(left_buf.at[slot], right_buf.at[slot], store)
        hooks(
            tile,
            (
                (3, start_core, (0, 1)),
                (5, start_one, (0,)),
                (6, start_one, (1,)),
                (7, start_core, (2, 3)),
            ),
        )
        return carry

    def hidden_of(block):
        return thin_hidden if blocks[block][2] else hidden.at[block]

    def block_copies(block):
        rows, base, source = blocks[block]
        q, k, v, gh, _ = kept[source]
        buf = left_buf if block % 2 == 0 else right_buf
        own = pl.ds(base - (p_rows if source else 0), rows)
        low, high = pl.ds(0, rows), pl.ds(span, rows)
        pairs = (
            (q.at[own], buf.at[0, low]),
            (k.at[own], buf.at[0, high]),
            (v.at[own], buf.at[1, low]),
            (ga.at[pl.ds(base, rows)], buf.at[1, high]),
            (gh.at[own], hidden_of(block)),
        )
        return [
            pltpu.make_async_copy(*pair, block_sem.at[block % 2, index])
            for index, pair in enumerate(pairs)
        ]

    def gx_copy(block):
        rows, base, source = blocks[block]
        target = gx_q if source else gx_p
        own = pl.ds(base - (p_rows if source else 0), rows)
        return pltpu.make_async_copy(hidden_of(block), target.at[own], gx_sem.at[block])

    def states(block):
        rows, base, _ = blocks[block]
        own = pl.ds(base, rows)
        hidden_of(block)[...] += (
            mm(grads[0, own], wq[...], NT)
            + mm(grads[1, own], wk[...], NT)
            + mm(grads[2, own], wv[...], NT)
        )
        gx_copy(block).start()

    def attention(block, plan):
        rows, base, source = blocks[block]
        buf = left_buf if block % 2 == 0 else right_buf
        low, high, own = pl.ds(0, rows), pl.ds(span, rows), pl.ds(base, rows)
        att = kept[source][4]
        q_ref, k_ref, v_ref, ga_ref = (
            buf.at[0, low],
            buf.at[0, high],
            buf.at[1, low],
            buf.at[1, high],
        )
        entry = 0 if source else block
        size = pl.ds(0, rows)

        def att_copy(pair):
            slot = lax.rem(pair, 2)
            return pltpu.make_async_copy(
                att.at[entry, pl.ds(2 * pair, 2)],
                att_buf.at[slot, :, size, size],
                att_sem.at[slot],
            )

        att_copy(0).start()
        for copy in block_copies(block):
            copy.wait()
        grads[2, own] = mm(ga_ref[...], wo[...], NT).astype(BF16)
        low_half = lax.broadcasted_iota(jnp.int32, (rows, 128), 1) < HEAD_DIM
        scale = HEAD_DIM ** (-0.5)

        def pair_body(pair, carry):
            cols = pl.ds(pl.multiple_of(pair * 128, 128), 128)
            slot = lax.rem(pair, 2)
            att_copy(pair).wait()
            pl.when(pair < HEADS // 2 - 1)(lambda: att_copy(pair + 1).start())
            q_pair, k_pair, v_pair = q_ref[:, cols], k_ref[:, cols], v_ref[:, cols]
            gc_pair = grads[2, own, cols]
            parts = []
            for half in range(2):
                mask = low_half if half == 0 else jnp.logical_not(low_half)
                low_att = att_buf[slot, half, size, size]
                wide_att = low_att.astype(F32)
                grad_att = mm(jnp.where(mask, gc_pair, jnp.zeros_like(gc_pair)), v_pair, NT)
                weighted = grad_att * wide_att
                grad_logits = (
                    weighted - wide_att * jnp.sum(weighted, axis=-1, keepdims=True)
                ).astype(BF16)
                parts.append(
                    (
                        mm(grad_logits, k_pair) * scale,
                        mm(grad_logits, q_pair, TN),
                        mm(low_att, gc_pair, TN),
                    )
                )
            for index in range(3):
                grads[index, own, cols] = jnp.where(
                    low_half, parts[0][index], parts[1][index]
                ).astype(BF16)
            hooks(pair, plan)
            return carry

        lax.fori_loop(0, HEADS // 2, pair_body, 0)
        accumulate(att_sums, 0, grads[0, own].astype(F32))
        accumulate(att_sums, 1, grads[2, own].astype(F32))

    def weight_copies():
        return [
            pltpu.make_async_copy(source, target, weight_sem.at[index])
            for index, (source, target) in enumerate(zip(sources, (wo, wq, wk, wv)))
        ]

    span = kept[0][4].shape[-1]
    blocks = [(span, base, 0) for base in range(0, p_rows, span)] + [(x_q.shape[0], p_rows, 1)]
    for copy in weight_copies():
        copy.start()
    att_sums[...] = jnp.zeros_like(att_sums)
    lax.fori_loop(0, TILES, tile_body, 0)
    load(TILES, True)
    slot = TILES % 2
    made = mm(left_buf[slot], thin_buf[...], TN).astype(BF16)
    for copy in block_copies(0):
        copy.start()
    lanes = thin_buf.shape[1]
    last = pl.ds(3 * part, 16)
    for shard in range(2 * n_z):
        for block in range(width // lanes):
            row = shard * part + block * 16
            both[0, 0, shard // 2, shard % 2, last, block * lanes : (block + 1) * lanes] = made[
                row : row + 16
            ]
    for copy in weight_copies():
        copy.wait()
    for copy in block_copies(1):
        copy.start()
    attention(0, ((0, start_one, (2, 3)), (3, start_two, (0, 1))))
    for copy in block_copies(2):
        copy.start()
    attention(
        1,
        (
            (0, start_far, (0, 1)),
            (2, start_two, (2, 3)),
            (5, start_far, (2, 3)),
        ),
    )
    x_copies = [
        pltpu.make_async_copy(x_p, right_buf.at[0, pl.ds(0, p_rows)], load_sem.at[0, 0]),
        pltpu.make_async_copy(
            x_q, right_buf.at[0, pl.ds(p_rows, total - p_rows)], load_sem.at[0, 1]
        ),
    ]
    for copy in x_copies:
        copy.start()
    attention(2, ((2, start_share, (0, 1)),))
    top = sums[0][:8] + sums[1][:8] + att_sums[...]
    tail = jnp.concatenate([top, sums[0][8:] + sums[1][8:]], axis=0).astype(BF16)
    for shard in range(2 * n_z):
        at_z, at_x = shard // 2, shard % 2
        both[1, 0, at_z, at_x, last] = tail
        both[0, 1, at_z, at_x, last] = jnp.zeros_like(tail)
        both[1, 1, at_z, at_x, last] = jnp.zeros_like(tail)
    for copy in x_copies:
        copy.wait()

    def late_body(tile, carry):
        halves(right_buf.at[0], grads.at[tile], lambda half, made: put(2, tile, half, made))
        pl.when(tile == 1)(lambda: late_copy(0).start())
        return carry

    lax.fori_loop(0, 3, late_body, 0)

    def start_late(index):
        late_copy(index).start()

    def wait_late(index):
        late_copy(index).wait_recv()

    def end_late(index):
        late_copy(index).wait_send()

    for step, units in (
        (start_late, (1, 2)),
        (start_share, (2, 3)),
        (wait_late, (0, 1)),
        (start_one, (5, 7, 9)),
        (wait_late, (2,)),
        (start_one, (4, 6, 8)),
        (forward, EARLY),
        (states, (0,)),
        (start_two, (5, 4)),
        (states, (1,)),
        (start_two, (7, 6)),
        (start_far, (5, 4)),
        (states, (2,)),
        (start_two, (8,)),
        (start_far, (7, 6)),
        (start_two, (9,)),
        (start_far, (8,)),
        (start_share, (5, 4)),
        (start_far, (9,)),
        (start_share, (7, 6, 8)),
        (forward, (5, 4, 7, 6)),
        (start_share, (9,)),
        (forward, (8, 9)),
        (finish, EARLY + LATE),
        (end_late, (0, 1, 2)),
        (lambda block: gx_copy(block).wait(), range(len(blocks))),
    ):
        for unit in units:
            step(unit)


def backward_tail(arrays, passage_kept, query_kept, weights, sums, n_wide):
    n_z = n_wide // 2
    go, x_p, x_q, gp = arrays[1], arrays[4], arrays[5], arrays[9]
    total, width = go.shape
    part = width // n_wide
    units = len(UNITS)
    span = passage_kept[4].shape[-1]
    sem = pltpu.SemaphoreType.DMA
    vmem = pl.BlockSpec(memory_space=pltpu.VMEM)
    return pl.pallas_call(
        functools.partial(tail_kernel, n_z, part),
        out_shape=(
            jax.ShapeDtypeStruct((4, SHARE_ROWS, width), BF16),
            jax.ShapeDtypeStruct(x_p.shape, F32),
            jax.ShapeDtypeStruct(x_q.shape, F32),
        ),
        in_specs=[ANY] * 24 + [vmem] * 2,
        out_specs=(vmem, ANY, ANY),
        scratch_shapes=[
            pltpu.VMEM((2, 2, n_z, 2, SHARE_ROWS, width), BF16),
            pltpu.VMEM((2, n_z, 2, SHARE_ROWS, width), BF16),
            pltpu.VMEM((n_z, 2, ROWS_A, width), BF16),
            pltpu.VMEM((2, n_z, ROWS_B, width), BF16),
            pltpu.VMEM((n_z, ROWS_A, width), BF16),
            pltpu.VMEM((n_z, ROWS_B, width), BF16),
            pltpu.VMEM((n_z - 1, SHARE_ROWS, width), BF16),
            pltpu.VMEM((2, total, width), BF16),
            pltpu.VMEM((2, total, width), BF16),
            pltpu.VMEM(gp.shape, BF16),
        ]
        + [pltpu.VMEM((width, width), BF16)] * 4
        + [
            pltpu.VMEM((2, 2, span, span), BF16),
            pltpu.VMEM((2, span, width), F32),
            pltpu.VMEM(x_q.shape, F32),
            pltpu.VMEM((3, total, width), BF16),
            pltpu.VMEM((8, width), F32),
            sem((2, 2)),
            sem((4,)),
            sem((2, 5)),
            sem((2,)),
            sem((3,)),
        ]
        + [sem((units,))] * 6
        + [sem((units * n_z,))] * 2
        + [sem((units * 3,))] * 2,
        compiler_params=pltpu.CompilerParams(
            collective_id=3, has_side_effects=True, vmem_limit_bytes=VMEM_LIMIT
        ),
        name="backward_tail",
    )(*arrays, *passage_kept, *query_kept, *weights, *sums)


def unpack_kernel(part, sums_ref, q_ref, k_ref, v_ref, o_ref, inner_ref, outer_ref, thin_ref, vec_ref):
    width = q_ref.shape[1]
    lanes = thin_ref.shape[1]
    for owner, ref in enumerate((q_ref, k_ref, v_ref, o_ref)):
        ref[...] = sums_ref[owner, 2 * part : 3 * part].astype(F32)
        inner_ref[:, owner * width : (owner + 1) * width] = sums_ref[
            owner, part : 2 * part
        ].astype(F32)
        outer_ref[owner * part : (owner + 1) * part] = sums_ref[owner, :part].astype(F32)
    tail = sums_ref[0, 3 * part :].astype(F32)
    for block in range(width // lanes):
        thin_ref[block * 16 : (block + 1) * 16] = tail[:, block * lanes : (block + 1) * lanes]
    vec_ref[...] = sums_ref[1, 3 * part :].astype(F32)


def unpack(summed, part, embed_width):
    width = summed.shape[-1]
    vmem = pl.BlockSpec(memory_space=pltpu.VMEM)
    shapes = [(part, width)] * 4 + [
        (part, 4 * width),
        (4 * part, width),
        (part, embed_width),
        (16, width),
    ]
    return pl.pallas_call(
        functools.partial(unpack_kernel, part),
        out_shape=[jax.ShapeDtypeStruct(shape, F32) for shape in shapes],
        in_specs=[vmem],
        out_specs=[vmem] * len(shapes),
        compiler_params=pltpu.CompilerParams(vmem_limit_bytes=VMEM_LIMIT),
        name="unpack_gradients",
    )(summed)


def outer(left, right):
    return lax.dot_general(left, right, TN, preferred_element_type=F32)


def local(
    query_states,
    passage_states,
    lengths,
    positives,
    query_weight,
    query_bias,
    key_weight,
    value_weight,
    value_bias,
    out_weight,
    out_bias,
    first_gain,
    first_shift,
    inner_weight,
    inner_bias,
    outer_weight,
    outer_bias,
    second_gain,
    second_shift,
    linear_weight,
):
    everyone = ("wide", "narrow")
    n_wide = lax.axis_size("wide")
    n_narrow = lax.axis_size("narrow")
    wide_index = lax.axis_index("wide")
    narrow_index = lax.axis_index("narrow")
    micro, own_queries, query_len, width = query_states.shape
    own_passages, slots = passage_states.shape[1:3]
    weights = (
        query_weight,
        key_weight,
        value_weight,
        out_weight,
        inner_weight,
        outer_weight,
        linear_weight,
    )
    embed_width = linear_weight.shape[1]
    vec = pack(
        (
            query_bias,
            value_bias,
            out_bias,
            first_gain,
            first_shift,
            outer_bias,
            second_gain,
            second_shift,
            inner_bias,
        ),
        width,
    )
    own_index = narrow_index * n_wide + wide_index
    own_lengths = lax.dynamic_slice_in_dim(lengths, own_index * own_passages, own_passages, axis=1)
    lens = own_lengths.reshape(-1)
    x_query = query_states.reshape(-1, width)
    x_passage = passage_states.reshape(-1, width)
    query_rows, passage_rows = x_query.shape[0], x_passage.shape[0]
    total = query_rows + passage_rows
    kept_q = encode(
        x_query, lens, vec, weights, 1, query_len, total, passage_rows, None, None
    )
    sizes = (n_wide, n_narrow)
    kept_p = encode(
        x_passage, lens, vec, weights, micro * own_passages, 0, total, 0, kept_q, sizes
    )
    queries = kept_p[16].reshape(n_wide * n_narrow, micro, -1, embed_width)
    ctx, first_low, act, final_low = (kept_p[index] for index in (4, 7, 8, 12))
    passages = kept_p[15].reshape(micro * own_passages, slots, embed_width)
    row_count = own_queries * n_narrow
    together = queries.size * slots <= 8 * 1024 * 1024 * embed_width
    if together:
        full, loss, grad_passage, grad_query = match(
            queries, passages, lens, positives, n_wide, n_narrow, query_len
        )
        block = lax.dynamic_slice_in_dim(full, narrow_index * n_wide, n_wide, axis=0)
        block = lax.dynamic_slice_in_dim(
            block[:, :own_queries].reshape(n_wide, own_queries, micro, -1),
            wide_index * n_narrow,
            n_narrow,
            axis=3,
        )
        scores = block.transpose(2, 3, 1, 0).reshape(micro, row_count, n_wide)
        losses = lax.dynamic_slice_in_dim(
            loss[:own_queries].reshape(own_queries, micro, -1),
            wide_index * n_narrow,
            n_narrow,
            axis=2,
        )
        losses = losses.transpose(1, 2, 0).reshape(micro, row_count)
    else:
        e, z = similarity(queries, passages, lens)
        best = SHARP + jnp.log(z)
        own_scores = jnp.sum(best.reshape(micro, -1, query_len), axis=-1) / SHARP
        full = share_scores(own_scores, n_wide, n_narrow)
        row_total = jax.nn.logsumexp(full, axis=0)
        passage_ids = jnp.arange(full.shape[0], dtype=jnp.int32)
        picked = jnp.sum(
            jnp.where(passage_ids[:, None, None] == positives[None], full, 0.0), axis=0
        )
        row_count = own_queries * n_narrow
        losses = lax.dynamic_slice_in_dim(row_total - picked, wide_index * row_count, row_count, axis=1)
        block = lax.dynamic_slice(
            full,
            (narrow_index * n_wide, 0, wide_index * row_count),
            (n_wide, micro, row_count),
        )
        scores = jnp.transpose(block, (1, 2, 0))
        grads = jnp.exp(own_scores - row_total) - (positives == own_index).astype(F32)
        token_weights = jnp.repeat(grads, query_len, axis=1).reshape(z.shape) / z
        grad_passage, grad_query = similarity_back(e, token_weights, queries, passages)
        grad_query = grad_query.reshape(-1, 2, query_rows, embed_width)
    grad_passage = grad_passage.reshape(passage_rows, embed_width)
    back_p = mlp_back(
        grad_passage,
        kept_p,
        vec,
        weights,
        micro * own_passages,
        total,
        0,
        None,
        grad_query if together else None,
        sizes if together else None,
    )
    grad_query = back_p[6] if together else exchange(grad_query, n_wide, n_narrow)
    back_q = mlp_back(
        grad_query, kept_q, vec, weights, 1, total, passage_rows, back_p, None, None
    )
    gp, go, gi, _, ga, sums_q = back_q[:6]
    part = width // n_wide
    if part == 96 and n_narrow == 4 and micro * own_passages == 2 and act.shape[1] == 4 * width:
        summed, grad_p, grad_q = backward_tail(
            (act, go, first_low, gi, x_passage, x_query, ctx, ga, final_low, gp),
            (*kept_p[:3], back_p[3], kept_p[3]),
            (*kept_q[:3], back_q[3], kept_q[3]),
            (out_weight, query_weight, key_weight, value_weight),
            (back_p[5], sums_q),
            n_wide,
        )
        r_q, r_k, r_v, r_out, r_inner, r_outer, r_linear, vectors = unpack(
            summed, part, embed_width
        )
        own = lax.dynamic_slice_in_dim(vectors[:8], wide_index * part, part, axis=1)
        v_q, v_v, v_o, v_g1, v_s1, v_2, v_g2, v_s2 = (
            own[row] for row in (0, 1, ROW_BO, ROW_G1, ROW_S1, ROW_B2, ROW_G2, ROW_S2)
        )
        v_i = lax.dynamic_slice_in_dim(
            vectors[ROW_BI : ROW_BI + 4].reshape(-1), wide_index * 4 * part, 4 * part
        )
    else:
        att_p = attention_back(
            ga, back_p[3], kept_p, weights, micro * own_passages, total, 0, None
        )
        att_q = attention_back(ga, back_q[3], kept_q, weights, 1, total, passage_rows, att_p[0])
        gqkv, grad_p, grad_q = att_q[0], att_p[1], att_q[1]

        def reduce(value):
            piece = lax.psum_scatter(value.astype(BF16), everyone, scatter_dimension=0, tiled=True)
            return lax.all_gather(piece, "narrow", axis=0, tiled=True).astype(F32)

        def vector(rows):
            flat = rows.reshape(-1)
            share = flat.shape[0] // n_wide
            return lax.dynamic_slice_in_dim(flat, wide_index * share, share)

        sums = jnp.concatenate([back_p[5] + sums_q, att_p[2] + att_q[2]], axis=0)
        sums = lax.psum(sums, everyone)
        x_all = jnp.concatenate([x_passage, x_query], axis=0)
        pairs = ((act, go), (first_low, gi), (final_low, gp), (ctx, ga), (x_all, gqkv))
        r_outer, r_inner, r_linear, r_out, r_qkv = (
            reduce(outer(*pair)) for pair in pairs
        )
        r_q, r_k, r_v = (r_qkv[:, index * width : (index + 1) * width] for index in range(3))
        v_q, v_v, v_o, v_g1, v_s1, v_2, v_g2, v_s2 = (
            vector(sums[pick])
            for pick in (16, 17, ROW_BO, ROW_G1, ROW_S1, ROW_B2, ROW_G2, ROW_S2)
        )
        v_i = vector(sums[ROW_BI : ROW_BI + 4])
    return (
        scores,
        losses,
        grad_q.reshape(query_states.shape),
        grad_p.reshape(passage_states.shape),
        r_q,
        v_q,
        r_k,
        r_v,
        v_v,
        r_out,
        v_o,
        v_g1,
        v_s1,
        r_inner,
        v_i,
        r_outer,
        v_2,
        v_g2,
        v_s2,
        r_linear,
    )


def solution(mesh):
    return jax.shard_map(
        local,
        mesh=mesh,
        in_specs=(
            P(None, ("wide", "narrow"), None, None),
            P(None, ("narrow", "wide"), None, None),
        )
        + (P(),) * 18,
        out_specs=(
            P(None, "wide", "narrow"),
            P(None, "wide"),
            P(None, ("wide", "narrow"), None, None),
            P(None, ("narrow", "wide"), None, None),
            P("wide", None),
            P("wide"),
            P("wide", None),
            P("wide", None),
            P("wide"),
            P("wide", None),
            P("wide"),
            P("wide"),
            P("wide"),
            P("wide", None),
            P("wide"),
            P("wide", None),
            P("wide"),
            P("wide"),
            P("wide"),
            P("wide", None),
        ),
        check_vma=False,
    )
```

```python
import functools

import jax
import jax.numpy as jnp
from jax import lax
from jax.experimental import pallas as pl
from jax.experimental.pallas import tpu as pltpu
from jax.sharding import PartitionSpec as P

HEADS = 12
HEAD_DIM = 64
SHARP = 16.0
LAYER_EPS = 1e-12
NORM_EPS = 1e-06
MASKED = -1e30
SLOPE_CONST = 0.3989422804014327
ROOT_HALF = 0.7071067811865476
BF16 = jnp.bfloat16
F32 = jnp.float32
VMEM_LIMIT = 62 * 1024 * 1024

NN = (((1,), (0,)), ((), ()))
NT = (((1,), (1,)), ((), ()))
TN = (((0,), (0,)), ((), ()))


def mm(left, right, dims=NN):
    return lax.dot_general(left, right, dims, preferred_element_type=F32)


ANY = pl.BlockSpec(memory_space=pl.ANY)

ROW_BQ, ROW_BV, ROW_BO, ROW_G1, ROW_S1, ROW_B2, ROW_G2, ROW_S2, ROW_BI = range(9)


def vec_row(vec_ref, row):
    return vec_ref[row : row + 1, :]


def mean_row(value):
    return jnp.sum(value, axis=-1, keepdims=True) * (1.0 / value.shape[-1])


class Loader:
    def __init__(self, sources, targets, sem):
        self.copies = [
            pltpu.make_async_copy(source, target, sem.at[index])
            for index, (source, target) in enumerate(zip(sources, targets))
        ]
        self.first = pl.program_id(0) == 0

    def start(self):
        @pl.when(self.first)
        def _():
            for copy in self.copies:
                copy.start()

    def need(self, *indices):
        @pl.when(self.first)
        def _():
            for index in indices:
                self.copies[index].wait()


MESH = pl.DeviceIdType.MESH


def remote(source, target, sems, index, device):
    return pltpu.make_async_remote_copy(
        src_ref=source,
        dst_ref=target,
        send_sem=sems[0].at[index],
        recv_sem=sems[1].at[index],
        device_id=device,
        device_id_type=MESH,
    )


class Chips:
    def __init__(self, n_wide, n_narrow):
        self.wide, self.narrow = lax.axis_index("wide"), lax.axis_index("narrow")
        self.core = lax.rem(self.narrow, 2)
        self.rows = n_narrow // 2
        self.count = n_wide * self.rows
        self.me = self.wide * self.rows + self.narrow // 2
        self.mate = (self.wide, self.narrow + 1 - 2 * self.core)

    def at(self, step):
        return lax.rem(self.me + step + self.count, self.count)

    def device(self, chip):
        return (chip // self.rows, lax.rem(chip, self.rows) * 2 + self.core)

    def loop(self, body):
        def step_body(step, carry):
            body(step)
            return carry

        lax.fori_loop(1, self.count, step_body, 0)

    def barrier(self):
        barrier = pltpu.get_barrier_semaphore()

        def signal(step):
            pl.semaphore_signal(
                barrier, inc=1, device_id=self.device(self.at(step)), device_id_type=MESH
            )

        pl.semaphore_signal(barrier, inc=1, device_id=self.mate, device_id_type=MESH)
        self.loop(signal)
        pl.semaphore_wait(barrier, self.count)


class Gather:
    def __init__(self, chips, own, out, sems):
        self.chips, self.own, self.out = chips, own, out
        self.far, self.pair, self.local = sems[:2], sems[2:4], sems[4]

    def far_copy(self, step, chip):
        slot = self.out.at[chip, self.chips.core]
        return remote(self.own, slot, self.far, step, self.chips.device(self.chips.at(step)))

    def mate_copy(self, core):
        block = self.out.at[:, core]
        return remote(block, block, self.pair, 0, self.chips.mate)

    def local_copy(self):
        slot = self.out.at[self.chips.me, self.chips.core]
        return pltpu.make_async_copy(self.own, slot, self.local.at[0])

    def start(self):
        self.local_copy().start()
        self.chips.barrier()
        self.chips.loop(lambda step: self.far_copy(step, self.chips.me).start())

    def forward(self):
        self.local_copy().wait()
        self.chips.loop(lambda step: self.far_copy(step, self.chips.at(-step)).wait_recv())
        self.mate_copy(self.chips.core).start()

    def finish(self):
        self.chips.loop(lambda step: self.far_copy(step, self.chips.me).wait_send())
        self.mate_copy(1 - self.chips.core).wait_recv()
        self.mate_copy(self.chips.core).wait_send()


class Exchange:
    def __init__(self, chips, grads, out, scratch):
        self.chips, self.grads, self.out = chips, grads, out
        self.half, self.arrived, self.inbox = scratch[:3]
        self.pair, self.far, self.local = scratch[3:5], scratch[5:7], scratch[7]

    def pair_copy(self):
        away = self.grads.at[:, 1 - self.chips.core]
        return remote(away, self.arrived, self.pair, 0, self.chips.mate)

    def local_copy(self):
        mine = self.grads.at[:, self.chips.core]
        return pltpu.make_async_copy(mine, self.half, self.local.at[0])

    def far_copy(self, step):
        chip = self.chips.at(step)
        return remote(
            self.half.at[chip], self.inbox.at[step], self.far, step, self.chips.device(chip)
        )

    def start(self):
        self.local_copy().start()
        self.chips.barrier()
        self.pair_copy().start()

    def push(self):
        self.local_copy().wait()
        self.pair_copy().wait_recv()

        def add(step):
            chip = self.chips.at(step)
            total = self.half[chip].astype(F32) + self.arrived[chip].astype(F32)
            self.half[chip] = total.astype(BF16)
            self.far_copy(step).start()

        self.chips.loop(add)
        me = self.chips.me
        self.out[...] = self.half[me].astype(F32) + self.arrived[me].astype(F32)

    def finish(self):
        def collect(step):
            copy = self.far_copy(step)
            copy.wait_recv()
            copy.wait_send()
            self.out[...] += self.inbox[step].astype(F32)

        self.chips.loop(collect)
        self.pair_copy().wait_send()


class Push:
    def __init__(self, chips, half, out, scratch):
        self.chips, self.half, self.out = chips, half, out
        self.inbox, self.far, self.own = scratch[0], scratch[1:3], scratch[3]

    def far_copy(self, step):
        chip = self.chips.at(step)
        return remote(
            self.half.at[chip], self.inbox.at[step], self.far, step, self.chips.device(chip)
        )

    def own_copy(self):
        return pltpu.make_async_copy(
            self.half.at[self.chips.me], self.inbox.at[0], self.own.at[0]
        )

    def start(self):
        self.own_copy().start()
        self.chips.barrier()
        self.chips.loop(lambda step: self.far_copy(step).start())

    def finish(self):
        self.own_copy().wait()
        self.out[...] = self.inbox[0].astype(F32)

        def collect(step):
            copy = self.far_copy(step)
            copy.wait_recv()
            copy.wait_send()
            self.out[...] += self.inbox[step].astype(F32)

        self.chips.loop(collect)


def push_scratch(chips, rows, width):
    sem = pltpu.SemaphoreType.DMA
    return [pltpu.VMEM((chips, rows, width), BF16), sem((chips,)), sem((chips,)), sem((1,))]


def exchange_scratch(chips, rows, width):
    sem = pltpu.SemaphoreType.DMA
    return [pltpu.VMEM((chips, rows, width), BF16)] * 3 + [
        sem((1,)),
        sem((1,)),
        sem((chips,)),
        sem((chips,)),
        sem((1,)),
    ]


def fwd_kernel(grouped, alias_count, sizes, offset, *refs):
    lens_ref, x_ref, vec_ref = refs[:3]
    sources = refs[3:10]
    refs = refs[10 + alias_count :]
    gather = None
    if sizes:
        gather = Gather(Chips(*sizes), refs[0], refs[17], refs[-5:])
        refs = refs[1:17] + refs[18:-5]
    (
        q_ref,
        k_ref,
        v_ref,
        att_ref,
        ctx_ref,
        n1_ref,
        r1_ref,
        first_ref,
        act_ref,
        slope_ref,
        n2_ref,
        r2_ref,
        final_ref,
        unit_ref,
        uinv_ref,
        embed_ref,
    ) = refs[:16]
    wq, wk, wv, wo, wi, w2, wl, sem, acc_ref, att_buf, act_buf, slope_buf, out_sem = refs[16:]
    loader = Loader(sources, (wq, wk, wv, wo, wi, w2, wl), sem)
    block_id = pl.program_id(0)
    loader.start()
    if gather:
        last = pl.program_id(0) == pl.num_programs(0) - 1
        pl.when(loader.first)(gather.start)
    rows = x_ref.shape[0]
    x = x_ref[...]
    scale = HEAD_DIM ** (-0.5)
    loader.need(0)
    q_ref[...] = ((mm(x, wq[...]) + vec_row(vec_ref, ROW_BQ)).astype(BF16) * scale).astype(BF16)
    loader.need(1)
    k_ref[...] = mm(x, wk[...]).astype(BF16)
    loader.need(2)
    v_ref[...] = (mm(x, wv[...]) + vec_row(vec_ref, ROW_BV)).astype(BF16)
    if grouped:
        valid = (
            lax.broadcasted_iota(jnp.int32, (rows, rows), 0) // grouped
            == lax.broadcasted_iota(jnp.int32, (rows, rows), 1) // grouped
        )
    else:
        length = lens_ref[pl.program_id(0)]
        valid = lax.broadcasted_iota(jnp.int32, (1, rows), 1) < length
    bias = jnp.where(valid, 0.0, MASKED)
    low_half = lax.broadcasted_iota(jnp.int32, (rows, 128), 1) < HEAD_DIM

    def att_copy(pair):
        slot = lax.rem(pair, 2)
        return pltpu.make_async_copy(
            att_buf.at[slot], att_ref.at[block_id, pl.ds(2 * pair, 2)], out_sem.at[slot]
        )

    def pair_body(pair, carry):
        cols = pl.ds(pl.multiple_of(pair * 128, 128), 128)
        slot = lax.rem(pair, 2)
        pl.when(pair >= 2)(lambda: att_copy(pair - 2).wait())
        q_pair, k_pair, v_pair = q_ref[:, cols], k_ref[:, cols], v_ref[:, cols]
        parts = []
        for half in range(2):
            mask = low_half if half == 0 else jnp.logical_not(low_half)
            logits = mm(jnp.where(mask, q_pair, jnp.zeros_like(q_pair)), k_pair, NT) + bias
            peak = jnp.max(logits, axis=-1, keepdims=True)
            e = jnp.exp(logits - peak)
            inv = 1.0 / jnp.sum(e, axis=-1, keepdims=True)
            low = (e * inv).astype(BF16)
            att_buf[slot, half] = low
            parts.append(mm(low, v_pair))
        att_copy(pair).start()
        ctx_ref[:, cols] = jnp.where(low_half, parts[0], parts[1]).astype(BF16)
        return carry

    lax.fori_loop(0, HEADS // 2, pair_body, 0)
    if gather:
        pl.when(last)(gather.forward)
    loader.need(3)
    field = x.astype(F32) + (mm(ctx_ref[...], wo[...]) + vec_row(vec_ref, ROW_BO))
    center = field - mean_row(field)
    inverse = lax.rsqrt(mean_row(center * center) + LAYER_EPS)
    normed = center * inverse
    n1_ref[...] = normed.astype(BF16)
    r1_ref[...] = jnp.broadcast_to(inverse, r1_ref.shape)
    first = normed * vec_row(vec_ref, ROW_G1) + vec_row(vec_ref, ROW_S1)
    first_ref[...] = first.astype(BF16)
    acc_ref[...] = first + vec_row(vec_ref, ROW_B2)
    loader.need(4, 5)
    width = x.shape[1]

    base = block_id * rows if offset is None else offset

    def chunk_copies(chunk):
        slot = lax.rem(chunk, 2)
        cols = pl.ds(pl.multiple_of(chunk * width, width), width)
        return (
            pltpu.make_async_copy(
                act_buf.at[slot], act_ref.at[pl.ds(base, rows), cols], out_sem.at[2 + slot]
            ),
            pltpu.make_async_copy(
                slope_buf.at[slot],
                slope_ref.at[pl.ds(block_id * rows, rows), cols],
                out_sem.at[4 + slot],
            ),
        )

    def chunk_body(chunk, carry):
        cols = pl.ds(pl.multiple_of(chunk * width, width), width)
        slot = lax.rem(chunk, 2)

        @pl.when(chunk >= 2)
        def _():
            for copy in chunk_copies(chunk - 2):
                copy.wait()

        inner = mm(first_ref[...], wi[:, cols]) + vec_ref[pl.ds(ROW_BI + chunk, 1), :]
        phi = 0.5 * (1.0 + lax.erf(inner * ROOT_HALF))
        activated = (inner * phi).astype(BF16)
        act_buf[slot] = activated
        slope_buf[slot] = (phi + inner * jnp.exp(-0.5 * inner * inner) * SLOPE_CONST).astype(BF16)
        for copy in chunk_copies(chunk):
            copy.start()
        acc_ref[...] += mm(activated, w2[cols, :])
        return carry

    chunks = wi.shape[1] // width
    lax.fori_loop(0, chunks, chunk_body, 0)
    field = acc_ref[...]
    center = field - mean_row(field)
    inverse = lax.rsqrt(mean_row(center * center) + LAYER_EPS)
    normed = center * inverse
    n2_ref[...] = normed.astype(BF16)
    r2_ref[...] = jnp.broadcast_to(inverse, r2_ref.shape)
    final = (normed * vec_row(vec_ref, ROW_G2) + vec_row(vec_ref, ROW_S2)).astype(BF16)
    final_ref[...] = final
    loader.need(6)
    projected = mm(final, wl[...])
    uinv = lax.rsqrt(jnp.sum(projected * projected, axis=-1, keepdims=True) + NORM_EPS)
    unit = projected * uinv
    unit_ref[...] = unit
    uinv_ref[...] = jnp.broadcast_to(uinv, uinv_ref.shape)
    embed_ref[...] = unit.astype(BF16)
    for back in (2, 1):
        att_copy(HEADS // 2 - back).wait()
        for copy in chunk_copies(chunks - back):
            copy.wait()
    if gather:
        pl.when(last)(gather.finish)


def encode(x, lens, vec, weights, blocks, grouped, total, offset, earlier, sizes):
    rows = x.shape[0] // blocks
    width = x.shape[1]
    wide = weights[4].shape[1]
    embed_width = weights[6].shape[1]
    base = offset // rows

    def row_spec(columns):
        return pl.BlockSpec((rows, columns), lambda i, lens: (base + i, 0))

    def own_spec(columns):
        return pl.BlockSpec((rows, columns), lambda i, lens: (i, 0))

    def shape(count, columns, dtype):
        return jax.ShapeDtypeStruct((count, columns), dtype)

    own = x.shape[0]
    out_shapes = [
        shape(own, width, BF16),
        shape(own, width, BF16),
        shape(own, width, BF16),
        jax.ShapeDtypeStruct((blocks, HEADS, rows, rows), BF16),
        shape(total, width, BF16),
        shape(own, width, BF16),
        shape(own, embed_width, F32),
        shape(total, width, BF16),
        shape(total, wide, BF16),
        shape(own, wide, BF16),
        shape(own, width, BF16),
        shape(own, embed_width, F32),
        shape(total, width, BF16),
        shape(own, embed_width, F32),
        shape(own, embed_width, F32),
        shape(own, embed_width, BF16),
    ]
    shared = (4, 7, 8, 12)
    out_specs = [
        ANY
        if index in (3, 8, 9)
        else (row_spec if index in shared else own_spec)(out.shape[1])
        for index, out in enumerate(out_shapes)
    ]
    aliased = [] if earlier is None else [earlier[index] for index in shared]
    sends, sem_shapes, params = [], [], {}
    if sizes:
        sends = [earlier[15]]
        chips = sizes[0] * sizes[1] // 2
        out_shapes.append(jax.ShapeDtypeStruct((chips, 2) + earlier[15].shape, BF16))
        out_specs.append(ANY)
        sem = pltpu.SemaphoreType.DMA
        sem_shapes = [sem((chips,)), sem((chips,)), sem((1,)), sem((1,)), sem((1,))]
        params = {"collective_id": 4, "has_side_effects": True}
    return pl.pallas_call(
        functools.partial(fwd_kernel, grouped, len(aliased), sizes, offset if blocks == 1 else None),
        out_shape=out_shapes,
        grid_spec=pltpu.PrefetchScalarGridSpec(
            num_scalar_prefetch=1,
            grid=(blocks,),
            in_specs=[
                own_spec(width),
                pl.BlockSpec(vec.shape, lambda i, lens: (0, 0)),
            ]
            + [ANY] * (7 + len(aliased) + len(sends)),
            out_specs=out_specs,
            scratch_shapes=[pltpu.VMEM(weight.shape, BF16) for weight in weights]
            + [
                pltpu.SemaphoreType.DMA((7,)),
                pltpu.VMEM((rows, width), F32),
                pltpu.VMEM((2, 2, rows, rows), BF16),
                pltpu.VMEM((2, rows, width), BF16),
                pltpu.VMEM((2, rows, width), BF16),
                pltpu.SemaphoreType.DMA((6,)),
            ]
            + sem_shapes,
        ),
        input_output_aliases={10 + index: shared[index] for index in range(len(aliased))},
        compiler_params=pltpu.CompilerParams(vmem_limit_bytes=VMEM_LIMIT, **params),
        name="encode_queries" if grouped else "encode_passages",
    )(lens, x, vec, *weights, *aliased, *sends)


def sims_kernel(lens_ref, q_ref, p_ref, e_ref, z_ref):
    count = q_ref.shape[0]
    tokens = count * q_ref.shape[2]
    query = q_ref[...].reshape(tokens, q_ref.shape[3])
    sims = mm(p_ref[0], query, NT)
    slot = lax.broadcasted_iota(jnp.int32, sims.shape, 0)
    e = jnp.where(slot < lens_ref[pl.program_id(0)], jnp.exp(SHARP * sims - SHARP), 0.0)
    e_ref[0] = e.astype(BF16)
    z = jnp.sum(e, axis=0, keepdims=True)
    step = q_ref.shape[2]
    for index in range(count):
        z_ref[0, index : index + 1, :] = z[:, index * step : (index + 1) * step]


def sims_back_kernel(e_ref, w_ref, q_ref, p_ref, gp_ref, gq_ref):
    count = q_ref.shape[0]
    step = q_ref.shape[2]
    query = q_ref[...].reshape(count * step, q_ref.shape[3])
    weight = jnp.concatenate([w_ref[0, index : index + 1, :] for index in range(count)], axis=1)
    grads = (e_ref[0].astype(F32) * weight).astype(BF16)
    part = mm(grads, query)

    @pl.when(pl.program_id(1) == 0)
    def _():
        gp_ref[0] = part

    @pl.when(pl.program_id(1) > 0)
    def _():
        gp_ref[0] += part

    gq_ref[...] = mm(grads, p_ref[0], TN).astype(BF16).reshape(gq_ref.shape)


def similarity(queries, passages, lens):
    devices, micro, tokens, width = queries.shape
    slots = passages.shape[1]
    group = 8
    e, z = pl.pallas_call(
        sims_kernel,
        out_shape=(
            jax.ShapeDtypeStruct((micro, slots, devices * tokens), BF16),
            jax.ShapeDtypeStruct((micro, devices, tokens), F32),
        ),
        grid_spec=pltpu.PrefetchScalarGridSpec(
            num_scalar_prefetch=1,
            grid=(micro, devices // group),
            in_specs=[
                pl.BlockSpec((group, 1, tokens, width), lambda m, b, lens: (b, m, 0, 0)),
                pl.BlockSpec((1, slots, width), lambda m, b, lens: (m, 0, 0)),
            ],
            out_specs=(
                pl.BlockSpec((1, slots, group * tokens), lambda m, b, lens: (m, 0, b)),
                pl.BlockSpec((1, group, tokens), lambda m, b, lens: (m, b, 0)),
            ),
        ),
        compiler_params=pltpu.CompilerParams(vmem_limit_bytes=VMEM_LIMIT),
        name="similarity",
    )(lens, queries, passages)
    return e, z


def similarity_back(e, weights, queries, passages):
    devices, micro, tokens, width = queries.shape
    slots = passages.shape[1]
    group = 8
    return pl.pallas_call(
        sims_back_kernel,
        out_shape=(
            jax.ShapeDtypeStruct((micro, slots, width), F32),
            jax.ShapeDtypeStruct((devices, micro, tokens, width), BF16),
        ),
        grid=(micro, devices // group),
        in_specs=[
            pl.BlockSpec((1, slots, group * tokens), lambda m, b: (m, 0, b)),
            pl.BlockSpec((1, group, tokens), lambda m, b: (m, b, 0)),
            pl.BlockSpec((group, 1, tokens, width), lambda m, b: (b, m, 0, 0)),
            pl.BlockSpec((1, slots, width), lambda m, b: (m, 0, 0)),
        ],
        out_specs=(
            pl.BlockSpec((1, slots, width), lambda m, b: (m, 0, 0)),
            pl.BlockSpec((group, 1, tokens, width), lambda m, b: (b, m, 0, 0)),
        ),
        compiler_params=pltpu.CompilerParams(vmem_limit_bytes=VMEM_LIMIT),
        name="similarity_back",
    )(e, weights, queries, passages)


def match_kernel(n_wide, n_narrow, group, query_len, *refs):
    lens_ref, q_ref, p_ref, pos_ref = refs[:4]
    all_ref, loss_ref, gp_ref, half_ref = refs[4:8]
    e_buf, z_buf, own_buf, grad_buf, near, share_send, share_recv, pair_send, pair_recv = refs[8:]
    devices, micro, tokens, width = q_ref.shape
    chips = Chips(n_wide, n_narrow)
    me = chips.narrow * n_wide + chips.wide
    share_sems, pair_sems = (share_send, share_recv), (pair_send, pair_recv)
    pairs = group // 2

    def device(index):
        return (lax.rem(index, n_wide), index // n_wide)

    def each(body):
        def step_body(step, carry):
            body(step)
            return carry

        lax.fori_loop(1, devices, step_body, 0)

    barrier = pltpu.get_barrier_semaphore()
    each(
        lambda step: pl.semaphore_signal(
            barrier, inc=1, device_id=device(lax.rem(me + step, devices)), device_id_type=MESH
        )
    )

    def query_rows(block, m):
        at = pl.ds(block * group, group)
        return q_ref[at, m].reshape(group * tokens, width)

    def forward(block, carry):
        for m in range(micro):
            sims = mm(p_ref[m], query_rows(block, m), NT)
            slot = lax.broadcasted_iota(jnp.int32, sims.shape, 0)
            e = jnp.where(slot < lens_ref[m], jnp.exp(SHARP * sims - SHARP), 0.0)
            e_buf[m, block] = e.astype(BF16)
            z = jnp.sum(e, axis=0, keepdims=True)
            for index in range(group):
                z_buf[m, pl.ds(block * group + index, 1)] = z[
                    :, index * tokens : (index + 1) * tokens
                ]
        return carry

    lax.fori_loop(0, devices // group, forward, 0)
    pl.semaphore_wait(barrier, devices - 1)
    best = SHARP + jnp.log(z_buf[...].reshape(micro * devices, tokens))
    member = (
        lax.broadcasted_iota(jnp.int32, (8, tokens), 0)
        == lax.broadcasted_iota(jnp.int32, (8, tokens), 1) // query_len
    ).astype(F32)
    own = (
        lax.dot_general(
            member, best, NT, precision=lax.Precision.HIGHEST, preferred_element_type=F32
        )
        / SHARP
    )
    own_buf[...] = own
    all_ref[me] = own

    def share(step, source):
        target = device(lax.rem(me + step, devices))
        return remote(own_buf, all_ref.at[source], share_sems, step, target)

    each(lambda step: share(step, me).start())
    each(lambda step: share(step, lax.rem(me - step + devices, devices)).wait_recv())
    each(lambda step: share(step, me).wait_send())
    full = all_ref[...]
    peak = jnp.max(full, axis=0)
    total = peak + jnp.log(jnp.sum(jnp.exp(full - peak[None]), axis=0))
    positive = pos_ref[...]
    passage = lax.broadcasted_iota(jnp.int32, full.shape, 0)
    picked = jnp.sum(jnp.where(passage == positive[None], full, 0.0), axis=0)
    loss_ref[...] = total - picked
    grads = jnp.exp(own - total) - (positive == me).astype(F32)
    spread = lax.dot_general(
        grads, member, TN, precision=lax.Precision.HIGHEST, preferred_element_type=F32
    )
    z_buf[...] = (spread / z_buf[...].reshape(micro * devices, tokens)).reshape(z_buf.shape)
    gp_ref[...] = jnp.zeros_like(gp_ref)

    def pair_copy(block):
        at = pl.ds(block * pairs, pairs)
        return remote(
            grad_buf.at[at, 1 - chips.core], near.at[at], pair_sems, block, chips.mate
        )

    def backward(block, carry):
        for m in range(micro):
            weight = jnp.concatenate(
                [z_buf[m, pl.ds(block * group + index, 1)] for index in range(group)], axis=1
            )
            grads = (e_buf[m, block].astype(F32) * weight).astype(BF16)
            gp_ref[m] += mm(grads, query_rows(block, m))
            part = mm(grads, p_ref[m], TN).astype(BF16)
            for index in range(group):
                grad_buf[block * pairs + index // 2, index % 2, m * tokens : (m + 1) * tokens] = (
                    part[index * tokens : (index + 1) * tokens]
                )
        pair_copy(block).start()
        return carry

    lax.fori_loop(0, devices // group, backward, 0)

    def join(block, carry):
        copy = pair_copy(block)
        copy.wait_recv()
        copy.wait_send()
        at = pl.ds(block * pairs, pairs)
        half_ref[at] = (
            grad_buf[at, chips.core].astype(F32) + near[at].astype(F32)
        ).astype(BF16)
        return carry

    lax.fori_loop(0, devices // group, join, 0)


def match(queries, passages, lens, positives, n_wide, n_narrow, query_len):
    devices, micro, tokens, width = queries.shape
    slots = passages.shape[1]
    group = 8
    own = tokens // query_len
    placed = positives.reshape(micro, devices, own).transpose(2, 0, 1).reshape(own, -1)
    placed = jnp.pad(placed, ((0, 8 - own), (0, 0)))
    sem = pltpu.SemaphoreType.DMA
    vmem = pl.BlockSpec(memory_space=pltpu.VMEM)
    columns = micro * devices
    return pl.pallas_call(
        functools.partial(match_kernel, n_wide, n_narrow, group, query_len),
        out_shape=(
            jax.ShapeDtypeStruct((devices, 8, columns), F32),
            jax.ShapeDtypeStruct((8, columns), F32),
            jax.ShapeDtypeStruct((micro, slots, width), F32),
            jax.ShapeDtypeStruct((devices // 2, micro * tokens, width), BF16),
        ),
        in_specs=[pl.BlockSpec(memory_space=pltpu.SMEM), vmem, vmem, vmem],
        out_specs=(vmem,) * 4,
        scratch_shapes=[
            pltpu.VMEM((micro, devices // group, slots, group * tokens), BF16),
            pltpu.VMEM((micro, devices, tokens), F32),
            pltpu.VMEM((8, columns), F32),
            pltpu.VMEM((devices // 2, 2, micro * tokens, width), BF16),
            pltpu.VMEM((devices // 2, micro * tokens, width), BF16),
            sem((devices,)),
            sem((devices,)),
            sem((devices // group,)),
            sem((devices // group,)),
        ],
        compiler_params=pltpu.CompilerParams(
            collective_id=1, has_side_effects=True, vmem_limit_bytes=VMEM_LIMIT
        ),
        name="match",
    )(lens, queries, passages, placed)


def accumulate(ref, row, value):
    ref[row : row + 1, :] += jnp.sum(value, axis=0, keepdims=True)


def mlp_back_kernel(alias_count, sizes, *refs):
    (
        ge_ref,
        unit_ref,
        uinv_ref,
        n2_ref,
        r2_ref,
        slope_ref,
        n1_ref,
        r1_ref,
        vec_ref,
    ) = refs[:9]
    sources = refs[9:12]
    refs = refs[12 + alias_count :]
    swap = None
    if sizes:
        swap = Push(Chips(*sizes), refs[0], refs[7], refs[-4:])
        refs = refs[1:7] + refs[8:-4]
    gp_ref, go_ref, gi_ref, gh_ref, ga_ref, sums_ref = refs[:6]
    wl, w2, wi, sem, acc_ref = refs[6:]
    loader = Loader(sources, (wl, w2, wi), sem)
    loader.start()
    if swap:
        pl.when(loader.first)(swap.start)

    @pl.when(loader.first)
    def _():
        sums_ref[...] = jnp.zeros_like(sums_ref)

    grad = ge_ref[...]
    unit = unit_ref[...]
    projected_low = (
        uinv_ref[...] * (grad - unit * jnp.sum(grad * unit, axis=-1, keepdims=True))
    ).astype(BF16)
    gp_ref[...] = projected_low
    loader.need(0)
    grad_final = mm(projected_low, wl[...], NT)
    normed = n2_ref[...].astype(F32)
    accumulate(sums_ref, ROW_G2, grad_final * normed)
    accumulate(sums_ref, ROW_S2, grad_final)
    scaled = grad_final * vec_row(vec_ref, ROW_G2)
    grad_second = r2_ref[:, :1] * (scaled - mean_row(scaled) - normed * mean_row(scaled * normed))
    outer_low = grad_second.astype(BF16)
    go_ref[...] = outer_low
    accumulate(sums_ref, ROW_B2, outer_low.astype(F32))
    acc_ref[...] = grad_second
    loader.need(1, 2)
    width = go_ref.shape[1]

    def chunk_body(chunk, carry):
        cols = pl.ds(pl.multiple_of(chunk * width, width), width)
        grad_act = mm(go_ref[...], w2[cols, :], NT)
        inner = (grad_act * slope_ref[:, cols].astype(F32)).astype(BF16)
        gi_ref[:, cols] = inner
        sums_ref[pl.ds(ROW_BI + chunk, 1), :] += jnp.sum(
            inner.astype(F32), axis=0, keepdims=True
        )
        acc_ref[...] += mm(inner, wi[:, cols], NT)
        return carry

    lax.fori_loop(0, wi.shape[1] // width, chunk_body, 0)
    grad_first = acc_ref[...]
    normed = n1_ref[...].astype(F32)
    accumulate(sums_ref, ROW_G1, grad_first * normed)
    accumulate(sums_ref, ROW_S1, grad_first)
    scaled = grad_first * vec_row(vec_ref, ROW_G1)
    hidden = r1_ref[:, :1] * (scaled - mean_row(scaled) - normed * mean_row(scaled * normed))
    gh_ref[...] = hidden
    low = hidden.astype(BF16)
    ga_ref[...] = low
    accumulate(sums_ref, ROW_BO, low.astype(F32))
    if swap:
        pl.when(pl.program_id(0) == pl.num_programs(0) - 1)(swap.finish)


def mlp_back(grad_embed, kept, vec, weights, blocks, total, offset, earlier, sent, sizes):
    own = grad_embed.shape[0]
    rows = own // blocks
    base = offset // rows
    _, _, _, _, wi, w2, wl = weights
    width, wide = wi.shape
    embed_width = wl.shape[1]

    def row_spec(columns):
        return pl.BlockSpec((rows, columns), lambda i: (base + i, 0))

    def own_spec(columns):
        return pl.BlockSpec((rows, columns), lambda i: (i, 0))

    args = [grad_embed] + [kept[index] for index in (13, 14, 10, 11, 9, 5, 6)]
    out_shapes = [
        jax.ShapeDtypeStruct((total, embed_width), BF16),
        jax.ShapeDtypeStruct((total, width), BF16),
        jax.ShapeDtypeStruct((total, wide), BF16),
        jax.ShapeDtypeStruct((own, width), F32),
        jax.ShapeDtypeStruct((total, width), BF16),
        jax.ShapeDtypeStruct((16, width), F32),
    ]
    shared = (0, 1, 2, 4)
    out_specs = [
        (row_spec if index in shared else own_spec)(out.shape[1])
        for index, out in enumerate(out_shapes[:5])
    ] + [pl.BlockSpec((16, width), lambda i: (0, 0))]
    aliased = [] if earlier is None else [earlier[index] for index in shared]
    sends, scratch, params = [], [], {}
    if sizes:
        sends = [sent]
        out_shapes.append(jax.ShapeDtypeStruct(sent.shape[1:], F32))
        out_specs.append(pl.BlockSpec(sent.shape[1:], lambda i: (0, 0)))
        scratch = push_scratch(*sent.shape)
        params = {"collective_id": 5, "has_side_effects": True}
    return pl.pallas_call(
        functools.partial(mlp_back_kernel, len(aliased), sizes),
        out_shape=out_shapes,
        grid=(blocks,),
        in_specs=[own_spec(arg.shape[1]) for arg in args]
        + [pl.BlockSpec(vec.shape, lambda i: (0, 0))]
        + [ANY] * (3 + len(aliased) + len(sends)),
        out_specs=out_specs,
        scratch_shapes=[pltpu.VMEM(weight.shape, BF16) for weight in (wl, w2, wi)]
        + [pltpu.SemaphoreType.DMA((3,)), pltpu.VMEM((rows, width), F32)]
        + scratch,
        input_output_aliases={12 + index: shared[index] for index in range(len(aliased))},
        compiler_params=pltpu.CompilerParams(vmem_limit_bytes=VMEM_LIMIT, **params),
        name="mlp_back_queries" if earlier is not None else "mlp_back_passages",
    )(*args, vec, wl, w2, wi, *aliased, *sends)


def attention_back_kernel(alias_count, *refs):
    ga_ref, gh_ref, att_ref, q_ref, k_ref, v_ref = refs[:6]
    sources = refs[6:10]
    refs = refs[10 + alias_count :]
    gqkv_ref, gx_ref, sums_ref = refs[:3]
    wo, wq, wk, wv, sem, gc_ref = refs[3:]
    loader = Loader(sources, (wo, wq, wk, wv), sem)
    loader.start()

    @pl.when(loader.first)
    def _():
        sums_ref[...] = jnp.zeros_like(sums_ref)

    rows, width = gh_ref.shape
    scale = HEAD_DIM ** (-0.5)
    loader.need(0)
    gc_ref[...] = mm(ga_ref[...], wo[...], NT).astype(BF16)
    low_half = lax.broadcasted_iota(jnp.int32, (rows, 128), 1) < HEAD_DIM

    def pair_body(pair, carry):
        cols = pl.ds(pl.multiple_of(pair * 128, 128), 128)
        q_pair, k_pair, v_pair, gc_pair = q_ref[:, cols], k_ref[:, cols], v_ref[:, cols], gc_ref[:, cols]
        parts = []
        for half in range(2):
            mask = low_half if half == 0 else jnp.logical_not(low_half)
            low = att_ref[0, 2 * pair + half]
            att = low.astype(F32)
            grad_att = mm(jnp.where(mask, gc_pair, jnp.zeros_like(gc_pair)), v_pair, NT)
            weighted = grad_att * att
            grad_logits = (weighted - att * jnp.sum(weighted, axis=-1, keepdims=True)).astype(BF16)
            parts.append(
                (
                    mm(grad_logits, k_pair) * scale,
                    mm(grad_logits, q_pair, TN),
                    mm(low, gc_pair, TN),
                )
            )
        for index in range(3):
            gqkv_ref[:, pl.ds(pl.multiple_of(index * width + pair * 128, 128), 128)] = jnp.where(
                low_half, parts[0][index], parts[1][index]
            ).astype(BF16)
        return carry

    lax.fori_loop(0, HEADS // 2, pair_body, 0)
    loader.need(1, 2, 3)
    grad_q, grad_k, grad_v = (
        gqkv_ref[:, :width],
        gqkv_ref[:, width : 2 * width],
        gqkv_ref[:, 2 * width :],
    )
    accumulate(sums_ref, 0, grad_q.astype(F32))
    accumulate(sums_ref, 1, grad_v.astype(F32))
    gx_ref[...] = (
        gh_ref[...]
        + mm(grad_q, wq[...], NT)
        + mm(grad_k, wk[...], NT)
        + mm(grad_v, wv[...], NT)
    )


def attention_back(attended, hidden, kept, weights, blocks, total, offset, earlier):
    own, width = hidden.shape
    rows = own // blocks
    base = offset // rows
    wq, wk, wv, wo = weights[:4]

    def row_spec(columns):
        return pl.BlockSpec((rows, columns), lambda i: (base + i, 0))

    def own_spec(columns):
        return pl.BlockSpec((rows, columns), lambda i: (i, 0))

    aliased = [] if earlier is None else [earlier]
    return pl.pallas_call(
        functools.partial(attention_back_kernel, len(aliased)),
        out_shape=(
            jax.ShapeDtypeStruct((total, 3 * width), BF16),
            jax.ShapeDtypeStruct((own, width), F32),
            jax.ShapeDtypeStruct((8, width), F32),
        ),
        grid=(blocks,),
        in_specs=[
            row_spec(width),
            own_spec(width),
            pl.BlockSpec((1, HEADS, rows, rows), lambda i: (i, 0, 0, 0)),
            own_spec(width),
            own_spec(width),
            own_spec(width),
        ]
        + [ANY] * (4 + len(aliased)),
        out_specs=(
            row_spec(3 * width),
            own_spec(width),
            pl.BlockSpec((8, width), lambda i: (0, 0)),
        ),
        scratch_shapes=[pltpu.VMEM(weight.shape, BF16) for weight in weights[:4]]
        + [pltpu.SemaphoreType.DMA((4,)), pltpu.VMEM((rows, width), BF16)],
        input_output_aliases={10: 0} if aliased else {},
        compiler_params=pltpu.CompilerParams(vmem_limit_bytes=VMEM_LIMIT),
        name="attention_back_queries" if aliased else "attention_back_passages",
    )(attended, hidden, kept[3], kept[0], kept[1], kept[2], wo, wq, wk, wv, *aliased)


def pack(vectors, width):
    count = sum(vector.shape[0] for vector in vectors)
    total = -(-count // (8 * width)) * 8 * width
    start, packed = 0, 0.0
    for vector in vectors:
        size = vector.shape[0]
        packed = packed + jnp.pad(vector.astype(F32), (start, total - start - size))
        start += size
    return packed.reshape(-1, width)


def share_kernel(n_wide, n_narrow, own_ref, all_ref, send_sem, recv_sem):
    me = lax.axis_index("narrow") * n_wide + lax.axis_index("wide")
    total = n_wide * n_narrow
    sems = (send_sem, recv_sem)

    def device(index):
        return (lax.rem(index, n_wide), index // n_wide)

    barrier = pltpu.get_barrier_semaphore()

    def signal(step, carry):
        pl.semaphore_signal(
            barrier, inc=1, device_id=device(lax.rem(me + step, total)), device_id_type=MESH
        )
        return carry

    def send(step, carry):
        target = device(lax.rem(me + step, total))
        remote(own_ref, all_ref.at[me], sems, step, target).start()
        return carry

    def wait(step, carry):
        source = lax.rem(me - step + total, total)
        copy = remote(own_ref, all_ref.at[source], sems, step, device(source))
        copy.wait_recv()
        copy.wait_send()
        return carry

    lax.fori_loop(1, total, signal, 0)
    all_ref[me] = own_ref[...]
    pl.semaphore_wait(barrier, total - 1)
    lax.fori_loop(1, total, send, 0)
    lax.fori_loop(1, total, wait, 0)


def share_scores(own, n_wide, n_narrow):
    total = n_wide * n_narrow
    return pl.pallas_call(
        functools.partial(share_kernel, n_wide, n_narrow),
        out_shape=jax.ShapeDtypeStruct((total,) + own.shape, own.dtype),
        in_specs=[pl.BlockSpec(memory_space=pltpu.VMEM)],
        out_specs=pl.BlockSpec(memory_space=pltpu.VMEM),
        scratch_shapes=[pltpu.SemaphoreType.DMA((total,))] * 2,
        compiler_params=pltpu.CompilerParams(collective_id=1, has_side_effects=True),
        name="share_scores",
    )(own)


def exchange_kernel(n_wide, n_narrow, g_ref, out_ref, *scratch):
    swap = Exchange(Chips(n_wide, n_narrow), g_ref, out_ref, scratch)
    swap.start()
    swap.push()
    swap.finish()


def exchange(grads, n_wide, n_narrow):
    chips, _, rows, width = grads.shape
    return pl.pallas_call(
        functools.partial(exchange_kernel, n_wide, n_narrow),
        out_shape=jax.ShapeDtypeStruct((rows, width), F32),
        in_specs=[ANY],
        out_specs=pl.BlockSpec(memory_space=pltpu.VMEM),
        scratch_shapes=exchange_scratch(chips, rows, width),
        compiler_params=pltpu.CompilerParams(
            collective_id=2, has_side_effects=True, vmem_limit_bytes=VMEM_LIMIT
        ),
        name="exchange_query_gradients",
    )(grads)


UNITS = (
    (0, 48, 0),
    (48, 48, 0),
    (96, 48, 48),
    (144, 48, 48),
    (192, 16, 96),
    (240, 16, 96),
    (208, 16, 112),
    (256, 16, 112),
    (224, 16, 128),
    (272, 32, 128),
)
EARLY = (0, 1, 2, 3)
LATE = (4, 5, 6, 7, 8, 9)
SHARE_ROWS = 304
LATE_B = 240
ROWS_A, ROWS_B = 144, 160
TILES = 9


def tail_kernel(n_z, part, *refs):
    act, go, first, gi, x_p, x_q, ctx, ga, final, gp = refs[:10]
    kept = (refs[10:15], refs[15:20])
    sources = refs[20:24]
    sums = refs[24:26]
    out_ref, gx_p, gx_q = refs[26:29]
    both, near, over_a, over_b, then_a, then_b, line, left_buf, right_buf, thin_buf = refs[29:39]
    wo, wq, wk, wv, att_buf, hidden, thin_hidden, grads, att_sums = refs[39:48]
    load_sem, weight_sem, block_sem, att_sem, gx_sem = refs[48:53]
    core_sems, one_sems, two_sems, line_sems, copy_sems = (
        refs[53 + 2 * index : 55 + 2 * index] for index in range(5)
    )
    wide, narrow = lax.axis_index("wide"), lax.axis_index("narrow")
    z, x = wide // 2, lax.rem(wide, 2)
    y, core = narrow // 2, lax.rem(narrow, 2)
    mate = (wide, y * 2 + 1 - core)
    over_y = (wide, (1 - y) * 2 + core)
    over_x = (z * 2 + 1 - x, narrow)
    total, width = go.shape
    p_rows = x_p.shape[0]
    held = both.at[core]

    def load(tile, wait):
        slot = lax.rem(tile, 2)
        block = pl.ds(pl.multiple_of(lax.rem(tile, 4) * width, width), width)

        def pair(source, other, target):
            for made in (
                pltpu.make_async_copy(source, left_buf.at[slot], load_sem.at[slot, 0]),
                pltpu.make_async_copy(other, target, load_sem.at[slot, 1]),
            ):
                if wait:
                    made.wait()
                else:
                    made.start()

        place = right_buf.at[slot]
        pl.when(tile < 4)(lambda: pair(act.at[:, block], go, place))
        pl.when(jnp.logical_and(tile >= 4, tile < 8))(lambda: pair(first, gi.at[:, block], place))
        pl.when(tile == 8)(lambda: pair(ctx, ga, place))
        pl.when(tile == TILES)(lambda: pair(final, gp, thin_buf))

    def rows_of(unit):
        start, count, _ = UNITS[unit]
        return pl.ds(start, count)

    def place_of(unit):
        _, count, place = UNITS[unit]
        return pl.ds(place, count)

    def core_copy(unit):
        rows = rows_of(unit)
        return remote(
            both.at[1 - core, :, :, :, rows], near.at[:, :, :, rows], core_sems, unit, mate
        )

    def late_copy(index):
        row_y, start, count = ((0, 2 * part, part + 16), (1, LATE_B, 64), (1, 2 * part, 48))[index]
        rows = pl.ds(start, count)
        return remote(
            both.at[1 - core, row_y, :, :, rows],
            near.at[row_y, :, :, rows],
            core_sems,
            len(EARLY) + index,
            mate,
        )

    def one_copy(unit):
        rows = rows_of(unit)
        place = place_of(unit)
        if unit % 2 == 0:
            return remote(
                held.at[1 - y, :, :, rows],
                over_a.at[:, :, place],
                one_sems,
                unit,
                over_y,
            )
        return remote(
            held.at[:, :, 1 - x, rows],
            over_b.at[:, :, place],
            one_sems,
            unit,
            over_x,
        )

    def two_copy(unit):
        rows = rows_of(unit)
        place = place_of(unit)
        if unit % 2 == 0:
            return remote(
                held.at[y, :, 1 - x, rows],
                then_a.at[:, place],
                two_sems,
                unit,
                over_x,
            )
        return remote(
            held.at[1 - y, :, x, rows],
            then_b.at[:, place],
            two_sems,
            unit,
            over_y,
        )

    def far_copy(unit, step):
        rows = rows_of(unit)
        target = lax.rem(z + step, n_z)
        return remote(
            held.at[y, target, x, rows],
            line.at[step - 1, rows],
            line_sems,
            unit * n_z + step,
            (target * 2 + x, narrow),
        )

    def share_copy(unit, step, arriving):
        rows = rows_of(unit)
        slots = (
            (y * 2 + 1 - core, (1 - y) * 2 + core, (1 - y) * 2 + 1 - core)
            if arriving
            else (narrow, narrow, (1 - y) * 2 + core)
        )
        block = out_ref.at[slots[step], rows]
        return remote(block, block, copy_sems, unit * 3 + step, over_y if step == 1 else mate)

    def add(target, extra):
        target[...] = target[...] + extra[...]

    def start_core(unit):
        core_copy(unit).start()

    def start_one(unit):
        rows = rows_of(unit)
        if unit in EARLY:
            core_copy(unit).wait_recv()

        def body(index, carry):
            row_y, rest = index // (n_z * 2), lax.rem(index, n_z * 2)
            at = (row_y, rest // 2, lax.rem(rest, 2), rows)
            add(held.at[at], near.at[at])
            return carry

        lax.fori_loop(0, 4 * n_z, body, 0)
        one_copy(unit).start()

    def start_two(unit):
        rows = rows_of(unit)
        place = place_of(unit)
        one_copy(unit).wait_recv()

        def body(index, carry):
            outer_at, inner_at = index // 2, lax.rem(index, 2)
            if unit % 2 == 0:
                add(
                    held.at[y, outer_at, inner_at, rows],
                    over_a.at[outer_at, inner_at, place],
                )
            else:
                add(
                    held.at[inner_at, outer_at, x, rows],
                    over_b.at[inner_at, outer_at, place],
                )
            return carry

        lax.fori_loop(0, 2 * n_z, body, 0)
        two_copy(unit).start()

    def start_far(unit):
        rows = rows_of(unit)
        place = place_of(unit)
        extra = then_a if unit % 2 == 0 else then_b
        two_copy(unit).wait_recv()

        def body(index, carry):
            add(held.at[y, index, x, rows], extra.at[index, place])
            return carry

        lax.fori_loop(0, n_z, body, 0)
        for step in range(1, n_z):
            far_copy(unit, step).start()

    def start_share(unit):
        rows = rows_of(unit)
        for step in range(1, n_z):
            far_copy(unit, step).wait_recv()
            add(held.at[y, z, x, rows], line.at[step - 1, rows])
        out_ref[narrow, rows] = both[core, y, z, x, rows]
        share_copy(unit, 1, False).start()
        share_copy(unit, 0, False).start()

    def forward(unit):
        share_copy(unit, 1, True).wait_recv()
        share_copy(unit, 2, False).start()

    def finish(unit):
        share_copy(unit, 0, True).wait_recv()
        share_copy(unit, 2, True).wait_recv()
        for step in range(3):
            share_copy(unit, step, False).wait_send()
        if unit in EARLY:
            core_copy(unit).wait_send()
        one_copy(unit).wait_send()
        two_copy(unit).wait_send()
        for step in range(1, n_z):
            far_copy(unit, step).wait_send()

    barrier = pltpu.get_barrier_semaphore()
    load(0, False)
    partners = [mate, over_y, over_x] + [
        (lax.rem(z + step, n_z) * 2 + x, narrow) for step in range(1, n_z)
    ]
    for device in partners:
        pl.semaphore_signal(barrier, inc=1, device_id=device, device_id_type=MESH)
    pl.semaphore_wait(barrier, len(partners))

    def put(kind, owner, half, made):
        rows = pl.ds(pl.multiple_of(kind * part, part), part)
        for index in range(4):
            both[lax.rem(owner, 2), owner // 2, 2 * half + index // 2, index % 2, rows] = made[
                index * part : (index + 1) * part
            ]

    def halves(left_ref, right_ref, store):
        def half_body(half, carry):
            cols = pl.ds(pl.multiple_of(half * 4 * part, 4 * part), 4 * part)
            store(half, mm(left_ref[:, cols], right_ref[...], TN).astype(BF16))
            return carry

        lax.fori_loop(0, 2, half_body, 0)

    def hooks(now, plan):
        for at, step, units in plan:

            @pl.when(now == at)
            def _(step=step, units=units):
                for unit in units:
                    step(unit)

    def tile_body(tile, carry):
        slot = lax.rem(tile, 2)
        load(tile, True)
        load(tile + 1, False)
        kind = tile // 4
        owner = jnp.where(tile == 8, 3, lax.rem(tile, 4))

        def store(half, made):
            @pl.when(kind == 0)
            def _():
                for index in range(4):
                    both[index % 2, index // 2, owner, half, :part] = made[
                        index * part : (index + 1) * part
                    ]

            pl.when(kind > 0)(lambda: put(kind, owner, half, made))

        halves(left_buf.at[slot], right_buf.at[slot], store)
        hooks(
            tile,
            (
                (3, start_core, (0, 1)),
                (5, start_one, (0,)),
                (6, start_one, (1,)),
                (7, start_core, (2, 3)),
            ),
        )
        return carry

    def hidden_of(block):
        return thin_hidden if blocks[block][2] else hidden.at[block]

    def block_copies(block):
        rows, base, source = blocks[block]
        q, k, v, gh, _ = kept[source]
        buf = left_buf if block % 2 == 0 else right_buf
        own = pl.ds(base - (p_rows if source else 0), rows)
        low, high = pl.ds(0, rows), pl.ds(span, rows)
        pairs = (
            (q.at[own], buf.at[0, low]),
            (k.at[own], buf.at[0, high]),
            (v.at[own], buf.at[1, low]),
            (ga.at[pl.ds(base, rows)], buf.at[1, high]),
            (gh.at[own], hidden_of(block)),
        )
        return [
            pltpu.make_async_copy(*pair, block_sem.at[block % 2, index])
            for index, pair in enumerate(pairs)
        ]

    def gx_copy(block):
        rows, base, source = blocks[block]
        target = gx_q if source else gx_p
        own = pl.ds(base - (p_rows if source else 0), rows)
        return pltpu.make_async_copy(hidden_of(block), target.at[own], gx_sem.at[block])

    def states(block):
        rows, base, _ = blocks[block]
        own = pl.ds(base, rows)
        hidden_of(block)[...] += (
            mm(grads[0, own], wq[...], NT)
            + mm(grads[1, own], wk[...], NT)
            + mm(grads[2, own], wv[...], NT)
        )
        gx_copy(block).start()

    def attention(block, plan):
        rows, base, source = blocks[block]
        buf = left_buf if block % 2 == 0 else right_buf
        low, high, own = pl.ds(0, rows), pl.ds(span, rows), pl.ds(base, rows)
        att = kept[source][4]
        q_ref, k_ref, v_ref, ga_ref = (
            buf.at[0, low],
            buf.at[0, high],
            buf.at[1, low],
            buf.at[1, high],
        )
        entry = 0 if source else block
        size = pl.ds(0, rows)

        def att_copy(pair):
            slot = lax.rem(pair, 2)
            return pltpu.make_async_copy(
                att.at[entry, pl.ds(2 * pair, 2)],
                att_buf.at[slot, :, size, size],
                att_sem.at[slot],
            )

        att_copy(0).start()
        for copy in block_copies(block):
            copy.wait()
        grads[2, own] = mm(ga_ref[...], wo[...], NT).astype(BF16)
        low_half = lax.broadcasted_iota(jnp.int32, (rows, 128), 1) < HEAD_DIM
        scale = HEAD_DIM ** (-0.5)

        def pair_body(pair, carry):
            cols = pl.ds(pl.multiple_of(pair * 128, 128), 128)
            slot = lax.rem(pair, 2)
            att_copy(pair).wait()
            pl.when(pair < HEADS // 2 - 1)(lambda: att_copy(pair + 1).start())
            q_pair, k_pair, v_pair = q_ref[:, cols], k_ref[:, cols], v_ref[:, cols]
            gc_pair = grads[2, own, cols]
            parts = []
            for half in range(2):
                mask = low_half if half == 0 else jnp.logical_not(low_half)
                low_att = att_buf[slot, half, size, size]
                wide_att = low_att.astype(F32)
                grad_att = mm(jnp.where(mask, gc_pair, jnp.zeros_like(gc_pair)), v_pair, NT)
                weighted = grad_att * wide_att
                grad_logits = (
                    weighted - wide_att * jnp.sum(weighted, axis=-1, keepdims=True)
                ).astype(BF16)
                parts.append(
                    (
                        mm(grad_logits, k_pair) * scale,
                        mm(grad_logits, q_pair, TN),
                        mm(low_att, gc_pair, TN),
                    )
                )
            for index in range(3):
                grads[index, own, cols] = jnp.where(
                    low_half, parts[0][index], parts[1][index]
                ).astype(BF16)
            hooks(pair, plan)
            return carry

        lax.fori_loop(0, HEADS // 2, pair_body, 0)
        accumulate(att_sums, 0, grads[0, own].astype(F32))
        accumulate(att_sums, 1, grads[2, own].astype(F32))

    def weight_copies():
        return [
            pltpu.make_async_copy(source, target, weight_sem.at[index])
            for index, (source, target) in enumerate(zip(sources, (wo, wq, wk, wv)))
        ]

    span = kept[0][4].shape[-1]
    blocks = [(span, base, 0) for base in range(0, p_rows, span)] + [(x_q.shape[0], p_rows, 1)]
    for copy in weight_copies():
        copy.start()
    att_sums[...] = jnp.zeros_like(att_sums)
    lax.fori_loop(0, TILES, tile_body, 0)
    load(TILES, True)
    slot = TILES % 2
    made = mm(left_buf[slot], thin_buf[...], TN).astype(BF16)
    for copy in block_copies(0):
        copy.start()
    lanes = thin_buf.shape[1]
    last = pl.ds(3 * part, 16)
    for shard in range(2 * n_z):
        for block in range(width // lanes):
            row = shard * part + block * 16
            both[0, 0, shard // 2, shard % 2, last, block * lanes : (block + 1) * lanes] = made[
                row : row + 16
            ]
    for copy in weight_copies():
        copy.wait()
    for copy in block_copies(1):
        copy.start()
    attention(0, ((0, start_one, (2, 3)), (3, start_two, (0, 1))))
    for copy in block_copies(2):
        copy.start()
    attention(
        1,
        (
            (0, start_far, (0, 1)),
            (2, start_two, (2, 3)),
            (5, start_far, (2, 3)),
        ),
    )
    x_copies = [
        pltpu.make_async_copy(x_p, right_buf.at[0, pl.ds(0, p_rows)], load_sem.at[0, 0]),
        pltpu.make_async_copy(
            x_q, right_buf.at[0, pl.ds(p_rows, total - p_rows)], load_sem.at[0, 1]
        ),
    ]
    for copy in x_copies:
        copy.start()
    attention(2, ((2, start_share, (0, 1)),))
    top = sums[0][:8] + sums[1][:8] + att_sums[...]
    tail = jnp.concatenate([top, sums[0][8:] + sums[1][8:]], axis=0).astype(BF16)
    for shard in range(2 * n_z):
        at_z, at_x = shard // 2, shard % 2
        both[1, 0, at_z, at_x, last] = tail
        both[0, 1, at_z, at_x, last] = jnp.zeros_like(tail)
        both[1, 1, at_z, at_x, last] = jnp.zeros_like(tail)
    for copy in x_copies:
        copy.wait()

    def late_body(tile, carry):
        halves(right_buf.at[0], grads.at[tile], lambda half, made: put(2, tile, half, made))
        pl.when(tile == 1)(lambda: late_copy(0).start())
        return carry

    lax.fori_loop(0, 3, late_body, 0)

    def start_late(index):
        late_copy(index).start()

    def wait_late(index):
        late_copy(index).wait_recv()

    def end_late(index):
        late_copy(index).wait_send()

    for step, units in (
        (start_late, (1, 2)),
        (start_share, (2, 3)),
        (wait_late, (0, 1)),
        (start_one, (5, 7, 9)),
        (wait_late, (2,)),
        (start_one, (4, 6, 8)),
        (forward, EARLY),
        (states, (0,)),
        (start_two, (5, 4)),
        (states, (1,)),
        (start_two, (7, 6)),
        (start_far, (5, 4)),
        (states, (2,)),
        (start_two, (8,)),
        (start_far, (7, 6)),
        (start_two, (9,)),
        (start_far, (8,)),
        (start_share, (5, 4)),
        (start_far, (9,)),
        (start_share, (7, 6, 8)),
        (forward, (5, 4, 7, 6)),
        (start_share, (9,)),
        (forward, (8, 9)),
        (finish, EARLY + LATE),
        (end_late, (0, 1, 2)),
        (lambda block: gx_copy(block).wait(), range(len(blocks))),
    ):
        for unit in units:
            step(unit)


def backward_tail(arrays, passage_kept, query_kept, weights, sums, n_wide):
    n_z = n_wide // 2
    go, x_p, x_q, gp = arrays[1], arrays[4], arrays[5], arrays[9]
    total, width = go.shape
    part = width // n_wide
    units = len(UNITS)
    span = passage_kept[4].shape[-1]
    sem = pltpu.SemaphoreType.DMA
    vmem = pl.BlockSpec(memory_space=pltpu.VMEM)
    return pl.pallas_call(
        functools.partial(tail_kernel, n_z, part),
        out_shape=(
            jax.ShapeDtypeStruct((4, SHARE_ROWS, width), BF16),
            jax.ShapeDtypeStruct(x_p.shape, F32),
            jax.ShapeDtypeStruct(x_q.shape, F32),
        ),
        in_specs=[ANY] * 24 + [vmem] * 2,
        out_specs=(vmem, ANY, ANY),
        scratch_shapes=[
            pltpu.VMEM((2, 2, n_z, 2, SHARE_ROWS, width), BF16),
            pltpu.VMEM((2, n_z, 2, SHARE_ROWS, width), BF16),
            pltpu.VMEM((n_z, 2, ROWS_A, width), BF16),
            pltpu.VMEM((2, n_z, ROWS_B, width), BF16),
            pltpu.VMEM((n_z, ROWS_A, width), BF16),
            pltpu.VMEM((n_z, ROWS_B, width), BF16),
            pltpu.VMEM((n_z - 1, SHARE_ROWS, width), BF16),
            pltpu.VMEM((2, total, width), BF16),
            pltpu.VMEM((2, total, width), BF16),
            pltpu.VMEM(gp.shape, BF16),
        ]
        + [pltpu.VMEM((width, width), BF16)] * 4
        + [
            pltpu.VMEM((2, 2, span, span), BF16),
            pltpu.VMEM((2, span, width), F32),
            pltpu.VMEM(x_q.shape, F32),
            pltpu.VMEM((3, total, width), BF16),
            pltpu.VMEM((8, width), F32),
            sem((2, 2)),
            sem((4,)),
            sem((2, 5)),
            sem((2,)),
            sem((3,)),
        ]
        + [sem((units,))] * 6
        + [sem((units * n_z,))] * 2
        + [sem((units * 3,))] * 2,
        compiler_params=pltpu.CompilerParams(
            collective_id=3, has_side_effects=True, vmem_limit_bytes=VMEM_LIMIT
        ),
        name="backward_tail",
    )(*arrays, *passage_kept, *query_kept, *weights, *sums)


def unpack_kernel(part, sums_ref, gx_p, gx_q, *refs):
    q_ref, k_ref, v_ref, o_ref, inner_ref, outer_ref, thin_ref, vec_ref, to_p, to_q = refs[:10]
    buf, in_sem, out_sem = refs[10:]
    width = q_ref.shape[1]
    rows = gx_q.shape[0]
    pieces = []
    for source, target in ((gx_p, to_p), (gx_q, to_q)):
        for start in range(0, source.shape[0], rows):
            at = pl.ds(start, rows)
            slot = len(pieces)
            pieces.append(
                (
                    pltpu.make_async_copy(source.at[at], buf.at[slot], in_sem.at[slot]),
                    pltpu.make_async_copy(buf.at[slot], target.at[at], out_sem.at[slot]),
                )
            )
    for arrive, _ in pieces:
        arrive.start()
    lanes = thin_ref.shape[1]
    for owner, ref in enumerate((q_ref, k_ref, v_ref, o_ref)):
        ref[...] = sums_ref[owner, 2 * part : 3 * part].astype(F32)
        inner_ref[:, owner * width : (owner + 1) * width] = sums_ref[
            owner, part : 2 * part
        ].astype(F32)
        outer_ref[owner * part : (owner + 1) * part] = sums_ref[owner, :part].astype(F32)
        pieces[owner][0].wait()
        pieces[owner][1].start()
    for arrive, leave in pieces[4:]:
        arrive.wait()
        leave.start()
    tail = sums_ref[0, 3 * part :].astype(F32)
    for block in range(width // lanes):
        thin_ref[block * 16 : (block + 1) * 16] = tail[:, block * lanes : (block + 1) * lanes]
    vec_ref[...] = sums_ref[1, 3 * part :].astype(F32)
    for _, leave in pieces:
        leave.wait()


def unpack(summed, grad_p, grad_q, part, embed_width):
    width = summed.shape[-1]
    rows = grad_q.shape[0]
    count = grad_p.shape[0] // rows + 1
    sem = pltpu.SemaphoreType.DMA
    vmem = pl.BlockSpec(memory_space=pltpu.VMEM)
    shapes = [(part, width)] * 4 + [
        (part, 4 * width),
        (4 * part, width),
        (part, embed_width),
        (16, width),
        grad_p.shape,
        grad_q.shape,
    ]
    return pl.pallas_call(
        functools.partial(unpack_kernel, part),
        out_shape=[jax.ShapeDtypeStruct(shape, F32) for shape in shapes],
        in_specs=[vmem, ANY, ANY],
        out_specs=[vmem] * (len(shapes) - 2) + [ANY] * 2,
        scratch_shapes=[pltpu.VMEM((count, rows, width), F32), sem((count,)), sem((count,))],
        compiler_params=pltpu.CompilerParams(vmem_limit_bytes=VMEM_LIMIT),
        name="unpack_gradients",
    )(summed, grad_p, grad_q)


def outer(left, right):
    return lax.dot_general(left, right, TN, preferred_element_type=F32)


def local(
    query_states,
    passage_states,
    lengths,
    positives,
    query_weight,
    query_bias,
    key_weight,
    value_weight,
    value_bias,
    out_weight,
    out_bias,
    first_gain,
    first_shift,
    inner_weight,
    inner_bias,
    outer_weight,
    outer_bias,
    second_gain,
    second_shift,
    linear_weight,
):
    everyone = ("wide", "narrow")
    n_wide = lax.axis_size("wide")
    n_narrow = lax.axis_size("narrow")
    wide_index = lax.axis_index("wide")
    narrow_index = lax.axis_index("narrow")
    micro, own_queries, query_len, width = query_states.shape
    own_passages, slots = passage_states.shape[1:3]
    weights = (
        query_weight,
        key_weight,
        value_weight,
        out_weight,
        inner_weight,
        outer_weight,
        linear_weight,
    )
    embed_width = linear_weight.shape[1]
    vec = pack(
        (
            query_bias,
            value_bias,
            out_bias,
            first_gain,
            first_shift,
            outer_bias,
            second_gain,
            second_shift,
            inner_bias,
        ),
        width,
    )
    own_index = narrow_index * n_wide + wide_index
    own_lengths = lax.dynamic_slice_in_dim(lengths, own_index * own_passages, own_passages, axis=1)
    lens = own_lengths.reshape(-1)
    x_query = query_states.reshape(-1, width)
    x_passage = passage_states.reshape(-1, width)
    query_rows, passage_rows = x_query.shape[0], x_passage.shape[0]
    total = query_rows + passage_rows
    kept_q = encode(
        x_query, lens, vec, weights, 1, query_len, total, passage_rows, None, None
    )
    sizes = (n_wide, n_narrow)
    kept_p = encode(
        x_passage, lens, vec, weights, micro * own_passages, 0, total, 0, kept_q, sizes
    )
    queries = kept_p[16].reshape(n_wide * n_narrow, micro, -1, embed_width)
    ctx, first_low, act, final_low = (kept_p[index] for index in (4, 7, 8, 12))
    passages = kept_p[15].reshape(micro * own_passages, slots, embed_width)
    row_count = own_queries * n_narrow
    together = queries.size * slots <= 8 * 1024 * 1024 * embed_width
    if together:
        full, loss, grad_passage, grad_query = match(
            queries, passages, lens, positives, n_wide, n_narrow, query_len
        )
        block = lax.dynamic_slice_in_dim(full, narrow_index * n_wide, n_wide, axis=0)
        block = lax.dynamic_slice_in_dim(
            block[:, :own_queries].reshape(n_wide, own_queries, micro, -1),
            wide_index * n_narrow,
            n_narrow,
            axis=3,
        )
        scores = block.transpose(2, 3, 1, 0).reshape(micro, row_count, n_wide)
        losses = lax.dynamic_slice_in_dim(
            loss[:own_queries].reshape(own_queries, micro, -1),
            wide_index * n_narrow,
            n_narrow,
            axis=2,
        )
        losses = losses.transpose(1, 2, 0).reshape(micro, row_count)
    else:
        e, z = similarity(queries, passages, lens)
        best = SHARP + jnp.log(z)
        own_scores = jnp.sum(best.reshape(micro, -1, query_len), axis=-1) / SHARP
        full = share_scores(own_scores, n_wide, n_narrow)
        row_total = jax.nn.logsumexp(full, axis=0)
        passage_ids = jnp.arange(full.shape[0], dtype=jnp.int32)
        picked = jnp.sum(
            jnp.where(passage_ids[:, None, None] == positives[None], full, 0.0), axis=0
        )
        row_count = own_queries * n_narrow
        losses = lax.dynamic_slice_in_dim(row_total - picked, wide_index * row_count, row_count, axis=1)
        block = lax.dynamic_slice(
            full,
            (narrow_index * n_wide, 0, wide_index * row_count),
            (n_wide, micro, row_count),
        )
        scores = jnp.transpose(block, (1, 2, 0))
        grads = jnp.exp(own_scores - row_total) - (positives == own_index).astype(F32)
        token_weights = jnp.repeat(grads, query_len, axis=1).reshape(z.shape) / z
        grad_passage, grad_query = similarity_back(e, token_weights, queries, passages)
        grad_query = grad_query.reshape(-1, 2, query_rows, embed_width)
    grad_passage = grad_passage.reshape(passage_rows, embed_width)
    back_p = mlp_back(
        grad_passage,
        kept_p,
        vec,
        weights,
        micro * own_passages,
        total,
        0,
        None,
        grad_query if together else None,
        sizes if together else None,
    )
    grad_query = back_p[6] if together else exchange(grad_query, n_wide, n_narrow)
    back_q = mlp_back(
        grad_query, kept_q, vec, weights, 1, total, passage_rows, back_p, None, None
    )
    gp, go, gi, _, ga, sums_q = back_q[:6]
    part = width // n_wide
    if part == 96 and n_narrow == 4 and micro * own_passages == 2 and act.shape[1] == 4 * width:
        summed, grad_p, grad_q = backward_tail(
            (act, go, first_low, gi, x_passage, x_query, ctx, ga, final_low, gp),
            (*kept_p[:3], back_p[3], kept_p[3]),
            (*kept_q[:3], back_q[3], kept_q[3]),
            (out_weight, query_weight, key_weight, value_weight),
            (back_p[5], sums_q),
            n_wide,
        )
        r_q, r_k, r_v, r_out, r_inner, r_outer, r_linear, vectors, grad_p, grad_q = unpack(
            summed, grad_p, grad_q, part, embed_width
        )
        own = lax.dynamic_slice_in_dim(vectors[:8], wide_index * part, part, axis=1)
        v_q, v_v, v_o, v_g1, v_s1, v_2, v_g2, v_s2 = (
            own[row] for row in (0, 1, ROW_BO, ROW_G1, ROW_S1, ROW_B2, ROW_G2, ROW_S2)
        )
        v_i = lax.dynamic_slice_in_dim(
            vectors[ROW_BI : ROW_BI + 4].reshape(-1), wide_index * 4 * part, 4 * part
        )
    else:
        att_p = attention_back(
            ga, back_p[3], kept_p, weights, micro * own_passages, total, 0, None
        )
        att_q = attention_back(ga, back_q[3], kept_q, weights, 1, total, passage_rows, att_p[0])
        gqkv, grad_p, grad_q = att_q[0], att_p[1], att_q[1]

        def reduce(value):
            piece = lax.psum_scatter(value.astype(BF16), everyone, scatter_dimension=0, tiled=True)
            return lax.all_gather(piece, "narrow", axis=0, tiled=True).astype(F32)

        def vector(rows):
            flat = rows.reshape(-1)
            share = flat.shape[0] // n_wide
            return lax.dynamic_slice_in_dim(flat, wide_index * share, share)

        sums = jnp.concatenate([back_p[5] + sums_q, att_p[2] + att_q[2]], axis=0)
        sums = lax.psum(sums, everyone)
        x_all = jnp.concatenate([x_passage, x_query], axis=0)
        pairs = ((act, go), (first_low, gi), (final_low, gp), (ctx, ga), (x_all, gqkv))
        r_outer, r_inner, r_linear, r_out, r_qkv = (
            reduce(outer(*pair)) for pair in pairs
        )
        r_q, r_k, r_v = (r_qkv[:, index * width : (index + 1) * width] for index in range(3))
        v_q, v_v, v_o, v_g1, v_s1, v_2, v_g2, v_s2 = (
            vector(sums[pick])
            for pick in (16, 17, ROW_BO, ROW_G1, ROW_S1, ROW_B2, ROW_G2, ROW_S2)
        )
        v_i = vector(sums[ROW_BI : ROW_BI + 4])
    return (
        scores,
        losses,
        grad_q.reshape(query_states.shape),
        grad_p.reshape(passage_states.shape),
        r_q,
        v_q,
        r_k,
        r_v,
        v_v,
        r_out,
        v_o,
        v_g1,
        v_s1,
        r_inner,
        v_i,
        r_outer,
        v_2,
        v_g2,
        v_s2,
        r_linear,
    )


def solution(mesh):
    return jax.shard_map(
        local,
        mesh=mesh,
        in_specs=(
            P(None, ("wide", "narrow"), None, None),
            P(None, ("narrow", "wide"), None, None),
        )
        + (P(),) * 18,
        out_specs=(
            P(None, "wide", "narrow"),
            P(None, "wide"),
            P(None, ("wide", "narrow"), None, None),
            P(None, ("narrow", "wide"), None, None),
            P("wide", None),
            P("wide"),
            P("wide", None),
            P("wide", None),
            P("wide"),
            P("wide", None),
            P("wide"),
            P("wide"),
            P("wide"),
            P("wide", None),
            P("wide"),
            P("wide", None),
            P("wide"),
            P("wide"),
            P("wide"),
            P("wide", None),
        ),
        check_vma=False,
    )
```

```python
import functools

import jax
import jax.numpy as jnp
from jax import lax
from jax.experimental import pallas as pl
from jax.experimental.pallas import tpu as pltpu
from jax.sharding import PartitionSpec as P

HEADS = 12
HEAD_DIM = 64
LOG2E = 1.4426950408889634
SHARP = 16.0
LAYER_EPS = 1e-12
NORM_EPS = 1e-06
MASKED = -1e30
SLOPE_CONST = 0.3989422804014327
ROOT_HALF = 0.7071067811865476
BF16 = jnp.bfloat16
F32 = jnp.float32
VMEM_LIMIT = 62 * 1024 * 1024

NN = (((1,), (0,)), ((), ()))
NT = (((1,), (1,)), ((), ()))
TN = (((0,), (0,)), ((), ()))


def mm(left, right, dims=NN):
    return lax.dot_general(left, right, dims, preferred_element_type=F32)


ANY = pl.BlockSpec(memory_space=pl.ANY)

ROW_BQ, ROW_BV, ROW_BO, ROW_G1, ROW_S1, ROW_B2, ROW_G2, ROW_S2, ROW_BI = range(9)


def vec_row(vec_ref, row):
    return vec_ref[row : row + 1, :]


def mean_row(value):
    return jnp.sum(value, axis=-1, keepdims=True) * (1.0 / value.shape[-1])


class Loader:
    def __init__(self, sources, targets, sem):
        self.copies = [
            pltpu.make_async_copy(source, target, sem.at[index])
            for index, (source, target) in enumerate(zip(sources, targets))
        ]
        self.first = pl.program_id(0) == 0

    def start(self):
        @pl.when(self.first)
        def _():
            for copy in self.copies:
                copy.start()

    def need(self, *indices):
        @pl.when(self.first)
        def _():
            for index in indices:
                self.copies[index].wait()


MESH = pl.DeviceIdType.MESH


def remote(source, target, sems, index, device):
    return pltpu.make_async_remote_copy(
        src_ref=source,
        dst_ref=target,
        send_sem=sems[0].at[index],
        recv_sem=sems[1].at[index],
        device_id=device,
        device_id_type=MESH,
    )


class Chips:
    def __init__(self, n_wide, n_narrow):
        self.wide, self.narrow = lax.axis_index("wide"), lax.axis_index("narrow")
        self.core = lax.rem(self.narrow, 2)
        self.rows = n_narrow // 2
        self.count = n_wide * self.rows
        self.me = self.wide * self.rows + self.narrow // 2
        self.mate = (self.wide, self.narrow + 1 - 2 * self.core)

    def at(self, step):
        return lax.rem(self.me + step + self.count, self.count)

    def device(self, chip):
        return (chip // self.rows, lax.rem(chip, self.rows) * 2 + self.core)

    def loop(self, body):
        def step_body(step, carry):
            body(step)
            return carry

        lax.fori_loop(1, self.count, step_body, 0)

    def barrier(self):
        barrier = pltpu.get_barrier_semaphore()

        def signal(step):
            pl.semaphore_signal(
                barrier, inc=1, device_id=self.device(self.at(step)), device_id_type=MESH
            )

        pl.semaphore_signal(barrier, inc=1, device_id=self.mate, device_id_type=MESH)
        self.loop(signal)
        pl.semaphore_wait(barrier, self.count)


class Gather:
    def __init__(self, chips, own, out, sems):
        self.chips, self.own, self.out = chips, own, out
        self.far, self.pair, self.local = sems[:2], sems[2:4], sems[4]

    def far_copy(self, step, chip):
        slot = self.out.at[chip, self.chips.core]
        return remote(self.own, slot, self.far, step, self.chips.device(self.chips.at(step)))

    def mate_copy(self, core):
        block = self.out.at[:, core]
        return remote(block, block, self.pair, 0, self.chips.mate)

    def local_copy(self):
        slot = self.out.at[self.chips.me, self.chips.core]
        return pltpu.make_async_copy(self.own, slot, self.local.at[0])

    def start(self):
        self.local_copy().start()
        self.chips.barrier()
        self.chips.loop(lambda step: self.far_copy(step, self.chips.me).start())

    def forward(self):
        self.local_copy().wait()
        self.chips.loop(lambda step: self.far_copy(step, self.chips.at(-step)).wait_recv())
        self.mate_copy(self.chips.core).start()

    def finish(self):
        self.chips.loop(lambda step: self.far_copy(step, self.chips.me).wait_send())
        self.mate_copy(1 - self.chips.core).wait_recv()
        self.mate_copy(self.chips.core).wait_send()


class Exchange:
    def __init__(self, chips, grads, out, scratch):
        self.chips, self.grads, self.out = chips, grads, out
        self.half, self.arrived, self.inbox = scratch[:3]
        self.pair, self.far, self.local = scratch[3:5], scratch[5:7], scratch[7]

    def pair_copy(self):
        away = self.grads.at[:, 1 - self.chips.core]
        return remote(away, self.arrived, self.pair, 0, self.chips.mate)

    def local_copy(self):
        mine = self.grads.at[:, self.chips.core]
        return pltpu.make_async_copy(mine, self.half, self.local.at[0])

    def far_copy(self, step):
        chip = self.chips.at(step)
        return remote(
            self.half.at[chip], self.inbox.at[step], self.far, step, self.chips.device(chip)
        )

    def start(self):
        self.local_copy().start()
        self.chips.barrier()
        self.pair_copy().start()

    def push(self):
        self.local_copy().wait()
        self.pair_copy().wait_recv()

        def add(step):
            chip = self.chips.at(step)
            total = self.half[chip].astype(F32) + self.arrived[chip].astype(F32)
            self.half[chip] = total.astype(BF16)
            self.far_copy(step).start()

        self.chips.loop(add)
        me = self.chips.me
        self.out[...] = self.half[me].astype(F32) + self.arrived[me].astype(F32)

    def finish(self):
        def collect(step):
            copy = self.far_copy(step)
            copy.wait_recv()
            copy.wait_send()
            self.out[...] += self.inbox[step].astype(F32)

        self.chips.loop(collect)
        self.pair_copy().wait_send()


class Push:
    def __init__(self, chips, half, out, scratch):
        self.chips, self.half, self.out = chips, half, out
        self.inbox, self.far, self.own = scratch[0], scratch[1:3], scratch[3]

    def far_copy(self, step):
        chip = self.chips.at(step)
        return remote(
            self.half.at[chip], self.inbox.at[step], self.far, step, self.chips.device(chip)
        )

    def own_copy(self):
        return pltpu.make_async_copy(
            self.half.at[self.chips.me], self.inbox.at[0], self.own.at[0]
        )

    def start(self):
        self.own_copy().start()
        self.chips.barrier()
        self.chips.loop(lambda step: self.far_copy(step).start())

    def finish(self):
        self.own_copy().wait()
        self.out[...] = self.inbox[0].astype(F32)

        def collect(step):
            copy = self.far_copy(step)
            copy.wait_recv()
            copy.wait_send()
            self.out[...] += self.inbox[step].astype(F32)

        self.chips.loop(collect)


def push_scratch(chips, rows, width):
    sem = pltpu.SemaphoreType.DMA
    return [pltpu.VMEM((chips, rows, width), BF16), sem((chips,)), sem((chips,)), sem((1,))]


def exchange_scratch(chips, rows, width):
    sem = pltpu.SemaphoreType.DMA
    return [pltpu.VMEM((chips, rows, width), BF16)] * 3 + [
        sem((1,)),
        sem((1,)),
        sem((chips,)),
        sem((chips,)),
        sem((1,)),
    ]


def fwd_kernel(grouped, alias_count, sizes, offset, *refs):
    lens_ref, x_ref, vec_ref = refs[:3]
    sources = refs[3:10]
    refs = refs[10 + alias_count :]
    gather = None
    if sizes:
        gather = Gather(Chips(*sizes), refs[0], refs[17], refs[-5:])
        refs = refs[1:17] + refs[18:-5]
    (
        q_ref,
        k_ref,
        v_ref,
        att_ref,
        ctx_ref,
        n1_ref,
        r1_ref,
        first_ref,
        act_ref,
        slope_ref,
        n2_ref,
        r2_ref,
        final_ref,
        unit_ref,
        uinv_ref,
        embed_ref,
    ) = refs[:16]
    wq, wk, wv, wo, wi, w2, wl, sem, acc_ref, att_buf, act_buf, slope_buf, out_sem = refs[16:]
    loader = Loader(sources, (wq, wk, wv, wo, wi, w2, wl), sem)
    block_id = pl.program_id(0)
    loader.start()
    if gather:
        last = pl.program_id(0) == pl.num_programs(0) - 1
        pl.when(loader.first)(gather.start)
    rows = x_ref.shape[0]
    x = x_ref[...]
    scale = HEAD_DIM ** (-0.5)
    loader.need(0)
    q_ref[...] = ((mm(x, wq[...]) + vec_row(vec_ref, ROW_BQ)).astype(BF16) * scale).astype(BF16)
    loader.need(1)
    k_ref[...] = mm(x, wk[...]).astype(BF16)
    loader.need(2)
    v_ref[...] = (mm(x, wv[...]) + vec_row(vec_ref, ROW_BV)).astype(BF16)
    if grouped:
        valid = (
            lax.broadcasted_iota(jnp.int32, (rows, rows), 0) // grouped
            == lax.broadcasted_iota(jnp.int32, (rows, rows), 1) // grouped
        )
    else:
        length = lens_ref[pl.program_id(0)]
        valid = lax.broadcasted_iota(jnp.int32, (1, rows), 1) < length
    bias = jnp.where(valid, 0.0, MASKED)
    low_half = lax.broadcasted_iota(jnp.int32, (rows, 128), 1) < HEAD_DIM

    def att_copy(pair):
        slot = lax.rem(pair, 2)
        return pltpu.make_async_copy(
            att_buf.at[slot], att_ref.at[block_id, pl.ds(2 * pair, 2)], out_sem.at[slot]
        )

    def pair_body(pair, carry):
        cols = pl.ds(pl.multiple_of(pair * 128, 128), 128)
        slot = lax.rem(pair, 2)
        pl.when(pair >= 2)(lambda: att_copy(pair - 2).wait())
        q_pair, k_pair, v_pair = q_ref[:, cols], k_ref[:, cols], v_ref[:, cols]
        parts = []
        for half in range(2):
            mask = low_half if half == 0 else jnp.logical_not(low_half)
            logits = mm(jnp.where(mask, q_pair, jnp.zeros_like(q_pair)), k_pair, NT) + bias
            peak = jnp.max(logits, axis=-1, keepdims=True)
            e = jnp.exp(logits - peak)
            inv = 1.0 / jnp.sum(e, axis=-1, keepdims=True)
            low = (e * inv).astype(BF16)
            att_buf[slot, half] = low
            parts.append(mm(low, v_pair))
        att_copy(pair).start()
        ctx_ref[:, cols] = jnp.where(low_half, parts[0], parts[1]).astype(BF16)
        return carry

    lax.fori_loop(0, HEADS // 2, pair_body, 0)
    if gather:
        pl.when(last)(gather.forward)
    loader.need(3)
    field = x.astype(F32) + (mm(ctx_ref[...], wo[...]) + vec_row(vec_ref, ROW_BO))
    center = field - mean_row(field)
    inverse = lax.rsqrt(mean_row(center * center) + LAYER_EPS)
    normed = center * inverse
    n1_ref[...] = normed.astype(BF16)
    r1_ref[...] = jnp.broadcast_to(inverse, r1_ref.shape)
    first = normed * vec_row(vec_ref, ROW_G1) + vec_row(vec_ref, ROW_S1)
    first_ref[...] = first.astype(BF16)
    acc_ref[...] = first + vec_row(vec_ref, ROW_B2)
    loader.need(4, 5)
    width = x.shape[1]

    base = block_id * rows if offset is None else offset

    def chunk_copies(chunk):
        slot = lax.rem(chunk, 2)
        cols = pl.ds(pl.multiple_of(chunk * width, width), width)
        return (
            pltpu.make_async_copy(
                act_buf.at[slot], act_ref.at[pl.ds(base, rows), cols], out_sem.at[2 + slot]
            ),
            pltpu.make_async_copy(
                slope_buf.at[slot],
                slope_ref.at[pl.ds(block_id * rows, rows), cols],
                out_sem.at[4 + slot],
            ),
        )

    def chunk_body(chunk, carry):
        cols = pl.ds(pl.multiple_of(chunk * width, width), width)
        slot = lax.rem(chunk, 2)

        @pl.when(chunk >= 2)
        def _():
            for copy in chunk_copies(chunk - 2):
                copy.wait()

        inner = mm(first_ref[...], wi[:, cols]) + vec_ref[pl.ds(ROW_BI + chunk, 1), :]
        phi = 0.5 * (1.0 + lax.erf(inner * ROOT_HALF))
        activated = (inner * phi).astype(BF16)
        act_buf[slot] = activated
        slope_buf[slot] = (phi + inner * jnp.exp(-0.5 * inner * inner) * SLOPE_CONST).astype(BF16)
        for copy in chunk_copies(chunk):
            copy.start()
        acc_ref[...] += mm(activated, w2[cols, :])
        return carry

    chunks = wi.shape[1] // width
    lax.fori_loop(0, chunks, chunk_body, 0)
    field = acc_ref[...]
    center = field - mean_row(field)
    inverse = lax.rsqrt(mean_row(center * center) + LAYER_EPS)
    normed = center * inverse
    n2_ref[...] = normed.astype(BF16)
    r2_ref[...] = jnp.broadcast_to(inverse, r2_ref.shape)
    final = (normed * vec_row(vec_ref, ROW_G2) + vec_row(vec_ref, ROW_S2)).astype(BF16)
    final_ref[...] = final
    loader.need(6)
    projected = mm(final, wl[...])
    uinv = lax.rsqrt(jnp.sum(projected * projected, axis=-1, keepdims=True) + NORM_EPS)
    unit = projected * uinv
    unit_ref[...] = unit
    uinv_ref[...] = jnp.broadcast_to(uinv, uinv_ref.shape)
    embed_ref[...] = unit.astype(BF16)
    for back in (2, 1):
        att_copy(HEADS // 2 - back).wait()
        for copy in chunk_copies(chunks - back):
            copy.wait()
    if gather:
        pl.when(last)(gather.finish)


def encode(x, lens, vec, weights, blocks, grouped, total, offset, earlier, sizes):
    rows = x.shape[0] // blocks
    width = x.shape[1]
    wide = weights[4].shape[1]
    embed_width = weights[6].shape[1]
    base = offset // rows

    def row_spec(columns):
        return pl.BlockSpec((rows, columns), lambda i, lens: (base + i, 0))

    def own_spec(columns):
        return pl.BlockSpec((rows, columns), lambda i, lens: (i, 0))

    def shape(count, columns, dtype):
        return jax.ShapeDtypeStruct((count, columns), dtype)

    own = x.shape[0]
    out_shapes = [
        shape(own, width, BF16),
        shape(own, width, BF16),
        shape(own, width, BF16),
        jax.ShapeDtypeStruct((blocks, HEADS, rows, rows), BF16),
        shape(total, width, BF16),
        shape(own, width, BF16),
        shape(own, embed_width, F32),
        shape(total, width, BF16),
        shape(total, wide, BF16),
        shape(own, wide, BF16),
        shape(own, width, BF16),
        shape(own, embed_width, F32),
        shape(total, width, BF16),
        shape(own, embed_width, F32),
        shape(own, embed_width, F32),
        shape(own, embed_width, BF16),
    ]
    shared = (4, 7, 8, 12)
    out_specs = [
        ANY
        if index in (3, 8, 9)
        else (row_spec if index in shared else own_spec)(out.shape[1])
        for index, out in enumerate(out_shapes)
    ]
    aliased = [] if earlier is None else [earlier[index] for index in shared]
    sends, sem_shapes, params = [], [], {}
    if sizes:
        sends = [earlier[15]]
        chips = sizes[0] * sizes[1] // 2
        out_shapes.append(jax.ShapeDtypeStruct((chips, 2) + earlier[15].shape, BF16))
        out_specs.append(ANY)
        sem = pltpu.SemaphoreType.DMA
        sem_shapes = [sem((chips,)), sem((chips,)), sem((1,)), sem((1,)), sem((1,))]
        params = {"collective_id": 4, "has_side_effects": True}
    return pl.pallas_call(
        functools.partial(fwd_kernel, grouped, len(aliased), sizes, offset if blocks == 1 else None),
        out_shape=out_shapes,
        grid_spec=pltpu.PrefetchScalarGridSpec(
            num_scalar_prefetch=1,
            grid=(blocks,),
            in_specs=[
                own_spec(width),
                pl.BlockSpec(vec.shape, lambda i, lens: (0, 0)),
            ]
            + [ANY] * (7 + len(aliased) + len(sends)),
            out_specs=out_specs,
            scratch_shapes=[pltpu.VMEM(weight.shape, BF16) for weight in weights]
            + [
                pltpu.SemaphoreType.DMA((7,)),
                pltpu.VMEM((rows, width), F32),
                pltpu.VMEM((2, 2, rows, rows), BF16),
                pltpu.VMEM((2, rows, width), BF16),
                pltpu.VMEM((2, rows, width), BF16),
                pltpu.SemaphoreType.DMA((6,)),
            ]
            + sem_shapes,
        ),
        input_output_aliases={10 + index: shared[index] for index in range(len(aliased))},
        compiler_params=pltpu.CompilerParams(vmem_limit_bytes=VMEM_LIMIT, **params),
        name="encode_queries" if grouped else "encode_passages",
    )(lens, x, vec, *weights, *aliased, *sends)


def sims_kernel(lens_ref, q_ref, p_ref, e_ref, z_ref):
    count = q_ref.shape[0]
    tokens = count * q_ref.shape[2]
    query = q_ref[...].reshape(tokens, q_ref.shape[3])
    sims = mm(p_ref[0], query, NT)
    slot = lax.broadcasted_iota(jnp.int32, sims.shape, 0)
    e = jnp.where(slot < lens_ref[pl.program_id(0)], jnp.exp(SHARP * sims - SHARP), 0.0)
    e_ref[0] = e.astype(BF16)
    z = jnp.sum(e, axis=0, keepdims=True)
    step = q_ref.shape[2]
    for index in range(count):
        z_ref[0, index : index + 1, :] = z[:, index * step : (index + 1) * step]


def sims_back_kernel(e_ref, w_ref, q_ref, p_ref, gp_ref, gq_ref):
    count = q_ref.shape[0]
    step = q_ref.shape[2]
    query = q_ref[...].reshape(count * step, q_ref.shape[3])
    weight = jnp.concatenate([w_ref[0, index : index + 1, :] for index in range(count)], axis=1)
    grads = (e_ref[0].astype(F32) * weight).astype(BF16)
    part = mm(grads, query)

    @pl.when(pl.program_id(1) == 0)
    def _():
        gp_ref[0] = part

    @pl.when(pl.program_id(1) > 0)
    def _():
        gp_ref[0] += part

    gq_ref[...] = mm(grads, p_ref[0], TN).astype(BF16).reshape(gq_ref.shape)


def similarity(queries, passages, lens):
    devices, micro, tokens, width = queries.shape
    slots = passages.shape[1]
    group = 8
    e, z = pl.pallas_call(
        sims_kernel,
        out_shape=(
            jax.ShapeDtypeStruct((micro, slots, devices * tokens), BF16),
            jax.ShapeDtypeStruct((micro, devices, tokens), F32),
        ),
        grid_spec=pltpu.PrefetchScalarGridSpec(
            num_scalar_prefetch=1,
            grid=(micro, devices // group),
            in_specs=[
                pl.BlockSpec((group, 1, tokens, width), lambda m, b, lens: (b, m, 0, 0)),
                pl.BlockSpec((1, slots, width), lambda m, b, lens: (m, 0, 0)),
            ],
            out_specs=(
                pl.BlockSpec((1, slots, group * tokens), lambda m, b, lens: (m, 0, b)),
                pl.BlockSpec((1, group, tokens), lambda m, b, lens: (m, b, 0)),
            ),
        ),
        compiler_params=pltpu.CompilerParams(vmem_limit_bytes=VMEM_LIMIT),
        name="similarity",
    )(lens, queries, passages)
    return e, z


def similarity_back(e, weights, queries, passages):
    devices, micro, tokens, width = queries.shape
    slots = passages.shape[1]
    group = 8
    return pl.pallas_call(
        sims_back_kernel,
        out_shape=(
            jax.ShapeDtypeStruct((micro, slots, width), F32),
            jax.ShapeDtypeStruct((devices, micro, tokens, width), BF16),
        ),
        grid=(micro, devices // group),
        in_specs=[
            pl.BlockSpec((1, slots, group * tokens), lambda m, b: (m, 0, b)),
            pl.BlockSpec((1, group, tokens), lambda m, b: (m, b, 0)),
            pl.BlockSpec((group, 1, tokens, width), lambda m, b: (b, m, 0, 0)),
            pl.BlockSpec((1, slots, width), lambda m, b: (m, 0, 0)),
        ],
        out_specs=(
            pl.BlockSpec((1, slots, width), lambda m, b: (m, 0, 0)),
            pl.BlockSpec((group, 1, tokens, width), lambda m, b: (b, m, 0, 0)),
        ),
        compiler_params=pltpu.CompilerParams(vmem_limit_bytes=VMEM_LIMIT),
        name="similarity_back",
    )(e, weights, queries, passages)


def match_kernel(n_wide, n_narrow, group, query_len, *refs):
    lens_ref, q_ref, p_ref, pos_ref = refs[:4]
    all_ref, loss_ref, gp_ref, half_ref = refs[4:8]
    e_buf, z_buf, own_buf, grad_buf, near, share_send, share_recv, pair_send, pair_recv = refs[8:]
    devices, micro, tokens, width = q_ref.shape
    chips = Chips(n_wide, n_narrow)
    me = chips.narrow * n_wide + chips.wide
    share_sems, pair_sems = (share_send, share_recv), (pair_send, pair_recv)
    pairs = group // 2

    def device(index):
        return (lax.rem(index, n_wide), index // n_wide)

    def each(body):
        def step_body(step, carry):
            body(step)
            return carry

        lax.fori_loop(1, devices, step_body, 0)

    barrier = pltpu.get_barrier_semaphore()
    each(
        lambda step: pl.semaphore_signal(
            barrier, inc=1, device_id=device(lax.rem(me + step, devices)), device_id_type=MESH
        )
    )

    def query_rows(block, m):
        at = pl.ds(block * group, group)
        return q_ref[at, m].reshape(group * tokens, width)

    def forward(block, carry):
        for m in range(micro):
            sims = mm(p_ref[m], query_rows(block, m), NT)
            slot = lax.broadcasted_iota(jnp.int32, (sims.shape[0], 1), 0)
            shift = jnp.where(slot < lens_ref[m], SHARP * LOG2E, -MASKED)
            e = jnp.exp2(SHARP * LOG2E * sims - shift)
            e_buf[m, block] = e.astype(BF16)
            z = jnp.sum(e, axis=0, keepdims=True)
            for index in range(group):
                z_buf[m, pl.ds(block * group + index, 1)] = z[
                    :, index * tokens : (index + 1) * tokens
                ]
        return carry

    lax.fori_loop(0, devices // group, forward, 0)
    pl.semaphore_wait(barrier, devices - 1)
    best = SHARP + jnp.log(z_buf[...].reshape(micro * devices, tokens))
    member = (
        lax.broadcasted_iota(jnp.int32, (8, tokens), 0)
        == lax.broadcasted_iota(jnp.int32, (8, tokens), 1) // query_len
    ).astype(F32)
    own = (
        lax.dot_general(
            member, best, NT, precision=lax.Precision.HIGHEST, preferred_element_type=F32
        )
        / SHARP
    )
    own_buf[...] = own
    all_ref[me] = own

    def share(step, source):
        target = device(lax.rem(me + step, devices))
        return remote(own_buf, all_ref.at[source], share_sems, step, target)

    each(lambda step: share(step, me).start())
    each(lambda step: share(step, lax.rem(me - step + devices, devices)).wait_recv())
    each(lambda step: share(step, me).wait_send())
    full = all_ref[...]
    peak = jnp.max(full, axis=0)
    total = peak + jnp.log(jnp.sum(jnp.exp(full - peak[None]), axis=0))
    positive = pos_ref[...]
    passage = lax.broadcasted_iota(jnp.int32, full.shape, 0)
    picked = jnp.sum(jnp.where(passage == positive[None], full, 0.0), axis=0)
    loss_ref[...] = total - picked
    grads = jnp.exp(own - total) - (positive == me).astype(F32)
    spread = lax.dot_general(
        grads, member, TN, precision=lax.Precision.HIGHEST, preferred_element_type=F32
    )
    z_buf[...] = (spread / z_buf[...].reshape(micro * devices, tokens)).reshape(z_buf.shape)
    gp_ref[...] = jnp.zeros_like(gp_ref)

    def pair_copy(block):
        at = pl.ds(block * pairs, pairs)
        return remote(
            grad_buf.at[at, 1 - chips.core], near.at[at], pair_sems, block, chips.mate
        )

    def backward(block, carry):
        for m in range(micro):
            weight = jnp.concatenate(
                [z_buf[m, pl.ds(block * group + index, 1)] for index in range(group)], axis=1
            )
            grads = e_buf[m, block] * weight.astype(BF16)
            gp_ref[m] += mm(grads, query_rows(block, m))
            part = mm(grads, p_ref[m], TN).astype(BF16)
            for index in range(group):
                grad_buf[block * pairs + index // 2, index % 2, m * tokens : (m + 1) * tokens] = (
                    part[index * tokens : (index + 1) * tokens]
                )
        pair_copy(block).start()
        return carry

    lax.fori_loop(0, devices // group, backward, 0)

    def join(block, carry):
        copy = pair_copy(block)
        copy.wait_recv()
        copy.wait_send()
        at = pl.ds(block * pairs, pairs)
        half_ref[at] = (
            grad_buf[at, chips.core].astype(F32) + near[at].astype(F32)
        ).astype(BF16)
        return carry

    lax.fori_loop(0, devices // group, join, 0)


def match(queries, passages, lens, positives, n_wide, n_narrow, query_len):
    devices, micro, tokens, width = queries.shape
    slots = passages.shape[1]
    group = 8
    own = tokens // query_len
    placed = positives.reshape(micro, devices, own).transpose(2, 0, 1).reshape(own, -1)
    placed = jnp.pad(placed, ((0, 8 - own), (0, 0)))
    sem = pltpu.SemaphoreType.DMA
    vmem = pl.BlockSpec(memory_space=pltpu.VMEM)
    columns = micro * devices
    return pl.pallas_call(
        functools.partial(match_kernel, n_wide, n_narrow, group, query_len),
        out_shape=(
            jax.ShapeDtypeStruct((devices, 8, columns), F32),
            jax.ShapeDtypeStruct((8, columns), F32),
            jax.ShapeDtypeStruct((micro, slots, width), F32),
            jax.ShapeDtypeStruct((devices // 2, micro * tokens, width), BF16),
        ),
        in_specs=[pl.BlockSpec(memory_space=pltpu.SMEM), vmem, vmem, vmem],
        out_specs=(vmem,) * 4,
        scratch_shapes=[
            pltpu.VMEM((micro, devices // group, slots, group * tokens), BF16),
            pltpu.VMEM((micro, devices, tokens), F32),
            pltpu.VMEM((8, columns), F32),
            pltpu.VMEM((devices // 2, 2, micro * tokens, width), BF16),
            pltpu.VMEM((devices // 2, micro * tokens, width), BF16),
            sem((devices,)),
            sem((devices,)),
            sem((devices // group,)),
            sem((devices // group,)),
        ],
        compiler_params=pltpu.CompilerParams(
            collective_id=1, has_side_effects=True, vmem_limit_bytes=VMEM_LIMIT
        ),
        name="match",
    )(lens, queries, passages, placed)


def accumulate(ref, row, value):
    ref[row : row + 1, :] += jnp.sum(value, axis=0, keepdims=True)


def mlp_back_kernel(alias_count, sizes, offset, *refs):
    (
        ge_ref,
        unit_ref,
        uinv_ref,
        n2_ref,
        r2_ref,
        slope_ref,
        n1_ref,
        r1_ref,
        vec_ref,
    ) = refs[:9]
    sources = refs[9:12]
    refs = refs[12 + alias_count :]
    swap = None
    if sizes:
        swap = Push(Chips(*sizes), refs[0], refs[7], refs[-4:])
        refs = refs[1:7] + refs[8:-4]
    gp_ref, go_ref, gi_ref, gh_ref, ga_ref, sums_ref = refs[:6]
    wl, w2, wi, sem, acc_ref, slope_buf, inner_buf, chunk_sem = refs[6:]
    loader = Loader(sources, (wl, w2, wi), sem)
    loader.start()
    rows, width = go_ref.shape
    own = pl.ds(pl.program_id(0) * rows, rows)
    placed = pl.ds(offset + pl.program_id(0) * rows, rows)

    def slope_copy(chunk):
        slot = lax.rem(chunk, 2)
        cols = pl.ds(pl.multiple_of(chunk * width, width), width)
        return pltpu.make_async_copy(
            slope_ref.at[own, cols], slope_buf.at[slot], chunk_sem.at[slot]
        )

    def inner_copy(chunk):
        slot = lax.rem(chunk, 2)
        cols = pl.ds(pl.multiple_of(chunk * width, width), width)
        return pltpu.make_async_copy(
            inner_buf.at[slot], gi_ref.at[placed, cols], chunk_sem.at[2 + slot]
        )

    slope_copy(0).start()
    if swap:
        pl.when(loader.first)(swap.start)

    @pl.when(loader.first)
    def _():
        sums_ref[...] = jnp.zeros_like(sums_ref)

    grad = ge_ref[...]
    unit = unit_ref[...]
    projected_low = (
        uinv_ref[...] * (grad - unit * jnp.sum(grad * unit, axis=-1, keepdims=True))
    ).astype(BF16)
    gp_ref[...] = projected_low
    loader.need(0)
    grad_final = mm(projected_low, wl[...], NT)
    normed = n2_ref[...].astype(F32)
    accumulate(sums_ref, ROW_G2, grad_final * normed)
    accumulate(sums_ref, ROW_S2, grad_final)
    scaled = grad_final * vec_row(vec_ref, ROW_G2)
    grad_second = r2_ref[:, :1] * (scaled - mean_row(scaled) - normed * mean_row(scaled * normed))
    outer_low = grad_second.astype(BF16)
    go_ref[...] = outer_low
    accumulate(sums_ref, ROW_B2, outer_low.astype(F32))
    acc_ref[...] = grad_second
    loader.need(1, 2)
    chunks = wi.shape[1] // width

    def chunk_body(chunk, carry):
        cols = pl.ds(pl.multiple_of(chunk * width, width), width)
        slot = lax.rem(chunk, 2)
        slope_copy(chunk).wait()
        pl.when(chunk < chunks - 1)(lambda: slope_copy(chunk + 1).start())
        pl.when(chunk >= 2)(lambda: inner_copy(chunk - 2).wait())
        grad_act = mm(go_ref[...], w2[cols, :], NT)
        inner = (grad_act * slope_buf[slot].astype(F32)).astype(BF16)
        inner_buf[slot] = inner
        inner_copy(chunk).start()
        sums_ref[pl.ds(ROW_BI + chunk, 1), :] += jnp.sum(
            inner.astype(F32), axis=0, keepdims=True
        )
        acc_ref[...] += mm(inner, wi[:, cols], NT)
        return carry

    lax.fori_loop(0, chunks, chunk_body, 0)
    grad_first = acc_ref[...]
    normed = n1_ref[...].astype(F32)
    accumulate(sums_ref, ROW_G1, grad_first * normed)
    accumulate(sums_ref, ROW_S1, grad_first)
    scaled = grad_first * vec_row(vec_ref, ROW_G1)
    hidden = r1_ref[:, :1] * (scaled - mean_row(scaled) - normed * mean_row(scaled * normed))
    gh_ref[...] = hidden
    low = hidden.astype(BF16)
    ga_ref[...] = low
    accumulate(sums_ref, ROW_BO, low.astype(F32))
    for back in (2, 1):
        inner_copy(chunks - back).wait()
    if swap:
        pl.when(pl.program_id(0) == pl.num_programs(0) - 1)(swap.finish)


def mlp_back(grad_embed, kept, vec, weights, blocks, total, offset, earlier, sent, sizes):
    own = grad_embed.shape[0]
    rows = own // blocks
    base = offset // rows
    _, _, _, _, wi, w2, wl = weights
    width, wide = wi.shape
    embed_width = wl.shape[1]

    def row_spec(columns):
        return pl.BlockSpec((rows, columns), lambda i: (base + i, 0))

    def own_spec(columns):
        return pl.BlockSpec((rows, columns), lambda i: (i, 0))

    args = [grad_embed] + [kept[index] for index in (13, 14, 10, 11, 9, 5, 6)]
    out_shapes = [
        jax.ShapeDtypeStruct((total, embed_width), BF16),
        jax.ShapeDtypeStruct((total, width), BF16),
        jax.ShapeDtypeStruct((total, wide), BF16),
        jax.ShapeDtypeStruct((own, width), F32),
        jax.ShapeDtypeStruct((total, width), BF16),
        jax.ShapeDtypeStruct((16, width), F32),
    ]
    shared = (0, 1, 2, 4)
    out_specs = [
        ANY if index == 2 else (row_spec if index in shared else own_spec)(out.shape[1])
        for index, out in enumerate(out_shapes[:5])
    ] + [pl.BlockSpec((16, width), lambda i: (0, 0))]
    aliased = [] if earlier is None else [earlier[index] for index in shared]
    sends, scratch, params = [], [], {}
    if sizes:
        sends = [sent]
        out_shapes.append(jax.ShapeDtypeStruct(sent.shape[1:], F32))
        out_specs.append(pl.BlockSpec(sent.shape[1:], lambda i: (0, 0)))
        scratch = push_scratch(*sent.shape)
        params = {"collective_id": 5, "has_side_effects": True}
    return pl.pallas_call(
        functools.partial(mlp_back_kernel, len(aliased), sizes, offset),
        out_shape=out_shapes,
        grid=(blocks,),
        in_specs=[
            ANY if index == 5 else own_spec(arg.shape[1]) for index, arg in enumerate(args)
        ]
        + [pl.BlockSpec(vec.shape, lambda i: (0, 0))]
        + [ANY] * (3 + len(aliased) + len(sends)),
        out_specs=out_specs,
        scratch_shapes=[pltpu.VMEM(weight.shape, BF16) for weight in (wl, w2, wi)]
        + [
            pltpu.SemaphoreType.DMA((3,)),
            pltpu.VMEM((rows, width), F32),
            pltpu.VMEM((2, rows, width), BF16),
            pltpu.VMEM((2, rows, width), BF16),
            pltpu.SemaphoreType.DMA((4,)),
        ]
        + scratch,
        input_output_aliases={12 + index: shared[index] for index in range(len(aliased))},
        compiler_params=pltpu.CompilerParams(vmem_limit_bytes=VMEM_LIMIT, **params),
        name="mlp_back_queries" if earlier is not None else "mlp_back_passages",
    )(*args, vec, wl, w2, wi, *aliased, *sends)


def attention_back_kernel(alias_count, *refs):
    ga_ref, gh_ref, att_ref, q_ref, k_ref, v_ref = refs[:6]
    sources = refs[6:10]
    refs = refs[10 + alias_count :]
    gqkv_ref, gx_ref, sums_ref = refs[:3]
    wo, wq, wk, wv, sem, gc_ref = refs[3:]
    loader = Loader(sources, (wo, wq, wk, wv), sem)
    loader.start()

    @pl.when(loader.first)
    def _():
        sums_ref[...] = jnp.zeros_like(sums_ref)

    rows, width = gh_ref.shape
    scale = HEAD_DIM ** (-0.5)
    loader.need(0)
    gc_ref[...] = mm(ga_ref[...], wo[...], NT).astype(BF16)
    low_half = lax.broadcasted_iota(jnp.int32, (rows, 128), 1) < HEAD_DIM

    def pair_body(pair, carry):
        cols = pl.ds(pl.multiple_of(pair * 128, 128), 128)
        q_pair, k_pair, v_pair, gc_pair = q_ref[:, cols], k_ref[:, cols], v_ref[:, cols], gc_ref[:, cols]
        parts = []
        for half in range(2):
            mask = low_half if half == 0 else jnp.logical_not(low_half)
            low = att_ref[0, 2 * pair + half]
            att = low.astype(F32)
            grad_att = mm(jnp.where(mask, gc_pair, jnp.zeros_like(gc_pair)), v_pair, NT)
            weighted = grad_att * att
            grad_logits = (weighted - att * jnp.sum(weighted, axis=-1, keepdims=True)).astype(BF16)
            parts.append(
                (
                    mm(grad_logits, k_pair) * scale,
                    mm(grad_logits, q_pair, TN),
                    mm(low, gc_pair, TN),
                )
            )
        for index in range(3):
            gqkv_ref[:, pl.ds(pl.multiple_of(index * width + pair * 128, 128), 128)] = jnp.where(
                low_half, parts[0][index], parts[1][index]
            ).astype(BF16)
        return carry

    lax.fori_loop(0, HEADS // 2, pair_body, 0)
    loader.need(1, 2, 3)
    grad_q, grad_k, grad_v = (
        gqkv_ref[:, :width],
        gqkv_ref[:, width : 2 * width],
        gqkv_ref[:, 2 * width :],
    )
    accumulate(sums_ref, 0, grad_q.astype(F32))
    accumulate(sums_ref, 1, grad_v.astype(F32))
    gx_ref[...] = (
        gh_ref[...]
        + mm(grad_q, wq[...], NT)
        + mm(grad_k, wk[...], NT)
        + mm(grad_v, wv[...], NT)
    )


def attention_back(attended, hidden, kept, weights, blocks, total, offset, earlier):
    own, width = hidden.shape
    rows = own // blocks
    base = offset // rows
    wq, wk, wv, wo = weights[:4]

    def row_spec(columns):
        return pl.BlockSpec((rows, columns), lambda i: (base + i, 0))

    def own_spec(columns):
        return pl.BlockSpec((rows, columns), lambda i: (i, 0))

    aliased = [] if earlier is None else [earlier]
    return pl.pallas_call(
        functools.partial(attention_back_kernel, len(aliased)),
        out_shape=(
            jax.ShapeDtypeStruct((total, 3 * width), BF16),
            jax.ShapeDtypeStruct((own, width), F32),
            jax.ShapeDtypeStruct((8, width), F32),
        ),
        grid=(blocks,),
        in_specs=[
            row_spec(width),
            own_spec(width),
            pl.BlockSpec((1, HEADS, rows, rows), lambda i: (i, 0, 0, 0)),
            own_spec(width),
            own_spec(width),
            own_spec(width),
        ]
        + [ANY] * (4 + len(aliased)),
        out_specs=(
            row_spec(3 * width),
            own_spec(width),
            pl.BlockSpec((8, width), lambda i: (0, 0)),
        ),
        scratch_shapes=[pltpu.VMEM(weight.shape, BF16) for weight in weights[:4]]
        + [pltpu.SemaphoreType.DMA((4,)), pltpu.VMEM((rows, width), BF16)],
        input_output_aliases={10: 0} if aliased else {},
        compiler_params=pltpu.CompilerParams(vmem_limit_bytes=VMEM_LIMIT),
        name="attention_back_queries" if aliased else "attention_back_passages",
    )(attended, hidden, kept[3], kept[0], kept[1], kept[2], wo, wq, wk, wv, *aliased)


def pack(vectors, width):
    count = sum(vector.shape[0] for vector in vectors)
    total = -(-count // (8 * width)) * 8 * width
    start, packed = 0, 0.0
    for vector in vectors:
        size = vector.shape[0]
        packed = packed + jnp.pad(vector.astype(F32), (start, total - start - size))
        start += size
    return packed.reshape(-1, width)


def share_kernel(n_wide, n_narrow, own_ref, all_ref, send_sem, recv_sem):
    me = lax.axis_index("narrow") * n_wide + lax.axis_index("wide")
    total = n_wide * n_narrow
    sems = (send_sem, recv_sem)

    def device(index):
        return (lax.rem(index, n_wide), index // n_wide)

    barrier = pltpu.get_barrier_semaphore()

    def signal(step, carry):
        pl.semaphore_signal(
            barrier, inc=1, device_id=device(lax.rem(me + step, total)), device_id_type=MESH
        )
        return carry

    def send(step, carry):
        target = device(lax.rem(me + step, total))
        remote(own_ref, all_ref.at[me], sems, step, target).start()
        return carry

    def wait(step, carry):
        source = lax.rem(me - step + total, total)
        copy = remote(own_ref, all_ref.at[source], sems, step, device(source))
        copy.wait_recv()
        copy.wait_send()
        return carry

    lax.fori_loop(1, total, signal, 0)
    all_ref[me] = own_ref[...]
    pl.semaphore_wait(barrier, total - 1)
    lax.fori_loop(1, total, send, 0)
    lax.fori_loop(1, total, wait, 0)


def share_scores(own, n_wide, n_narrow):
    total = n_wide * n_narrow
    return pl.pallas_call(
        functools.partial(share_kernel, n_wide, n_narrow),
        out_shape=jax.ShapeDtypeStruct((total,) + own.shape, own.dtype),
        in_specs=[pl.BlockSpec(memory_space=pltpu.VMEM)],
        out_specs=pl.BlockSpec(memory_space=pltpu.VMEM),
        scratch_shapes=[pltpu.SemaphoreType.DMA((total,))] * 2,
        compiler_params=pltpu.CompilerParams(collective_id=1, has_side_effects=True),
        name="share_scores",
    )(own)


def exchange_kernel(n_wide, n_narrow, g_ref, out_ref, *scratch):
    swap = Exchange(Chips(n_wide, n_narrow), g_ref, out_ref, scratch)
    swap.start()
    swap.push()
    swap.finish()


def exchange(grads, n_wide, n_narrow):
    chips, _, rows, width = grads.shape
    return pl.pallas_call(
        functools.partial(exchange_kernel, n_wide, n_narrow),
        out_shape=jax.ShapeDtypeStruct((rows, width), F32),
        in_specs=[ANY],
        out_specs=pl.BlockSpec(memory_space=pltpu.VMEM),
        scratch_shapes=exchange_scratch(chips, rows, width),
        compiler_params=pltpu.CompilerParams(
            collective_id=2, has_side_effects=True, vmem_limit_bytes=VMEM_LIMIT
        ),
        name="exchange_query_gradients",
    )(grads)


UNITS = (
    (0, 48, 0),
    (48, 48, 0),
    (96, 48, 48),
    (144, 48, 48),
    (192, 16, 96),
    (240, 16, 96),
    (208, 16, 112),
    (256, 16, 112),
    (224, 16, 128),
    (272, 32, 128),
)
EARLY = (0, 1, 2, 3)
LATE = (4, 5, 6, 7, 8, 9)
SHARE_ROWS = 304
LATE_B = 240
ROWS_A, ROWS_B = 144, 160
TILES = 9


def tail_kernel(n_z, part, *refs):
    act, go, first, gi, x_p, x_q, ctx, ga, final, gp = refs[:10]
    kept = (refs[10:15], refs[15:20])
    sources = refs[20:24]
    sums = refs[24:26]
    out_ref, gx_p, gx_q = refs[26:29]
    both, near, over_a, over_b, then_a, then_b, line, left_buf, right_buf, thin_buf = refs[29:39]
    wo, wq, wk, wv, att_buf, hidden, thin_hidden, grads, att_sums = refs[39:48]
    load_sem, weight_sem, block_sem, att_sem, gx_sem = refs[48:53]
    core_sems, one_sems, two_sems, line_sems, copy_sems = (
        refs[53 + 2 * index : 55 + 2 * index] for index in range(5)
    )
    wide, narrow = lax.axis_index("wide"), lax.axis_index("narrow")
    z, x = wide // 2, lax.rem(wide, 2)
    y, core = narrow // 2, lax.rem(narrow, 2)
    mate = (wide, y * 2 + 1 - core)
    over_y = (wide, (1 - y) * 2 + core)
    over_x = (z * 2 + 1 - x, narrow)
    total, width = go.shape
    p_rows = x_p.shape[0]
    held = both.at[core]

    def load(tile, wait):
        slot = lax.rem(tile, 2)
        block = pl.ds(pl.multiple_of(lax.rem(tile, 4) * width, width), width)

        def pair(source, other, target):
            for made in (
                pltpu.make_async_copy(source, left_buf.at[slot], load_sem.at[slot, 0]),
                pltpu.make_async_copy(other, target, load_sem.at[slot, 1]),
            ):
                if wait:
                    made.wait()
                else:
                    made.start()

        place = right_buf.at[slot]
        pl.when(tile < 4)(lambda: pair(act.at[:, block], go, place))
        pl.when(jnp.logical_and(tile >= 4, tile < 8))(lambda: pair(first, gi.at[:, block], place))
        pl.when(tile == 8)(lambda: pair(ctx, ga, place))
        pl.when(tile == TILES)(lambda: pair(final, gp, thin_buf))

    def rows_of(unit):
        start, count, _ = UNITS[unit]
        return pl.ds(start, count)

    def place_of(unit):
        _, count, place = UNITS[unit]
        return pl.ds(place, count)

    def core_copy(unit):
        rows = rows_of(unit)
        return remote(
            both.at[1 - core, :, :, :, rows], near.at[:, :, :, rows], core_sems, unit, mate
        )

    def late_copy(index):
        row_y, start, count = ((0, 2 * part, part + 16), (1, LATE_B, 64), (1, 2 * part, 48))[index]
        rows = pl.ds(start, count)
        return remote(
            both.at[1 - core, row_y, :, :, rows],
            near.at[row_y, :, :, rows],
            core_sems,
            len(EARLY) + index,
            mate,
        )

    def one_copy(unit):
        rows = rows_of(unit)
        place = place_of(unit)
        if unit % 2 == 0:
            return remote(
                held.at[1 - y, :, :, rows],
                over_a.at[:, :, place],
                one_sems,
                unit,
                over_y,
            )
        return remote(
            held.at[:, :, 1 - x, rows],
            over_b.at[:, :, place],
            one_sems,
            unit,
            over_x,
        )

    def two_copy(unit):
        rows = rows_of(unit)
        place = place_of(unit)
        if unit % 2 == 0:
            return remote(
                held.at[y, :, 1 - x, rows],
                then_a.at[:, place],
                two_sems,
                unit,
                over_x,
            )
        return remote(
            held.at[1 - y, :, x, rows],
            then_b.at[:, place],
            two_sems,
            unit,
            over_y,
        )

    def far_copy(unit, step):
        rows = rows_of(unit)
        target = lax.rem(z + step, n_z)
        return remote(
            held.at[y, target, x, rows],
            line.at[step - 1, rows],
            line_sems,
            unit * n_z + step,
            (target * 2 + x, narrow),
        )

    def share_copy(unit, step, arriving):
        rows = rows_of(unit)
        slots = (
            (y * 2 + 1 - core, (1 - y) * 2 + core, (1 - y) * 2 + 1 - core)
            if arriving
            else (narrow, narrow, (1 - y) * 2 + core)
        )
        block = out_ref.at[slots[step], rows]
        return remote(block, block, copy_sems, unit * 3 + step, over_y if step == 1 else mate)

    def add(target, extra):
        target[...] = target[...] + extra[...]

    def start_core(unit):
        core_copy(unit).start()

    def start_one(unit):
        rows = rows_of(unit)
        if unit in EARLY:
            core_copy(unit).wait_recv()

        def body(index, carry):
            row_y, rest = index // (n_z * 2), lax.rem(index, n_z * 2)
            at = (row_y, rest // 2, lax.rem(rest, 2), rows)
            add(held.at[at], near.at[at])
            return carry

        lax.fori_loop(0, 4 * n_z, body, 0)
        one_copy(unit).start()

    def start_two(unit):
        rows = rows_of(unit)
        place = place_of(unit)
        one_copy(unit).wait_recv()

        def body(index, carry):
            outer_at, inner_at = index // 2, lax.rem(index, 2)
            if unit % 2 == 0:
                add(
                    held.at[y, outer_at, inner_at, rows],
                    over_a.at[outer_at, inner_at, place],
                )
            else:
                add(
                    held.at[inner_at, outer_at, x, rows],
                    over_b.at[inner_at, outer_at, place],
                )
            return carry

        lax.fori_loop(0, 2 * n_z, body, 0)
        two_copy(unit).start()

    def start_far(unit):
        rows = rows_of(unit)
        place = place_of(unit)
        extra = then_a if unit % 2 == 0 else then_b
        two_copy(unit).wait_recv()

        def body(index, carry):
            add(held.at[y, index, x, rows], extra.at[index, place])
            return carry

        lax.fori_loop(0, n_z, body, 0)
        for step in range(1, n_z):
            far_copy(unit, step).start()

    def start_share(unit):
        rows = rows_of(unit)
        for step in range(1, n_z):
            far_copy(unit, step).wait_recv()
            add(held.at[y, z, x, rows], line.at[step - 1, rows])
        out_ref[narrow, rows] = both[core, y, z, x, rows]
        share_copy(unit, 1, False).start()
        share_copy(unit, 0, False).start()

    def forward(unit):
        share_copy(unit, 1, True).wait_recv()
        share_copy(unit, 2, False).start()

    def finish(unit):
        share_copy(unit, 0, True).wait_recv()
        share_copy(unit, 2, True).wait_recv()
        for step in range(3):
            share_copy(unit, step, False).wait_send()
        if unit in EARLY:
            core_copy(unit).wait_send()
        one_copy(unit).wait_send()
        two_copy(unit).wait_send()
        for step in range(1, n_z):
            far_copy(unit, step).wait_send()

    barrier = pltpu.get_barrier_semaphore()
    load(0, False)
    partners = [mate, over_y, over_x] + [
        (lax.rem(z + step, n_z) * 2 + x, narrow) for step in range(1, n_z)
    ]
    for device in partners:
        pl.semaphore_signal(barrier, inc=1, device_id=device, device_id_type=MESH)
    pl.semaphore_wait(barrier, len(partners))

    def put(kind, owner, half, made):
        rows = pl.ds(pl.multiple_of(kind * part, part), part)
        for index in range(4):
            both[lax.rem(owner, 2), owner // 2, 2 * half + index // 2, index % 2, rows] = made[
                index * part : (index + 1) * part
            ]

    def halves(left_ref, right_ref, store):
        def half_body(half, carry):
            cols = pl.ds(pl.multiple_of(half * 4 * part, 4 * part), 4 * part)
            store(half, mm(left_ref[:, cols], right_ref[...], TN).astype(BF16))
            return carry

        lax.fori_loop(0, 2, half_body, 0)

    def hooks(now, plan):
        for at, step, units in plan:

            @pl.when(now == at)
            def _(step=step, units=units):
                for unit in units:
                    step(unit)

    def tile_body(tile, carry):
        slot = lax.rem(tile, 2)
        load(tile, True)
        load(tile + 1, False)
        kind = tile // 4
        owner = jnp.where(tile == 8, 3, lax.rem(tile, 4))

        def store(half, made):
            @pl.when(kind == 0)
            def _():
                for index in range(4):
                    both[index % 2, index // 2, owner, half, :part] = made[
                        index * part : (index + 1) * part
                    ]

            pl.when(kind > 0)(lambda: put(kind, owner, half, made))

        halves(left_buf.at[slot], right_buf.at[slot], store)
        hooks(
            tile,
            (
                (3, start_core, (0, 1)),
                (5, start_one, (0,)),
                (6, start_one, (1,)),
                (7, start_core, (2, 3)),
            ),
        )
        return carry

    def hidden_of(block):
        return thin_hidden if blocks[block][2] else hidden.at[block]

    def block_copies(block):
        rows, base, source = blocks[block]
        q, k, v, gh, _ = kept[source]
        buf = left_buf if block % 2 == 0 else right_buf
        own = pl.ds(base - (p_rows if source else 0), rows)
        low, high = pl.ds(0, rows), pl.ds(span, rows)
        pairs = (
            (q.at[own], buf.at[0, low]),
            (k.at[own], buf.at[0, high]),
            (v.at[own], buf.at[1, low]),
            (ga.at[pl.ds(base, rows)], buf.at[1, high]),
            (gh.at[own], hidden_of(block)),
        )
        return [
            pltpu.make_async_copy(*pair, block_sem.at[block % 2, index])
            for index, pair in enumerate(pairs)
        ]

    def gx_copy(block):
        rows, base, source = blocks[block]
        target = gx_q if source else gx_p
        own = pl.ds(base - (p_rows if source else 0), rows)
        return pltpu.make_async_copy(hidden_of(block), target.at[own], gx_sem.at[block])

    def states(block):
        rows, base, _ = blocks[block]
        own = pl.ds(base, rows)
        hidden_of(block)[...] += (
            mm(grads[0, own], wq[...], NT)
            + mm(grads[1, own], wk[...], NT)
            + mm(grads[2, own], wv[...], NT)
        )
        gx_copy(block).start()

    def attention(block, plan):
        rows, base, source = blocks[block]
        buf = left_buf if block % 2 == 0 else right_buf
        low, high, own = pl.ds(0, rows), pl.ds(span, rows), pl.ds(base, rows)
        att = kept[source][4]
        q_ref, k_ref, v_ref, ga_ref = (
            buf.at[0, low],
            buf.at[0, high],
            buf.at[1, low],
            buf.at[1, high],
        )
        entry = 0 if source else block
        size = pl.ds(0, rows)

        def att_copy(pair):
            slot = lax.rem(pair, 2)
            return pltpu.make_async_copy(
                att.at[entry, pl.ds(2 * pair, 2)],
                att_buf.at[slot, :, size, size],
                att_sem.at[slot],
            )

        att_copy(0).start()
        for copy in block_copies(block):
            copy.wait()
        grads[2, own] = mm(ga_ref[...], wo[...], NT).astype(BF16)
        low_half = lax.broadcasted_iota(jnp.int32, (rows, 128), 1) < HEAD_DIM
        scale = HEAD_DIM ** (-0.5)

        def pair_body(pair, carry):
            cols = pl.ds(pl.multiple_of(pair * 128, 128), 128)
            slot = lax.rem(pair, 2)
            att_copy(pair).wait()
            pl.when(pair < HEADS // 2 - 1)(lambda: att_copy(pair + 1).start())
            q_pair, k_pair, v_pair = q_ref[:, cols], k_ref[:, cols], v_ref[:, cols]
            gc_pair = grads[2, own, cols]
            parts = []
            for half in range(2):
                mask = low_half if half == 0 else jnp.logical_not(low_half)
                low_att = att_buf[slot, half, size, size]
                wide_att = low_att.astype(F32)
                grad_att = mm(jnp.where(mask, gc_pair, jnp.zeros_like(gc_pair)), v_pair, NT)
                weighted = grad_att * wide_att
                grad_logits = (
                    weighted - wide_att * jnp.sum(weighted, axis=-1, keepdims=True)
                ).astype(BF16)
                parts.append(
                    (
                        mm(grad_logits, k_pair) * scale,
                        mm(grad_logits, q_pair, TN),
                        mm(low_att, gc_pair, TN),
                    )
                )
            for index in range(3):
                grads[index, own, cols] = jnp.where(
                    low_half, parts[0][index], parts[1][index]
                ).astype(BF16)
            hooks(pair, plan)
            return carry

        lax.fori_loop(0, HEADS // 2, pair_body, 0)
        accumulate(att_sums, 0, grads[0, own].astype(F32))
        accumulate(att_sums, 1, grads[2, own].astype(F32))

    def weight_copies():
        return [
            pltpu.make_async_copy(source, target, weight_sem.at[index])
            for index, (source, target) in enumerate(zip(sources, (wo, wq, wk, wv)))
        ]

    span = kept[0][4].shape[-1]
    blocks = [(span, base, 0) for base in range(0, p_rows, span)] + [(x_q.shape[0], p_rows, 1)]
    for copy in weight_copies():
        copy.start()
    att_sums[...] = jnp.zeros_like(att_sums)
    lax.fori_loop(0, TILES, tile_body, 0)
    load(TILES, True)
    slot = TILES % 2
    made = mm(left_buf[slot], thin_buf[...], TN).astype(BF16)
    for copy in block_copies(0):
        copy.start()
    lanes = thin_buf.shape[1]
    last = pl.ds(3 * part, 16)
    for shard in range(2 * n_z):
        for block in range(width // lanes):
            row = shard * part + block * 16
            both[0, 0, shard // 2, shard % 2, last, block * lanes : (block + 1) * lanes] = made[
                row : row + 16
            ]
    for copy in weight_copies():
        copy.wait()
    for copy in block_copies(1):
        copy.start()
    attention(0, ((0, start_one, (2, 3)), (3, start_two, (0, 1))))
    for copy in block_copies(2):
        copy.start()
    attention(
        1,
        (
            (0, start_far, (0, 1)),
            (2, start_two, (2, 3)),
            (5, start_far, (2, 3)),
        ),
    )
    x_copies = [
        pltpu.make_async_copy(x_p, right_buf.at[0, pl.ds(0, p_rows)], load_sem.at[0, 0]),
        pltpu.make_async_copy(
            x_q, right_buf.at[0, pl.ds(p_rows, total - p_rows)], load_sem.at[0, 1]
        ),
    ]
    for copy in x_copies:
        copy.start()
    attention(2, ((2, start_share, (0, 1)),))
    top = sums[0][:8] + sums[1][:8] + att_sums[...]
    tail = jnp.concatenate([top, sums[0][8:] + sums[1][8:]], axis=0).astype(BF16)
    for shard in range(2 * n_z):
        at_z, at_x = shard // 2, shard % 2
        both[1, 0, at_z, at_x, last] = tail
        both[0, 1, at_z, at_x, last] = jnp.zeros_like(tail)
        both[1, 1, at_z, at_x, last] = jnp.zeros_like(tail)
    for copy in x_copies:
        copy.wait()

    def late_body(tile, carry):
        halves(right_buf.at[0], grads.at[tile], lambda half, made: put(2, tile, half, made))
        pl.when(tile == 1)(lambda: late_copy(0).start())
        return carry

    lax.fori_loop(0, 3, late_body, 0)

    def start_late(index):
        late_copy(index).start()

    def wait_late(index):
        late_copy(index).wait_recv()

    def end_late(index):
        late_copy(index).wait_send()

    for step, units in (
        (start_late, (1, 2)),
        (start_share, (2, 3)),
        (wait_late, (0, 1)),
        (start_one, (5, 7, 9)),
        (wait_late, (2,)),
        (start_one, (4, 6, 8)),
        (forward, EARLY),
        (states, (0,)),
        (start_two, (5, 4)),
        (states, (1,)),
        (start_two, (7, 6)),
        (start_far, (5, 4)),
        (states, (2,)),
        (start_two, (8,)),
        (start_far, (7, 6)),
        (start_two, (9,)),
        (start_far, (8,)),
        (start_share, (5, 4)),
        (start_far, (9,)),
        (start_share, (7, 6, 8)),
        (forward, (5, 4, 7, 6)),
        (start_share, (9,)),
        (forward, (8, 9)),
        (finish, EARLY + LATE),
        (end_late, (0, 1, 2)),
        (lambda block: gx_copy(block).wait(), range(len(blocks))),
    ):
        for unit in units:
            step(unit)


def backward_tail(arrays, passage_kept, query_kept, weights, sums, n_wide):
    n_z = n_wide // 2
    go, x_p, x_q, gp = arrays[1], arrays[4], arrays[5], arrays[9]
    total, width = go.shape
    part = width // n_wide
    units = len(UNITS)
    span = passage_kept[4].shape[-1]
    sem = pltpu.SemaphoreType.DMA
    vmem = pl.BlockSpec(memory_space=pltpu.VMEM)
    return pl.pallas_call(
        functools.partial(tail_kernel, n_z, part),
        out_shape=(
            jax.ShapeDtypeStruct((4, SHARE_ROWS, width), BF16),
            jax.ShapeDtypeStruct(x_p.shape, F32),
            jax.ShapeDtypeStruct(x_q.shape, F32),
        ),
        in_specs=[ANY] * 24 + [vmem] * 2,
        out_specs=(vmem, ANY, ANY),
        scratch_shapes=[
            pltpu.VMEM((2, 2, n_z, 2, SHARE_ROWS, width), BF16),
            pltpu.VMEM((2, n_z, 2, SHARE_ROWS, width), BF16),
            pltpu.VMEM((n_z, 2, ROWS_A, width), BF16),
            pltpu.VMEM((2, n_z, ROWS_B, width), BF16),
            pltpu.VMEM((n_z, ROWS_A, width), BF16),
            pltpu.VMEM((n_z, ROWS_B, width), BF16),
            pltpu.VMEM((n_z - 1, SHARE_ROWS, width), BF16),
            pltpu.VMEM((2, total, width), BF16),
            pltpu.VMEM((2, total, width), BF16),
            pltpu.VMEM(gp.shape, BF16),
        ]
        + [pltpu.VMEM((width, width), BF16)] * 4
        + [
            pltpu.VMEM((2, 2, span, span), BF16),
            pltpu.VMEM((2, span, width), F32),
            pltpu.VMEM(x_q.shape, F32),
            pltpu.VMEM((3, total, width), BF16),
            pltpu.VMEM((8, width), F32),
            sem((2, 2)),
            sem((4,)),
            sem((2, 5)),
            sem((2,)),
            sem((3,)),
        ]
        + [sem((units,))] * 6
        + [sem((units * n_z,))] * 2
        + [sem((units * 3,))] * 2,
        compiler_params=pltpu.CompilerParams(
            collective_id=3, has_side_effects=True, vmem_limit_bytes=VMEM_LIMIT
        ),
        name="backward_tail",
    )(*arrays, *passage_kept, *query_kept, *weights, *sums)


def unpack_kernel(part, sums_ref, gx_p, gx_q, *refs):
    q_ref, k_ref, v_ref, o_ref, inner_ref, outer_ref, thin_ref, vec_ref, to_p, to_q = refs[:10]
    buf, in_sem, out_sem = refs[10:]
    width = q_ref.shape[1]
    rows = gx_q.shape[0]
    pieces = []
    for source, target in ((gx_p, to_p), (gx_q, to_q)):
        for start in range(0, source.shape[0], rows):
            at = pl.ds(start, rows)
            slot = len(pieces)
            pieces.append(
                (
                    pltpu.make_async_copy(source.at[at], buf.at[slot], in_sem.at[slot]),
                    pltpu.make_async_copy(buf.at[slot], target.at[at], out_sem.at[slot]),
                )
            )
    for arrive, _ in pieces:
        arrive.start()
    lanes = thin_ref.shape[1]
    for owner, ref in enumerate((q_ref, k_ref, v_ref, o_ref)):
        ref[...] = sums_ref[owner, 2 * part : 3 * part].astype(F32)
        inner_ref[:, owner * width : (owner + 1) * width] = sums_ref[
            owner, part : 2 * part
        ].astype(F32)
        outer_ref[owner * part : (owner + 1) * part] = sums_ref[owner, :part].astype(F32)
        pieces[owner][0].wait()
        pieces[owner][1].start()
    for arrive, leave in pieces[4:]:
        arrive.wait()
        leave.start()
    tail = sums_ref[0, 3 * part :].astype(F32)
    for block in range(width // lanes):
        thin_ref[block * 16 : (block + 1) * 16] = tail[:, block * lanes : (block + 1) * lanes]
    vec_ref[...] = sums_ref[1, 3 * part :].astype(F32)
    for _, leave in pieces:
        leave.wait()


def unpack(summed, grad_p, grad_q, part, embed_width):
    width = summed.shape[-1]
    rows = grad_q.shape[0]
    count = grad_p.shape[0] // rows + 1
    sem = pltpu.SemaphoreType.DMA
    vmem = pl.BlockSpec(memory_space=pltpu.VMEM)
    shapes = [(part, width)] * 4 + [
        (part, 4 * width),
        (4 * part, width),
        (part, embed_width),
        (16, width),
        grad_p.shape,
        grad_q.shape,
    ]
    return pl.pallas_call(
        functools.partial(unpack_kernel, part),
        out_shape=[jax.ShapeDtypeStruct(shape, F32) for shape in shapes],
        in_specs=[vmem, ANY, ANY],
        out_specs=[vmem] * (len(shapes) - 2) + [ANY] * 2,
        scratch_shapes=[pltpu.VMEM((count, rows, width), F32), sem((count,)), sem((count,))],
        compiler_params=pltpu.CompilerParams(vmem_limit_bytes=VMEM_LIMIT),
        name="unpack_gradients",
    )(summed, grad_p, grad_q)


def outer(left, right):
    return lax.dot_general(left, right, TN, preferred_element_type=F32)


def local(
    query_states,
    passage_states,
    lengths,
    positives,
    query_weight,
    query_bias,
    key_weight,
    value_weight,
    value_bias,
    out_weight,
    out_bias,
    first_gain,
    first_shift,
    inner_weight,
    inner_bias,
    outer_weight,
    outer_bias,
    second_gain,
    second_shift,
    linear_weight,
):
    everyone = ("wide", "narrow")
    n_wide = lax.axis_size("wide")
    n_narrow = lax.axis_size("narrow")
    wide_index = lax.axis_index("wide")
    narrow_index = lax.axis_index("narrow")
    micro, own_queries, query_len, width = query_states.shape
    own_passages, slots = passage_states.shape[1:3]
    weights = (
        query_weight,
        key_weight,
        value_weight,
        out_weight,
        inner_weight,
        outer_weight,
        linear_weight,
    )
    embed_width = linear_weight.shape[1]
    vec = pack(
        (
            query_bias,
            value_bias,
            out_bias,
            first_gain,
            first_shift,
            outer_bias,
            second_gain,
            second_shift,
            inner_bias,
        ),
        width,
    )
    own_index = narrow_index * n_wide + wide_index
    own_lengths = lax.dynamic_slice_in_dim(lengths, own_index * own_passages, own_passages, axis=1)
    lens = own_lengths.reshape(-1)
    x_query = query_states.reshape(-1, width)
    x_passage = passage_states.reshape(-1, width)
    query_rows, passage_rows = x_query.shape[0], x_passage.shape[0]
    total = query_rows + passage_rows
    kept_q = encode(
        x_query, lens, vec, weights, 1, query_len, total, passage_rows, None, None
    )
    sizes = (n_wide, n_narrow)
    kept_p = encode(
        x_passage, lens, vec, weights, micro * own_passages, 0, total, 0, kept_q, sizes
    )
    queries = kept_p[16].reshape(n_wide * n_narrow, micro, -1, embed_width)
    ctx, first_low, act, final_low = (kept_p[index] for index in (4, 7, 8, 12))
    passages = kept_p[15].reshape(micro * own_passages, slots, embed_width)
    row_count = own_queries * n_narrow
    together = queries.size * slots <= 8 * 1024 * 1024 * embed_width
    if together:
        full, loss, grad_passage, grad_query = match(
            queries, passages, lens, positives, n_wide, n_narrow, query_len
        )
        block = lax.dynamic_slice_in_dim(full, narrow_index * n_wide, n_wide, axis=0)
        block = lax.dynamic_slice_in_dim(
            block[:, :own_queries].reshape(n_wide, own_queries, micro, -1),
            wide_index * n_narrow,
            n_narrow,
            axis=3,
        )
        scores = block.transpose(2, 3, 1, 0).reshape(micro, row_count, n_wide)
        losses = lax.dynamic_slice_in_dim(
            loss[:own_queries].reshape(own_queries, micro, -1),
            wide_index * n_narrow,
            n_narrow,
            axis=2,
        )
        losses = losses.transpose(1, 2, 0).reshape(micro, row_count)
    else:
        e, z = similarity(queries, passages, lens)
        best = SHARP + jnp.log(z)
        own_scores = jnp.sum(best.reshape(micro, -1, query_len), axis=-1) / SHARP
        full = share_scores(own_scores, n_wide, n_narrow)
        row_total = jax.nn.logsumexp(full, axis=0)
        passage_ids = jnp.arange(full.shape[0], dtype=jnp.int32)
        picked = jnp.sum(
            jnp.where(passage_ids[:, None, None] == positives[None], full, 0.0), axis=0
        )
        row_count = own_queries * n_narrow
        losses = lax.dynamic_slice_in_dim(row_total - picked, wide_index * row_count, row_count, axis=1)
        block = lax.dynamic_slice(
            full,
            (narrow_index * n_wide, 0, wide_index * row_count),
            (n_wide, micro, row_count),
        )
        scores = jnp.transpose(block, (1, 2, 0))
        grads = jnp.exp(own_scores - row_total) - (positives == own_index).astype(F32)
        token_weights = jnp.repeat(grads, query_len, axis=1).reshape(z.shape) / z
        grad_passage, grad_query = similarity_back(e, token_weights, queries, passages)
        grad_query = grad_query.reshape(-1, 2, query_rows, embed_width)
    grad_passage = grad_passage.reshape(passage_rows, embed_width)
    back_p = mlp_back(
        grad_passage,
        kept_p,
        vec,
        weights,
        micro * own_passages,
        total,
        0,
        None,
        grad_query if together else None,
        sizes if together else None,
    )
    grad_query = back_p[6] if together else exchange(grad_query, n_wide, n_narrow)
    back_q = mlp_back(
        grad_query, kept_q, vec, weights, 1, total, passage_rows, back_p, None, None
    )
    gp, go, gi, _, ga, sums_q = back_q[:6]
    part = width // n_wide
    if part == 96 and n_narrow == 4 and micro * own_passages == 2 and act.shape[1] == 4 * width:
        summed, grad_p, grad_q = backward_tail(
            (act, go, first_low, gi, x_passage, x_query, ctx, ga, final_low, gp),
            (*kept_p[:3], back_p[3], kept_p[3]),
            (*kept_q[:3], back_q[3], kept_q[3]),
            (out_weight, query_weight, key_weight, value_weight),
            (back_p[5], sums_q),
            n_wide,
        )
        r_q, r_k, r_v, r_out, r_inner, r_outer, r_linear, vectors, grad_p, grad_q = unpack(
            summed, grad_p, grad_q, part, embed_width
        )
        own = lax.dynamic_slice_in_dim(vectors[:8], wide_index * part, part, axis=1)
        v_q, v_v, v_o, v_g1, v_s1, v_2, v_g2, v_s2 = (
            own[row] for row in (0, 1, ROW_BO, ROW_G1, ROW_S1, ROW_B2, ROW_G2, ROW_S2)
        )
        v_i = lax.dynamic_slice_in_dim(
            vectors[ROW_BI : ROW_BI + 4].reshape(-1), wide_index * 4 * part, 4 * part
        )
    else:
        att_p = attention_back(
            ga, back_p[3], kept_p, weights, micro * own_passages, total, 0, None
        )
        att_q = attention_back(ga, back_q[3], kept_q, weights, 1, total, passage_rows, att_p[0])
        gqkv, grad_p, grad_q = att_q[0], att_p[1], att_q[1]

        def reduce(value):
            piece = lax.psum_scatter(value.astype(BF16), everyone, scatter_dimension=0, tiled=True)
            return lax.all_gather(piece, "narrow", axis=0, tiled=True).astype(F32)

        def vector(rows):
            flat = rows.reshape(-1)
            share = flat.shape[0] // n_wide
            return lax.dynamic_slice_in_dim(flat, wide_index * share, share)

        sums = jnp.concatenate([back_p[5] + sums_q, att_p[2] + att_q[2]], axis=0)
        sums = lax.psum(sums, everyone)
        x_all = jnp.concatenate([x_passage, x_query], axis=0)
        pairs = ((act, go), (first_low, gi), (final_low, gp), (ctx, ga), (x_all, gqkv))
        r_outer, r_inner, r_linear, r_out, r_qkv = (
            reduce(outer(*pair)) for pair in pairs
        )
        r_q, r_k, r_v = (r_qkv[:, index * width : (index + 1) * width] for index in range(3))
        v_q, v_v, v_o, v_g1, v_s1, v_2, v_g2, v_s2 = (
            vector(sums[pick])
            for pick in (16, 17, ROW_BO, ROW_G1, ROW_S1, ROW_B2, ROW_G2, ROW_S2)
        )
        v_i = vector(sums[ROW_BI : ROW_BI + 4])
    return (
        scores,
        losses,
        grad_q.reshape(query_states.shape),
        grad_p.reshape(passage_states.shape),
        r_q,
        v_q,
        r_k,
        r_v,
        v_v,
        r_out,
        v_o,
        v_g1,
        v_s1,
        r_inner,
        v_i,
        r_outer,
        v_2,
        v_g2,
        v_s2,
        r_linear,
    )


def solution(mesh):
    return jax.shard_map(
        local,
        mesh=mesh,
        in_specs=(
            P(None, ("wide", "narrow"), None, None),
            P(None, ("narrow", "wide"), None, None),
        )
        + (P(),) * 18,
        out_specs=(
            P(None, "wide", "narrow"),
            P(None, "wide"),
            P(None, ("wide", "narrow"), None, None),
            P(None, ("narrow", "wide"), None, None),
            P("wide", None),
            P("wide"),
            P("wide", None),
            P("wide", None),
            P("wide"),
            P("wide", None),
            P("wide"),
            P("wide"),
            P("wide"),
            P("wide", None),
            P("wide"),
            P("wide", None),
            P("wide"),
            P("wide"),
            P("wide"),
            P("wide", None),
        ),
        check_vma=False,
    )
```

```python
import functools

import jax
import jax.numpy as jnp
from jax import lax
from jax.experimental import pallas as pl
from jax.experimental.pallas import tpu as pltpu
from jax.sharding import PartitionSpec as P

HEADS = 12
HEAD_DIM = 64
LOG2E = 1.4426950408889634
SHARP = 16.0
LAYER_EPS = 1e-12
NORM_EPS = 1e-06
MASKED = -1e30
SLOPE_CONST = 0.3989422804014327
ROOT_HALF = 0.7071067811865476
BF16 = jnp.bfloat16
F32 = jnp.float32
VMEM_LIMIT = 62 * 1024 * 1024

NN = (((1,), (0,)), ((), ()))
NT = (((1,), (1,)), ((), ()))
TN = (((0,), (0,)), ((), ()))


def mm(left, right, dims=NN):
    return lax.dot_general(left, right, dims, preferred_element_type=F32)


ANY = pl.BlockSpec(memory_space=pl.ANY)

ROW_BQ, ROW_BV, ROW_BO, ROW_G1, ROW_S1, ROW_B2, ROW_G2, ROW_S2, ROW_BI = range(9)


def vec_row(vec_ref, row):
    return vec_ref[row : row + 1, :]


def mean_row(value):
    return jnp.sum(value, axis=-1, keepdims=True) * (1.0 / value.shape[-1])


class Loader:
    def __init__(self, sources, targets, sem):
        self.copies = [
            pltpu.make_async_copy(source, target, sem.at[index])
            for index, (source, target) in enumerate(zip(sources, targets))
        ]
        self.first = pl.program_id(0) == 0

    def start(self):
        @pl.when(self.first)
        def _():
            for copy in self.copies:
                copy.start()

    def need(self, *indices):
        @pl.when(self.first)
        def _():
            for index in indices:
                self.copies[index].wait()


MESH = pl.DeviceIdType.MESH


def remote(source, target, sems, index, device):
    return pltpu.make_async_remote_copy(
        src_ref=source,
        dst_ref=target,
        send_sem=sems[0].at[index],
        recv_sem=sems[1].at[index],
        device_id=device,
        device_id_type=MESH,
    )


class Chips:
    def __init__(self, n_wide, n_narrow):
        self.wide, self.narrow = lax.axis_index("wide"), lax.axis_index("narrow")
        self.core = lax.rem(self.narrow, 2)
        self.rows = n_narrow // 2
        self.count = n_wide * self.rows
        self.me = self.wide * self.rows + self.narrow // 2
        self.mate = (self.wide, self.narrow + 1 - 2 * self.core)

    def at(self, step):
        return lax.rem(self.me + step + self.count, self.count)

    def device(self, chip):
        return (chip // self.rows, lax.rem(chip, self.rows) * 2 + self.core)

    def loop(self, body):
        def step_body(step, carry):
            body(step)
            return carry

        lax.fori_loop(1, self.count, step_body, 0)

    def barrier(self):
        barrier = pltpu.get_barrier_semaphore()

        def signal(step):
            pl.semaphore_signal(
                barrier, inc=1, device_id=self.device(self.at(step)), device_id_type=MESH
            )

        pl.semaphore_signal(barrier, inc=1, device_id=self.mate, device_id_type=MESH)
        self.loop(signal)
        pl.semaphore_wait(barrier, self.count)


class Gather:
    def __init__(self, chips, own, out, sems):
        self.chips, self.own, self.out = chips, own, out
        self.far, self.pair, self.local = sems[:2], sems[2:4], sems[4]

    def far_copy(self, step, chip):
        slot = self.out.at[chip, self.chips.core]
        return remote(self.own, slot, self.far, step, self.chips.device(self.chips.at(step)))

    def mate_copy(self, core):
        block = self.out.at[:, core]
        return remote(block, block, self.pair, 0, self.chips.mate)

    def local_copy(self):
        slot = self.out.at[self.chips.me, self.chips.core]
        return pltpu.make_async_copy(self.own, slot, self.local.at[0])

    def start(self):
        self.local_copy().start()
        self.chips.barrier()
        self.chips.loop(lambda step: self.far_copy(step, self.chips.me).start())

    def forward(self):
        self.local_copy().wait()
        self.chips.loop(lambda step: self.far_copy(step, self.chips.at(-step)).wait_recv())
        self.mate_copy(self.chips.core).start()

    def finish(self):
        self.chips.loop(lambda step: self.far_copy(step, self.chips.me).wait_send())
        self.mate_copy(1 - self.chips.core).wait_recv()
        self.mate_copy(self.chips.core).wait_send()


class Exchange:
    def __init__(self, chips, grads, out, scratch):
        self.chips, self.grads, self.out = chips, grads, out
        self.half, self.arrived, self.inbox = scratch[:3]
        self.pair, self.far, self.local = scratch[3:5], scratch[5:7], scratch[7]

    def pair_copy(self):
        away = self.grads.at[:, 1 - self.chips.core]
        return remote(away, self.arrived, self.pair, 0, self.chips.mate)

    def local_copy(self):
        mine = self.grads.at[:, self.chips.core]
        return pltpu.make_async_copy(mine, self.half, self.local.at[0])

    def far_copy(self, step):
        chip = self.chips.at(step)
        return remote(
            self.half.at[chip], self.inbox.at[step], self.far, step, self.chips.device(chip)
        )

    def start(self):
        self.local_copy().start()
        self.chips.barrier()
        self.pair_copy().start()

    def push(self):
        self.local_copy().wait()
        self.pair_copy().wait_recv()

        def add(step):
            chip = self.chips.at(step)
            total = self.half[chip].astype(F32) + self.arrived[chip].astype(F32)
            self.half[chip] = total.astype(BF16)
            self.far_copy(step).start()

        self.chips.loop(add)
        me = self.chips.me
        self.out[...] = self.half[me].astype(F32) + self.arrived[me].astype(F32)

    def finish(self):
        def collect(step):
            copy = self.far_copy(step)
            copy.wait_recv()
            copy.wait_send()
            self.out[...] += self.inbox[step].astype(F32)

        self.chips.loop(collect)
        self.pair_copy().wait_send()


class Push:
    def __init__(self, chips, half, out, scratch):
        self.chips, self.half, self.out = chips, half, out
        self.inbox, self.far, self.own = scratch[0], scratch[1:3], scratch[3]

    def far_copy(self, step):
        chip = self.chips.at(step)
        return remote(
            self.half.at[chip], self.inbox.at[step], self.far, step, self.chips.device(chip)
        )

    def own_copy(self):
        return pltpu.make_async_copy(
            self.half.at[self.chips.me], self.inbox.at[0], self.own.at[0]
        )

    def start(self):
        self.own_copy().start()
        self.chips.barrier()
        self.chips.loop(lambda step: self.far_copy(step).start())

    def finish(self):
        self.own_copy().wait()
        self.out[...] = self.inbox[0].astype(F32)

        def collect(step):
            copy = self.far_copy(step)
            copy.wait_recv()
            copy.wait_send()
            self.out[...] += self.inbox[step].astype(F32)

        self.chips.loop(collect)


def push_scratch(chips, rows, width):
    sem = pltpu.SemaphoreType.DMA
    return [pltpu.VMEM((chips, rows, width), BF16), sem((chips,)), sem((chips,)), sem((1,))]


def exchange_scratch(chips, rows, width):
    sem = pltpu.SemaphoreType.DMA
    return [pltpu.VMEM((chips, rows, width), BF16)] * 3 + [
        sem((1,)),
        sem((1,)),
        sem((chips,)),
        sem((chips,)),
        sem((1,)),
    ]


def fwd_kernel(grouped, alias_count, sizes, offset, *refs):
    lens_ref, x_ref, vec_ref = refs[:3]
    sources = refs[3:10]
    refs = refs[10 + alias_count :]
    gather = None
    if sizes:
        gather = Gather(Chips(*sizes), refs[0], refs[17], refs[-5:])
        refs = refs[1:17] + refs[18:-5]
    (
        q_ref,
        k_ref,
        v_ref,
        att_ref,
        ctx_ref,
        n1_ref,
        r1_ref,
        first_ref,
        act_ref,
        slope_ref,
        n2_ref,
        r2_ref,
        final_ref,
        unit_ref,
        uinv_ref,
        embed_ref,
    ) = refs[:16]
    wq, wk, wv, wo, wi, w2, wl, sem, acc_ref, att_buf, act_buf, slope_buf, out_sem = refs[16:]
    loader = Loader(sources, (wq, wk, wv, wo, wi, w2, wl), sem)
    block_id = pl.program_id(0)
    loader.start()
    if gather:
        last = pl.program_id(0) == pl.num_programs(0) - 1
        pl.when(loader.first)(gather.start)
    rows = x_ref.shape[0]
    x = x_ref[...]
    scale = HEAD_DIM ** (-0.5)
    loader.need(0)
    q_ref[...] = ((mm(x, wq[...]) + vec_row(vec_ref, ROW_BQ)).astype(BF16) * scale).astype(BF16)
    loader.need(1)
    k_ref[...] = mm(x, wk[...]).astype(BF16)
    loader.need(2)
    v_ref[...] = (mm(x, wv[...]) + vec_row(vec_ref, ROW_BV)).astype(BF16)
    if grouped:
        valid = (
            lax.broadcasted_iota(jnp.int32, (rows, rows), 0) // grouped
            == lax.broadcasted_iota(jnp.int32, (rows, rows), 1) // grouped
        )
    else:
        length = lens_ref[pl.program_id(0)]
        valid = lax.broadcasted_iota(jnp.int32, (1, rows), 1) < length
    bias = jnp.where(valid, 0.0, MASKED)
    low_half = lax.broadcasted_iota(jnp.int32, (rows, 128), 1) < HEAD_DIM

    def att_copy(pair):
        slot = lax.rem(pair, 2)
        return pltpu.make_async_copy(
            att_buf.at[slot], att_ref.at[block_id, pl.ds(2 * pair, 2)], out_sem.at[slot]
        )

    def pair_body(pair, carry):
        cols = pl.ds(pl.multiple_of(pair * 128, 128), 128)
        slot = lax.rem(pair, 2)
        pl.when(pair >= 2)(lambda: att_copy(pair - 2).wait())
        q_pair, k_pair, v_pair = q_ref[:, cols], k_ref[:, cols], v_ref[:, cols]
        parts = []
        for half in range(2):
            mask = low_half if half == 0 else jnp.logical_not(low_half)
            logits = mm(jnp.where(mask, q_pair, jnp.zeros_like(q_pair)), k_pair, NT) + bias
            peak = jnp.max(logits, axis=-1, keepdims=True)
            e = jnp.exp(logits - peak)
            inv = 1.0 / jnp.sum(e, axis=-1, keepdims=True)
            low = (e * inv).astype(BF16)
            att_buf[slot, half] = low
            parts.append(mm(low, v_pair))
        att_copy(pair).start()
        ctx_ref[:, cols] = jnp.where(low_half, parts[0], parts[1]).astype(BF16)
        return carry

    lax.fori_loop(0, HEADS // 2, pair_body, 0)
    if gather:
        pl.when(last)(gather.forward)
    loader.need(3)
    field = x.astype(F32) + (mm(ctx_ref[...], wo[...]) + vec_row(vec_ref, ROW_BO))
    center = field - mean_row(field)
    inverse = lax.rsqrt(mean_row(center * center) + LAYER_EPS)
    normed = center * inverse
    n1_ref[...] = normed.astype(BF16)
    r1_ref[...] = jnp.broadcast_to(inverse, r1_ref.shape)
    first = normed * vec_row(vec_ref, ROW_G1) + vec_row(vec_ref, ROW_S1)
    first_ref[...] = first.astype(BF16)
    acc_ref[...] = first + vec_row(vec_ref, ROW_B2)
    loader.need(4, 5)
    width = x.shape[1]

    base = block_id * rows if offset is None else offset

    def chunk_copies(chunk):
        slot = lax.rem(chunk, 2)
        cols = pl.ds(pl.multiple_of(chunk * width, width), width)
        return (
            pltpu.make_async_copy(
                act_buf.at[slot], act_ref.at[pl.ds(base, rows), cols], out_sem.at[2 + slot]
            ),
            pltpu.make_async_copy(
                slope_buf.at[slot],
                slope_ref.at[pl.ds(block_id * rows, rows), cols],
                out_sem.at[4 + slot],
            ),
        )

    def chunk_body(chunk, carry):
        cols = pl.ds(pl.multiple_of(chunk * width, width), width)
        slot = lax.rem(chunk, 2)

        @pl.when(chunk >= 2)
        def _():
            for copy in chunk_copies(chunk - 2):
                copy.wait()

        inner = mm(first_ref[...], wi[:, cols]) + vec_ref[pl.ds(ROW_BI + chunk, 1), :]
        phi = 0.5 * (1.0 + lax.erf(inner * ROOT_HALF))
        activated = (inner * phi).astype(BF16)
        act_buf[slot] = activated
        slope_buf[slot] = (phi + inner * jnp.exp(-0.5 * inner * inner) * SLOPE_CONST).astype(BF16)
        for copy in chunk_copies(chunk):
            copy.start()
        acc_ref[...] += mm(activated, w2[cols, :])
        return carry

    chunks = wi.shape[1] // width
    lax.fori_loop(0, chunks, chunk_body, 0)
    field = acc_ref[...]
    center = field - mean_row(field)
    inverse = lax.rsqrt(mean_row(center * center) + LAYER_EPS)
    normed = center * inverse
    n2_ref[...] = normed.astype(BF16)
    r2_ref[...] = jnp.broadcast_to(inverse, r2_ref.shape)
    final = (normed * vec_row(vec_ref, ROW_G2) + vec_row(vec_ref, ROW_S2)).astype(BF16)
    final_ref[...] = final
    loader.need(6)
    projected = mm(final, wl[...])
    uinv = lax.rsqrt(jnp.sum(projected * projected, axis=-1, keepdims=True) + NORM_EPS)
    unit = projected * uinv
    unit_ref[...] = unit
    uinv_ref[...] = jnp.broadcast_to(uinv, uinv_ref.shape)
    embed_ref[...] = unit.astype(BF16)
    for back in (2, 1):
        att_copy(HEADS // 2 - back).wait()
        for copy in chunk_copies(chunks - back):
            copy.wait()
    if gather:
        pl.when(last)(gather.finish)


def encode(x, lens, vec, weights, blocks, grouped, total, offset, earlier, sizes):
    rows = x.shape[0] // blocks
    width = x.shape[1]
    wide = weights[4].shape[1]
    embed_width = weights[6].shape[1]
    base = offset // rows

    def row_spec(columns):
        return pl.BlockSpec((rows, columns), lambda i, lens: (base + i, 0))

    def own_spec(columns):
        return pl.BlockSpec((rows, columns), lambda i, lens: (i, 0))

    def shape(count, columns, dtype):
        return jax.ShapeDtypeStruct((count, columns), dtype)

    own = x.shape[0]
    out_shapes = [
        shape(own, width, BF16),
        shape(own, width, BF16),
        shape(own, width, BF16),
        jax.ShapeDtypeStruct((blocks, HEADS, rows, rows), BF16),
        shape(total, width, BF16),
        shape(own, width, BF16),
        shape(own, embed_width, F32),
        shape(total, width, BF16),
        shape(total, wide, BF16),
        shape(own, wide, BF16),
        shape(own, width, BF16),
        shape(own, embed_width, F32),
        shape(total, width, BF16),
        shape(own, embed_width, F32),
        shape(own, embed_width, F32),
        shape(own, embed_width, BF16),
    ]
    shared = (4, 7, 8, 12)
    out_specs = [
        ANY
        if index in (3, 8, 9)
        else (row_spec if index in shared else own_spec)(out.shape[1])
        for index, out in enumerate(out_shapes)
    ]
    aliased = [] if earlier is None else [earlier[index] for index in shared]
    sends, sem_shapes, params = [], [], {}
    if sizes:
        sends = [earlier[15]]
        chips = sizes[0] * sizes[1] // 2
        out_shapes.append(jax.ShapeDtypeStruct((chips, 2) + earlier[15].shape, BF16))
        out_specs.append(ANY)
        sem = pltpu.SemaphoreType.DMA
        sem_shapes = [sem((chips,)), sem((chips,)), sem((1,)), sem((1,)), sem((1,))]
        params = {"collective_id": 4, "has_side_effects": True}
    return pl.pallas_call(
        functools.partial(fwd_kernel, grouped, len(aliased), sizes, offset if blocks == 1 else None),
        out_shape=out_shapes,
        grid_spec=pltpu.PrefetchScalarGridSpec(
            num_scalar_prefetch=1,
            grid=(blocks,),
            in_specs=[
                own_spec(width),
                pl.BlockSpec(vec.shape, lambda i, lens: (0, 0)),
            ]
            + [ANY] * (7 + len(aliased) + len(sends)),
            out_specs=out_specs,
            scratch_shapes=[pltpu.VMEM(weight.shape, BF16) for weight in weights]
            + [
                pltpu.SemaphoreType.DMA((7,)),
                pltpu.VMEM((rows, width), F32),
                pltpu.VMEM((2, 2, rows, rows), BF16),
                pltpu.VMEM((2, rows, width), BF16),
                pltpu.VMEM((2, rows, width), BF16),
                pltpu.SemaphoreType.DMA((6,)),
            ]
            + sem_shapes,
        ),
        input_output_aliases={10 + index: shared[index] for index in range(len(aliased))},
        compiler_params=pltpu.CompilerParams(vmem_limit_bytes=VMEM_LIMIT, **params),
        name="encode_queries" if grouped else "encode_passages",
    )(lens, x, vec, *weights, *aliased, *sends)


def sims_kernel(lens_ref, q_ref, p_ref, e_ref, z_ref):
    count = q_ref.shape[0]
    tokens = count * q_ref.shape[2]
    query = q_ref[...].reshape(tokens, q_ref.shape[3])
    sims = mm(p_ref[0], query, NT)
    slot = lax.broadcasted_iota(jnp.int32, sims.shape, 0)
    e = jnp.where(slot < lens_ref[pl.program_id(0)], jnp.exp(SHARP * sims - SHARP), 0.0)
    e_ref[0] = e.astype(BF16)
    z = jnp.sum(e, axis=0, keepdims=True)
    step = q_ref.shape[2]
    for index in range(count):
        z_ref[0, index : index + 1, :] = z[:, index * step : (index + 1) * step]


def sims_back_kernel(e_ref, w_ref, q_ref, p_ref, gp_ref, gq_ref):
    count = q_ref.shape[0]
    step = q_ref.shape[2]
    query = q_ref[...].reshape(count * step, q_ref.shape[3])
    weight = jnp.concatenate([w_ref[0, index : index + 1, :] for index in range(count)], axis=1)
    grads = (e_ref[0].astype(F32) * weight).astype(BF16)
    part = mm(grads, query)

    @pl.when(pl.program_id(1) == 0)
    def _():
        gp_ref[0] = part

    @pl.when(pl.program_id(1) > 0)
    def _():
        gp_ref[0] += part

    gq_ref[...] = mm(grads, p_ref[0], TN).astype(BF16).reshape(gq_ref.shape)


def similarity(queries, passages, lens):
    devices, micro, tokens, width = queries.shape
    slots = passages.shape[1]
    group = 8
    e, z = pl.pallas_call(
        sims_kernel,
        out_shape=(
            jax.ShapeDtypeStruct((micro, slots, devices * tokens), BF16),
            jax.ShapeDtypeStruct((micro, devices, tokens), F32),
        ),
        grid_spec=pltpu.PrefetchScalarGridSpec(
            num_scalar_prefetch=1,
            grid=(micro, devices // group),
            in_specs=[
                pl.BlockSpec((group, 1, tokens, width), lambda m, b, lens: (b, m, 0, 0)),
                pl.BlockSpec((1, slots, width), lambda m, b, lens: (m, 0, 0)),
            ],
            out_specs=(
                pl.BlockSpec((1, slots, group * tokens), lambda m, b, lens: (m, 0, b)),
                pl.BlockSpec((1, group, tokens), lambda m, b, lens: (m, b, 0)),
            ),
        ),
        compiler_params=pltpu.CompilerParams(vmem_limit_bytes=VMEM_LIMIT),
        name="similarity",
    )(lens, queries, passages)
    return e, z


def similarity_back(e, weights, queries, passages):
    devices, micro, tokens, width = queries.shape
    slots = passages.shape[1]
    group = 8
    return pl.pallas_call(
        sims_back_kernel,
        out_shape=(
            jax.ShapeDtypeStruct((micro, slots, width), F32),
            jax.ShapeDtypeStruct((devices, micro, tokens, width), BF16),
        ),
        grid=(micro, devices // group),
        in_specs=[
            pl.BlockSpec((1, slots, group * tokens), lambda m, b: (m, 0, b)),
            pl.BlockSpec((1, group, tokens), lambda m, b: (m, b, 0)),
            pl.BlockSpec((group, 1, tokens, width), lambda m, b: (b, m, 0, 0)),
            pl.BlockSpec((1, slots, width), lambda m, b: (m, 0, 0)),
        ],
        out_specs=(
            pl.BlockSpec((1, slots, width), lambda m, b: (m, 0, 0)),
            pl.BlockSpec((group, 1, tokens, width), lambda m, b: (b, m, 0, 0)),
        ),
        compiler_params=pltpu.CompilerParams(vmem_limit_bytes=VMEM_LIMIT),
        name="similarity_back",
    )(e, weights, queries, passages)


def match_kernel(n_wide, n_narrow, group, query_len, *refs):
    lens_ref, q_ref, p_ref, pos_ref = refs[:4]
    all_ref, loss_ref, gp_ref, half_ref = refs[4:8]
    e_buf, z_buf, own_buf, grad_buf, near, share_send, share_recv, pair_send, pair_recv = refs[8:]
    devices, micro, tokens, width = q_ref.shape
    chips = Chips(n_wide, n_narrow)
    me = chips.narrow * n_wide + chips.wide
    share_sems, pair_sems = (share_send, share_recv), (pair_send, pair_recv)
    pairs = group // 2

    def device(index):
        return (lax.rem(index, n_wide), index // n_wide)

    def each(body):
        def step_body(step, carry):
            body(step)
            return carry

        lax.fori_loop(1, devices, step_body, 0)

    barrier = pltpu.get_barrier_semaphore()
    each(
        lambda step: pl.semaphore_signal(
            barrier, inc=1, device_id=device(lax.rem(me + step, devices)), device_id_type=MESH
        )
    )

    def query_rows(block, m):
        at = pl.ds(block * group, group)
        return q_ref[at, m].reshape(group * tokens, width)

    def forward(block, carry):
        for m in range(micro):
            sims = mm(p_ref[m], query_rows(block, m), NT)
            slot = lax.broadcasted_iota(jnp.int32, (sims.shape[0], 1), 0)
            shift = jnp.where(slot < lens_ref[m], SHARP * LOG2E, -MASKED)
            e = jnp.exp2(SHARP * LOG2E * sims - shift)
            e_buf[m, block] = e.astype(BF16)
            z = jnp.sum(e, axis=0, keepdims=True)
            for index in range(group):
                z_buf[m, pl.ds(block * group + index, 1)] = z[
                    :, index * tokens : (index + 1) * tokens
                ]
        return carry

    lax.fori_loop(0, devices // group, forward, 0)
    pl.semaphore_wait(barrier, devices - 1)
    best = SHARP + jnp.log(z_buf[...].reshape(micro * devices, tokens))
    member = (
        lax.broadcasted_iota(jnp.int32, (8, tokens), 0)
        == lax.broadcasted_iota(jnp.int32, (8, tokens), 1) // query_len
    ).astype(F32)
    own = (
        lax.dot_general(
            member, best, NT, precision=lax.Precision.HIGHEST, preferred_element_type=F32
        )
        / SHARP
    )
    own_buf[...] = own
    all_ref[me] = own

    def share(step, source):
        target = device(lax.rem(me + step, devices))
        return remote(own_buf, all_ref.at[source], share_sems, step, target)

    each(lambda step: share(step, me).start())
    each(lambda step: share(step, lax.rem(me - step + devices, devices)).wait_recv())
    each(lambda step: share(step, me).wait_send())
    full = all_ref[...]
    peak = jnp.max(full, axis=0)
    total = peak + jnp.log(jnp.sum(jnp.exp(full - peak[None]), axis=0))
    positive = pos_ref[...]
    passage = lax.broadcasted_iota(jnp.int32, full.shape, 0)
    picked = jnp.sum(jnp.where(passage == positive[None], full, 0.0), axis=0)
    loss_ref[...] = total - picked
    grads = jnp.exp(own - total) - (positive == me).astype(F32)
    spread = lax.dot_general(
        grads, member, TN, precision=lax.Precision.HIGHEST, preferred_element_type=F32
    )
    z_buf[...] = (spread / z_buf[...].reshape(micro * devices, tokens)).reshape(z_buf.shape)
    gp_ref[...] = jnp.zeros_like(gp_ref)

    def pair_copy(block):
        at = pl.ds(block * pairs, pairs)
        return remote(
            grad_buf.at[at, 1 - chips.core], near.at[at], pair_sems, block, chips.mate
        )

    def backward(block, carry):
        for m in range(micro):
            weight = jnp.concatenate(
                [z_buf[m, pl.ds(block * group + index, 1)] for index in range(group)], axis=1
            )
            grads = e_buf[m, block] * weight.astype(BF16)
            gp_ref[m] += mm(grads, query_rows(block, m))
            part = mm(grads, p_ref[m], TN).astype(BF16)
            for index in range(group):
                grad_buf[block * pairs + index // 2, index % 2, m * tokens : (m + 1) * tokens] = (
                    part[index * tokens : (index + 1) * tokens]
                )
        pair_copy(block).start()
        return carry

    lax.fori_loop(0, devices // group, backward, 0)

    def join(block, carry):
        copy = pair_copy(block)
        copy.wait_recv()
        copy.wait_send()
        at = pl.ds(block * pairs, pairs)
        half_ref[at] = (
            grad_buf[at, chips.core].astype(F32) + near[at].astype(F32)
        ).astype(BF16)
        return carry

    lax.fori_loop(0, devices // group, join, 0)


def match(queries, passages, lens, positives, n_wide, n_narrow, query_len):
    devices, micro, tokens, width = queries.shape
    slots = passages.shape[1]
    group = 8
    own = tokens // query_len
    placed = positives.reshape(micro, devices, own).transpose(2, 0, 1).reshape(own, -1)
    placed = jnp.pad(placed, ((0, 8 - own), (0, 0)))
    sem = pltpu.SemaphoreType.DMA
    vmem = pl.BlockSpec(memory_space=pltpu.VMEM)
    columns = micro * devices
    return pl.pallas_call(
        functools.partial(match_kernel, n_wide, n_narrow, group, query_len),
        out_shape=(
            jax.ShapeDtypeStruct((devices, 8, columns), F32),
            jax.ShapeDtypeStruct((8, columns), F32),
            jax.ShapeDtypeStruct((micro, slots, width), F32),
            jax.ShapeDtypeStruct((devices // 2, micro * tokens, width), BF16),
        ),
        in_specs=[pl.BlockSpec(memory_space=pltpu.SMEM), vmem, vmem, vmem],
        out_specs=(vmem,) * 4,
        scratch_shapes=[
            pltpu.VMEM((micro, devices // group, slots, group * tokens), BF16),
            pltpu.VMEM((micro, devices, tokens), F32),
            pltpu.VMEM((8, columns), F32),
            pltpu.VMEM((devices // 2, 2, micro * tokens, width), BF16),
            pltpu.VMEM((devices // 2, micro * tokens, width), BF16),
            sem((devices,)),
            sem((devices,)),
            sem((devices // group,)),
            sem((devices // group,)),
        ],
        compiler_params=pltpu.CompilerParams(
            collective_id=1, has_side_effects=True, vmem_limit_bytes=VMEM_LIMIT
        ),
        name="match",
    )(lens, queries, passages, placed)


def accumulate(ref, row, value):
    ref[row : row + 1, :] += jnp.sum(value, axis=0, keepdims=True)


def mlp_back_kernel(alias_count, sizes, offset, *refs):
    (
        ge_ref,
        unit_ref,
        uinv_ref,
        n2_ref,
        r2_ref,
        slope_ref,
        n1_ref,
        r1_ref,
        vec_ref,
    ) = refs[:9]
    sources = refs[9:12]
    refs = refs[12 + alias_count :]
    swap = None
    if sizes:
        swap = Push(Chips(*sizes), refs[0], refs[7], refs[-4:])
        refs = refs[1:7] + refs[8:-4]
    gp_ref, go_ref, gi_ref, gh_ref, ga_ref, sums_ref = refs[:6]
    wl, w2, wi, sem, acc_ref, slope_buf, inner_buf, chunk_sem = refs[6:]
    loader = Loader(sources, (wl, w2, wi), sem)
    loader.start()
    rows, width = go_ref.shape
    own = pl.ds(pl.program_id(0) * rows, rows)
    placed = pl.ds(offset + pl.program_id(0) * rows, rows)

    def slope_copy(chunk):
        slot = lax.rem(chunk, 2)
        cols = pl.ds(pl.multiple_of(chunk * width, width), width)
        return pltpu.make_async_copy(
            slope_ref.at[own, cols], slope_buf.at[slot], chunk_sem.at[slot]
        )

    def inner_copy(chunk):
        slot = lax.rem(chunk, 2)
        cols = pl.ds(pl.multiple_of(chunk * width, width), width)
        return pltpu.make_async_copy(
            inner_buf.at[slot], gi_ref.at[placed, cols], chunk_sem.at[2 + slot]
        )

    slope_copy(0).start()
    if swap:
        pl.when(loader.first)(swap.start)

    @pl.when(loader.first)
    def _():
        sums_ref[...] = jnp.zeros_like(sums_ref)

    grad = ge_ref[...]
    unit = unit_ref[...]
    projected_low = (
        uinv_ref[...] * (grad - unit * jnp.sum(grad * unit, axis=-1, keepdims=True))
    ).astype(BF16)
    gp_ref[...] = projected_low
    loader.need(0)
    grad_final = mm(projected_low, wl[...], NT)
    normed = n2_ref[...].astype(F32)
    accumulate(sums_ref, ROW_G2, grad_final * normed)
    accumulate(sums_ref, ROW_S2, grad_final)
    scaled = grad_final * vec_row(vec_ref, ROW_G2)
    grad_second = r2_ref[:, :1] * (scaled - mean_row(scaled) - normed * mean_row(scaled * normed))
    outer_low = grad_second.astype(BF16)
    go_ref[...] = outer_low
    accumulate(sums_ref, ROW_B2, outer_low.astype(F32))
    acc_ref[...] = grad_second
    loader.need(1, 2)
    chunks = wi.shape[1] // width

    def chunk_body(chunk, carry):
        cols = pl.ds(pl.multiple_of(chunk * width, width), width)
        slot = lax.rem(chunk, 2)
        slope_copy(chunk).wait()
        pl.when(chunk < chunks - 1)(lambda: slope_copy(chunk + 1).start())
        pl.when(chunk >= 2)(lambda: inner_copy(chunk - 2).wait())
        grad_act = mm(go_ref[...], w2[cols, :], NT)
        inner = (grad_act * slope_buf[slot].astype(F32)).astype(BF16)
        inner_buf[slot] = inner
        inner_copy(chunk).start()
        sums_ref[pl.ds(ROW_BI + chunk, 1), :] += jnp.sum(
            inner.astype(F32), axis=0, keepdims=True
        )
        acc_ref[...] += mm(inner, wi[:, cols], NT)
        return carry

    lax.fori_loop(0, chunks, chunk_body, 0)
    grad_first = acc_ref[...]
    normed = n1_ref[...].astype(F32)
    accumulate(sums_ref, ROW_G1, grad_first * normed)
    accumulate(sums_ref, ROW_S1, grad_first)
    scaled = grad_first * vec_row(vec_ref, ROW_G1)
    hidden = r1_ref[:, :1] * (scaled - mean_row(scaled) - normed * mean_row(scaled * normed))
    gh_ref[...] = hidden
    low = hidden.astype(BF16)
    ga_ref[...] = low
    accumulate(sums_ref, ROW_BO, low.astype(F32))
    for back in (2, 1):
        inner_copy(chunks - back).wait()
    if swap:
        pl.when(pl.program_id(0) == pl.num_programs(0) - 1)(swap.finish)


def mlp_back(grad_embed, kept, vec, weights, blocks, total, offset, earlier, sent, sizes):
    own = grad_embed.shape[0]
    rows = own // blocks
    base = offset // rows
    _, _, _, _, wi, w2, wl = weights
    width, wide = wi.shape
    embed_width = wl.shape[1]

    def row_spec(columns):
        return pl.BlockSpec((rows, columns), lambda i: (base + i, 0))

    def own_spec(columns):
        return pl.BlockSpec((rows, columns), lambda i: (i, 0))

    args = [grad_embed] + [kept[index] for index in (13, 14, 10, 11, 9, 5, 6)]
    out_shapes = [
        jax.ShapeDtypeStruct((total, embed_width), BF16),
        jax.ShapeDtypeStruct((total, width), BF16),
        jax.ShapeDtypeStruct((total, wide), BF16),
        jax.ShapeDtypeStruct((own, width), F32),
        jax.ShapeDtypeStruct((total, width), BF16),
        jax.ShapeDtypeStruct((16, width), F32),
    ]
    shared = (0, 1, 2, 4)
    out_specs = [
        ANY if index == 2 else (row_spec if index in shared else own_spec)(out.shape[1])
        for index, out in enumerate(out_shapes[:5])
    ] + [pl.BlockSpec((16, width), lambda i: (0, 0))]
    aliased = [] if earlier is None else [earlier[index] for index in shared]
    sends, scratch, params = [], [], {}
    if sizes:
        sends = [sent]
        out_shapes.append(jax.ShapeDtypeStruct(sent.shape[1:], F32))
        out_specs.append(pl.BlockSpec(sent.shape[1:], lambda i: (0, 0)))
        scratch = push_scratch(*sent.shape)
        params = {"collective_id": 5, "has_side_effects": True}
    return pl.pallas_call(
        functools.partial(mlp_back_kernel, len(aliased), sizes, offset),
        out_shape=out_shapes,
        grid=(blocks,),
        in_specs=[
            ANY if index == 5 else own_spec(arg.shape[1]) for index, arg in enumerate(args)
        ]
        + [pl.BlockSpec(vec.shape, lambda i: (0, 0))]
        + [ANY] * (3 + len(aliased) + len(sends)),
        out_specs=out_specs,
        scratch_shapes=[pltpu.VMEM(weight.shape, BF16) for weight in (wl, w2, wi)]
        + [
            pltpu.SemaphoreType.DMA((3,)),
            pltpu.VMEM((rows, width), F32),
            pltpu.VMEM((2, rows, width), BF16),
            pltpu.VMEM((2, rows, width), BF16),
            pltpu.SemaphoreType.DMA((4,)),
        ]
        + scratch,
        input_output_aliases={12 + index: shared[index] for index in range(len(aliased))},
        compiler_params=pltpu.CompilerParams(vmem_limit_bytes=VMEM_LIMIT, **params),
        name="mlp_back_queries" if earlier is not None else "mlp_back_passages",
    )(*args, vec, wl, w2, wi, *aliased, *sends)


def attention_back_kernel(alias_count, *refs):
    ga_ref, gh_ref, att_ref, q_ref, k_ref, v_ref = refs[:6]
    sources = refs[6:10]
    refs = refs[10 + alias_count :]
    gqkv_ref, gx_ref, sums_ref = refs[:3]
    wo, wq, wk, wv, sem, gc_ref = refs[3:]
    loader = Loader(sources, (wo, wq, wk, wv), sem)
    loader.start()

    @pl.when(loader.first)
    def _():
        sums_ref[...] = jnp.zeros_like(sums_ref)

    rows, width = gh_ref.shape
    scale = HEAD_DIM ** (-0.5)
    loader.need(0)
    gc_ref[...] = mm(ga_ref[...], wo[...], NT).astype(BF16)
    low_half = lax.broadcasted_iota(jnp.int32, (rows, 128), 1) < HEAD_DIM

    def pair_body(pair, carry):
        cols = pl.ds(pl.multiple_of(pair * 128, 128), 128)
        q_pair, k_pair, v_pair, gc_pair = q_ref[:, cols], k_ref[:, cols], v_ref[:, cols], gc_ref[:, cols]
        parts = []
        for half in range(2):
            mask = low_half if half == 0 else jnp.logical_not(low_half)
            low = att_ref[0, 2 * pair + half]
            att = low.astype(F32)
            grad_att = mm(jnp.where(mask, gc_pair, jnp.zeros_like(gc_pair)), v_pair, NT)
            weighted = grad_att * att
            grad_logits = (weighted - att * jnp.sum(weighted, axis=-1, keepdims=True)).astype(BF16)
            parts.append(
                (
                    mm(grad_logits, k_pair) * scale,
                    mm(grad_logits, q_pair, TN),
                    mm(low, gc_pair, TN),
                )
            )
        for index in range(3):
            gqkv_ref[:, pl.ds(pl.multiple_of(index * width + pair * 128, 128), 128)] = jnp.where(
                low_half, parts[0][index], parts[1][index]
            ).astype(BF16)
        return carry

    lax.fori_loop(0, HEADS // 2, pair_body, 0)
    loader.need(1, 2, 3)
    grad_q, grad_k, grad_v = (
        gqkv_ref[:, :width],
        gqkv_ref[:, width : 2 * width],
        gqkv_ref[:, 2 * width :],
    )
    accumulate(sums_ref, 0, grad_q.astype(F32))
    accumulate(sums_ref, 1, grad_v.astype(F32))
    gx_ref[...] = (
        gh_ref[...]
        + mm(grad_q, wq[...], NT)
        + mm(grad_k, wk[...], NT)
        + mm(grad_v, wv[...], NT)
    )


def attention_back(attended, hidden, kept, weights, blocks, total, offset, earlier):
    own, width = hidden.shape
    rows = own // blocks
    base = offset // rows
    wq, wk, wv, wo = weights[:4]

    def row_spec(columns):
        return pl.BlockSpec((rows, columns), lambda i: (base + i, 0))

    def own_spec(columns):
        return pl.BlockSpec((rows, columns), lambda i: (i, 0))

    aliased = [] if earlier is None else [earlier]
    return pl.pallas_call(
        functools.partial(attention_back_kernel, len(aliased)),
        out_shape=(
            jax.ShapeDtypeStruct((total, 3 * width), BF16),
            jax.ShapeDtypeStruct((own, width), F32),
            jax.ShapeDtypeStruct((8, width), F32),
        ),
        grid=(blocks,),
        in_specs=[
            row_spec(width),
            own_spec(width),
            pl.BlockSpec((1, HEADS, rows, rows), lambda i: (i, 0, 0, 0)),
            own_spec(width),
            own_spec(width),
            own_spec(width),
        ]
        + [ANY] * (4 + len(aliased)),
        out_specs=(
            row_spec(3 * width),
            own_spec(width),
            pl.BlockSpec((8, width), lambda i: (0, 0)),
        ),
        scratch_shapes=[pltpu.VMEM(weight.shape, BF16) for weight in weights[:4]]
        + [pltpu.SemaphoreType.DMA((4,)), pltpu.VMEM((rows, width), BF16)],
        input_output_aliases={10: 0} if aliased else {},
        compiler_params=pltpu.CompilerParams(vmem_limit_bytes=VMEM_LIMIT),
        name="attention_back_queries" if aliased else "attention_back_passages",
    )(attended, hidden, kept[3], kept[0], kept[1], kept[2], wo, wq, wk, wv, *aliased)


def pack(vectors, width):
    count = sum(vector.shape[0] for vector in vectors)
    total = -(-count // (8 * width)) * 8 * width
    start, packed = 0, 0.0
    for vector in vectors:
        size = vector.shape[0]
        packed = packed + jnp.pad(vector.astype(F32), (start, total - start - size))
        start += size
    return packed.reshape(-1, width)


def share_kernel(n_wide, n_narrow, own_ref, all_ref, send_sem, recv_sem):
    me = lax.axis_index("narrow") * n_wide + lax.axis_index("wide")
    total = n_wide * n_narrow
    sems = (send_sem, recv_sem)

    def device(index):
        return (lax.rem(index, n_wide), index // n_wide)

    barrier = pltpu.get_barrier_semaphore()

    def signal(step, carry):
        pl.semaphore_signal(
            barrier, inc=1, device_id=device(lax.rem(me + step, total)), device_id_type=MESH
        )
        return carry

    def send(step, carry):
        target = device(lax.rem(me + step, total))
        remote(own_ref, all_ref.at[me], sems, step, target).start()
        return carry

    def wait(step, carry):
        source = lax.rem(me - step + total, total)
        copy = remote(own_ref, all_ref.at[source], sems, step, device(source))
        copy.wait_recv()
        copy.wait_send()
        return carry

    lax.fori_loop(1, total, signal, 0)
    all_ref[me] = own_ref[...]
    pl.semaphore_wait(barrier, total - 1)
    lax.fori_loop(1, total, send, 0)
    lax.fori_loop(1, total, wait, 0)


def share_scores(own, n_wide, n_narrow):
    total = n_wide * n_narrow
    return pl.pallas_call(
        functools.partial(share_kernel, n_wide, n_narrow),
        out_shape=jax.ShapeDtypeStruct((total,) + own.shape, own.dtype),
        in_specs=[pl.BlockSpec(memory_space=pltpu.VMEM)],
        out_specs=pl.BlockSpec(memory_space=pltpu.VMEM),
        scratch_shapes=[pltpu.SemaphoreType.DMA((total,))] * 2,
        compiler_params=pltpu.CompilerParams(collective_id=1, has_side_effects=True),
        name="share_scores",
    )(own)


def exchange_kernel(n_wide, n_narrow, g_ref, out_ref, *scratch):
    swap = Exchange(Chips(n_wide, n_narrow), g_ref, out_ref, scratch)
    swap.start()
    swap.push()
    swap.finish()


def exchange(grads, n_wide, n_narrow):
    chips, _, rows, width = grads.shape
    return pl.pallas_call(
        functools.partial(exchange_kernel, n_wide, n_narrow),
        out_shape=jax.ShapeDtypeStruct((rows, width), F32),
        in_specs=[ANY],
        out_specs=pl.BlockSpec(memory_space=pltpu.VMEM),
        scratch_shapes=exchange_scratch(chips, rows, width),
        compiler_params=pltpu.CompilerParams(
            collective_id=2, has_side_effects=True, vmem_limit_bytes=VMEM_LIMIT
        ),
        name="exchange_query_gradients",
    )(grads)


UNITS = (
    (0, 48, 0),
    (48, 48, 0),
    (96, 48, 48),
    (144, 48, 48),
    (192, 16, 96),
    (240, 16, 96),
    (208, 16, 112),
    (256, 16, 112),
    (224, 16, 128),
    (272, 32, 128),
)
EARLY = (0, 1, 2, 3)
LATE = (4, 5, 6, 7, 8, 9)
SHARE_ROWS = 304
LATE_B = 240
ROWS_A, ROWS_B = 144, 160
TILES = 9


def tail_kernel(n_z, part, *refs):
    act, go, first, gi, x_p, x_q, ctx, ga, final, gp = refs[:10]
    kept = (refs[10:15], refs[15:20])
    sources = refs[20:24]
    sums = refs[24:26]
    out_ref, gx_p, gx_q = refs[26:29]
    both, near, over_a, over_b, then_a, then_b, line, left_buf, right_buf, thin_buf = refs[29:39]
    wo, wq, wk, wv, att_buf, hidden, thin_hidden, grads, att_sums = refs[39:48]
    load_sem, weight_sem, block_sem, att_sem, gx_sem = refs[48:53]
    core_sems, one_sems, two_sems, line_sems, copy_sems = (
        refs[53 + 2 * index : 55 + 2 * index] for index in range(5)
    )
    wide, narrow = lax.axis_index("wide"), lax.axis_index("narrow")
    z, x = wide // 2, lax.rem(wide, 2)
    y, core = narrow // 2, lax.rem(narrow, 2)
    mate = (wide, y * 2 + 1 - core)
    over_y = (wide, (1 - y) * 2 + core)
    over_x = (z * 2 + 1 - x, narrow)
    total, width = go.shape
    p_rows = x_p.shape[0]
    held = both.at[core]

    def load(tile, wait):
        slot = lax.rem(tile, 2)
        block = pl.ds(pl.multiple_of(lax.rem(tile, 4) * width, width), width)

        def pair(source, other, target):
            for made in (
                pltpu.make_async_copy(source, left_buf.at[slot], load_sem.at[slot, 0]),
                pltpu.make_async_copy(other, target, load_sem.at[slot, 1]),
            ):
                if wait:
                    made.wait()
                else:
                    made.start()

        place = right_buf.at[slot]
        pl.when(tile < 4)(lambda: pair(act.at[:, block], go, place))
        pl.when(jnp.logical_and(tile >= 4, tile < 8))(lambda: pair(first, gi.at[:, block], place))
        pl.when(tile == 8)(lambda: pair(ctx, ga, place))
        pl.when(tile == TILES)(lambda: pair(final, gp, thin_buf))

    def rows_of(unit):
        start, count, _ = UNITS[unit]
        return pl.ds(start, count)

    def place_of(unit):
        _, count, place = UNITS[unit]
        return pl.ds(place, count)

    def core_copy(unit):
        rows = rows_of(unit)
        return remote(
            both.at[1 - core, :, :, :, rows], near.at[:, :, :, rows], core_sems, unit, mate
        )

    def late_copy(index):
        row_y, start, count = ((0, 2 * part, part + 16), (1, LATE_B, 64), (1, 2 * part, 48))[index]
        rows = pl.ds(start, count)
        return remote(
            both.at[1 - core, row_y, :, :, rows],
            near.at[row_y, :, :, rows],
            core_sems,
            len(EARLY) + index,
            mate,
        )

    def one_copy(unit):
        rows = rows_of(unit)
        place = place_of(unit)
        if unit % 2 == 0:
            return remote(
                held.at[1 - y, :, :, rows],
                over_a.at[:, :, place],
                one_sems,
                unit,
                over_y,
            )
        return remote(
            held.at[:, :, 1 - x, rows],
            over_b.at[:, :, place],
            one_sems,
            unit,
            over_x,
        )

    def two_copy(unit):
        rows = rows_of(unit)
        place = place_of(unit)
        if unit % 2 == 0:
            return remote(
                held.at[y, :, 1 - x, rows],
                then_a.at[:, place],
                two_sems,
                unit,
                over_x,
            )
        return remote(
            held.at[1 - y, :, x, rows],
            then_b.at[:, place],
            two_sems,
            unit,
            over_y,
        )

    def far_copy(unit, step):
        rows = rows_of(unit)
        target = lax.rem(z + step, n_z)
        return remote(
            held.at[y, target, x, rows],
            line.at[step - 1, rows],
            line_sems,
            unit * n_z + step,
            (target * 2 + x, narrow),
        )

    def share_copy(unit, step, arriving):
        rows = rows_of(unit)
        slots = (
            (y * 2 + 1 - core, (1 - y) * 2 + core, (1 - y) * 2 + 1 - core)
            if arriving
            else (narrow, narrow, (1 - y) * 2 + core)
        )
        block = out_ref.at[slots[step], rows]
        return remote(block, block, copy_sems, unit * 3 + step, over_y if step == 1 else mate)

    def add(target, extra):
        target[...] = target[...] + extra[...]

    def start_core(unit):
        core_copy(unit).start()

    def start_one(unit):
        rows = rows_of(unit)
        if unit in EARLY:
            core_copy(unit).wait_recv()

        def body(index, carry):
            row_y, rest = index // (n_z * 2), lax.rem(index, n_z * 2)
            at = (row_y, rest // 2, lax.rem(rest, 2), rows)
            add(held.at[at], near.at[at])
            return carry

        lax.fori_loop(0, 4 * n_z, body, 0)
        one_copy(unit).start()

    def start_two(unit):
        rows = rows_of(unit)
        place = place_of(unit)
        one_copy(unit).wait_recv()

        def body(index, carry):
            outer_at, inner_at = index // 2, lax.rem(index, 2)
            if unit % 2 == 0:
                add(
                    held.at[y, outer_at, inner_at, rows],
                    over_a.at[outer_at, inner_at, place],
                )
            else:
                add(
                    held.at[inner_at, outer_at, x, rows],
                    over_b.at[inner_at, outer_at, place],
                )
            return carry

        lax.fori_loop(0, 2 * n_z, body, 0)
        two_copy(unit).start()

    def start_far(unit):
        rows = rows_of(unit)
        place = place_of(unit)
        extra = then_a if unit % 2 == 0 else then_b
        two_copy(unit).wait_recv()

        def body(index, carry):
            add(held.at[y, index, x, rows], extra.at[index, place])
            return carry

        lax.fori_loop(0, n_z, body, 0)
        for step in range(1, n_z):
            far_copy(unit, step).start()

    def start_share(unit):
        rows = rows_of(unit)
        for step in range(1, n_z):
            far_copy(unit, step).wait_recv()
            add(held.at[y, z, x, rows], line.at[step - 1, rows])
        out_ref[narrow, rows] = both[core, y, z, x, rows]
        share_copy(unit, 1, False).start()
        share_copy(unit, 0, False).start()

    def forward(unit):
        share_copy(unit, 1, True).wait_recv()
        share_copy(unit, 2, False).start()

    def finish(unit):
        share_copy(unit, 0, True).wait_recv()
        share_copy(unit, 2, True).wait_recv()
        for step in range(3):
            share_copy(unit, step, False).wait_send()
        if unit in EARLY:
            core_copy(unit).wait_send()
        one_copy(unit).wait_send()
        two_copy(unit).wait_send()
        for step in range(1, n_z):
            far_copy(unit, step).wait_send()

    barrier = pltpu.get_barrier_semaphore()
    load(0, False)
    partners = [mate, over_y, over_x] + [
        (lax.rem(z + step, n_z) * 2 + x, narrow) for step in range(1, n_z)
    ]
    for device in partners:
        pl.semaphore_signal(barrier, inc=1, device_id=device, device_id_type=MESH)
    pl.semaphore_wait(barrier, len(partners))

    def put(kind, owner, half, made):
        rows = pl.ds(pl.multiple_of(kind * part, part), part)
        for index in range(4):
            both[lax.rem(owner, 2), owner // 2, 2 * half + index // 2, index % 2, rows] = made[
                index * part : (index + 1) * part
            ]

    def halves(left_ref, right_ref, store):
        def half_body(half, carry):
            cols = pl.ds(pl.multiple_of(half * 4 * part, 4 * part), 4 * part)
            store(half, mm(left_ref[:, cols], right_ref[...], TN).astype(BF16))
            return carry

        lax.fori_loop(0, 2, half_body, 0)

    def hooks(now, plan):
        for at, step, units in plan:

            @pl.when(now == at)
            def _(step=step, units=units):
                for unit in units:
                    step(unit)

    def tile_body(tile, carry):
        slot = lax.rem(tile, 2)
        load(tile, True)
        load(tile + 1, False)
        kind = tile // 4
        owner = jnp.where(tile == 8, 3, lax.rem(tile, 4))

        def store(half, made):
            @pl.when(kind == 0)
            def _():
                for index in range(4):
                    both[index % 2, index // 2, owner, half, :part] = made[
                        index * part : (index + 1) * part
                    ]

            pl.when(kind > 0)(lambda: put(kind, owner, half, made))

        halves(left_buf.at[slot], right_buf.at[slot], store)
        hooks(
            tile,
            (
                (3, start_core, (0, 1)),
                (5, start_one, (0,)),
                (6, start_one, (1,)),
                (7, start_core, (2, 3)),
            ),
        )
        return carry

    def hidden_of(block):
        return thin_hidden if blocks[block][2] else hidden.at[block]

    def block_copies(block):
        rows, base, source = blocks[block]
        q, k, v, gh, _ = kept[source]
        buf = left_buf if block % 2 == 0 else right_buf
        own = pl.ds(base - (p_rows if source else 0), rows)
        low, high = pl.ds(0, rows), pl.ds(span, rows)
        pairs = (
            (q.at[own], buf.at[0, low]),
            (k.at[own], buf.at[0, high]),
            (v.at[own], buf.at[1, low]),
            (ga.at[pl.ds(base, rows)], buf.at[1, high]),
            (gh.at[own], hidden_of(block)),
            (ctx.at[pl.ds(base, rows)], grads.at[0, pl.ds(base, rows)]),
        )
        return [
            pltpu.make_async_copy(*pair, block_sem.at[block % 2, index])
            for index, pair in enumerate(pairs)
        ]

    def gx_copy(block):
        rows, base, source = blocks[block]
        target = gx_q if source else gx_p
        own = pl.ds(base - (p_rows if source else 0), rows)
        return pltpu.make_async_copy(hidden_of(block), target.at[own], gx_sem.at[block])

    def states(block):
        rows, base, _ = blocks[block]
        own = pl.ds(base, rows)
        hidden_of(block)[...] += (
            mm(grads[0, own], wq[...], NT)
            + mm(grads[1, own], wk[...], NT)
            + mm(grads[2, own], wv[...], NT)
        )
        gx_copy(block).start()

    def attention(block, plan):
        rows, base, source = blocks[block]
        buf = left_buf if block % 2 == 0 else right_buf
        low, high, own = pl.ds(0, rows), pl.ds(span, rows), pl.ds(base, rows)
        att = kept[source][4]
        q_ref, k_ref, v_ref, ga_ref = (
            buf.at[0, low],
            buf.at[0, high],
            buf.at[1, low],
            buf.at[1, high],
        )
        entry = 0 if source else block
        size = pl.ds(0, rows)

        def att_copy(pair):
            slot = lax.rem(pair, 2)
            return pltpu.make_async_copy(
                att.at[entry, pl.ds(2 * pair, 2)],
                att_buf.at[slot, :, size, size],
                att_sem.at[slot],
            )

        att_copy(0).start()
        for copy in block_copies(block):
            copy.wait()
        grads[2, own] = mm(ga_ref[...], wo[...], NT).astype(BF16)
        low_half = lax.broadcasted_iota(jnp.int32, (rows, 128), 1) < HEAD_DIM
        scale = HEAD_DIM ** (-0.5)

        def pair_body(pair, carry):
            cols = pl.ds(pl.multiple_of(pair * 128, 128), 128)
            slot = lax.rem(pair, 2)
            att_copy(pair).wait()
            pl.when(pair < HEADS // 2 - 1)(lambda: att_copy(pair + 1).start())
            q_pair, k_pair, v_pair = q_ref[:, cols], k_ref[:, cols], v_ref[:, cols]
            gc_pair = grads[2, own, cols]
            shares = gc_pair.astype(F32) * grads[0, own, cols].astype(F32)
            parts = []
            for half in range(2):
                mask = low_half if half == 0 else jnp.logical_not(low_half)
                low_att = att_buf[slot, half, size, size]
                wide_att = low_att.astype(F32)
                grad_att = mm(jnp.where(mask, gc_pair, jnp.zeros_like(gc_pair)), v_pair, NT)
                overlap = jnp.sum(jnp.where(mask, shares, 0.0), axis=-1, keepdims=True)
                grad_logits = (wide_att * (grad_att - overlap)).astype(BF16)
                parts.append(
                    (
                        mm(grad_logits, k_pair) * scale,
                        mm(grad_logits, q_pair, TN),
                        mm(low_att, gc_pair, TN),
                    )
                )
            for index in range(3):
                grads[index, own, cols] = jnp.where(
                    low_half, parts[0][index], parts[1][index]
                ).astype(BF16)
            hooks(pair, plan)
            return carry

        lax.fori_loop(0, HEADS // 2, pair_body, 0)
        accumulate(att_sums, 0, grads[0, own].astype(F32))
        accumulate(att_sums, 1, grads[2, own].astype(F32))

    def weight_copies():
        return [
            pltpu.make_async_copy(source, target, weight_sem.at[index])
            for index, (source, target) in enumerate(zip(sources, (wo, wq, wk, wv)))
        ]

    span = kept[0][4].shape[-1]
    blocks = [(span, base, 0) for base in range(0, p_rows, span)] + [(x_q.shape[0], p_rows, 1)]
    for copy in weight_copies():
        copy.start()
    att_sums[...] = jnp.zeros_like(att_sums)
    lax.fori_loop(0, TILES, tile_body, 0)
    load(TILES, True)
    slot = TILES % 2
    made = mm(left_buf[slot], thin_buf[...], TN).astype(BF16)
    for copy in block_copies(0):
        copy.start()
    lanes = thin_buf.shape[1]
    last = pl.ds(3 * part, 16)
    for shard in range(2 * n_z):
        for block in range(width // lanes):
            row = shard * part + block * 16
            both[0, 0, shard // 2, shard % 2, last, block * lanes : (block + 1) * lanes] = made[
                row : row + 16
            ]
    for copy in weight_copies():
        copy.wait()
    for copy in block_copies(1):
        copy.start()
    attention(0, ((0, start_one, (2, 3)), (3, start_two, (0, 1))))
    for copy in block_copies(2):
        copy.start()
    attention(
        1,
        (
            (0, start_far, (0, 1)),
            (2, start_two, (2, 3)),
            (5, start_far, (2, 3)),
        ),
    )
    x_copies = [
        pltpu.make_async_copy(x_p, right_buf.at[0, pl.ds(0, p_rows)], load_sem.at[0, 0]),
        pltpu.make_async_copy(
            x_q, right_buf.at[0, pl.ds(p_rows, total - p_rows)], load_sem.at[0, 1]
        ),
    ]
    for copy in x_copies:
        copy.start()
    attention(2, ((2, start_share, (0, 1)),))
    top = sums[0][:8] + sums[1][:8] + att_sums[...]
    tail = jnp.concatenate([top, sums[0][8:] + sums[1][8:]], axis=0).astype(BF16)
    for shard in range(2 * n_z):
        at_z, at_x = shard // 2, shard % 2
        both[1, 0, at_z, at_x, last] = tail
        both[0, 1, at_z, at_x, last] = jnp.zeros_like(tail)
        both[1, 1, at_z, at_x, last] = jnp.zeros_like(tail)
    for copy in x_copies:
        copy.wait()

    def late_body(tile, carry):
        halves(right_buf.at[0], grads.at[tile], lambda half, made: put(2, tile, half, made))
        pl.when(tile == 1)(lambda: late_copy(0).start())
        return carry

    lax.fori_loop(0, 3, late_body, 0)

    def start_late(index):
        late_copy(index).start()

    def wait_late(index):
        late_copy(index).wait_recv()

    def end_late(index):
        late_copy(index).wait_send()

    for step, units in (
        (start_late, (1, 2)),
        (start_share, (2, 3)),
        (wait_late, (0, 1)),
        (start_one, (5, 7, 9)),
        (wait_late, (2,)),
        (start_one, (4, 6, 8)),
        (forward, EARLY),
        (states, (0,)),
        (start_two, (5, 4)),
        (states, (1,)),
        (start_two, (7, 6)),
        (start_far, (5, 4)),
        (states, (2,)),
        (start_two, (8,)),
        (start_far, (7, 6)),
        (start_two, (9,)),
        (start_far, (8,)),
        (start_share, (5, 4)),
        (start_far, (9,)),
        (start_share, (7, 6, 8)),
        (forward, (5, 4, 7, 6)),
        (start_share, (9,)),
        (forward, (8, 9)),
        (finish, EARLY + LATE),
        (end_late, (0, 1, 2)),
        (lambda block: gx_copy(block).wait(), range(len(blocks))),
    ):
        for unit in units:
            step(unit)


def backward_tail(arrays, passage_kept, query_kept, weights, sums, n_wide):
    n_z = n_wide // 2
    go, x_p, x_q, gp = arrays[1], arrays[4], arrays[5], arrays[9]
    total, width = go.shape
    part = width // n_wide
    units = len(UNITS)
    span = passage_kept[4].shape[-1]
    sem = pltpu.SemaphoreType.DMA
    vmem = pl.BlockSpec(memory_space=pltpu.VMEM)
    return pl.pallas_call(
        functools.partial(tail_kernel, n_z, part),
        out_shape=(
            jax.ShapeDtypeStruct((4, SHARE_ROWS, width), BF16),
            jax.ShapeDtypeStruct(x_p.shape, F32),
            jax.ShapeDtypeStruct(x_q.shape, F32),
        ),
        in_specs=[ANY] * 24 + [vmem] * 2,
        out_specs=(vmem, ANY, ANY),
        scratch_shapes=[
            pltpu.VMEM((2, 2, n_z, 2, SHARE_ROWS, width), BF16),
            pltpu.VMEM((2, n_z, 2, SHARE_ROWS, width), BF16),
            pltpu.VMEM((n_z, 2, ROWS_A, width), BF16),
            pltpu.VMEM((2, n_z, ROWS_B, width), BF16),
            pltpu.VMEM((n_z, ROWS_A, width), BF16),
            pltpu.VMEM((n_z, ROWS_B, width), BF16),
            pltpu.VMEM((n_z - 1, SHARE_ROWS, width), BF16),
            pltpu.VMEM((2, total, width), BF16),
            pltpu.VMEM((2, total, width), BF16),
            pltpu.VMEM(gp.shape, BF16),
        ]
        + [pltpu.VMEM((width, width), BF16)] * 4
        + [
            pltpu.VMEM((2, 2, span, span), BF16),
            pltpu.VMEM((2, span, width), F32),
            pltpu.VMEM(x_q.shape, F32),
            pltpu.VMEM((3, total, width), BF16),
            pltpu.VMEM((8, width), F32),
            sem((2, 2)),
            sem((4,)),
            sem((2, 6)),
            sem((2,)),
            sem((3,)),
        ]
        + [sem((units,))] * 6
        + [sem((units * n_z,))] * 2
        + [sem((units * 3,))] * 2,
        compiler_params=pltpu.CompilerParams(
            collective_id=3, has_side_effects=True, vmem_limit_bytes=VMEM_LIMIT
        ),
        name="backward_tail",
    )(*arrays, *passage_kept, *query_kept, *weights, *sums)


def unpack_kernel(part, sums_ref, gx_p, gx_q, *refs):
    q_ref, k_ref, v_ref, o_ref, inner_ref, outer_ref, thin_ref, vec_ref, to_p, to_q = refs[:10]
    buf, in_sem, out_sem = refs[10:]
    width = q_ref.shape[1]
    rows = gx_q.shape[0]
    pieces = []
    for source, target in ((gx_p, to_p), (gx_q, to_q)):
        for start in range(0, source.shape[0], rows):
            at = pl.ds(start, rows)
            slot = len(pieces)
            pieces.append(
                (
                    pltpu.make_async_copy(source.at[at], buf.at[slot], in_sem.at[slot]),
                    pltpu.make_async_copy(buf.at[slot], target.at[at], out_sem.at[slot]),
                )
            )
    for arrive, _ in pieces:
        arrive.start()
    lanes = thin_ref.shape[1]
    for owner, ref in enumerate((q_ref, k_ref, v_ref, o_ref)):
        ref[...] = sums_ref[owner, 2 * part : 3 * part].astype(F32)
        inner_ref[:, owner * width : (owner + 1) * width] = sums_ref[
            owner, part : 2 * part
        ].astype(F32)
        outer_ref[owner * part : (owner + 1) * part] = sums_ref[owner, :part].astype(F32)
        pieces[owner][0].wait()
        pieces[owner][1].start()
    for arrive, leave in pieces[4:]:
        arrive.wait()
        leave.start()
    tail = sums_ref[0, 3 * part :].astype(F32)
    for block in range(width // lanes):
        thin_ref[block * 16 : (block + 1) * 16] = tail[:, block * lanes : (block + 1) * lanes]
    vec_ref[...] = sums_ref[1, 3 * part :].astype(F32)
    for _, leave in pieces:
        leave.wait()


def unpack(summed, grad_p, grad_q, part, embed_width):
    width = summed.shape[-1]
    rows = grad_q.shape[0]
    count = grad_p.shape[0] // rows + 1
    sem = pltpu.SemaphoreType.DMA
    vmem = pl.BlockSpec(memory_space=pltpu.VMEM)
    shapes = [(part, width)] * 4 + [
        (part, 4 * width),
        (4 * part, width),
        (part, embed_width),
        (16, width),
        grad_p.shape,
        grad_q.shape,
    ]
    return pl.pallas_call(
        functools.partial(unpack_kernel, part),
        out_shape=[jax.ShapeDtypeStruct(shape, F32) for shape in shapes],
        in_specs=[vmem, ANY, ANY],
        out_specs=[vmem] * (len(shapes) - 2) + [ANY] * 2,
        scratch_shapes=[pltpu.VMEM((count, rows, width), F32), sem((count,)), sem((count,))],
        compiler_params=pltpu.CompilerParams(vmem_limit_bytes=VMEM_LIMIT),
        name="unpack_gradients",
    )(summed, grad_p, grad_q)


def outer(left, right):
    return lax.dot_general(left, right, TN, preferred_element_type=F32)


def local(
    query_states,
    passage_states,
    lengths,
    positives,
    query_weight,
    query_bias,
    key_weight,
    value_weight,
    value_bias,
    out_weight,
    out_bias,
    first_gain,
    first_shift,
    inner_weight,
    inner_bias,
    outer_weight,
    outer_bias,
    second_gain,
    second_shift,
    linear_weight,
):
    everyone = ("wide", "narrow")
    n_wide = lax.axis_size("wide")
    n_narrow = lax.axis_size("narrow")
    wide_index = lax.axis_index("wide")
    narrow_index = lax.axis_index("narrow")
    micro, own_queries, query_len, width = query_states.shape
    own_passages, slots = passage_states.shape[1:3]
    weights = (
        query_weight,
        key_weight,
        value_weight,
        out_weight,
        inner_weight,
        outer_weight,
        linear_weight,
    )
    embed_width = linear_weight.shape[1]
    vec = pack(
        (
            query_bias,
            value_bias,
            out_bias,
            first_gain,
            first_shift,
            outer_bias,
            second_gain,
            second_shift,
            inner_bias,
        ),
        width,
    )
    own_index = narrow_index * n_wide + wide_index
    own_lengths = lax.dynamic_slice_in_dim(lengths, own_index * own_passages, own_passages, axis=1)
    lens = own_lengths.reshape(-1)
    x_query = query_states.reshape(-1, width)
    x_passage = passage_states.reshape(-1, width)
    query_rows, passage_rows = x_query.shape[0], x_passage.shape[0]
    total = query_rows + passage_rows
    kept_q = encode(
        x_query, lens, vec, weights, 1, query_len, total, passage_rows, None, None
    )
    sizes = (n_wide, n_narrow)
    kept_p = encode(
        x_passage, lens, vec, weights, micro * own_passages, 0, total, 0, kept_q, sizes
    )
    queries = kept_p[16].reshape(n_wide * n_narrow, micro, -1, embed_width)
    ctx, first_low, act, final_low = (kept_p[index] for index in (4, 7, 8, 12))
    passages = kept_p[15].reshape(micro * own_passages, slots, embed_width)
    row_count = own_queries * n_narrow
    together = queries.size * slots <= 8 * 1024 * 1024 * embed_width
    if together:
        full, loss, grad_passage, grad_query = match(
            queries, passages, lens, positives, n_wide, n_narrow, query_len
        )
        block = lax.dynamic_slice_in_dim(full, narrow_index * n_wide, n_wide, axis=0)
        block = lax.dynamic_slice_in_dim(
            block[:, :own_queries].reshape(n_wide, own_queries, micro, -1),
            wide_index * n_narrow,
            n_narrow,
            axis=3,
        )
        scores = block.transpose(2, 3, 1, 0).reshape(micro, row_count, n_wide)
        losses = lax.dynamic_slice_in_dim(
            loss[:own_queries].reshape(own_queries, micro, -1),
            wide_index * n_narrow,
            n_narrow,
            axis=2,
        )
        losses = losses.transpose(1, 2, 0).reshape(micro, row_count)
    else:
        e, z = similarity(queries, passages, lens)
        best = SHARP + jnp.log(z)
        own_scores = jnp.sum(best.reshape(micro, -1, query_len), axis=-1) / SHARP
        full = share_scores(own_scores, n_wide, n_narrow)
        row_total = jax.nn.logsumexp(full, axis=0)
        passage_ids = jnp.arange(full.shape[0], dtype=jnp.int32)
        picked = jnp.sum(
            jnp.where(passage_ids[:, None, None] == positives[None], full, 0.0), axis=0
        )
        row_count = own_queries * n_narrow
        losses = lax.dynamic_slice_in_dim(row_total - picked, wide_index * row_count, row_count, axis=1)
        block = lax.dynamic_slice(
            full,
            (narrow_index * n_wide, 0, wide_index * row_count),
            (n_wide, micro, row_count),
        )
        scores = jnp.transpose(block, (1, 2, 0))
        grads = jnp.exp(own_scores - row_total) - (positives == own_index).astype(F32)
        token_weights = jnp.repeat(grads, query_len, axis=1).reshape(z.shape) / z
        grad_passage, grad_query = similarity_back(e, token_weights, queries, passages)
        grad_query = grad_query.reshape(-1, 2, query_rows, embed_width)
    grad_passage = grad_passage.reshape(passage_rows, embed_width)
    back_p = mlp_back(
        grad_passage,
        kept_p,
        vec,
        weights,
        micro * own_passages,
        total,
        0,
        None,
        grad_query if together else None,
        sizes if together else None,
    )
    grad_query = back_p[6] if together else exchange(grad_query, n_wide, n_narrow)
    back_q = mlp_back(
        grad_query, kept_q, vec, weights, 1, total, passage_rows, back_p, None, None
    )
    gp, go, gi, _, ga, sums_q = back_q[:6]
    part = width // n_wide
    if part == 96 and n_narrow == 4 and micro * own_passages == 2 and act.shape[1] == 4 * width:
        summed, grad_p, grad_q = backward_tail(
            (act, go, first_low, gi, x_passage, x_query, ctx, ga, final_low, gp),
            (*kept_p[:3], back_p[3], kept_p[3]),
            (*kept_q[:3], back_q[3], kept_q[3]),
            (out_weight, query_weight, key_weight, value_weight),
            (back_p[5], sums_q),
            n_wide,
        )
        r_q, r_k, r_v, r_out, r_inner, r_outer, r_linear, vectors, grad_p, grad_q = unpack(
            summed, grad_p, grad_q, part, embed_width
        )
        own = lax.dynamic_slice_in_dim(vectors[:8], wide_index * part, part, axis=1)
        v_q, v_v, v_o, v_g1, v_s1, v_2, v_g2, v_s2 = (
            own[row] for row in (0, 1, ROW_BO, ROW_G1, ROW_S1, ROW_B2, ROW_G2, ROW_S2)
        )
        v_i = lax.dynamic_slice_in_dim(
            vectors[ROW_BI : ROW_BI + 4].reshape(-1), wide_index * 4 * part, 4 * part
        )
    else:
        att_p = attention_back(
            ga, back_p[3], kept_p, weights, micro * own_passages, total, 0, None
        )
        att_q = attention_back(ga, back_q[3], kept_q, weights, 1, total, passage_rows, att_p[0])
        gqkv, grad_p, grad_q = att_q[0], att_p[1], att_q[1]

        def reduce(value):
            piece = lax.psum_scatter(value.astype(BF16), everyone, scatter_dimension=0, tiled=True)
            return lax.all_gather(piece, "narrow", axis=0, tiled=True).astype(F32)

        def vector(rows):
            flat = rows.reshape(-1)
            share = flat.shape[0] // n_wide
            return lax.dynamic_slice_in_dim(flat, wide_index * share, share)

        sums = jnp.concatenate([back_p[5] + sums_q, att_p[2] + att_q[2]], axis=0)
        sums = lax.psum(sums, everyone)
        x_all = jnp.concatenate([x_passage, x_query], axis=0)
        pairs = ((act, go), (first_low, gi), (final_low, gp), (ctx, ga), (x_all, gqkv))
        r_outer, r_inner, r_linear, r_out, r_qkv = (
            reduce(outer(*pair)) for pair in pairs
        )
        r_q, r_k, r_v = (r_qkv[:, index * width : (index + 1) * width] for index in range(3))
        v_q, v_v, v_o, v_g1, v_s1, v_2, v_g2, v_s2 = (
            vector(sums[pick])
            for pick in (16, 17, ROW_BO, ROW_G1, ROW_S1, ROW_B2, ROW_G2, ROW_S2)
        )
        v_i = vector(sums[ROW_BI : ROW_BI + 4])
    return (
        scores,
        losses,
        grad_q.reshape(query_states.shape),
        grad_p.reshape(passage_states.shape),
        r_q,
        v_q,
        r_k,
        r_v,
        v_v,
        r_out,
        v_o,
        v_g1,
        v_s1,
        r_inner,
        v_i,
        r_outer,
        v_2,
        v_g2,
        v_s2,
        r_linear,
    )


def solution(mesh):
    return jax.shard_map(
        local,
        mesh=mesh,
        in_specs=(
            P(None, ("wide", "narrow"), None, None),
            P(None, ("narrow", "wide"), None, None),
        )
        + (P(),) * 18,
        out_specs=(
            P(None, "wide", "narrow"),
            P(None, "wide"),
            P(None, ("wide", "narrow"), None, None),
            P(None, ("narrow", "wide"), None, None),
            P("wide", None),
            P("wide"),
            P("wide", None),
            P("wide", None),
            P("wide"),
            P("wide", None),
            P("wide"),
            P("wide"),
            P("wide"),
            P("wide", None),
            P("wide"),
            P("wide", None),
            P("wide"),
            P("wide"),
            P("wide"),
            P("wide", None),
        ),
        check_vma=False,
    )
```
